32 devices in a mesh: seq: 4 (over y, x), fsdp: 8 (over z, core).
Axes of the slice: x: 2, y: 2, z: 4, core: 2. Of those that a mesh axis runs over, the one named last changes fastest.
Arguments:
- inputs: bfloat16 [8, 1024, 2048], P('fsdp', 'seq'), may hold values from -6 to 6
- out_grad: bfloat16 [8, 1024, 2048], P('fsdp', 'seq'), may hold values from -6 to 6
- doc_ids: int32 [8, 1024], P('fsdp'), may hold values from 0 to 7, never falling along the last dimension, each value on 1 to 512 neighbouring positions
- routes: int32 [8, 1024, 8], P('fsdp', 'seq'), may hold values from 0 to 15, all different within a row; in each aligned block of 256 rows (0 to 255, 256 to 511, ..., all dimensions but the last counted through in order) at most 136 rows name the same one
- w_query: bfloat16 [2048, 2048], P(('seq', 'fsdp')), may hold values from -0.125 to 0.125
- w_key: bfloat16 [2048, 2048], P(('seq', 'fsdp')), may hold values from -0.125 to 0.125
- w_value: bfloat16 [2048, 2048], P(('seq', 'fsdp')), may hold values from -0.125 to 0.125
- w_output: bfloat16 [2048, 2048], P(('seq', 'fsdp')), may hold values from -1 to 1
- w_router: bfloat16 [2048, 16], P(('seq', 'fsdp')), may hold values from -0.0625 to 0.0625
- attn_gain: bfloat16 [2048], P(('seq', 'fsdp')), may hold values from 0.099609375 to 1.8984375
- ffn_gain: bfloat16 [2048], P(('seq', 'fsdp')), may hold values from 0.099609375 to 1.8984375
- query_gain: bfloat16 [2048], P(('seq', 'fsdp')), may hold values from 0.099609375 to 1.8984375
- key_gain: bfloat16 [2048], P(('seq', 'fsdp')), may hold values from 0.099609375 to 1.8984375
- w_gate: bfloat16 [16, 2048, 1024], P('fsdp', 'seq'), may hold values from -0.125 to 0.125
- w_up: bfloat16 [16, 2048, 1024], P('fsdp', 'seq'), may hold values from -0.125 to 0.125
- w_down: bfloat16 [16, 1024, 2048], P('fsdp', 'seq'), may hold values from -1 to 1
Outputs:
- output: bfloat16 [8, 1024, 2048], P('fsdp', 'seq')
- input_grad: float32 [8, 1024, 2048], P('fsdp', 'seq')
- g_query: float32 [2048, 2048], P(('seq', 'fsdp'))
- g_key: float32 [2048, 2048], P(('seq', 'fsdp'))
- g_value: float32 [2048, 2048], P(('seq', 'fsdp'))
- g_output: float32 [2048, 2048], P(('seq', 'fsdp'))
- g_router: float32 [2048, 16], P(('seq', 'fsdp'))
- g_attn_gain: float32 [2048], P(('seq', 'fsdp'))
- g_ffn_gain: float32 [2048], P(('seq', 'fsdp'))
- g_query_gain: float32 [2048], P(('seq', 'fsdp'))
- g_key_gain: float32 [2048], P(('seq', 'fsdp'))
- g_gate: float32 [16, 2048, 1024], P('fsdp', 'seq')
- g_up: float32 [16, 2048, 1024], P('fsdp', 'seq')
- g_down: float32 [16, 1024, 2048], P('fsdp', 'seq')
The draws below stay inside these ranges and needn't reach their ends.
Inputs may be any that keep to these rules, and one draw needn't show every extreme that they name: `doc_ids`: document numbers never fall along a sequence; a document has 1 to 512 tokens, and one of them exactly that many. `routes`: each token names 8 different experts. Within the 256 tokens of one device (aligned blocks), no expert is named by more than 136 tokens, a bound that some block reaches.
All inputs are finite; a program needn't handle non-finite values.
Results may differ from the reference program's by a relative error of at most 0.017.
Values may be sent and summed in bfloat16 or wider, within the bound.
A program may use at most 320 MiB of HBM per device.

```python
import math
import jax
import jax.numpy as jnp
import numpy as np
from jax import lax

D = 2048
HEADS = 16
H = 1024
EXPERTS = 16
TOP = 8
DOCS = 8
TOK_DEV = 256
SEQ_LEN = 1024
SEQS = 8
CAP = 136
N_SEQ = 4


def block_levels(key, dims, cuts, low, high):
    def one(position, blocks):
        heights = jax.random.uniform(jax.random.fold_in(jax.random.fold_in(key, 6), position), (blocks,), jnp.float32, low / len(cuts), high / len(cuts))
        return jnp.repeat(jnp.exp(heights), dims[position] // blocks).reshape((-1,) + (1,) * (len(dims) - position - 1))

    gain = one(*cuts[0])
    for cut in cuts[1:]:
        gain = gain * one(*cut)
    return gain


def length_profile(count, total, most, slope):
    loads = [(1 << 20) // math.isqrt(rank ** slope) + 1 for rank in range(2, count + 1)]
    rest, given = total - most - (count - 1), [1] * (count - 1)
    while rest > 0:
        movable = [i for i in range(count - 1) if given[i] < most]
        mass, left = sum([loads[i] for i in movable]), rest
        for i in movable:
            extra = min(most - given[i], max(1, left * loads[i] // mass), rest)
            given[i] = given[i] + extra
            rest = rest - extra
    return np.array([most] + given)


def uneven_parts(own_key, amount, total, reach, skew):
    if amount == 2:
        one = jax.random.randint(own_key, (), max(1, total - reach), min(reach, total - 1) + 1)
        return jnp.stack([one, total - one])
    tallies = jnp.asarray(length_profile(amount, total, reach, skew), jnp.int32)
    pairs = (amount - 1) // 2
    source_of, sink = tallies[1:1 + 2 * pairs:2], tallies[2:2 + 2 * pairs:2]
    slack = jnp.minimum(source_of - 1, reach - sink)
    passed = jax.random.randint(jax.random.fold_in(own_key, 1), (pairs,), 0, 1 << 20) % (slack + 1)
    tallies = tallies.at[1:1 + 2 * pairs:2].set(source_of - passed).at[2:2 + 2 * pairs:2].set(sink + passed)
    return tallies[jax.random.permutation(jax.random.fold_in(own_key, 2), amount)]


def deal_out(stream_key, own, number, rows, count, top, most, slope):
    order = jax.random.permutation(stream_key, count)
    crowded, ordinary = portions_of(count, rows * top, most, slope, True), portions_of(count, rows * top, most, slope, False)
    places = jnp.arange(count)

    def named(tallies, offset_by):
        used = int((tallies > 0).sum())
        fixed = max(1, used // 4)
        moved = fixed + (places - fixed + offset_by * (used - fixed)) % max(1, count - fixed)
        return jnp.zeros((count,), jnp.int32).at[order[jnp.where(places < fixed, places, moved)]].set(jnp.asarray(tallies, jnp.int32))

    tallies = jnp.where(number % 4 == 0, named(crowded, number // 4), named(ordinary, number - number // 4 - 1))
    mixed = jax.random.permutation(jax.random.fold_in(own, 3), count)
    giver, receiver = mixed[0:count // 2 * 2:2], mixed[1:count // 2 * 2:2]
    room = jnp.minimum(tallies[giver] - 1, most - tallies[receiver]) // 2
    room = jnp.where((giver == order[0]) | (receiver == order[0]) | (tallies[receiver] == 0), 0, jnp.maximum(room, 0))
    moved = jax.random.randint(jax.random.fold_in(own, 4), (count // 2,), 0, 1 << 20) % (room + 1)
    tallies = tallies.at[giver].add(-moved).at[receiver].add(moved)
    items = jnp.searchsorted(jnp.cumsum(tallies), jnp.arange(rows * top), side="right").astype(jnp.int32)
    grid = items.reshape(top, rows).T
    grid = grid[jax.random.permutation(jax.random.fold_in(own, 1), rows)]
    offset_by = jax.random.randint(jax.random.fold_in(own, 2), (rows, 1), 0, top)
    return jnp.take_along_axis(grid, (jnp.arange(top)[None, :] + offset_by) % top, axis=1)


def portions_of(number_of, total, most, lean, full):
    loads = [(1 << 20) // math.isqrt(standing ** lean) + 1 for standing in range(1, number_of + 1)]
    largest = most if full else min(most, max(-(-total // number_of), total * loads[0] // sum(loads)))
    least = 1 if total - largest >= number_of - 1 else 0
    holding, spare = [largest] + [least] * (number_of - 1), total - largest - least * (number_of - 1)
    while spare > 0:
        free = [i for i in range(1, number_of) if holding[i] < largest] or [i for i in range(1, number_of) if holding[i] < most]
        pool, left = sum([loads[i] for i in free]), spare
        for i in free:
            addition = min(most - holding[i], max(1, left * loads[i] // pool), spare)
            holding[i] = holding[i] + addition
            spare = spare - addition
    return np.array(holding)


def scatter_about(stream_key, shape, width, bound, pieces=(), kind=jnp.bfloat16):
    array = width * jax.random.normal(stream_key, shape, jnp.float32)
    if pieces:
        array = array * block_levels(stream_key, shape, pieces, -0.22, 0.18)
    return jnp.clip(array, -bound, bound).astype(kind)


def setup_inputs(seed: int = 0) -> dict:
    key_list = jax.random.split(jax.random.key(seed), 17)
    inputs = scatter_about(key_list[0], (SEQS, SEQ_LEN, D), 1.0, 6.0, ((0, 8), (1, 4)))
    out_grad = scatter_about(key_list[1], (SEQS, SEQ_LEN, D), 1.0, 6.0, ((0, 8), (1, 4)))
    doc_ids = jax.vmap(lambda own: jnp.searchsorted(jnp.cumsum(uneven_parts(own, DOCS, SEQ_LEN, SEQ_LEN // 2, 2)), jnp.arange(SEQ_LEN), side="right"))(jax.random.split(key_list[2], SEQS)).reshape((SEQS, SEQ_LEN)).astype(jnp.int32)
    routes_keys = jax.random.split(jax.random.fold_in(key_list[3], 1), SEQS * SEQ_LEN // TOK_DEV)
    routes_turns = jax.random.permutation(jax.random.fold_in(key_list[3], 3), SEQS * SEQ_LEN // TOK_DEV)
    routes = jax.vmap(lambda own, number: deal_out(jax.random.fold_in(key_list[3], 2), own, number, TOK_DEV, EXPERTS, TOP, CAP, 1))(routes_keys, routes_turns).reshape((SEQS, SEQ_LEN, TOP))
    w_query = scatter_about(key_list[4], (D, D), D ** -0.5, 0.125, ((0, 32),))
    w_key = scatter_about(key_list[5], (D, D), D ** -0.5, 0.125, ((0, 32),))
    w_value = scatter_about(key_list[6], (D, D), D ** -0.5, 0.125, ((0, 32),))
    w_output = scatter_about(key_list[7], (D, D), (D // 64) ** -0.5, 1.0, ((0, 32),))
    w_router = scatter_about(key_list[8], (D, EXPERTS), (4 * D) ** -0.5, 0.0625, ((0, 32),))
    attn_gain = jnp.clip(1.0 + 0.18 * jax.random.normal(key_list[9], (D,), jnp.float32), 0.099609375, 1.8984375).astype(jnp.bfloat16)
    ffn_gain = jnp.clip(1.0 + 0.18 * jax.random.normal(key_list[10], (D,), jnp.float32), 0.099609375, 1.8984375).astype(jnp.bfloat16)
    query_gain = jnp.clip(1.0 + 0.18 * jax.random.normal(key_list[11], (D,), jnp.float32), 0.099609375, 1.8984375).astype(jnp.bfloat16)
    key_gain = jnp.clip(1.0 + 0.18 * jax.random.normal(key_list[12], (D,), jnp.float32), 0.099609375, 1.8984375).astype(jnp.bfloat16)
    w_gate = scatter_about(key_list[13], (EXPERTS, D, H), D ** -0.5, 0.125, ((0, 8), (1, 4)))
    w_up = scatter_about(key_list[14], (EXPERTS, D, H), D ** -0.5, 0.125, ((0, 8), (1, 4)))
    w_down = scatter_about(key_list[15], (EXPERTS, H, D), (H // 32) ** -0.5, 1.0, ((0, 8), (1, 4)))
    return {"inputs": inputs, "out_grad": out_grad, "doc_ids": doc_ids, "routes": routes, "w_query": w_query, "w_key": w_key, "w_value": w_value, "w_output": w_output, "w_router": w_router, "attn_gain": attn_gain, "ffn_gain": ffn_gain, "query_gain": query_gain, "key_gain": key_gain, "w_gate": w_gate, "w_up": w_up, "w_down": w_down}


EPSILON = 1e-05
ROPE_BASE = 10000.0
MASKED_OUT = -1e+30
PRECISE = lax.Precision.HIGHEST

@jax.custom_vjp
def low(v):
    return lax.optimization_barrier(v.astype(jnp.bfloat16)).astype(jnp.float32)

@jax.custom_vjp
def low_back(v):
    return v

def low_keep(v):
    return (low(v), None)

def low_pass(kept, grad):
    return (grad,)

def back_keep(v):
    return (v, None)

def back_low(kept, grad):
    return (low(grad),)
low.defvjp(low_keep, low_pass)
low_back.defvjp(back_keep, back_low)

def rms_scale(vector, gain_row):
    return vector * lax.rsqrt(lax.optimization_barrier(jnp.mean(vector * vector, axis=-1, keepdims=True)) + EPSILON) * gain_row

def rope_tables(positions, head_dim):
    half_dim = head_dim // 2
    inverse = ROPE_BASE ** (-(jnp.arange(half_dim, dtype=jnp.float32) * 2.0 / head_dim))
    angles = positions.astype(jnp.float32)[:, None] * inverse[None, :]
    angles = jnp.concatenate([angles, angles], axis=-1)
    return (jnp.cos(angles), jnp.sin(angles))

def rotate_heads(vector, cos_table, sin_table):
    rows_here = vector.shape[0]
    split = vector.reshape(rows_here, HEADS, -1)
    half_dim = split.shape[2] // 2
    turned = jnp.concatenate([-split[..., half_dim:], split[..., :half_dim]], axis=-1)
    return (split * cos_table[:, None, :] + turned * sin_table[:, None, :]).reshape(rows_here, -1)

def query_path(raw_rows, gain_row, cos_table, sin_table):
    return rotate_heads(rms_scale(raw_rows, gain_row), cos_table, sin_table)

def product(left, right):
    return jnp.dot(left, right, precision=PRECISE, preferred_element_type=jnp.float32)

def softmax_rows(scores):
    shifted = jnp.exp(scores - lax.optimization_barrier(jnp.max(scores, axis=-1, keepdims=True)))
    return shifted / lax.optimization_barrier(jnp.sum(shifted, axis=-1, keepdims=True))

def silu_value(vector):
    return vector / (1.0 + jnp.exp(-vector))

def slot_tables(route_rows):
    per_block = TOK_DEV * TOP
    flat_routes = route_rows.reshape(N_SEQ, per_block)
    onehot = (flat_routes[:, :, None] == jnp.arange(EXPERTS, dtype=jnp.int32)[None, None, :]).astype(jnp.int32)
    earlier = jnp.cumsum(onehot, axis=1) - onehot
    slot_pos = lax.optimization_barrier(jnp.sum(earlier * onehot, axis=2))
    block_ids = jnp.arange(N_SEQ, dtype=jnp.int32)[:, None]
    places = (flat_routes * (N_SEQ * CAP) + block_ids * CAP + slot_pos).reshape(-1).astype(jnp.int32)
    count_all = N_SEQ * per_block
    owners = jnp.full((EXPERTS * N_SEQ * CAP,), count_all, jnp.int32).at[places].set(jnp.arange(count_all, dtype=jnp.int32))
    return (places, (owners // TOP).astype(jnp.int32))

def forward(params, rows_in, doc_row, places, token_of, route_rows):
    w_q, w_k, w_v, w_o, w_r, gain_a, gain_f, gain_q, gain_k, w_g, w_u, w_d = params
    seq_len = rows_in.shape[0]
    model_width = rows_in.shape[1]
    head_dim = model_width // HEADS
    h1_low = low(rms_scale(rows_in, gain_a))
    q_raw = low_back(product(h1_low, w_q))
    k_raw = low_back(product(h1_low, w_k))
    v_low = low(low_back(product(h1_low, w_v)))
    cos_table, sin_table = rope_tables(jnp.arange(seq_len, dtype=jnp.int32), head_dim)
    q_low = low(low_back(query_path(q_raw, gain_q, cos_table, sin_table)))
    k_low = low(low_back(query_path(k_raw, gain_k, cos_table, sin_table)))
    queries = q_low.reshape(seq_len, HEADS, head_dim)
    keys = k_low.reshape(seq_len, HEADS, head_dim)
    values = v_low.reshape(seq_len, HEADS, head_dim)
    raw_scores = jnp.einsum('qhd,khd->hqk', queries, keys, precision=PRECISE) * head_dim ** (-0.5)
    scores = low_back(raw_scores)
    places_seq = jnp.arange(seq_len, dtype=jnp.int32)
    allowed = (doc_row[:, None] == doc_row[None, :]) & (places_seq[None, :] <= places_seq[:, None])
    probs = softmax_rows(jnp.where(allowed[None], scores, MASKED_OUT))
    heads_out = jnp.einsum('hqk,khd->qhd', low(probs), values, precision=PRECISE).reshape(seq_len, model_width)
    attended = low(low_back(heads_out))
    x_mid = rows_in + low_back(product(attended, w_o))
    h2_low = low(rms_scale(x_mid, gain_f))
    gate_probs = softmax_rows(product(h2_low, w_r))
    gates = jnp.take_along_axis(gate_probs, route_rows, axis=1)
    padded = jnp.concatenate([h2_low, jnp.zeros((1, model_width), h2_low.dtype)], axis=0)
    expert_in = low_back(jnp.take(padded, token_of, axis=0)).reshape(EXPERTS, -1, model_width)
    gate_h = low_back(jnp.einsum('erd,edh->erh', expert_in, w_g, precision=PRECISE))
    up_h = low_back(jnp.einsum('erd,edh->erh', expert_in, w_u, precision=PRECISE))
    act_low = low(silu_value(gate_h) * up_h)
    expert_out = low(low_back(jnp.einsum('erh,ehd->erd', act_low, w_d, precision=PRECISE)))
    chosen = jnp.take(expert_out.reshape(-1, model_width), places, axis=0).reshape(seq_len, TOP, model_width)
    return x_mid + jnp.einsum('tk,tkd->td', gates, chosen, precision=PRECISE)

def add_pair(first_part, second_part):
    return first_part + second_part

def reference(inputs, out_grad, doc_ids, routes, w_query, w_key, w_value, w_output, w_router, attn_gain, ffn_gain, query_gain, key_gain, w_gate, w_up, w_down):
    params = tuple((weight.astype(jnp.float32) for weight in (w_query, w_key, w_value, w_output, w_router, attn_gain, ffn_gain, query_gain, key_gain, w_gate, w_up, w_down)))

    def one_sequence(totals, item):
        rows_in, grad_rows, doc_row, route_rows = item
        places, token_of = slot_tables(route_rows)

        def run_layer(prm, rows_float):
            return forward(prm, rows_float, doc_row, places, token_of, route_rows)
        result, pull_back = jax.vjp(run_layer, params, rows_in.astype(jnp.float32))
        grads, grad_in = pull_back(grad_rows.astype(jnp.float32))
        totals = jax.tree.map(add_pair, totals, grads)
        return (totals, (result.astype(jnp.bfloat16), grad_in))
    start = jax.tree.map(jnp.zeros_like, params)
    totals, (outputs, in_grads) = lax.scan(one_sequence, start, (inputs, out_grad, doc_ids, routes))
    return (outputs, in_grads, totals[0], totals[1], totals[2], totals[3], totals[4], totals[5], totals[6], totals[7], totals[8], totals[9], totals[10], totals[11])
```

```python
from functools import partial

import jax
import jax.numpy as jnp
from jax import lax
from jax.experimental import pallas as pl
from jax.experimental.pallas import tpu as pltpu
from jax.sharding import PartitionSpec as P

CAP = 136
HEAD = 128
EPSILON = 1e-05
ROPE_BASE = 10000.0
MASKED_OUT = -1e30
ANY = pl.ANY
MESH = pl.DeviceIdType.MESH
DMA = pltpu.SemaphoreType.DMA
BF = jnp.bfloat16
F32 = jnp.float32


def remote(src, dst, send, recv, **where):
    return pltpu.make_async_remote_copy(
        src_ref=src, dst_ref=dst, send_sem=send, recv_sem=recv, device_id=where, device_id_type=MESH
    )


def greet(count, places, seq_count=1):
    i, p, sib = places
    barrier = pltpu.get_barrier_semaphore()
    pl.semaphore_signal(barrier, inc=1, device_id={"fsdp": sib}, device_id_type=MESH)
    here = lax.axis_index("seq")
    for d in range(1, seq_count):
        peer = lax.rem(here + d, seq_count)
        pl.semaphore_signal(barrier, inc=1, device_id={"seq": peer}, device_id_type=MESH)

    @pl.when(p > 0)
    def _():
        pl.semaphore_signal(barrier, inc=1, device_id={"fsdp": i - 2}, device_id_type=MESH)

    @pl.when(p < count - 1)
    def _():
        pl.semaphore_signal(barrier, inc=1, device_id={"fsdp": i + 2}, device_id_type=MESH)

    last = count - 1
    pl.semaphore_wait(barrier, seq_count + (p + last) // count + (last - p + last) // count)


def slot_of(ref, axis, index):
    return ref.at[index] if axis == 0 else ref.at[:, index]


class LineGather:
    def __init__(self, count, places, refs, axes, send_r, send_l, send_s, recv):
        self.count, self.places = count, places
        self.refs, self.axes = refs, axes
        self.sems = (send_r, send_l, send_s, recv)

    def copy(self, a, slot, kind, t, device):
        send = self.sems[kind].at[a, t]
        ref = slot_of(self.refs[a], self.axes[a], slot)
        return remote(ref, ref, send, self.sems[3].at[a, slot], fsdp=device)

    def first(self, a):
        i, p, sib = self.places

        @pl.when(p < self.count - 1)
        def _():
            self.copy(a, i, 0, 0, i + 2).start()

        @pl.when(p > 0)
        def _():
            self.copy(a, i, 1, 0, i - 2).start()

        self.copy(a, i, 2, 0, sib).start()

    def forward(self, t):
        i, p, sib = self.places
        count = self.count
        for a in range(len(self.refs)):

            @pl.when(p - t >= 0)
            def _():
                slot = i - 2 * t
                self.copy(a, slot, 0, t, sib).wait_recv()

                @pl.when(p < count - 1)
                def _():
                    self.copy(a, slot, 0, t, i + 2).start()

                self.copy(a, slot, 2, t, sib).start()

            @pl.when(p + t < count)
            def _():
                slot = i + 2 * t
                self.copy(a, slot, 1, t, sib).wait_recv()

                @pl.when(p > 0)
                def _():
                    self.copy(a, slot, 1, t, i - 2).start()

                self.copy(a, slot, 2, count + t, sib).start()

    def finish(self):
        i, p, sib = self.places
        count = self.count
        for a in range(len(self.refs)):
            for q in range(count):
                self.copy(a, 2 * q + lax.rem(sib, 2), 2, 0, sib).wait_recv()
            self.copy(a, i, 2, 0, sib).wait_send()

            @pl.when(p < count - 1)
            def _():
                self.copy(a, i, 0, 0, i + 2).wait_send()

            @pl.when(p > 0)
            def _():
                self.copy(a, i, 1, 0, i - 2).wait_send()

            for t in range(1, count):

                @pl.when(p - t >= 0)
                def _():
                    slot = i - 2 * t

                    @pl.when(p < count - 1)
                    def _():
                        self.copy(a, slot, 0, t, i + 2).wait_send()

                    self.copy(a, slot, 2, t, sib).wait_send()

                @pl.when(p + t < count)
                def _():
                    slot = i + 2 * t

                    @pl.when(p > 0)
                    def _():
                        self.copy(a, slot, 1, t, i - 2).wait_send()

                    self.copy(a, slot, 2, count + t, sib).wait_send()


def line_sems(arrays, count):
    return [DMA((arrays, count)), DMA((arrays, count)), DMA((arrays, 2 * count)), DMA((arrays, 2 * count))]


def where_am_i():
    i = lax.axis_index("fsdp")
    p = i // 2
    c = i % 2
    return i, p, 2 * p + 1 - c


def gather_kernel(count, x_ref, o_ref, hold, send_r, send_l, send_s, recv, local):
    places = where_am_i()
    i = places[0]
    take = pltpu.make_async_copy(x_ref, hold, local.at[0])
    take.start()
    greet(count, places)
    take.wait()
    put = pltpu.make_async_copy(hold, o_ref.at[i], local.at[1])
    put.start()
    put.wait()
    line = LineGather(count, places, [o_ref], [0], send_r, send_l, send_s, recv)
    line.first(0)
    for t in range(1, count):
        line.forward(t)
    line.finish()


def line_gather(block, shards, collective):
    count = shards // 2
    return pl.pallas_call(
        partial(gather_kernel, count),
        out_shape=jax.ShapeDtypeStruct((shards,) + block.shape, block.dtype),
        in_specs=[pl.BlockSpec(memory_space=ANY)],
        out_specs=pl.BlockSpec(memory_space=ANY),
        scratch_shapes=[pltpu.VMEM(block.shape, block.dtype)] + line_sems(1, count) + [DMA((2,))],
        compiler_params=pltpu.CompilerParams(collective_id=collective, has_side_effects=True),
        name="line_gather",
    )(block)


def start_kernel(count, seq_count, *refs):
    wq, wk, wv, wo, small, gains, routes = refs[:7]
    outs = refs[7:14]
    holds = refs[14:21]
    send_x, recv_x, local, send_r, send_l, send_s, recv = refs[21:]
    places = where_am_i()
    i = places[0]
    here = lax.axis_index("seq")
    width = wq.shape[1] // seq_count

    def columns(ref, peer):
        return ref.at[:, pl.ds(pl.multiple_of(peer * width, width), width)]

    own = [columns(wq, here), columns(wk, here), columns(wv, here), wo, small, gains, routes]
    for a in range(7):
        pltpu.make_async_copy(own[a], holds[a], local.at[a]).start()
    greet(count, places, seq_count)

    def piece(a, d):
        peer = lax.rem(here + d, seq_count)
        src = small if a == 4 else columns((wq, wk, wv)[a], peer)
        slot = 3 if a == 4 else a
        return remote(
            src, outs[a].at[here, i], send_x.at[slot, d - 1], recv_x.at[slot, d - 1], seq=peer
        )

    def arrived(a, d):
        origin = lax.rem(here + seq_count - d, seq_count)
        slot = 3 if a == 4 else a
        return remote(
            outs[a].at[origin, i],
            outs[a].at[origin, i],
            send_x.at[slot, d - 1],
            recv_x.at[slot, d - 1],
            seq=origin,
        )

    for a in (4, 0, 1, 2):
        for d in range(1, seq_count):
            piece(a, d).start()
    axes = [1, 1, 1, 0, 1, 0, 0]
    for a in (3, 5, 6, 4, 0, 1, 2):
        pltpu.make_async_copy(own[a], holds[a], local.at[a]).wait()
        target = outs[a].at[here, i] if axes[a] == 1 else outs[a].at[i]
        pltpu.make_async_copy(holds[a], target, local.at[a]).start()
    line = LineGather(count, places, outs, axes, send_r, send_l, send_s, recv)
    for a in (5, 6, 4, 0, 1, 2, 3):
        target = outs[a].at[here, i] if axes[a] == 1 else outs[a].at[i]
        pltpu.make_async_copy(holds[a], target, local.at[a]).wait()
        if axes[a] == 1:
            for d in range(1, seq_count):
                arrived(a, d).wait_recv()
        line.first(a)
    for t in range(1, count):
        line.forward(t)
    line.finish()
    for a in (4, 0, 1, 2):
        for d in range(1, seq_count):
            piece(a, d).wait_send()


def gather_start(arrays, seq_count, shards, collective):
    count = shards // 2
    wq, wk, wv, wo, small, gains, routes = arrays
    rows, model_width = wq.shape
    width = model_width // seq_count
    sheet = jax.ShapeDtypeStruct((seq_count, shards, rows, width), BF)
    shapes = [
        sheet,
        sheet,
        sheet,
        jax.ShapeDtypeStruct((shards,) + wo.shape, BF),
        jax.ShapeDtypeStruct((seq_count, shards) + small.shape, BF),
        jax.ShapeDtypeStruct((shards,) + gains.shape, BF),
        jax.ShapeDtypeStruct((shards,) + routes.shape, jnp.int32),
    ]
    holds = [pltpu.VMEM((rows, width), BF)] * 3 + [
        pltpu.VMEM(wo.shape, BF),
        pltpu.VMEM(small.shape, BF),
        pltpu.VMEM(gains.shape, BF),
        pltpu.VMEM(routes.shape, jnp.int32),
    ]
    return pl.pallas_call(
        partial(start_kernel, count, seq_count),
        out_shape=shapes,
        in_specs=[pl.BlockSpec(memory_space=ANY)] * 7,
        out_specs=[pl.BlockSpec(memory_space=ANY)] * 7,
        scratch_shapes=holds
        + [DMA((4, seq_count - 1)), DMA((4, seq_count - 1)), DMA((7,))]
        + line_sems(7, count),
        compiler_params=pltpu.CompilerParams(collective_id=collective, has_side_effects=True),
        name="gather_start",
    )(*arrays)


class LineScatter:
    def __init__(self, count, places, sources, axes, bufs, sems):
        self.count, self.places = count, places
        self.sources, self.axes = sources, axes
        self.own, self.sib, self.in_r, self.in_l = bufs
        self.sems = sems

    def load(self, a, q):
        i = self.places[0]
        src = slot_of(self.sources[a], self.axes[a], 2 * q + lax.rem(i, 2))
        return pltpu.make_async_copy(src, self.own[a].at[q], self.sems[6].at[a, q])

    def to_sib(self, a, q):
        sib = self.places[2]
        src = slot_of(self.sources[a], self.axes[a], 2 * q + lax.rem(sib, 2))
        return remote(src, self.sib[a].at[q], self.sems[2].at[a, q], self.sems[5].at[a, q], fsdp=sib)

    def right(self, a, q):
        i = self.places[0]
        return remote(
            self.own[a].at[q], self.in_r[a].at[q], self.sems[0].at[a, q], self.sems[3].at[a, q], fsdp=i + 2
        )

    def left(self, a, q):
        i = self.places[0]
        return remote(
            self.own[a].at[q], self.in_l[a].at[q], self.sems[1].at[a, q], self.sems[4].at[a, q], fsdp=i - 2
        )

    def order(self):
        order, low, high = [], 0, self.count - 1
        while low <= high:
            order.append(high)
            if low < high:
                order.append(low)
            low, high = low + 1, high - 1
        return order

    def begin_loads(self):
        for q in self.order():
            for a in range(len(self.sources)):
                self.load(a, q).start()

    def begin(self):
        for q in self.order():
            for a in range(len(self.sources)):
                self.to_sib(a, q).start()

    def add(self, a, q, others):
        own = self.own[a]
        lead = own.shape[1:-2]
        rows, width = own.shape[-2:]
        step = rows
        while step * width > 65536 and step % 16 == 0:
            step //= 2

        def strip(index):
            total = own[index].astype(F32) + self.sib[a][index].astype(F32)
            for other in others:
                total += other[a][index].astype(F32)
            own[index] = total.astype(own.dtype)

        def rows_of(prefix):
            if step == rows:
                strip(prefix)
                return

            @pl.loop(0, rows // step)
            def _(k):
                strip(prefix + (pl.ds(pl.multiple_of(k * step, step), step),))

        if lead:
            for b in range(lead[0]):
                rows_of((q, b))
        else:
            rows_of((q,))

    def ready(self, a, q):
        self.load(a, q).wait()
        self.to_sib(a, q).wait_recv()

    def run(self, after):
        i, p, sib = self.places
        count = self.count
        arrays = range(len(self.sources))
        for j in range(count - 1):
            q = count - 1 - j

            @pl.when(q > p)
            def _():
                for a in arrays:
                    self.ready(a, q)

                    @pl.when(p > 0)
                    def _():
                        self.right(a, q).wait_recv()
                        self.add(a, q, [self.in_r])

                    @pl.when(p == 0)
                    def _():
                        self.add(a, q, [])

                    self.right(a, q).start()

            @pl.when(j < p)
            def _():
                for a in arrays:
                    self.ready(a, j)

                    @pl.when(p < count - 1)
                    def _():
                        self.left(a, j).wait_recv()
                        self.add(a, j, [self.in_l])

                    @pl.when(p == count - 1)
                    def _():
                        self.add(a, j, [])

                    self.left(a, j).start()

        for q in range(count):

            @pl.when(q == p)
            def _():
                for a in arrays:
                    self.ready(a, q)
                    if q > 0:
                        self.right(a, q).wait_recv()
                    if q < count - 1:
                        self.left(a, q).wait_recv()
                    sides = ([self.in_r] if q > 0 else []) + ([self.in_l] if q < count - 1 else [])
                    self.add(a, q, sides)
                    after(a, q)

    def finish(self):
        i, p, sib = self.places
        for a in range(len(self.sources)):
            for q in range(self.count):
                self.to_sib(a, q).wait_send()

                @pl.when(q > p)
                def _():
                    self.right(a, q).wait_send()

                @pl.when(q < p)
                def _():
                    self.left(a, q).wait_send()


def scatter_kernel(count, x_ref, o_ref, own, sibling, in_r, in_l, s0, s1, s2, r0, r1, r2, local):
    places = where_am_i()
    line = LineScatter(
        count, places, [x_ref], [0], ([own], [sibling], [in_r], [in_l]), (s0, s1, s2, r0, r1, r2, local)
    )
    line.begin_loads()
    greet(count, places)
    line.begin()

    def after(a, q):
        out = pltpu.make_async_copy(own.at[q], o_ref, local.at[0, q])
        out.start()
        out.wait()

    line.run(after)
    line.finish()


def line_scatter(blocks, shards, collective):
    count = shards // 2
    block = blocks.shape[1:]
    return pl.pallas_call(
        partial(scatter_kernel, count),
        out_shape=jax.ShapeDtypeStruct(block, blocks.dtype),
        in_specs=[pl.BlockSpec(memory_space=ANY)],
        out_specs=pl.BlockSpec(memory_space=ANY),
        scratch_shapes=[pltpu.VMEM((count,) + block, blocks.dtype)] * 4 + [DMA((1, count))] * 7,
        compiler_params=pltpu.CompilerParams(
            collective_id=collective, has_side_effects=True, vmem_limit_bytes=48 << 20
        ),
        name="line_scatter",
    )(blocks)


def end_kernel(count, seq_count, *refs):
    sources = refs[:6]
    outs = refs[6:12]
    bufs = tuple(refs[12 + 6 * k : 18 + 6 * k] for k in range(4))
    landing = refs[36]
    sems = refs[37:44]
    send_x, recv_x, local = refs[44:]
    places = where_am_i()
    here = lax.axis_index("seq")
    width = sources[0].shape[3]
    line = LineScatter(count, places, sources, [1, 1, 1, 0, 1, 0], bufs, sems)
    line.begin_loads()
    greet(count, places, seq_count)
    line.begin()
    own = bufs[0]

    def at_home(a, block):
        if a == 4:
            return landing.at[block]
        start = pl.multiple_of(block * width, width)
        return outs[a].at[:, pl.ds(start, width)]

    def piece(a, q, d):
        peer = lax.rem(here + d, seq_count)
        slot = 3 if a == 4 else a
        return remote(
            own[a].at[q, peer], at_home(a, here), send_x.at[slot, d - 1], recv_x.at[slot, d - 1], seq=peer
        )

    def arrived(a, d):
        origin = lax.rem(here + seq_count - d, seq_count)
        slot = 3 if a == 4 else a
        return remote(
            at_home(a, origin), at_home(a, origin), send_x.at[slot, d - 1], recv_x.at[slot, d - 1], seq=origin
        )

    def after(a, q):
        if a in (3, 5):
            pltpu.make_async_copy(own[a].at[q], outs[a], local.at[a]).start()
        else:
            for d in range(1, seq_count):
                piece(a, q, d).start()
            pltpu.make_async_copy(own[a].at[q, here], at_home(a, here), local.at[a]).start()

    line.run(after)
    for q in range(count):

        @pl.when(q == places[1])
        def _():
            for a in range(6):
                if a in (3, 5):
                    pltpu.make_async_copy(own[a].at[q], outs[a], local.at[a]).wait()
                else:
                    pltpu.make_async_copy(own[a].at[q, here], at_home(a, here), local.at[a]).wait()
                    for d in range(1, seq_count):
                        piece(a, q, d).wait_send()
                        arrived(a, d).wait_recv()

    total = landing[0]
    for block in range(1, seq_count):
        total += landing[block]
    landing[0] = total
    last = pltpu.make_async_copy(landing.at[0], outs[4], local.at[4])
    last.start()
    last.wait()
    line.finish()


def scatter_end(arrays, seq_count, shards, collective):
    count = shards // 2
    gq, gk, gv, go, small, gains = arrays
    rows, width = gq.shape[2:]
    home = jax.ShapeDtypeStruct((rows, width * seq_count), BF)
    shapes = [
        home,
        home,
        home,
        jax.ShapeDtypeStruct(go.shape[1:], BF),
        jax.ShapeDtypeStruct(small.shape[2:], F32),
        jax.ShapeDtypeStruct(gains.shape[1:], F32),
    ]
    blocks = []
    for a in range(6):
        shape = arrays[a].shape
        block = (shape[0],) + shape[2:] if a in (0, 1, 2, 4) else shape[1:]
        blocks.append(pltpu.VMEM((count,) + block, arrays[a].dtype))
    return pl.pallas_call(
        partial(end_kernel, count, seq_count),
        out_shape=shapes,
        in_specs=[pl.BlockSpec(memory_space=ANY)] * 6,
        out_specs=[pl.BlockSpec(memory_space=ANY)] * 6,
        scratch_shapes=blocks * 4
        + [pltpu.VMEM((seq_count,) + small.shape[2:], F32)]
        + [DMA((6, count))] * 7
        + [DMA((4, seq_count - 1)), DMA((4, seq_count - 1)), DMA((6,))],
        compiler_params=pltpu.CompilerParams(
            collective_id=collective, has_side_effects=True, vmem_limit_bytes=56 << 20
        ),
        name="scatter_end",
    )(*arrays)


def greet_seq(seq_count):
    here = lax.axis_index("seq")
    barrier = pltpu.get_barrier_semaphore()
    for d in range(1, seq_count):
        peer = lax.rem(here + d, seq_count)
        pl.semaphore_signal(barrier, inc=1, device_id={"seq": peer}, device_id_type=MESH)
    pl.semaphore_wait(barrier, seq_count - 1)
    return here


def seq_scatter_kernel(seq_count, x_ref, o_ref, own, inbox, send, recv, local):
    take = pltpu.make_async_copy(x_ref.at[lax.axis_index("seq")], own, local)
    take.start()
    here = greet_seq(seq_count)
    copies = []
    for d in range(1, seq_count):
        peer = lax.rem(here + d, seq_count)
        copies.append(
            remote(x_ref.at[peer], inbox.at[d - 1], send.at[d - 1], recv.at[d - 1], seq=peer)
        )
    for copy in copies:
        copy.start()
    take.wait()
    for copy in copies:
        copy.wait_recv()
    rows = own.shape[0]
    step = min(32, rows)

    @pl.loop(0, rows // step)
    def _(k):
        strip = pl.ds(pl.multiple_of(k * step, step), step)
        total = own[strip, :].astype(F32)
        for d in range(seq_count - 1):
            total += inbox[d, strip, :].astype(F32)
        o_ref[strip, :] = total

    for copy in copies:
        copy.wait_send()


def seq_scatter(blocks, collective):
    seq_count = blocks.shape[0]
    block = blocks.shape[1:]
    return pl.pallas_call(
        partial(seq_scatter_kernel, seq_count),
        out_shape=jax.ShapeDtypeStruct(block, F32),
        in_specs=[pl.BlockSpec(memory_space=ANY)],
        out_specs=pl.BlockSpec(memory_space=pltpu.VMEM),
        scratch_shapes=[
            pltpu.VMEM(block, blocks.dtype),
            pltpu.VMEM((seq_count - 1,) + block, blocks.dtype),
            DMA((seq_count - 1,)),
            DMA((seq_count - 1,)),
            DMA,
        ],
        compiler_params=pltpu.CompilerParams(
            collective_id=collective, has_side_effects=True, vmem_limit_bytes=32 << 20
        ),
        name="seq_scatter",
    )(blocks)


def seq_sum_kernel(seq_count, x_ref, o_ref, inbox, send, recv):
    here = greet_seq(seq_count)
    copies = []
    for d in range(1, seq_count):
        peer = lax.rem(here + d, seq_count)
        copies.append(remote(x_ref, inbox.at[d - 1], send.at[d - 1], recv.at[d - 1], seq=peer))
    for copy in copies:
        copy.start()
    for copy in copies:
        copy.wait_recv()
    total = x_ref[...]
    for d in range(seq_count - 1):
        total += inbox[d]
    o_ref[...] = total
    for copy in copies:
        copy.wait_send()


def seq_sum(value, seq_count, collective):
    return pl.pallas_call(
        partial(seq_sum_kernel, seq_count),
        out_shape=jax.ShapeDtypeStruct(value.shape, F32),
        in_specs=[pl.BlockSpec(memory_space=pltpu.VMEM)],
        out_specs=pl.BlockSpec(memory_space=pltpu.VMEM),
        scratch_shapes=[
            pltpu.VMEM((seq_count - 1,) + value.shape, F32),
            DMA((seq_count - 1,)),
            DMA((seq_count - 1,)),
        ],
        compiler_params=pltpu.CompilerParams(collective_id=collective, has_side_effects=True),
        name="seq_sum",
    )(value)


def seq_gather_kernel(seq_count, x_ref, o_ref, hold, send, recv, local):
    take = pltpu.make_async_copy(x_ref, hold, local)
    take.start()
    here = greet_seq(seq_count)
    for d in range(1, seq_count):
        peer = lax.rem(here + d, seq_count)
        remote(x_ref, o_ref.at[here], send.at[d - 1], recv.at[d - 1], seq=peer).start()
    take.wait()
    put = pltpu.make_async_copy(hold, o_ref.at[here], local)
    put.start()
    put.wait()
    for d in range(1, seq_count):
        origin = lax.rem(here + seq_count - d, seq_count)
        remote(x_ref, o_ref.at[origin], send.at[d - 1], recv.at[d - 1], seq=origin).wait()


def seq_gather(block, seq_count, collective):
    return pl.pallas_call(
        partial(seq_gather_kernel, seq_count),
        out_shape=jax.ShapeDtypeStruct((seq_count,) + block.shape, block.dtype),
        in_specs=[pl.BlockSpec(memory_space=ANY)],
        out_specs=pl.BlockSpec(memory_space=ANY),
        scratch_shapes=[
            pltpu.VMEM(block.shape, block.dtype),
            DMA((seq_count - 1,)),
            DMA((seq_count - 1,)),
            DMA,
        ],
        compiler_params=pltpu.CompilerParams(collective_id=collective, has_side_effects=True),
        name="seq_gather",
    )(block)


def half_sign(shape):
    lane = lax.broadcasted_iota(jnp.int32, shape, 1)
    return jnp.where(lane < shape[1] // 2, -1.0, 1.0)


def turn(value):
    return pltpu.roll(value, value.shape[1] // 2, 1)


def block_probs(q_rows, keys, doc_col, doc_row, start, scale_by):
    end = keys.shape[0]
    scores = (
        lax.dot_general(q_rows, keys, (((1,), (1,)), ((), ())), preferred_element_type=F32) * scale_by
    )
    shape = scores.shape
    query_pos = start + lax.broadcasted_iota(jnp.int32, shape, 0)
    key_pos = lax.broadcasted_iota(jnp.int32, shape, 1)
    allowed = (doc_col == doc_row) & (key_pos <= query_pos)
    scores = jnp.where(allowed, scores, MASKED_OUT)
    weights = jnp.exp(scores - jnp.max(scores, axis=-1, keepdims=True))
    return weights * (1.0 / jnp.sum(weights, axis=-1, keepdims=True))


def attend_kernel(
    row_block, q_raw, k_raw, v_ref, rq, rk, gq, gk, cos, sin, doc_col, doc_row, o_ref, q_out, k_out
):
    seq_len = q_raw.shape[0]
    sign = half_sign(cos.shape)

    def rotated(raw, scale, gain):
        value = raw[...] * scale[...] * gain[...]
        return (value * cos[...] + turn(value) * (sin[...] * sign)).astype(BF)

    q_out[...] = rotated(q_raw, rq, gq)
    k_out[...] = rotated(k_raw, rk, gk)
    scale_by = HEAD ** (-0.5)
    for start in range(0, seq_len, row_block):
        end = start + row_block
        probs = block_probs(
            q_out[start:end, :], k_out[:end, :], doc_col[start:end, :], doc_row[:, :end], start, scale_by
        )
        o_ref[start:end, :] = jnp.dot(
            probs.astype(BF), v_ref[:end, :], preferred_element_type=F32
        ).astype(BF)


def attend(q_raw, k_raw, values, rq, rk, gq, gk, cos, sin, doc_col, doc_row):
    seq_len, width = q_raw.shape
    head = pl.BlockSpec((seq_len, HEAD), lambda h: (0, h))
    gain = pl.BlockSpec((1, HEAD), lambda h: (0, h))

    def whole(x):
        return pl.BlockSpec(x.shape, lambda h: (0, 0))

    out = jax.ShapeDtypeStruct((seq_len, width), BF)
    return pl.pallas_call(
        partial(attend_kernel, 256),
        grid=(width // HEAD,),
        out_shape=[out, out, out],
        in_specs=[head, head, head, whole(rq), whole(rk), gain, gain, whole(cos), whole(sin)]
        + [whole(doc_col), whole(doc_row)],
        out_specs=[head, head, head],
        compiler_params=pltpu.CompilerParams(vmem_limit_bytes=48 << 20),
        name="attend",
    )(q_raw, k_raw, values, rq, rk, gq, gk, cos, sin, doc_col, doc_row)


def attend_back_kernel(
    row_block,
    q_low,
    k_low,
    v_ref,
    do_ref,
    q_raw,
    k_raw,
    rq,
    rk,
    gq,
    gk,
    cos,
    sin,
    doc_col,
    doc_row,
    uq_ref,
    uk_ref,
    dv_ref,
    dots,
    gain_q,
    gain_k,
    dq_acc,
    dk_acc,
    dv_acc,
):
    seq_len = q_low.shape[0]
    scale_by = HEAD ** (-0.5)
    dk_acc[...] = jnp.zeros_like(dk_acc)
    dv_acc[...] = jnp.zeros_like(dv_acc)
    for start in range(0, seq_len, row_block):
        end = start + row_block
        rows = slice(start, end)
        probs = block_probs(
            q_low[rows, :], k_low[:end, :], doc_col[rows, :], doc_row[:, :end], start, scale_by
        )
        grad_rows = do_ref[rows, :]
        grad_probs = lax.dot_general(
            grad_rows, v_ref[:end, :], (((1,), (1,)), ((), ())), preferred_element_type=F32
        )
        centre = jnp.sum(probs * grad_probs, axis=-1, keepdims=True)
        grad_scores = (probs * (grad_probs - centre)).astype(BF)
        dq_acc[rows, :] = jnp.dot(grad_scores, k_low[:end, :], preferred_element_type=F32)
        over_rows = (((0,), (0,)), ((), ()))
        dk_acc[:end, :] += lax.dot_general(
            grad_scores, q_low[rows, :], over_rows, preferred_element_type=F32
        )
        dv_acc[:end, :] += lax.dot_general(
            probs.astype(BF), grad_rows, over_rows, preferred_element_type=F32
        )
    dv_ref[...] = dv_acc[...].astype(BF)
    sign = half_sign(cos.shape)

    def unrotated(acc, raw, scale, gain, u_ref, gain_ref, lane):
        low = (acc[...] * scale_by).astype(BF).astype(F32)
        back = low * cos[...] - turn(low * sin[...]) * sign
        gain_ref[...] = jnp.sum(back * raw[...] * scale[...], axis=0, keepdims=True)
        u = back * gain[...]
        u_ref[...] = u
        dot = jnp.sum(u * raw[...], axis=1, keepdims=True)

        @pl.when(pl.program_id(0) == 0)
        def _():
            dots[:, lane : lane + 1] = dot

        @pl.when(pl.program_id(0) > 0)
        def _():
            dots[:, lane : lane + 1] += dot

    unrotated(dq_acc, q_raw, rq, gq, uq_ref, gain_q, 0)
    unrotated(dk_acc, k_raw, rk, gk, uk_ref, gain_k, 1)


def attend_back(q_low, k_low, values, d_heads, q_raw, k_raw, rq, rk, gq, gk, cos, sin, doc_col, doc_row):
    seq_len, width = q_raw.shape
    head = pl.BlockSpec((seq_len, HEAD), lambda h: (0, h))
    gain = pl.BlockSpec((1, HEAD), lambda h: (0, h))

    def whole(x):
        return pl.BlockSpec(x.shape, lambda h: (0, 0))

    wide = jax.ShapeDtypeStruct((seq_len, width), F32)
    row = jax.ShapeDtypeStruct((1, width), F32)
    return pl.pallas_call(
        partial(attend_back_kernel, 256),
        grid=(width // HEAD,),
        out_shape=[
            wide,
            wide,
            jax.ShapeDtypeStruct((seq_len, width), BF),
            jax.ShapeDtypeStruct((seq_len, 2), F32),
            row,
            row,
        ],
        in_specs=[head] * 6
        + [whole(rq), whole(rk), gain, gain, whole(cos), whole(sin), whole(doc_col), whole(doc_row)],
        out_specs=[head, head, head, pl.BlockSpec((seq_len, 2), lambda h: (0, 0)), gain, gain],
        scratch_shapes=[pltpu.VMEM((seq_len, HEAD), F32)] * 3,
        compiler_params=pltpu.CompilerParams(vmem_limit_bytes=56 << 20),
        name="attend_back",
    )(q_low, k_low, values, d_heads, q_raw, k_raw, rq, rk, gq, gk, cos, sin, doc_col, doc_row)


def rope_tables(positions, head_dim):
    half_dim = head_dim // 2
    inverse = ROPE_BASE ** (-(jnp.arange(half_dim, dtype=F32) * 2.0 / head_dim))
    angles = positions.astype(F32)[:, None] * inverse[None, :]
    angles = jnp.concatenate([angles, angles], axis=-1)
    return (jnp.cos(angles), jnp.sin(angles))


def dot(left, right, sides=(1, 0), out=F32):
    return lax.dot_general(
        left, right, (((sides[0],), (sides[1],)), ((), ())), preferred_element_type=F32
    ).astype(out)


def inverse_rms(rows):
    return lax.rsqrt(jnp.mean(rows * rows, axis=-1, keepdims=True) + EPSILON)


def on_device(
    inputs,
    out_grad,
    doc_ids,
    routes,
    w_query,
    w_key,
    w_value,
    w_output,
    w_router,
    attn_gain,
    ffn_gain,
    query_gain,
    key_gain,
    w_gate,
    w_up,
    w_down,
):
    seq_count = lax.axis_size("seq")
    shards = lax.axis_size("fsdp")
    tok_rows, model_width = inputs.shape[1:]
    seq_len = tok_rows * seq_count
    rows = w_query.shape[0]
    width = model_width // seq_count
    local_experts = w_gate.shape[0]
    experts = w_router.shape[1]
    top_k = routes.shape[2]
    lanes = 128

    small = jnp.concatenate(
        [
            w_router,
            attn_gain[:, None],
            ffn_gain[:, None],
            jnp.zeros((rows, lanes - experts - 2), BF),
        ],
        axis=1,
    )
    gains = jnp.pad(jnp.stack([query_gain, key_gain]), ((0, 14), (0, lanes - rows)))
    routes_flat = routes.reshape(tok_rows * top_k // lanes, lanes)
    wq, wk, wv, wo, small_all, gains_all, routes_all = gather_start(
        (w_query, w_key, w_value, w_output, small, gains, routes_flat), seq_count, shards, 0
    )
    x_all = lax.all_gather(inputs[0], "seq", axis=0, tiled=True)
    full_gate = lax.all_gather(w_gate, "seq", axis=1, tiled=True)
    full_up = lax.all_gather(w_up, "seq", axis=1, tiled=True)
    full_down = lax.all_gather(w_down, "seq", axis=1, tiled=True)
    dy_all = lax.all_gather(out_grad[0], "fsdp", axis=0, tiled=False)

    wq = wq.reshape(model_width, width)
    wk = wk.reshape(model_width, width)
    wv = wv.reshape(model_width, width)
    wo = wo.reshape(width, model_width)
    small_all = small_all.reshape(model_width, lanes)
    w_r = small_all[:, :experts]
    gain_a = small_all[:, experts].astype(F32)
    gain_f = small_all[:, experts + 1].astype(F32)
    gq = gains_all[:, 0, :rows].reshape(1, width).astype(F32)
    gk = gains_all[:, 1, :rows].reshape(1, width).astype(F32)

    x_float = x_all.astype(F32)
    h1 = (x_float * inverse_rms(x_float) * gain_a).astype(BF)
    q_raw = dot(h1, wq)
    k_raw = dot(h1, wk)
    values = dot(h1, wv, out=BF)
    squares = jnp.stack([jnp.sum(q_raw * q_raw, axis=1), jnp.sum(k_raw * k_raw, axis=1)])
    squares = seq_sum(squares, seq_count, 1)
    scales = lax.rsqrt(squares / model_width + EPSILON)
    rq, rk = scales[0][:, None], scales[1][:, None]
    cos, sin = rope_tables(jnp.arange(seq_len, dtype=jnp.int32), HEAD)
    doc_row = doc_ids
    doc_col = doc_ids.reshape(seq_len, 1)
    attended, q_low, k_low = attend(q_raw, k_raw, values, rq, rk, gq, gk, cos, sin, doc_col, doc_row)
    projected = dot(attended, wo, out=BF).reshape(seq_count, tok_rows, model_width)
    rows_in = inputs[0].astype(F32)
    grad_rows = out_grad[0].astype(F32)
    x_mid = rows_in + seq_scatter(projected, 2)
    scale_f = inverse_rms(x_mid)
    h2 = (x_mid * scale_f * gain_f).astype(BF)

    h2_all = line_gather(h2, shards, 3)
    count = shards * tok_rows
    h2_flat = h2_all.reshape(count, model_width)
    logits = dot(h2_flat, w_r)
    shifted = jnp.exp(logits - jnp.max(logits, axis=-1, keepdims=True))
    gate_probs = shifted / jnp.sum(shifted, axis=-1, keepdims=True)
    routes_all = routes_all.reshape(shards, tok_rows, top_k)
    first_expert = lax.axis_index("fsdp") * local_experts
    expert_ids = jnp.arange(experts, dtype=jnp.int32)
    slots = jnp.arange(CAP, dtype=jnp.int32)

    out_parts = 0.0
    grad_parts = 0.0
    grad_probs = 0.0
    g_gate, g_up, g_down = [], [], []
    for e in range(local_experts):
        expert = first_expert + e
        is_expert = (expert_ids == expert).astype(F32)
        chosen = jnp.any(routes_all == expert, axis=2)
        place = jnp.cumsum(chosen.astype(jnp.int32), axis=1) - 1
        pick = (place[:, None, :] == slots[None, :, None]) & chosen[:, None, :]
        pick_low = pick.astype(BF)
        gate_rows = jnp.sum(gate_probs * is_expert, axis=1).reshape(shards, 1, tok_rows)
        gate_slots = jnp.sum(jnp.where(pick, gate_rows, 0.0), axis=2).reshape(shards * CAP, 1)

        def dispatch(blocks):
            picked = jnp.einsum("jct,jtd->jcd", pick_low, blocks, preferred_element_type=F32)
            return picked.astype(BF).reshape(shards * CAP, model_width)

        def collect(slot_rows):
            blocks = slot_rows.reshape(shards, CAP, model_width)
            return jnp.einsum("jct,jcd->jtd", pick_low, blocks, preferred_element_type=F32)

        expert_in = dispatch(h2_all)
        gate_h = dot(expert_in, full_gate[e])
        up_h = dot(expert_in, full_up[e])
        sigmoid = 1.0 / (1.0 + jnp.exp(-gate_h))
        silu = gate_h * sigmoid
        act = silu * up_h
        act_gated = (act * gate_slots).astype(BF)
        expert_out = dot(act_gated, full_down[e], out=BF)
        out_parts = out_parts + collect(expert_out)

        grad_slots = dispatch(dy_all)
        grad_act = dot(grad_slots, full_down[e], (1, 1))
        g_down.append(dot(act_gated, grad_slots, (0, 0), BF))
        grad_gate_slots = jnp.sum(act * grad_act, axis=1).reshape(shards, CAP, 1)
        grad_act = grad_act * gate_slots
        d_gate = (grad_act * up_h * sigmoid * (1.0 + gate_h * (1.0 - sigmoid))).astype(BF)
        d_up = (grad_act * silu).astype(BF)
        g_gate.append(dot(expert_in, d_gate, (0, 0), BF))
        g_up.append(dot(expert_in, d_up, (0, 0), BF))
        grad_in = (dot(d_gate, full_gate[e], (1, 1)) + dot(d_up, full_up[e], (1, 1))).astype(BF)
        grad_parts = grad_parts + collect(grad_in)
        grad_gates = jnp.sum(jnp.where(pick, grad_gate_slots, 0.0), axis=1).reshape(count, 1)
        grad_probs = grad_probs + grad_gates * is_expert

    grad_logits = gate_probs * (grad_probs - jnp.sum(gate_probs * grad_probs, axis=-1, keepdims=True))
    grad_logits_low = grad_logits.astype(BF)
    router_back = dot(grad_logits_low, w_r, (1, 1)).reshape(shards, tok_rows, model_width)
    router_part = dot(h2_flat, grad_logits_low, (0, 0))
    result = x_mid + lax.psum_scatter(
        out_parts.astype(BF).reshape(count, model_width), "fsdp", scatter_dimension=0, tiled=True
    ).astype(F32)
    grad_h2 = line_scatter((grad_parts + router_back).astype(BF), shards, 4).astype(F32)

    def spread(parts):
        return lax.psum_scatter(jnp.stack(parts), "seq", scatter_dimension=1, tiled=True).astype(F32)

    g_down, g_gate, g_up = spread(g_down), spread(g_gate), spread(g_up)

    u_rows = gain_f * grad_h2
    grad_mid = (
        grad_rows
        + scale_f * u_rows
        - x_mid * scale_f**3 * jnp.mean(u_rows * x_mid, axis=-1, keepdims=True)
    )
    ffn_part = jnp.sum(grad_h2 * x_mid * scale_f, axis=0)

    d_attn = seq_gather(grad_mid.astype(BF), seq_count, 5).reshape(seq_len, model_width)
    d_heads = dot(d_attn, wo, (1, 1), BF)
    u_q, u_k, dv_low, dots, gain_q_part, gain_k_part = attend_back(
        q_low, k_low, values, d_heads, q_raw, k_raw, rq, rk, gq, gk, cos, sin, doc_col, doc_row
    )
    dots = seq_sum(dots.T, seq_count, 6) / model_width

    def norm_back(u, raw, scale, product):
        return (scale * u - raw * (scale**3 * product[:, None])).astype(BF)

    dq_low = norm_back(u_q, q_raw, rq, dots[0])
    dk_low = norm_back(u_k, k_raw, rk, dots[1])
    grad_h1 = dot(dq_low, wq, (1, 1)) + dot(dk_low, wk, (1, 1)) + dot(dv_low, wv, (1, 1))
    grad_h1 = seq_scatter(grad_h1.astype(BF).reshape(seq_count, tok_rows, model_width), 7)

    sheet = (seq_count, shards, rows, width)
    small_part = jnp.concatenate(
        [router_part, ffn_part[:, None], jnp.zeros((model_width, lanes - experts - 1), F32)], axis=1
    ).reshape(seq_count, shards, rows, lanes)
    gains_part = jnp.stack([gain_q_part.reshape(shards, rows), gain_k_part.reshape(shards, rows)], axis=1)
    gains_part = jnp.pad(gains_part, ((0, 0), (0, 6), (0, lanes - rows)))
    g_query, g_key, g_value, g_output, g_small, g_gains = scatter_end(
        (
            dot(h1, dq_low, (0, 0), BF).reshape(sheet),
            dot(h1, dk_low, (0, 0), BF).reshape(sheet),
            dot(h1, dv_low, (0, 0), BF).reshape(sheet),
            dot(attended, d_attn, (0, 0), BF).reshape(shards, rows, model_width),
            small_part,
            gains_part,
        ),
        seq_count,
        shards,
        8,
    )
    g_query, g_key, g_value = (g_query.astype(F32), g_key.astype(F32), g_value.astype(F32))

    scale_a = inverse_rms(rows_in)
    u_rows = gain_a * grad_h1
    input_grad = (
        grad_mid
        + scale_a * u_rows
        - rows_in * scale_a**3 * jnp.mean(u_rows * rows_in, axis=-1, keepdims=True)
    )
    pairs = (
        w_query.astype(F32) * g_query + w_key.astype(F32) * g_key + w_value.astype(F32) * g_value
    )
    g_attn_gain = jnp.sum(pairs, axis=1) / attn_gain.astype(F32)

    return (
        result.astype(BF)[None],
        input_grad[None],
        g_query,
        g_key,
        g_value,
        g_output.astype(F32),
        g_small[:, :experts],
        g_attn_gain,
        g_small[:, experts],
        g_gains[0, :rows],
        g_gains[1, :rows],
        g_gate,
        g_up,
        g_down,
    )


def solution(mesh):
    rows = P("fsdp", "seq", None)
    sheet = P(("seq", "fsdp"), None)
    line = P(("seq", "fsdp"))
    return jax.shard_map(
        on_device,
        mesh=mesh,
        in_specs=(rows, rows, P("fsdp", None), rows) + (sheet,) * 5 + (line,) * 4 + (rows,) * 3,
        out_specs=(rows, rows) + (sheet,) * 5 + (line,) * 4 + (rows,) * 3,
        check_vma=False,
    )
```

```python
from functools import partial

import jax
import jax.numpy as jnp
from jax import lax
from jax.experimental import pallas as pl
from jax.experimental.pallas import tpu as pltpu
from jax.sharding import PartitionSpec as P

CAP = 136
HEAD = 128
EPSILON = 1e-05
ROPE_BASE = 10000.0
MASKED_OUT = -1e30
ANY = pl.ANY
MESH = pl.DeviceIdType.MESH
DMA = pltpu.SemaphoreType.DMA
BF = jnp.bfloat16
F32 = jnp.float32


def remote(src, dst, send, recv, **where):
    return pltpu.make_async_remote_copy(
        src_ref=src, dst_ref=dst, send_sem=send, recv_sem=recv, device_id=where, device_id_type=MESH
    )


def greet(count, places, seq_count=1):
    i, p, sib = places
    barrier = pltpu.get_barrier_semaphore()
    pl.semaphore_signal(barrier, inc=1, device_id={"fsdp": sib}, device_id_type=MESH)
    here = lax.axis_index("seq")
    for d in range(1, seq_count):
        peer = lax.rem(here + d, seq_count)
        pl.semaphore_signal(barrier, inc=1, device_id={"seq": peer}, device_id_type=MESH)

    @pl.when(p > 0)
    def _():
        pl.semaphore_signal(barrier, inc=1, device_id={"fsdp": i - 2}, device_id_type=MESH)

    @pl.when(p < count - 1)
    def _():
        pl.semaphore_signal(barrier, inc=1, device_id={"fsdp": i + 2}, device_id_type=MESH)

    last = count - 1
    pl.semaphore_wait(barrier, seq_count + (p + last) // count + (last - p + last) // count)


def slot_of(ref, axis, index):
    return ref.at[index] if axis == 0 else ref.at[:, index]


class LineGather:
    def __init__(self, count, places, refs, axes, send_r, send_l, send_s, recv):
        self.count, self.places = count, places
        self.refs, self.axes = refs, axes
        self.sems = (send_r, send_l, send_s, recv)

    def copy(self, a, slot, kind, t, device):
        send = self.sems[kind].at[a, t]
        ref = slot_of(self.refs[a], self.axes[a], slot)
        return remote(ref, ref, send, self.sems[3].at[a, slot], fsdp=device)

    def first(self, a):
        i, p, sib = self.places

        @pl.when(p < self.count - 1)
        def _():
            self.copy(a, i, 0, 0, i + 2).start()

        @pl.when(p > 0)
        def _():
            self.copy(a, i, 1, 0, i - 2).start()

        self.copy(a, i, 2, 0, sib).start()

    def forward(self, t):
        i, p, sib = self.places
        count = self.count
        for a in range(len(self.refs)):

            @pl.when(p - t >= 0)
            def _():
                slot = i - 2 * t
                self.copy(a, slot, 0, t, sib).wait_recv()

                @pl.when(p < count - 1)
                def _():
                    self.copy(a, slot, 0, t, i + 2).start()

                self.copy(a, slot, 2, t, sib).start()

            @pl.when(p + t < count)
            def _():
                slot = i + 2 * t
                self.copy(a, slot, 1, t, sib).wait_recv()

                @pl.when(p > 0)
                def _():
                    self.copy(a, slot, 1, t, i - 2).start()

                self.copy(a, slot, 2, count + t, sib).start()

    def finish(self):
        i, p, sib = self.places
        count = self.count
        for a in range(len(self.refs)):
            for q in range(count):
                self.copy(a, 2 * q + lax.rem(sib, 2), 2, 0, sib).wait_recv()
            self.copy(a, i, 2, 0, sib).wait_send()

            @pl.when(p < count - 1)
            def _():
                self.copy(a, i, 0, 0, i + 2).wait_send()

            @pl.when(p > 0)
            def _():
                self.copy(a, i, 1, 0, i - 2).wait_send()

            for t in range(1, count):

                @pl.when(p - t >= 0)
                def _():
                    slot = i - 2 * t

                    @pl.when(p < count - 1)
                    def _():
                        self.copy(a, slot, 0, t, i + 2).wait_send()

                    self.copy(a, slot, 2, t, sib).wait_send()

                @pl.when(p + t < count)
                def _():
                    slot = i + 2 * t

                    @pl.when(p > 0)
                    def _():
                        self.copy(a, slot, 1, t, i - 2).wait_send()

                    self.copy(a, slot, 2, count + t, sib).wait_send()


def line_sems(arrays, count):
    return [DMA((arrays, count)), DMA((arrays, count)), DMA((arrays, 2 * count)), DMA((arrays, 2 * count))]


def where_am_i():
    i = lax.axis_index("fsdp")
    p = i // 2
    c = i % 2
    return i, p, 2 * p + 1 - c


def gather_kernel(count, x_ref, o_ref, hold, send_r, send_l, send_s, recv, local):
    places = where_am_i()
    i = places[0]
    take = pltpu.make_async_copy(x_ref, hold, local.at[0])
    take.start()
    greet(count, places)
    take.wait()
    put = pltpu.make_async_copy(hold, o_ref.at[i], local.at[1])
    put.start()
    put.wait()
    line = LineGather(count, places, [o_ref], [0], send_r, send_l, send_s, recv)
    line.first(0)
    for t in range(1, count):
        line.forward(t)
    line.finish()


def line_gather(block, shards, collective):
    count = shards // 2
    return pl.pallas_call(
        partial(gather_kernel, count),
        out_shape=jax.ShapeDtypeStruct((shards,) + block.shape, block.dtype),
        in_specs=[pl.BlockSpec(memory_space=ANY)],
        out_specs=pl.BlockSpec(memory_space=ANY),
        scratch_shapes=[pltpu.VMEM(block.shape, block.dtype)] + line_sems(1, count) + [DMA((2,))],
        compiler_params=pltpu.CompilerParams(collective_id=collective, has_side_effects=True),
        name="line_gather",
    )(block)


def start_kernel(count, seq_count, *refs):
    wq, wk, wv, wo, small, gains, routes = refs[:7]
    outs = refs[7:14]
    holds = refs[14:21]
    send_x, recv_x, local, send_r, send_l, send_s, recv = refs[21:]
    places = where_am_i()
    i = places[0]
    here = lax.axis_index("seq")
    width = wq.shape[1] // seq_count

    def columns(ref, peer):
        return ref.at[:, pl.ds(pl.multiple_of(peer * width, width), width)]

    own = [columns(wq, here), columns(wk, here), columns(wv, here), wo, small, gains, routes]
    for a in range(7):
        pltpu.make_async_copy(own[a], holds[a], local.at[a]).start()
    greet(count, places, seq_count)

    def piece(a, d):
        peer = lax.rem(here + d, seq_count)
        src = small if a == 4 else columns((wq, wk, wv)[a], peer)
        slot = 3 if a == 4 else a
        return remote(
            src, outs[a].at[here, i], send_x.at[slot, d - 1], recv_x.at[slot, d - 1], seq=peer
        )

    def arrived(a, d):
        origin = lax.rem(here + seq_count - d, seq_count)
        slot = 3 if a == 4 else a
        return remote(
            outs[a].at[origin, i],
            outs[a].at[origin, i],
            send_x.at[slot, d - 1],
            recv_x.at[slot, d - 1],
            seq=origin,
        )

    for a in (4, 0, 1, 2):
        for d in range(1, seq_count):
            piece(a, d).start()
    axes = [1, 1, 1, 0, 1, 0, 0]
    for a in (3, 5, 6, 4, 0, 1, 2):
        pltpu.make_async_copy(own[a], holds[a], local.at[a]).wait()
        target = outs[a].at[here, i] if axes[a] == 1 else outs[a].at[i]
        pltpu.make_async_copy(holds[a], target, local.at[a]).start()
    line = LineGather(count, places, outs, axes, send_r, send_l, send_s, recv)
    for a in (5, 6, 4, 0, 1, 2, 3):
        target = outs[a].at[here, i] if axes[a] == 1 else outs[a].at[i]
        pltpu.make_async_copy(holds[a], target, local.at[a]).wait()
        if axes[a] == 1:
            for d in range(1, seq_count):
                arrived(a, d).wait_recv()
        line.first(a)
    for t in range(1, count):
        line.forward(t)
    line.finish()
    for a in (4, 0, 1, 2):
        for d in range(1, seq_count):
            piece(a, d).wait_send()


def gather_start(arrays, seq_count, shards, collective):
    count = shards // 2
    wq, wk, wv, wo, small, gains, routes = arrays
    rows, model_width = wq.shape
    width = model_width // seq_count
    sheet = jax.ShapeDtypeStruct((seq_count, shards, rows, width), BF)
    shapes = [
        sheet,
        sheet,
        sheet,
        jax.ShapeDtypeStruct((shards,) + wo.shape, BF),
        jax.ShapeDtypeStruct((seq_count, shards) + small.shape, BF),
        jax.ShapeDtypeStruct((shards,) + gains.shape, BF),
        jax.ShapeDtypeStruct((shards,) + routes.shape, jnp.int32),
    ]
    holds = [pltpu.VMEM((rows, width), BF)] * 3 + [
        pltpu.VMEM(wo.shape, BF),
        pltpu.VMEM(small.shape, BF),
        pltpu.VMEM(gains.shape, BF),
        pltpu.VMEM(routes.shape, jnp.int32),
    ]
    return pl.pallas_call(
        partial(start_kernel, count, seq_count),
        out_shape=shapes,
        in_specs=[pl.BlockSpec(memory_space=ANY)] * 7,
        out_specs=[pl.BlockSpec(memory_space=ANY)] * 7,
        scratch_shapes=holds
        + [DMA((4, seq_count - 1)), DMA((4, seq_count - 1)), DMA((7,))]
        + line_sems(7, count),
        compiler_params=pltpu.CompilerParams(collective_id=collective, has_side_effects=True),
        name="gather_start",
    )(*arrays)


class LineScatter:
    def __init__(self, count, places, sources, axes, bufs, sems):
        self.count, self.places = count, places
        self.sources, self.axes = sources, axes
        self.own, self.sib, self.in_r, self.in_l = bufs
        self.sems = sems

    def load(self, a, q):
        i = self.places[0]
        src = slot_of(self.sources[a], self.axes[a], 2 * q + lax.rem(i, 2))
        return pltpu.make_async_copy(src, self.own[a].at[q], self.sems[6].at[a, q])

    def to_sib(self, a, q):
        sib = self.places[2]
        src = slot_of(self.sources[a], self.axes[a], 2 * q + lax.rem(sib, 2))
        return remote(src, self.sib[a].at[q], self.sems[2].at[a, q], self.sems[5].at[a, q], fsdp=sib)

    def right(self, a, q):
        i = self.places[0]
        return remote(
            self.own[a].at[q], self.in_r[a].at[q], self.sems[0].at[a, q], self.sems[3].at[a, q], fsdp=i + 2
        )

    def left(self, a, q):
        i = self.places[0]
        return remote(
            self.own[a].at[q], self.in_l[a].at[q], self.sems[1].at[a, q], self.sems[4].at[a, q], fsdp=i - 2
        )

    def order(self):
        order, low, high = [], 0, self.count - 1
        while low <= high:
            order.append(high)
            if low < high:
                order.append(low)
            low, high = low + 1, high - 1
        return order

    def begin_loads(self):
        for q in self.order():
            for a in range(len(self.sources)):
                self.load(a, q).start()

    def begin(self):
        for q in self.order():
            for a in range(len(self.sources)):
                self.to_sib(a, q).start()

    def add(self, a, q, others):
        own = self.own[a]
        lead = own.shape[1:-2]
        rows, width = own.shape[-2:]
        step = rows
        while step * width > 65536 and step % 16 == 0:
            step //= 2

        def strip(index):
            total = own[index].astype(F32) + self.sib[a][index].astype(F32)
            for other in others:
                total += other[a][index].astype(F32)
            own[index] = total.astype(own.dtype)

        def rows_of(prefix):
            if step == rows:
                strip(prefix)
                return

            @pl.loop(0, rows // step)
            def _(k):
                strip(prefix + (pl.ds(pl.multiple_of(k * step, step), step),))

        if lead:
            for b in range(lead[0]):
                rows_of((q, b))
        else:
            rows_of((q,))

    def ready(self, a, q):
        self.load(a, q).wait()
        self.to_sib(a, q).wait_recv()

    def run(self, after):
        i, p, sib = self.places
        count = self.count
        arrays = range(len(self.sources))
        for j in range(count - 1):
            q = count - 1 - j

            @pl.when(q > p)
            def _():
                for a in arrays:
                    self.ready(a, q)

                    @pl.when(p > 0)
                    def _():
                        self.right(a, q).wait_recv()
                        self.add(a, q, [self.in_r])

                    @pl.when(p == 0)
                    def _():
                        self.add(a, q, [])

                    self.right(a, q).start()

            @pl.when(j < p)
            def _():
                for a in arrays:
                    self.ready(a, j)

                    @pl.when(p < count - 1)
                    def _():
                        self.left(a, j).wait_recv()
                        self.add(a, j, [self.in_l])

                    @pl.when(p == count - 1)
                    def _():
                        self.add(a, j, [])

                    self.left(a, j).start()

        for q in range(count):

            @pl.when(q == p)
            def _():
                for a in arrays:
                    self.ready(a, q)
                    if q > 0:
                        self.right(a, q).wait_recv()
                    if q < count - 1:
                        self.left(a, q).wait_recv()
                    sides = ([self.in_r] if q > 0 else []) + ([self.in_l] if q < count - 1 else [])
                    self.add(a, q, sides)
                    after(a, q)

    def finish(self):
        i, p, sib = self.places
        for a in range(len(self.sources)):
            for q in range(self.count):
                self.to_sib(a, q).wait_send()

                @pl.when(q > p)
                def _():
                    self.right(a, q).wait_send()

                @pl.when(q < p)
                def _():
                    self.left(a, q).wait_send()


def scatter_kernel(count, x_ref, o_ref, own, sibling, in_r, in_l, s0, s1, s2, r0, r1, r2, local):
    places = where_am_i()
    line = LineScatter(
        count, places, [x_ref], [0], ([own], [sibling], [in_r], [in_l]), (s0, s1, s2, r0, r1, r2, local)
    )
    line.begin_loads()
    greet(count, places)
    line.begin()

    def after(a, q):
        out = pltpu.make_async_copy(own.at[q], o_ref, local.at[0, q])
        out.start()
        out.wait()

    line.run(after)
    line.finish()


def line_scatter(blocks, shards, collective):
    count = shards // 2
    block = blocks.shape[1:]
    return pl.pallas_call(
        partial(scatter_kernel, count),
        out_shape=jax.ShapeDtypeStruct(block, blocks.dtype),
        in_specs=[pl.BlockSpec(memory_space=ANY)],
        out_specs=pl.BlockSpec(memory_space=ANY),
        scratch_shapes=[pltpu.VMEM((count,) + block, blocks.dtype)] * 4 + [DMA((1, count))] * 7,
        compiler_params=pltpu.CompilerParams(
            collective_id=collective, has_side_effects=True, vmem_limit_bytes=48 << 20
        ),
        name="line_scatter",
    )(blocks)


def end_kernel(count, seq_count, *refs):
    sources = refs[:6]
    rows_ref = refs[6]
    outs = refs[7:13]
    sum_ref = refs[13]
    bufs = tuple(refs[14 + 6 * k : 20 + 6 * k] for k in range(4))
    landing = refs[38]
    sems = refs[39:46]
    send_x, recv_x, local = refs[46:49]
    seq = SeqScatter(seq_count, rows_ref, *refs[49:])
    places = where_am_i()
    here = lax.axis_index("seq")
    width = sources[0].shape[3]
    line = LineScatter(count, places, sources, [1, 1, 1, 0, 1, 0], bufs, sems)
    line.begin_loads()
    seq.take.start()
    greet(count, places, seq_count)
    seq.begin()
    line.begin()
    own = bufs[0]

    def at_home(a, block):
        if a == 4:
            return landing.at[block]
        start = pl.multiple_of(block * width, width)
        return outs[a].at[:, pl.ds(start, width)]

    def piece(a, q, d):
        peer = lax.rem(here + d, seq_count)
        slot = 3 if a == 4 else a
        return remote(
            own[a].at[q, peer], at_home(a, here), send_x.at[slot, d - 1], recv_x.at[slot, d - 1], seq=peer
        )

    def arrived(a, d):
        origin = lax.rem(here + seq_count - d, seq_count)
        slot = 3 if a == 4 else a
        return remote(
            at_home(a, origin), at_home(a, origin), send_x.at[slot, d - 1], recv_x.at[slot, d - 1], seq=origin
        )

    def after(a, q):
        if a in (3, 5):
            pltpu.make_async_copy(own[a].at[q], outs[a], local.at[a]).start()
        else:
            for d in range(1, seq_count):
                piece(a, q, d).start()
            pltpu.make_async_copy(own[a].at[q, here], at_home(a, here), local.at[a]).start()

    line.run(after)
    seq.total(sum_ref)
    for q in range(count):

        @pl.when(q == places[1])
        def _():
            for a in range(6):
                if a in (3, 5):
                    pltpu.make_async_copy(own[a].at[q], outs[a], local.at[a]).wait()
                else:
                    pltpu.make_async_copy(own[a].at[q, here], at_home(a, here), local.at[a]).wait()
                    for d in range(1, seq_count):
                        piece(a, q, d).wait_send()
                        arrived(a, d).wait_recv()

    total = landing[0]
    for block in range(1, seq_count):
        total += landing[block]
    landing[0] = total
    last = pltpu.make_async_copy(landing.at[0], outs[4], local.at[4])
    last.start()
    last.wait()
    line.finish()
    seq.finish()


def scatter_end(arrays, row_blocks, seq_count, shards, collective):
    count = shards // 2
    gq, gk, gv, go, small, gains = arrays
    rows, width = gq.shape[2:]
    home = jax.ShapeDtypeStruct((rows, width * seq_count), BF)
    shapes = [
        home,
        home,
        home,
        jax.ShapeDtypeStruct(go.shape[1:], BF),
        jax.ShapeDtypeStruct(small.shape[2:], F32),
        jax.ShapeDtypeStruct(gains.shape[1:], F32),
        jax.ShapeDtypeStruct(row_blocks.shape[1:], F32),
    ]
    blocks = []
    for a in range(6):
        shape = arrays[a].shape
        block = (shape[0],) + shape[2:] if a in (0, 1, 2, 4) else shape[1:]
        blocks.append(pltpu.VMEM((count,) + block, arrays[a].dtype))
    return pl.pallas_call(
        partial(end_kernel, count, seq_count),
        out_shape=shapes,
        in_specs=[pl.BlockSpec(memory_space=ANY)] * 7,
        out_specs=[pl.BlockSpec(memory_space=ANY)] * 6 + [pl.BlockSpec(memory_space=pltpu.VMEM)],
        scratch_shapes=blocks * 4
        + [pltpu.VMEM((seq_count,) + small.shape[2:], F32)]
        + [DMA((6, count))] * 7
        + [DMA((4, seq_count - 1)), DMA((4, seq_count - 1)), DMA((6,))]
        + seq_scatter_scratch(row_blocks.shape[1:], row_blocks.dtype, seq_count),
        compiler_params=pltpu.CompilerParams(
            collective_id=collective, has_side_effects=True, vmem_limit_bytes=56 << 20
        ),
        name="scatter_end",
    )(*arrays, row_blocks)


def greet_seq(seq_count):
    here = lax.axis_index("seq")
    barrier = pltpu.get_barrier_semaphore()
    for d in range(1, seq_count):
        peer = lax.rem(here + d, seq_count)
        pl.semaphore_signal(barrier, inc=1, device_id={"seq": peer}, device_id_type=MESH)
    pl.semaphore_wait(barrier, seq_count - 1)
    return here


class SeqScatter:
    def __init__(self, seq_count, x_ref, own, inbox, send, recv, local):
        here = lax.axis_index("seq")
        self.own, self.inbox, self.count = own, inbox, seq_count
        self.take = pltpu.make_async_copy(x_ref.at[here], own, local)
        self.copies = []
        for d in range(1, seq_count):
            peer = lax.rem(here + d, seq_count)
            self.copies.append(
                remote(x_ref.at[peer], inbox.at[d - 1], send.at[d - 1], recv.at[d - 1], seq=peer)
            )

    def begin(self):
        for copy in self.copies:
            copy.start()

    def total(self, o_ref):
        self.take.wait()
        for copy in self.copies:
            copy.wait_recv()
        rows = self.own.shape[0]
        step = min(32, rows)

        @pl.loop(0, rows // step)
        def _(k):
            strip = pl.ds(pl.multiple_of(k * step, step), step)
            total = self.own[strip, :].astype(F32)
            for d in range(self.count - 1):
                total += self.inbox[d, strip, :].astype(F32)
            o_ref[strip, :] = total

    def finish(self):
        for copy in self.copies:
            copy.wait_send()


def seq_scatter_scratch(block, dtype, seq_count):
    return [
        pltpu.VMEM(block, dtype),
        pltpu.VMEM((seq_count - 1,) + block, dtype),
        DMA((seq_count - 1,)),
        DMA((seq_count - 1,)),
        DMA,
    ]


def middle_kernel(
    count, seq_count, x_ref, dy_ref, o_ref, all_ref, own, inbox, xs, xr, xl, hold, s0, s1, s2, recv, local
):
    places = where_am_i()
    i = places[0]
    seq = SeqScatter(seq_count, x_ref, own, inbox, xs, xr, xl)
    seq.take.start()
    take = pltpu.make_async_copy(dy_ref, hold, local.at[0])
    take.start()
    greet(count, places, seq_count)
    seq.begin()
    take.wait()
    put = pltpu.make_async_copy(hold, all_ref.at[i], local.at[1])
    put.start()
    put.wait()
    line = LineGather(count, places, [all_ref], [0], s0, s1, s2, recv)
    line.first(0)
    for t in range(1, count):
        line.forward(t)
        if t == 1:
            seq.total(o_ref)
    line.finish()
    seq.finish()


def middle(blocks, dy, shards, collective):
    count = shards // 2
    seq_count = blocks.shape[0]
    block = blocks.shape[1:]
    return pl.pallas_call(
        partial(middle_kernel, count, seq_count),
        out_shape=[
            jax.ShapeDtypeStruct(block, F32),
            jax.ShapeDtypeStruct((shards,) + dy.shape, dy.dtype),
        ],
        in_specs=[pl.BlockSpec(memory_space=ANY)] * 2,
        out_specs=[pl.BlockSpec(memory_space=pltpu.VMEM), pl.BlockSpec(memory_space=ANY)],
        scratch_shapes=seq_scatter_scratch(block, blocks.dtype, seq_count)
        + [pltpu.VMEM(dy.shape, dy.dtype)]
        + line_sems(1, count)
        + [DMA((2,))],
        compiler_params=pltpu.CompilerParams(
            collective_id=collective, has_side_effects=True, vmem_limit_bytes=32 << 20
        ),
        name="middle",
    )(blocks, dy)


def seq_sum_kernel(seq_count, x_ref, o_ref, inbox, send, recv):
    here = greet_seq(seq_count)
    copies = []
    for d in range(1, seq_count):
        peer = lax.rem(here + d, seq_count)
        copies.append(remote(x_ref, inbox.at[d - 1], send.at[d - 1], recv.at[d - 1], seq=peer))
    for copy in copies:
        copy.start()
    for copy in copies:
        copy.wait_recv()
    total = x_ref[...]
    for d in range(seq_count - 1):
        total += inbox[d]
    o_ref[...] = total
    for copy in copies:
        copy.wait_send()


def seq_sum(value, seq_count, collective):
    return pl.pallas_call(
        partial(seq_sum_kernel, seq_count),
        out_shape=jax.ShapeDtypeStruct(value.shape, F32),
        in_specs=[pl.BlockSpec(memory_space=pltpu.VMEM)],
        out_specs=pl.BlockSpec(memory_space=pltpu.VMEM),
        scratch_shapes=[
            pltpu.VMEM((seq_count - 1,) + value.shape, F32),
            DMA((seq_count - 1,)),
            DMA((seq_count - 1,)),
        ],
        compiler_params=pltpu.CompilerParams(collective_id=collective, has_side_effects=True),
        name="seq_sum",
    )(value)


def turn_kernel(
    count, seq_count, x_ref, parts_ref, o_ref, sum_ref, hold, send, recv, one, own, sib, in_r, in_l, *sems
):
    places = where_am_i()
    here = lax.axis_index("seq")
    line = LineScatter(count, places, [parts_ref], [0], ([own], [sib], [in_r], [in_l]), sems)
    line.begin_loads()
    take = pltpu.make_async_copy(x_ref, hold, one)
    take.start()
    greet(count, places, seq_count)
    for d in range(1, seq_count):
        peer = lax.rem(here + d, seq_count)
        remote(x_ref, o_ref.at[here], send.at[d - 1], recv.at[d - 1], seq=peer).start()
    line.begin()
    take.wait()
    put = pltpu.make_async_copy(hold, o_ref.at[here], one)
    put.start()

    def after(a, q):
        out = pltpu.make_async_copy(own.at[q], sum_ref, sems[6].at[0, q])
        out.start()
        out.wait()

    line.run(after)
    put.wait()
    for d in range(1, seq_count):
        origin = lax.rem(here + seq_count - d, seq_count)
        remote(x_ref, o_ref.at[origin], send.at[d - 1], recv.at[d - 1], seq=origin).wait()
    line.finish()


def turn_back(block, parts, seq_count, shards, collective):
    count = shards // 2
    part = parts.shape[1:]
    return pl.pallas_call(
        partial(turn_kernel, count, seq_count),
        out_shape=[
            jax.ShapeDtypeStruct((seq_count,) + block.shape, block.dtype),
            jax.ShapeDtypeStruct(part, parts.dtype),
        ],
        in_specs=[pl.BlockSpec(memory_space=ANY)] * 2,
        out_specs=[pl.BlockSpec(memory_space=ANY)] * 2,
        scratch_shapes=[
            pltpu.VMEM(block.shape, block.dtype),
            DMA((seq_count - 1,)),
            DMA((seq_count - 1,)),
            DMA,
        ]
        + [pltpu.VMEM((count,) + part, parts.dtype)] * 4
        + [DMA((1, count))] * 7,
        compiler_params=pltpu.CompilerParams(
            collective_id=collective, has_side_effects=True, vmem_limit_bytes=48 << 20
        ),
        name="turn_back",
    )(block, parts)


def half_sign(shape):
    lane = lax.broadcasted_iota(jnp.int32, shape, 1)
    return jnp.where(lane < shape[1] // 2, -1.0, 1.0)


def turn(value):
    return pltpu.roll(value, value.shape[1] // 2, 1)


def block_probs(q_rows, keys, doc_col, doc_row, start, scale_by):
    end = keys.shape[0]
    scores = (
        lax.dot_general(q_rows, keys, (((1,), (1,)), ((), ())), preferred_element_type=F32) * scale_by
    )
    shape = scores.shape
    query_pos = start + lax.broadcasted_iota(jnp.int32, shape, 0)
    key_pos = lax.broadcasted_iota(jnp.int32, shape, 1)
    allowed = (doc_col == doc_row) & (key_pos <= query_pos)
    scores = jnp.where(allowed, scores, MASKED_OUT)
    weights = jnp.exp(scores - jnp.max(scores, axis=-1, keepdims=True))
    return weights * (1.0 / jnp.sum(weights, axis=-1, keepdims=True))


def attend_kernel(
    row_block, q_raw, k_raw, v_ref, rq, rk, gq, gk, cos, sin, doc_col, doc_row, o_ref, q_out, k_out
):
    seq_len = q_raw.shape[0]
    sign = half_sign(cos.shape)

    def rotated(raw, scale, gain):
        value = raw[...] * scale[...] * gain[...]
        return (value * cos[...] + turn(value) * (sin[...] * sign)).astype(BF)

    q_out[...] = rotated(q_raw, rq, gq)
    k_out[...] = rotated(k_raw, rk, gk)
    scale_by = HEAD ** (-0.5)
    for start in range(0, seq_len, row_block):
        end = start + row_block
        probs = block_probs(
            q_out[start:end, :], k_out[:end, :], doc_col[start:end, :], doc_row[:, :end], start, scale_by
        )
        o_ref[start:end, :] = jnp.dot(
            probs.astype(BF), v_ref[:end, :], preferred_element_type=F32
        ).astype(BF)


def attend(q_raw, k_raw, values, rq, rk, gq, gk, cos, sin, doc_col, doc_row):
    seq_len, width = q_raw.shape
    head = pl.BlockSpec((seq_len, HEAD), lambda h: (0, h))
    gain = pl.BlockSpec((1, HEAD), lambda h: (0, h))

    def whole(x):
        return pl.BlockSpec(x.shape, lambda h: (0, 0))

    out = jax.ShapeDtypeStruct((seq_len, width), BF)
    return pl.pallas_call(
        partial(attend_kernel, 256),
        grid=(width // HEAD,),
        out_shape=[out, out, out],
        in_specs=[head, head, head, whole(rq), whole(rk), gain, gain, whole(cos), whole(sin)]
        + [whole(doc_col), whole(doc_row)],
        out_specs=[head, head, head],
        compiler_params=pltpu.CompilerParams(vmem_limit_bytes=48 << 20),
        name="attend",
    )(q_raw, k_raw, values, rq, rk, gq, gk, cos, sin, doc_col, doc_row)


def attend_back_kernel(
    row_block,
    q_low,
    k_low,
    v_ref,
    do_ref,
    q_raw,
    k_raw,
    rq,
    rk,
    gq,
    gk,
    cos,
    sin,
    doc_col,
    doc_row,
    uq_ref,
    uk_ref,
    dv_ref,
    dots,
    gain_q,
    gain_k,
    dq_acc,
    dk_acc,
    dv_acc,
):
    seq_len = q_low.shape[0]
    scale_by = HEAD ** (-0.5)
    dk_acc[...] = jnp.zeros_like(dk_acc)
    dv_acc[...] = jnp.zeros_like(dv_acc)
    for start in range(0, seq_len, row_block):
        end = start + row_block
        rows = slice(start, end)
        probs = block_probs(
            q_low[rows, :], k_low[:end, :], doc_col[rows, :], doc_row[:, :end], start, scale_by
        )
        grad_rows = do_ref[rows, :]
        grad_probs = lax.dot_general(
            grad_rows, v_ref[:end, :], (((1,), (1,)), ((), ())), preferred_element_type=F32
        )
        centre = jnp.sum(probs * grad_probs, axis=-1, keepdims=True)
        grad_scores = (probs * (grad_probs - centre)).astype(BF)
        dq_acc[rows, :] = jnp.dot(grad_scores, k_low[:end, :], preferred_element_type=F32)
        over_rows = (((0,), (0,)), ((), ()))
        dk_acc[:end, :] += lax.dot_general(
            grad_scores, q_low[rows, :], over_rows, preferred_element_type=F32
        )
        dv_acc[:end, :] += lax.dot_general(
            probs.astype(BF), grad_rows, over_rows, preferred_element_type=F32
        )
    dv_ref[...] = dv_acc[...].astype(BF)
    sign = half_sign(cos.shape)

    def unrotated(acc, raw, scale, gain, u_ref, gain_ref, lane):
        low = (acc[...] * scale_by).astype(BF).astype(F32)
        back = low * cos[...] - turn(low * sin[...]) * sign
        gain_ref[...] = jnp.sum(back * raw[...] * scale[...], axis=0, keepdims=True)
        u = back * gain[...]
        u_ref[...] = u
        dot = jnp.sum(u * raw[...], axis=1, keepdims=True)

        @pl.when(pl.program_id(0) == 0)
        def _():
            dots[:, lane : lane + 1] = dot

        @pl.when(pl.program_id(0) > 0)
        def _():
            dots[:, lane : lane + 1] += dot

    unrotated(dq_acc, q_raw, rq, gq, uq_ref, gain_q, 0)
    unrotated(dk_acc, k_raw, rk, gk, uk_ref, gain_k, 1)


def attend_back(q_low, k_low, values, d_heads, q_raw, k_raw, rq, rk, gq, gk, cos, sin, doc_col, doc_row):
    seq_len, width = q_raw.shape
    head = pl.BlockSpec((seq_len, HEAD), lambda h: (0, h))
    gain = pl.BlockSpec((1, HEAD), lambda h: (0, h))

    def whole(x):
        return pl.BlockSpec(x.shape, lambda h: (0, 0))

    wide = jax.ShapeDtypeStruct((seq_len, width), F32)
    row = jax.ShapeDtypeStruct((1, width), F32)
    return pl.pallas_call(
        partial(attend_back_kernel, 256),
        grid=(width // HEAD,),
        out_shape=[
            wide,
            wide,
            jax.ShapeDtypeStruct((seq_len, width), BF),
            jax.ShapeDtypeStruct((seq_len, 2), F32),
            row,
            row,
        ],
        in_specs=[head] * 6
        + [whole(rq), whole(rk), gain, gain, whole(cos), whole(sin), whole(doc_col), whole(doc_row)],
        out_specs=[head, head, head, pl.BlockSpec((seq_len, 2), lambda h: (0, 0)), gain, gain],
        scratch_shapes=[pltpu.VMEM((seq_len, HEAD), F32)] * 3,
        compiler_params=pltpu.CompilerParams(vmem_limit_bytes=56 << 20),
        name="attend_back",
    )(q_low, k_low, values, d_heads, q_raw, k_raw, rq, rk, gq, gk, cos, sin, doc_col, doc_row)


def chunk_order(k, p, count):
    near = jnp.minimum(p, count - 1 - p)
    step = (k + 1) // 2
    both = jnp.where(k % 2 == 1, p - step, p + step)
    return jnp.where(k <= 2 * near, both, jnp.where(p < count - 1 - p, k, count - 1 - k))


def experts_in_kernel(
    count,
    cap,
    h2_ref,
    dy_ref,
    targets,
    router_t,
    wg_ref,
    wu_ref,
    h2_out,
    x_out,
    y_out,
    act_out,
    by_up_out,
    by_gate_out,
    gate_slots,
    probs_out,
    h2,
    wg,
    wu,
    dy,
    xs,
    ys,
    acts,
    by_up,
    by_gate,
    s0,
    s1,
    s2,
    recv,
    w_sem,
    dy_sem,
    h_sem,
    out_sem,
):
    places = where_am_i()
    i, p, sib = places
    local_experts, model_width, hidden = wg_ref.shape
    tokens = h2_ref.shape[0]
    experts = router_t.shape[0]
    own_in = pltpu.make_async_copy(h2_ref, h2.at[i], h_sem.at[0])
    own_in.start()

    def fetch(q, buf):
        src = dy_ref.at[pl.ds(2 * q, 2)]
        return pltpu.make_async_copy(src, dy.at[buf], dy_sem.at[buf])

    fetch(p, 0).start()
    for e in range(local_experts):
        pltpu.make_async_copy(wg_ref.at[e], wg.at[e], w_sem.at[0, e]).start()
        pltpu.make_async_copy(wu_ref.at[e], wu.at[e], w_sem.at[1, e]).start()
    greet(count, places)
    own_in.wait()
    line = LineGather(count, places, [h2], [0], s0, s1, s2, recv)
    line.first(0)
    staged = ((xs, x_out), (ys, y_out), (acts, act_out), (by_up, by_up_out), (by_gate, by_gate_out))

    def store(n, e, q):
        return pltpu.make_async_copy(staged[n][0].at[e], staged[n][1].at[e, q], out_sem.at[n, e])

    def keep(q):
        src = h2.at[pl.ds(2 * q, 2)]
        return pltpu.make_async_copy(src, h2_out.at[pl.ds(2 * q, 2)], h_sem.at[1])

    slot_rows = lax.broadcasted_iota(jnp.int32, (local_experts * cap, tokens), 0)
    expert_rows = lax.broadcasted_iota(jnp.int32, (experts, tokens), 0)

    @pl.loop(0, count)
    def _(k):
        q = chunk_order(k, p, count)
        buf = k % 2

        @pl.when(k > 0)
        def _():
            line.forward(k)

        line.copy(0, 2 * q + lax.rem(sib, 2), 2, 0, sib).wait_recv()
        fetch(q, buf).wait()

        @pl.when(k + 1 < count)
        def _():
            fetch(chunk_order(k + 1, p, count), 1 - buf).start()

        @pl.when(k > 0)
        def _():
            for n in range(5):
                for e in range(local_experts):
                    store(n, e, q).wait()
            keep(q).wait()

        keep(q).start()
        picks = []
        for j in range(2):
            slot = 2 * q + j
            tokens_j = h2[slot]
            logits = lax.dot_general(
                router_t[...], tokens_j, (((1,), (1,)), ((), ())), preferred_element_type=F32
            )
            shifted = jnp.exp(logits - jnp.max(logits, axis=0, keepdims=True))
            probs = shifted / jnp.sum(shifted, axis=0, keepdims=True)
            probs_out[slot] = probs
            pick = None
            for e in range(local_experts):
                mask = slot_rows == targets[slot, e : e + 1, :]
                gate = jnp.sum(
                    jnp.where(expert_rows == i * local_experts + e, probs, 0.0), axis=0, keepdims=True
                )
                part = slice(e * cap, (e + 1) * cap)
                gate_slots[e, q, j * cap : (j + 1) * cap, :] = jnp.sum(
                    jnp.where(mask[part], gate, 0.0), axis=1, keepdims=True
                )
                pick = mask if pick is None else pick | mask
            picks.append(jnp.where(pick, 1.0, 0.0).astype(BF))

        block = 512

        @pl.loop(0, model_width // block)
        def _(n):
            cols = pl.ds(pl.multiple_of(n * block, block), block)
            for source, target in ((0, xs), (1, ys)):
                got = []
                for j in range(2):
                    rows = h2[2 * q + j, :, cols] if source == 0 else dy[buf, j, :, cols]
                    got.append(jnp.dot(picks[j], rows, preferred_element_type=F32))
                for e in range(local_experts):
                    part = slice(e * cap, (e + 1) * cap)
                    target[e, :, cols] = jnp.concatenate([got[0][part], got[1][part]], axis=0).astype(BF)

        for e in range(local_experts):
            store(0, e, q).start()
            store(1, e, q).start()

            @pl.when(k == 0)
            def _():
                pltpu.make_async_copy(wg_ref.at[e], wg.at[e], w_sem.at[0, e]).wait()
                pltpu.make_async_copy(wu_ref.at[e], wu.at[e], w_sem.at[1, e]).wait()

            wide = 256

            @pl.loop(0, hidden // wide)
            def _(n):
                cols = pl.ds(pl.multiple_of(n * wide, wide), wide)
                gate = jnp.dot(xs[e], wg[e, :, cols], preferred_element_type=F32)
                up = jnp.dot(xs[e], wu[e, :, cols], preferred_element_type=F32)
                sigmoid = 1.0 / (1.0 + jnp.exp(-gate))
                silu = gate * sigmoid
                acts[e, :, cols] = (silu * up).astype(BF)
                by_up[e, :, cols] = silu.astype(BF)
                by_gate[e, :, cols] = (up * sigmoid * (1.0 + gate * (1.0 - sigmoid))).astype(BF)

            for n in (2, 3, 4):
                store(n, e, q).start()

    for n in range(5):
        for e in range(local_experts):
            store(n, e, 0).wait()
    keep(0).wait()
    sends_done(line)


def sends_done(line):
    i, p, sib = line.places
    count = line.count
    line.copy(0, i, 2, 0, sib).wait_send()

    @pl.when(p < count - 1)
    def _():
        line.copy(0, i, 0, 0, i + 2).wait_send()

    @pl.when(p > 0)
    def _():
        line.copy(0, i, 1, 0, i - 2).wait_send()

    for t in range(1, count):

        @pl.when(p - t >= 0)
        def _():
            slot = i - 2 * t

            @pl.when(p < count - 1)
            def _():
                line.copy(0, slot, 0, t, i + 2).wait_send()

            line.copy(0, slot, 2, t, sib).wait_send()

        @pl.when(p + t < count)
        def _():
            slot = i + 2 * t

            @pl.when(p > 0)
            def _():
                line.copy(0, slot, 1, t, i - 2).wait_send()

            line.copy(0, slot, 2, count + t, sib).wait_send()


def experts_in(h2, dy_all, targets, router_t, w_gate, w_up, collective):
    shards, tokens, model_width = dy_all.shape
    local_experts, _, hidden = w_gate.shape
    experts = router_t.shape[0]
    count = shards // 2
    wide = jax.ShapeDtypeStruct((local_experts, count, 2 * CAP, model_width), BF)
    thin = jax.ShapeDtypeStruct((local_experts, count, 2 * CAP, hidden), BF)
    anywhere = pl.BlockSpec(memory_space=ANY)
    vmem = pl.BlockSpec(memory_space=pltpu.VMEM)
    return pl.pallas_call(
        partial(experts_in_kernel, count, CAP),
        out_shape=[
            jax.ShapeDtypeStruct((shards, tokens, model_width), BF),
            wide,
            wide,
            thin,
            thin,
            thin,
            jax.ShapeDtypeStruct((local_experts, count, 2 * CAP, 1), F32),
            jax.ShapeDtypeStruct((shards, experts, tokens), F32),
        ],
        in_specs=[anywhere, anywhere, vmem, vmem, anywhere, anywhere],
        out_specs=[anywhere] * 6 + [vmem, vmem],
        scratch_shapes=[
            pltpu.VMEM((shards, tokens, model_width), BF),
            pltpu.VMEM(w_gate.shape, BF),
            pltpu.VMEM(w_up.shape, BF),
            pltpu.VMEM((2, 2, tokens, model_width), BF),
        ]
        + [pltpu.VMEM((local_experts, 2 * CAP, model_width), BF)] * 2
        + [pltpu.VMEM((local_experts, 2 * CAP, hidden), BF)] * 3
        + line_sems(1, count)
        + [DMA((2, local_experts)), DMA((2,)), DMA((2,)), DMA((5, local_experts))],
        compiler_params=pltpu.CompilerParams(
            collective_id=collective, has_side_effects=True, vmem_limit_bytes=60 << 20
        ),
        name="experts_in",
    )(h2, dy_all, targets, router_t, w_gate, w_up)


def experts_out_kernel(
    cap,
    y_ref,
    act_ref,
    by_up_ref,
    by_gate_ref,
    gate_slots,
    targets,
    targets_t,
    probs_ref,
    router_t,
    wg,
    wu,
    wd,
    gated_ref,
    d_gate_ref,
    d_up_ref,
    out_ref,
    back_ref,
    logit_ref,
):
    local_experts, hidden, model_width = wd.shape
    tokens = targets.shape[2]
    experts = router_t.shape[0]
    first = lax.axis_index("fsdp") * local_experts
    over_lanes = (((1,), (1,)), ((), ()))
    over_rows = (((0,), (0,)), ((), ()))
    dots = []
    for e in range(local_experts):
        wide = 256

        def step(n, dot):
            cols = pl.ds(pl.multiple_of(n * wide, wide), wide)
            grad_act = lax.dot_general(
                y_ref[e, 0], wd[e, cols, :], over_lanes, preferred_element_type=F32
            )
            act = act_ref[e, 0, :, cols].astype(F32)
            gate = gate_slots[e, 0]
            dot = dot + jnp.sum(act * grad_act, axis=1, keepdims=True)
            grad_act = grad_act * gate
            gated_ref[e, 0, :, cols] = (act * gate).astype(BF)
            d_up_ref[e, 0, :, cols] = (grad_act * by_up_ref[e, 0, :, cols].astype(F32)).astype(BF)
            d_gate_ref[e, 0, :, cols] = (grad_act * by_gate_ref[e, 0, :, cols].astype(F32)).astype(BF)
            return dot

        dots.append(lax.fori_loop(0, hidden // wide, step, jnp.zeros((2 * cap, 1), F32)))

    slot_rows = lax.broadcasted_iota(jnp.int32, (local_experts * cap, tokens), 0)
    slot_lanes = lax.broadcasted_iota(jnp.int32, (tokens, local_experts * cap), 1)
    expert_rows = lax.broadcasted_iota(jnp.int32, (experts, tokens), 0)
    picks, logits_low = [], []
    for j in range(2):
        grad_probs = jnp.zeros((experts, tokens), F32)
        pick = None
        for e in range(local_experts):
            part = slice(e * cap, (e + 1) * cap)
            mask = (slot_rows == targets[j, e : e + 1, :])[part]
            row = jnp.sum(jnp.where(mask, dots[e][j * cap : (j + 1) * cap], 0.0), axis=0, keepdims=True)
            grad_probs = jnp.where(expert_rows == first + e, row, grad_probs)
            hit = slot_lanes == targets_t[j, :, e : e + 1]
            pick = hit if pick is None else pick | hit
        probs = probs_ref[j]
        grad_logits = probs * (grad_probs - jnp.sum(probs * grad_probs, axis=0, keepdims=True))
        logit_ref[j] = grad_logits.astype(BF)
        picks.append(jnp.where(pick, 1.0, 0.0).astype(BF))
        logits_low.append(grad_logits.T.astype(BF))

    block = 512

    @pl.loop(0, model_width // block)
    def _(n):
        cols = pl.ds(pl.multiple_of(n * block, block), block)
        results, grads = [], []
        for e in range(local_experts):
            results.append(jnp.dot(gated_ref[e, 0], wd[e, :, cols], preferred_element_type=F32))
            grads.append(
                lax.dot_general(d_gate_ref[e, 0], wg[e, cols, :], over_lanes, preferred_element_type=F32)
                + lax.dot_general(d_up_ref[e, 0], wu[e, cols, :], over_lanes, preferred_element_type=F32)
            )
        for j in range(2):
            part = slice(j * cap, (j + 1) * cap)
            mine = jnp.concatenate([value[part] for value in results], axis=0).astype(BF)
            back = jnp.concatenate([value[part] for value in grads], axis=0).astype(BF)
            out_ref[j, :, cols] = jnp.dot(picks[j], mine, preferred_element_type=F32).astype(BF)
            back_ref[j, :, cols] = (
                jnp.dot(picks[j], back, preferred_element_type=F32)
                + jnp.dot(logits_low[j], router_t[:, cols], preferred_element_type=F32)
            ).astype(BF)


def experts_out(
    grads, act, by_up, by_gate, gate_slots, targets, targets_t, probs, router_t, w_gate, w_up, w_down
):
    local_experts, count, slots, model_width = grads.shape
    hidden = act.shape[3]
    shards, experts, tokens = probs.shape

    def chunk(x):
        return pl.BlockSpec((x.shape[0], 1) + x.shape[2:], lambda q: (0, q, 0, 0))

    def pair(x):
        return pl.BlockSpec((2,) + x.shape[1:], lambda q: (q, 0, 0))

    def fixed(x):
        return pl.BlockSpec(
            x.shape, lambda q: (0,) * len(x.shape), pipeline_mode=pl.Buffered(1)
        )

    thin = jax.ShapeDtypeStruct(act.shape, BF)
    full = jax.ShapeDtypeStruct((shards, tokens, model_width), BF)
    logit = jax.ShapeDtypeStruct(probs.shape, BF)
    return pl.pallas_call(
        partial(experts_out_kernel, CAP),
        grid=(count,),
        out_shape=[thin, thin, thin, full, full, logit],
        in_specs=[chunk(grads), chunk(act), chunk(by_up), chunk(by_gate), chunk(gate_slots)]
        + [pair(targets), pair(targets_t), pair(probs)]
        + [fixed(router_t), fixed(w_gate), fixed(w_up), fixed(w_down)],
        out_specs=[chunk(act)] * 3 + [pair(full)] * 2 + [pair(logit)],
        compiler_params=pltpu.CompilerParams(vmem_limit_bytes=63 << 20),
        name="experts_out",
    )(grads, act, by_up, by_gate, gate_slots, targets, targets_t, probs, router_t, w_gate, w_up, w_down)


def rope_tables(positions, head_dim):
    half_dim = head_dim // 2
    inverse = ROPE_BASE ** (-(jnp.arange(half_dim, dtype=F32) * 2.0 / head_dim))
    angles = positions.astype(F32)[:, None] * inverse[None, :]
    angles = jnp.concatenate([angles, angles], axis=-1)
    return (jnp.cos(angles), jnp.sin(angles))


def dot(left, right, sides=(1, 0), out=F32):
    return lax.dot_general(
        left, right, (((sides[0],), (sides[1],)), ((), ())), preferred_element_type=F32
    ).astype(out)


def inverse_rms(rows):
    return lax.rsqrt(jnp.mean(rows * rows, axis=-1, keepdims=True) + EPSILON)


def on_device(
    inputs,
    out_grad,
    doc_ids,
    routes,
    w_query,
    w_key,
    w_value,
    w_output,
    w_router,
    attn_gain,
    ffn_gain,
    query_gain,
    key_gain,
    w_gate,
    w_up,
    w_down,
):
    seq_count = lax.axis_size("seq")
    shards = lax.axis_size("fsdp")
    tok_rows, model_width = inputs.shape[1:]
    seq_len = tok_rows * seq_count
    rows = w_query.shape[0]
    width = model_width // seq_count
    local_experts = w_gate.shape[0]
    experts = w_router.shape[1]
    top_k = routes.shape[2]
    lanes = 128

    small = jnp.concatenate(
        [
            w_router,
            attn_gain[:, None],
            ffn_gain[:, None],
            jnp.zeros((rows, lanes - experts - 2), BF),
        ],
        axis=1,
    )
    gains = jnp.pad(jnp.stack([query_gain, key_gain]), ((0, 14), (0, lanes - rows)))
    routes_flat = routes.reshape(tok_rows * top_k // lanes, lanes)
    wq, wk, wv, wo, small_all, gains_all, routes_all = gather_start(
        (w_query, w_key, w_value, w_output, small, gains, routes_flat), seq_count, shards, 0
    )
    x_all = lax.all_gather(inputs[0], "seq", axis=0, tiled=True)
    full_gate = lax.all_gather(w_gate, "seq", axis=1, tiled=True)
    full_up = lax.all_gather(w_up, "seq", axis=1, tiled=True)
    full_down = lax.all_gather(w_down, "seq", axis=1, tiled=True)

    wq = wq.reshape(model_width, width)
    wk = wk.reshape(model_width, width)
    wv = wv.reshape(model_width, width)
    wo = wo.reshape(width, model_width)
    small_all = small_all.reshape(model_width, lanes)
    w_r = small_all[:, :experts]
    gain_a = small_all[:, experts].astype(F32)
    gain_f = small_all[:, experts + 1].astype(F32)
    gq = gains_all[:, 0, :rows].reshape(1, width).astype(F32)
    gk = gains_all[:, 1, :rows].reshape(1, width).astype(F32)

    x_float = x_all.astype(F32)
    h1 = (x_float * inverse_rms(x_float) * gain_a).astype(BF)
    q_raw = dot(h1, wq)
    k_raw = dot(h1, wk)
    values = dot(h1, wv, out=BF)
    squares = jnp.stack([jnp.sum(q_raw * q_raw, axis=1), jnp.sum(k_raw * k_raw, axis=1)])
    squares = seq_sum(squares, seq_count, 1)
    scales = lax.rsqrt(squares / model_width + EPSILON)
    rq, rk = scales[0][:, None], scales[1][:, None]
    cos, sin = rope_tables(jnp.arange(seq_len, dtype=jnp.int32), HEAD)
    doc_row = doc_ids
    doc_col = doc_ids.reshape(seq_len, 1)
    attended, q_low, k_low = attend(q_raw, k_raw, values, rq, rk, gq, gk, cos, sin, doc_col, doc_row)
    projected = dot(attended, wo, out=BF).reshape(seq_count, tok_rows, model_width)
    rows_in = inputs[0].astype(F32)
    grad_rows = out_grad[0].astype(F32)
    summed, dy_all = middle(projected, out_grad[0], shards, 2)
    x_mid = rows_in + summed
    scale_f = inverse_rms(x_mid)
    h2 = (x_mid * scale_f * gain_f).astype(BF)

    routes_all = routes_all.reshape(shards, tok_rows, top_k)
    local_ids = lax.axis_index("fsdp") * local_experts + jnp.arange(local_experts, dtype=jnp.int32)
    chosen = jnp.any(routes_all[:, None] == local_ids[None, :, None, None], axis=3)
    slot = jnp.cumsum(chosen.astype(jnp.int32), axis=2) - 1
    slot = slot + CAP * jnp.arange(local_experts, dtype=jnp.int32)[None, :, None]
    targets = jnp.where(chosen, slot, -1)
    targets_t = jnp.swapaxes(targets, 1, 2)
    router_t = w_r.T
    h2_all, expert_in, grad_slots, act, by_up, by_gate, gate_slots, gate_probs = experts_in(
        h2, dy_all, targets, router_t, full_gate, full_up, 3
    )
    gated, d_gate, d_up, out_parts, grad_parts, grad_logits = experts_out(
        grad_slots,
        act,
        by_up,
        by_gate,
        gate_slots,
        targets,
        targets_t,
        gate_probs,
        router_t,
        full_gate,
        full_up,
        full_down,
    )
    router_part = jnp.einsum("jet,jtd->de", grad_logits, h2_all, preferred_element_type=F32)

    def outer(left, right):
        return jnp.einsum("ejra,ejrb->eab", left, right, preferred_element_type=F32).astype(BF)

    def spread(part):
        return lax.psum_scatter(part, "seq", scatter_dimension=1, tiled=True).astype(F32)

    g_down = spread(outer(gated, grad_slots))
    g_gate = spread(outer(expert_in, d_gate))
    g_up = spread(outer(expert_in, d_up))
    grad_h2 = line_scatter(grad_parts, shards, 4).astype(F32)
    u_rows = gain_f * grad_h2
    grad_mid = (
        grad_rows
        + scale_f * u_rows
        - x_mid * scale_f**3 * jnp.mean(u_rows * x_mid, axis=-1, keepdims=True)
    )
    ffn_part = jnp.sum(grad_h2 * x_mid * scale_f, axis=0)

    d_attn, out_sum = turn_back(grad_mid.astype(BF), out_parts, seq_count, shards, 5)
    d_attn = d_attn.reshape(seq_len, model_width)
    result = x_mid + out_sum.astype(F32)
    d_heads = dot(d_attn, wo, (1, 1), BF)
    u_q, u_k, dv_low, dots, gain_q_part, gain_k_part = attend_back(
        q_low, k_low, values, d_heads, q_raw, k_raw, rq, rk, gq, gk, cos, sin, doc_col, doc_row
    )
    dots = seq_sum(dots.T, seq_count, 6) / model_width

    def norm_back(u, raw, scale, product):
        return (scale * u - raw * (scale**3 * product[:, None])).astype(BF)

    dq_low = norm_back(u_q, q_raw, rq, dots[0])
    dk_low = norm_back(u_k, k_raw, rk, dots[1])
    grad_h1 = dot(dq_low, wq, (1, 1)) + dot(dk_low, wk, (1, 1)) + dot(dv_low, wv, (1, 1))
    grad_h1 = grad_h1.astype(BF).reshape(seq_count, tok_rows, model_width)

    sheet = (seq_count, shards, rows, width)
    small_part = jnp.concatenate(
        [router_part, ffn_part[:, None], jnp.zeros((model_width, lanes - experts - 1), F32)], axis=1
    ).reshape(seq_count, shards, rows, lanes)
    gains_part = jnp.stack([gain_q_part.reshape(shards, rows), gain_k_part.reshape(shards, rows)], axis=1)
    gains_part = jnp.pad(gains_part, ((0, 0), (0, 6), (0, lanes - rows)))
    g_query, g_key, g_value, g_output, g_small, g_gains, grad_h1 = scatter_end(
        (
            dot(h1, dq_low, (0, 0), BF).reshape(sheet),
            dot(h1, dk_low, (0, 0), BF).reshape(sheet),
            dot(h1, dv_low, (0, 0), BF).reshape(sheet),
            dot(attended, d_attn, (0, 0), BF).reshape(shards, rows, model_width),
            small_part,
            gains_part,
        ),
        grad_h1,
        seq_count,
        shards,
        8,
    )
    g_query, g_key, g_value = (g_query.astype(F32), g_key.astype(F32), g_value.astype(F32))

    scale_a = inverse_rms(rows_in)
    u_rows = gain_a * grad_h1
    input_grad = (
        grad_mid
        + scale_a * u_rows
        - rows_in * scale_a**3 * jnp.mean(u_rows * rows_in, axis=-1, keepdims=True)
    )
    pairs = (
        w_query.astype(F32) * g_query + w_key.astype(F32) * g_key + w_value.astype(F32) * g_value
    )
    g_attn_gain = jnp.sum(pairs, axis=1) / attn_gain.astype(F32)

    return (
        result.astype(BF)[None],
        input_grad[None],
        g_query,
        g_key,
        g_value,
        g_output.astype(F32),
        g_small[:, :experts],
        g_attn_gain,
        g_small[:, experts],
        g_gains[0, :rows],
        g_gains[1, :rows],
        g_gate,
        g_up,
        g_down,
    )


def solution(mesh):
    rows = P("fsdp", "seq", None)
    sheet = P(("seq", "fsdp"), None)
    line = P(("seq", "fsdp"))
    return jax.shard_map(
        on_device,
        mesh=mesh,
        in_specs=(rows, rows, P("fsdp", None), rows) + (sheet,) * 5 + (line,) * 4 + (rows,) * 3,
        out_specs=(rows, rows) + (sheet,) * 5 + (line,) * 4 + (rows,) * 3,
        check_vma=False,
    )
```

```python
from functools import partial

import jax
import jax.numpy as jnp
from jax import lax
from jax.experimental import pallas as pl
from jax.experimental.pallas import tpu as pltpu
from jax.sharding import PartitionSpec as P

CAP = 136
HEAD = 128
EPSILON = 1e-05
ROPE_BASE = 10000.0
MASKED_OUT = -1e30
ANY = pl.ANY
MESH = pl.DeviceIdType.MESH
DMA = pltpu.SemaphoreType.DMA
BF = jnp.bfloat16
F32 = jnp.float32


def remote(src, dst, send, recv, **where):
    return pltpu.make_async_remote_copy(
        src_ref=src, dst_ref=dst, send_sem=send, recv_sem=recv, device_id=where, device_id_type=MESH
    )


def greet(count, places, seq_count=1):
    i, p, sib = places
    barrier = pltpu.get_barrier_semaphore()
    pl.semaphore_signal(barrier, inc=1, device_id={"fsdp": sib}, device_id_type=MESH)
    here = lax.axis_index("seq")
    for d in range(1, seq_count):
        peer = lax.rem(here + d, seq_count)
        pl.semaphore_signal(barrier, inc=1, device_id={"seq": peer}, device_id_type=MESH)

    @pl.when(p > 0)
    def _():
        pl.semaphore_signal(barrier, inc=1, device_id={"fsdp": i - 2}, device_id_type=MESH)

    @pl.when(p < count - 1)
    def _():
        pl.semaphore_signal(barrier, inc=1, device_id={"fsdp": i + 2}, device_id_type=MESH)

    last = count - 1
    pl.semaphore_wait(barrier, seq_count + (p + last) // count + (last - p + last) // count)


def slot_of(ref, axis, index):
    return ref.at[index] if axis == 0 else ref.at[:, index]


class LineGather:
    def __init__(self, count, places, refs, axes, send_r, send_l, send_s, recv):
        self.count, self.places = count, places
        self.refs, self.axes = refs, axes
        self.sems = (send_r, send_l, send_s, recv)

    def copy(self, a, slot, kind, t, device):
        send = self.sems[kind].at[a, t]
        ref = slot_of(self.refs[a], self.axes[a], slot)
        return remote(ref, ref, send, self.sems[3].at[a, slot], fsdp=device)

    def first(self, a):
        i, p, sib = self.places

        @pl.when(p < self.count - 1)
        def _():
            self.copy(a, i, 0, 0, i + 2).start()

        @pl.when(p > 0)
        def _():
            self.copy(a, i, 1, 0, i - 2).start()

        self.copy(a, i, 2, 0, sib).start()

    def forward(self, t):
        i, p, sib = self.places
        count = self.count
        for a in range(len(self.refs)):

            @pl.when(p - t >= 0)
            def _():
                slot = i - 2 * t
                self.copy(a, slot, 0, t, sib).wait_recv()

                @pl.when(p < count - 1)
                def _():
                    self.copy(a, slot, 0, t, i + 2).start()

                self.copy(a, slot, 2, t, sib).start()

            @pl.when(p + t < count)
            def _():
                slot = i + 2 * t
                self.copy(a, slot, 1, t, sib).wait_recv()

                @pl.when(p > 0)
                def _():
                    self.copy(a, slot, 1, t, i - 2).start()

                self.copy(a, slot, 2, count + t, sib).start()

    def finish(self):
        i, p, sib = self.places
        count = self.count
        for a in range(len(self.refs)):
            for q in range(count):
                self.copy(a, 2 * q + lax.rem(sib, 2), 2, 0, sib).wait_recv()
            self.copy(a, i, 2, 0, sib).wait_send()

            @pl.when(p < count - 1)
            def _():
                self.copy(a, i, 0, 0, i + 2).wait_send()

            @pl.when(p > 0)
            def _():
                self.copy(a, i, 1, 0, i - 2).wait_send()

            for t in range(1, count):

                @pl.when(p - t >= 0)
                def _():
                    slot = i - 2 * t

                    @pl.when(p < count - 1)
                    def _():
                        self.copy(a, slot, 0, t, i + 2).wait_send()

                    self.copy(a, slot, 2, t, sib).wait_send()

                @pl.when(p + t < count)
                def _():
                    slot = i + 2 * t

                    @pl.when(p > 0)
                    def _():
                        self.copy(a, slot, 1, t, i - 2).wait_send()

                    self.copy(a, slot, 2, count + t, sib).wait_send()


def line_sems(arrays, count):
    return [DMA((arrays, count)), DMA((arrays, count)), DMA((arrays, 2 * count)), DMA((arrays, 2 * count))]


def where_am_i():
    i = lax.axis_index("fsdp")
    p = i // 2
    c = i % 2
    return i, p, 2 * p + 1 - c


def start_kernel(count, seq_count, *refs):
    wq, wk, wv, wo, small, gains, routes, rows = refs[:8]
    outs = refs[8:15]
    rows_out = refs[15]
    holds = refs[16:24]
    send_x, recv_x, local, send_r, send_l, send_s, recv = refs[24:]
    places = where_am_i()
    i = places[0]
    here = lax.axis_index("seq")
    width = wq.shape[1] // seq_count

    def columns(ref, peer):
        return ref.at[:, pl.ds(pl.multiple_of(peer * width, width), width)]

    own = [columns(wq, here), columns(wk, here), columns(wv, here), wo, small, gains, routes, rows]
    for a in range(8):
        pltpu.make_async_copy(own[a], holds[a], local.at[a]).start()
    greet(count, places, seq_count)

    def piece(a, d):
        peer = lax.rem(here + d, seq_count)
        src = small if a == 4 else columns((wq, wk, wv)[a], peer)
        slot = 3 if a == 4 else a
        return remote(
            src, outs[a].at[here, i], send_x.at[slot, d - 1], recv_x.at[slot, d - 1], seq=peer
        )

    def arrived(a, d):
        origin = lax.rem(here + seq_count - d, seq_count)
        slot = 3 if a == 4 else a
        return remote(
            outs[a].at[origin, i],
            outs[a].at[origin, i],
            send_x.at[slot, d - 1],
            recv_x.at[slot, d - 1],
            seq=origin,
        )

    for a in (4, 0, 1, 2):
        for d in range(1, seq_count):
            piece(a, d).start()
    for d in range(1, seq_count):
        peer = lax.rem(here + d, seq_count)
        remote(rows, rows_out.at[here], send_x.at[4, d - 1], recv_x.at[4, d - 1], seq=peer).start()
    axes = [1, 1, 1, 0, 1, 0, 0]
    for a in (3, 5, 6, 4, 0, 1, 2):
        pltpu.make_async_copy(own[a], holds[a], local.at[a]).wait()
        target = outs[a].at[here, i] if axes[a] == 1 else outs[a].at[i]
        pltpu.make_async_copy(holds[a], target, local.at[a]).start()
    line = LineGather(count, places, outs, axes, send_r, send_l, send_s, recv)
    for a in (5, 6, 4, 0, 1, 2, 3):
        target = outs[a].at[here, i] if axes[a] == 1 else outs[a].at[i]
        pltpu.make_async_copy(holds[a], target, local.at[a]).wait()
        if axes[a] == 1:
            for d in range(1, seq_count):
                arrived(a, d).wait_recv()
        line.first(a)
    pltpu.make_async_copy(rows, holds[7], local.at[7]).wait()
    pltpu.make_async_copy(holds[7], rows_out.at[here], local.at[7]).start()
    for t in range(1, count):
        line.forward(t)
    line.finish()
    pltpu.make_async_copy(holds[7], rows_out.at[here], local.at[7]).wait()
    for d in range(1, seq_count):
        origin = lax.rem(here + seq_count - d, seq_count)
        remote(rows, rows_out.at[origin], send_x.at[4, d - 1], recv_x.at[4, d - 1], seq=origin).wait()
    for a in (4, 0, 1, 2):
        for d in range(1, seq_count):
            piece(a, d).wait_send()


def gather_start(arrays, seq_count, shards, collective):
    count = shards // 2
    wq, wk, wv, wo, small, gains, routes, tokens = arrays
    rows, model_width = wq.shape
    width = model_width // seq_count
    sheet = jax.ShapeDtypeStruct((seq_count, shards, rows, width), BF)
    shapes = [
        sheet,
        sheet,
        sheet,
        jax.ShapeDtypeStruct((shards,) + wo.shape, BF),
        jax.ShapeDtypeStruct((seq_count, shards) + small.shape, BF),
        jax.ShapeDtypeStruct((shards,) + gains.shape, BF),
        jax.ShapeDtypeStruct((shards,) + routes.shape, jnp.int32),
        jax.ShapeDtypeStruct((seq_count,) + tokens.shape, BF),
    ]
    holds = [pltpu.VMEM((rows, width), BF)] * 3 + [
        pltpu.VMEM(wo.shape, BF),
        pltpu.VMEM(small.shape, BF),
        pltpu.VMEM(gains.shape, BF),
        pltpu.VMEM(routes.shape, jnp.int32),
        pltpu.VMEM(tokens.shape, BF),
    ]
    return pl.pallas_call(
        partial(start_kernel, count, seq_count),
        out_shape=shapes,
        in_specs=[pl.BlockSpec(memory_space=ANY)] * 8,
        out_specs=[pl.BlockSpec(memory_space=ANY)] * 8,
        scratch_shapes=holds
        + [DMA((5, seq_count - 1)), DMA((5, seq_count - 1)), DMA((8,))]
        + line_sems(7, count),
        compiler_params=pltpu.CompilerParams(collective_id=collective, has_side_effects=True),
        name="gather_start",
    )(*arrays)


def chunk_order(k, p, count):
    near = jnp.minimum(p, count - 1 - p)
    step = (k + 1) // 2
    both = jnp.where(k % 2 == 1, p - step, p + step)
    return jnp.where(k <= 2 * near, both, jnp.where(p < count - 1 - p, k, count - 1 - k))


class LineScatter:
    def __init__(self, count, places, sources, axes, bufs, sems):
        self.count, self.places = count, places
        self.sources, self.axes = sources, axes
        self.own, self.sib, self.inbox = bufs
        self.sems = sems

    def load(self, a, q):
        i = self.places[0]
        src = slot_of(self.sources[a], self.axes[a], 2 * q + lax.rem(i, 2))
        return pltpu.make_async_copy(src, self.own[a].at[q], self.sems[6].at[a, q])

    def to_sib(self, a, q):
        sib = self.places[2]
        src = slot_of(self.sources[a], self.axes[a], 2 * q + lax.rem(sib, 2))
        return remote(src, self.sib[a].at[q], self.sems[2].at[a, q], self.sems[5].at[a, q], fsdp=sib)

    def right(self, a, q):
        i = self.places[0]
        return remote(
            self.own[a].at[q], self.inbox[a].at[q], self.sems[0].at[a, q], self.sems[3].at[a, q], fsdp=i + 2
        )

    def left(self, a, q):
        i, p, sib = self.places
        slot = jnp.where(q == p - 1, self.count, q)
        return remote(
            self.own[a].at[q], self.inbox[a].at[slot], self.sems[1].at[a, q], self.sems[4].at[a, q], fsdp=i - 2
        )

    def begin_loads(self):
        for k in range(self.count):
            q = chunk_order(self.count - 1 - k, self.places[1], self.count)
            for a in range(len(self.sources)):
                self.load(a, q).start()

    def begin(self):
        for k in range(self.count):
            q = chunk_order(self.count - 1 - k, self.places[1], self.count)
            for a in range(len(self.sources)):
                self.to_sib(a, q).start()

    def add(self, a, q, others):
        own = self.own[a]
        lead = own.shape[1:-2]
        rows, width = own.shape[-2:]
        step = rows
        while step * width > 65536 and step % 16 == 0:
            step //= 2

        def strip(index):
            total = own[index].astype(F32) + self.sib[a][index].astype(F32)
            for slot in others:
                total += self.inbox[a][(slot,) + index[1:]].astype(F32)
            own[index] = total.astype(own.dtype)

        def rows_of(prefix):
            if step == rows:
                strip(prefix)
                return

            @pl.loop(0, rows // step)
            def _(k):
                strip(prefix + (pl.ds(pl.multiple_of(k * step, step), step),))

        if lead:
            for b in range(lead[0]):
                rows_of((q, b))
        else:
            rows_of((q,))

    def ready(self, a, q):
        self.load(a, q).wait()
        self.to_sib(a, q).wait_recv()

    def run(self, after, between=None):
        i, p, sib = self.places
        count = self.count
        arrays = range(len(self.sources))

        @pl.loop(0, count - 1)
        def _(step):
            @pl.when(step >= p)
            def _():
                q = count - 1 - (step - p)
                for a in arrays:
                    self.ready(a, q)

                    @pl.when(p > 0)
                    def _():
                        self.right(a, q).wait_recv()
                        self.add(a, q, [q])

                    @pl.when(p == 0)
                    def _():
                        self.add(a, q, [])

                    self.right(a, q).start()

            @pl.when(step >= count - 1 - p)
            def _():
                q = step - (count - 1 - p)
                for a in arrays:
                    self.ready(a, q)

                    @pl.when(p < count - 1)
                    def _():
                        self.left(a, q).wait_recv()
                        self.add(a, q, [q])

                    @pl.when(p == count - 1)
                    def _():
                        self.add(a, q, [])

                    self.left(a, q).start()

            if between is not None:
                between(step)

        for a in arrays:
            self.ready(a, p)

            @pl.when(p > 0)
            def _():
                self.right(a, p).wait_recv()

            @pl.when(p < count - 1)
            def _():
                self.left(a, p).wait_recv()

            @pl.when(p == 0)
            def _():
                self.add(a, p, [count])

            @pl.when(p == count - 1)
            def _():
                self.add(a, p, [p])

            @pl.when((p > 0) & (p < count - 1))
            def _():
                self.add(a, p, [p, count])

            after(a, p)

    def finish(self):
        i, p, sib = self.places
        for a in range(len(self.sources)):
            for q in range(self.count):
                self.to_sib(a, q).wait_send()

                @pl.when(q > p)
                def _():
                    self.right(a, q).wait_send()

                @pl.when(q < p)
                def _():
                    self.left(a, q).wait_send()


def end_kernel(count, seq_count, *refs):
    sources = refs[:6]
    rows_ref = refs[6]
    outs = refs[7:13]
    sum_ref = refs[13]
    bufs = tuple(refs[14 + 6 * k : 20 + 6 * k] for k in range(3))
    landing = refs[32]
    sems = refs[33:40]
    send_x, recv_x, local = refs[40:43]
    seq = SeqScatter(seq_count, rows_ref, *refs[43:48])
    places = where_am_i()
    here = lax.axis_index("seq")
    width = sources[0].shape[3]
    line = LineScatter(count, places, sources, [1, 1, 1, 0, 1, 0], bufs, sems)
    line.begin_loads()
    seq.take.start()
    greet(count, places, seq_count)
    seq.begin()
    line.begin()
    own = bufs[0]

    def at_home(a, block):
        if a == 4:
            return landing.at[block]
        start = pl.multiple_of(block * width, width)
        return outs[a].at[:, pl.ds(start, width)]

    def piece(a, q, d):
        peer = lax.rem(here + d, seq_count)
        slot = 3 if a == 4 else a
        return remote(
            own[a].at[q, peer], at_home(a, here), send_x.at[slot, d - 1], recv_x.at[slot, d - 1], seq=peer
        )

    def arrived(a, d):
        origin = lax.rem(here + seq_count - d, seq_count)
        slot = 3 if a == 4 else a
        return remote(
            at_home(a, origin), at_home(a, origin), send_x.at[slot, d - 1], recv_x.at[slot, d - 1], seq=origin
        )

    def after(a, q):
        if a in (3, 5):
            pltpu.make_async_copy(own[a].at[q], outs[a], local.at[a]).start()
        else:
            for d in range(1, seq_count):
                piece(a, q, d).start()
            pltpu.make_async_copy(own[a].at[q, here], at_home(a, here), local.at[a]).start()

    line.run(after)
    seq.total(sum_ref)
    for q in range(count):

        @pl.when(q == places[1])
        def _():
            for a in range(6):
                if a in (3, 5):
                    pltpu.make_async_copy(own[a].at[q], outs[a], local.at[a]).wait()
                else:
                    pltpu.make_async_copy(own[a].at[q, here], at_home(a, here), local.at[a]).wait()
                    for d in range(1, seq_count):
                        piece(a, q, d).wait_send()
                        arrived(a, d).wait_recv()

    total = landing[0]
    for block in range(1, seq_count):
        total += landing[block]
    landing[0] = total
    last = pltpu.make_async_copy(landing.at[0], outs[4], local.at[4])
    last.start()
    last.wait()
    line.finish()
    seq.finish()


def scatter_end(arrays, row_blocks, seq_count, shards, collective):
    count = shards // 2
    gq, gk, gv, go, small, gains = arrays
    rows, width = gq.shape[2:]
    home = jax.ShapeDtypeStruct((rows, width * seq_count), BF)
    shapes = [
        home,
        home,
        home,
        jax.ShapeDtypeStruct(go.shape[1:], BF),
        jax.ShapeDtypeStruct(small.shape[2:], F32),
        jax.ShapeDtypeStruct(gains.shape[1:], F32),
        jax.ShapeDtypeStruct(row_blocks.shape[1:], F32),
    ]
    blocks, inboxes = [], []
    for a in range(6):
        shape = arrays[a].shape
        block = (shape[0],) + shape[2:] if a in (0, 1, 2, 4) else shape[1:]
        blocks.append(pltpu.VMEM((count,) + block, arrays[a].dtype))
        inboxes.append(pltpu.VMEM((count + 1,) + block, arrays[a].dtype))
    return pl.pallas_call(
        partial(end_kernel, count, seq_count),
        out_shape=shapes,
        in_specs=[pl.BlockSpec(memory_space=ANY)] * 7,
        out_specs=[pl.BlockSpec(memory_space=ANY)] * 6 + [pl.BlockSpec(memory_space=pltpu.VMEM)],
        scratch_shapes=blocks * 2
        + inboxes
        + [pltpu.VMEM((seq_count,) + small.shape[2:], F32)]
        + [DMA((6, count))] * 7
        + [DMA((4, seq_count - 1)), DMA((4, seq_count - 1)), DMA((6,))]
        + seq_scatter_scratch(row_blocks.shape[1:], row_blocks.dtype, seq_count),
        compiler_params=pltpu.CompilerParams(
            collective_id=collective, has_side_effects=True, vmem_limit_bytes=62 << 20
        ),
        name="scatter_end",
    )(*arrays, row_blocks)


def greet_seq(seq_count):
    here = lax.axis_index("seq")
    barrier = pltpu.get_barrier_semaphore()
    for d in range(1, seq_count):
        peer = lax.rem(here + d, seq_count)
        pl.semaphore_signal(barrier, inc=1, device_id={"seq": peer}, device_id_type=MESH)
    pl.semaphore_wait(barrier, seq_count - 1)
    return here


class SeqScatter:
    def __init__(self, seq_count, x_ref, own, inbox, send, recv, local):
        here = lax.axis_index("seq")
        self.own, self.inbox, self.count = own, inbox, seq_count
        self.take = pltpu.make_async_copy(x_ref.at[here], own, local)
        self.copies = []
        for d in range(1, seq_count):
            peer = lax.rem(here + d, seq_count)
            self.copies.append(
                remote(x_ref.at[peer], inbox.at[d - 1], send.at[d - 1], recv.at[d - 1], seq=peer)
            )

    def begin(self):
        for copy in self.copies:
            copy.start()

    def total(self, o_ref):
        self.take.wait()
        for copy in self.copies:
            copy.wait_recv()
        rows = self.own.shape[0]
        step = min(32, rows)

        @pl.loop(0, rows // step)
        def _(k):
            strip = pl.ds(pl.multiple_of(k * step, step), step)
            total = self.own[strip, :].astype(F32)
            for d in range(self.count - 1):
                total += self.inbox[d, strip, :].astype(F32)
            o_ref[strip, :] = total

    def finish(self):
        for copy in self.copies:
            copy.wait_send()


def seq_scatter_scratch(block, dtype, seq_count):
    return [
        pltpu.VMEM(block, dtype),
        pltpu.VMEM((seq_count - 1,) + block, dtype),
        DMA((seq_count - 1,)),
        DMA((seq_count - 1,)),
        DMA,
    ]


def middle_kernel(
    count, seq_count, x_ref, dy_ref, o_ref, all_ref, own, inbox, xs, xr, xl, hold, s0, s1, s2, recv, local
):
    places = where_am_i()
    i = places[0]
    seq = SeqScatter(seq_count, x_ref, own, inbox, xs, xr, xl)
    seq.take.start()
    take = pltpu.make_async_copy(dy_ref, hold, local.at[0])
    take.start()
    greet(count, places, seq_count)
    seq.begin()
    take.wait()
    put = pltpu.make_async_copy(hold, all_ref.at[i], local.at[1])
    put.start()
    put.wait()
    line = LineGather(count, places, [all_ref], [0], s0, s1, s2, recv)
    line.first(0)
    for t in range(1, count):
        line.forward(t)
    seq.total(o_ref)
    line.finish()
    seq.finish()


def middle(blocks, dy, shards, collective):
    count = shards // 2
    seq_count = blocks.shape[0]
    block = blocks.shape[1:]
    return pl.pallas_call(
        partial(middle_kernel, count, seq_count),
        out_shape=[
            jax.ShapeDtypeStruct(block, F32),
            jax.ShapeDtypeStruct((shards,) + dy.shape, dy.dtype),
        ],
        in_specs=[pl.BlockSpec(memory_space=ANY)] * 2,
        out_specs=[pl.BlockSpec(memory_space=pltpu.VMEM), pl.BlockSpec(memory_space=ANY)],
        scratch_shapes=seq_scatter_scratch(block, blocks.dtype, seq_count)
        + [pltpu.VMEM(dy.shape, dy.dtype)]
        + line_sems(1, count)
        + [DMA((2,))],
        compiler_params=pltpu.CompilerParams(
            collective_id=collective, has_side_effects=True, vmem_limit_bytes=32 << 20
        ),
        name="middle",
    )(blocks, dy)


def seq_sum_kernel(seq_count, x_ref, o_ref, inbox, send, recv):
    here = greet_seq(seq_count)
    copies = []
    for d in range(1, seq_count):
        peer = lax.rem(here + d, seq_count)
        copies.append(remote(x_ref, inbox.at[d - 1], send.at[d - 1], recv.at[d - 1], seq=peer))
    for copy in copies:
        copy.start()
    for copy in copies:
        copy.wait_recv()
    total = x_ref[...]
    for d in range(seq_count - 1):
        total += inbox[d]
    o_ref[...] = total
    for copy in copies:
        copy.wait_send()


def seq_sum(value, seq_count, collective):
    return pl.pallas_call(
        partial(seq_sum_kernel, seq_count),
        out_shape=jax.ShapeDtypeStruct(value.shape, F32),
        in_specs=[pl.BlockSpec(memory_space=pltpu.VMEM)],
        out_specs=pl.BlockSpec(memory_space=pltpu.VMEM),
        scratch_shapes=[
            pltpu.VMEM((seq_count - 1,) + value.shape, F32),
            DMA((seq_count - 1,)),
            DMA((seq_count - 1,)),
        ],
        compiler_params=pltpu.CompilerParams(collective_id=collective, has_side_effects=True),
        name="seq_sum",
    )(value)


class GateUpGrads:
    def __init__(self, ins, outs, scratch, steps):
        self.ins, self.outs = ins, outs
        self.held, self.staged, self.in_sem, self.out_sem = scratch
        self.experts, self.width, self.hidden = outs[0].shape
        self.tile = self.staged[0].shape[1]
        self.tiles = self.width // self.tile
        self.units = self.experts * self.tiles
        self.share = -(-self.units // steps)

    def fetch(self, n, e):
        return pltpu.make_async_copy(self.ins[n].at[e], self.held[n].at[e], self.in_sem.at[n, e])

    def begin(self):
        for e in range(self.experts):
            for n in range(3):
                self.fetch(n, e).start()
        self.logits().start()
        self.pair(0).start()

    def logits(self):
        return pltpu.make_async_copy(self.ins[4], self.held[4], self.in_sem.at[3, 0])

    def pair(self, q):
        buf = lax.rem(q, 2)
        src = self.ins[3].at[pl.ds(2 * q, 2)]
        return pltpu.make_async_copy(src, self.held[3].at[buf], self.in_sem.at[4, buf])

    def put(self, n, u, buf):
        rows = pl.ds(pl.multiple_of(lax.rem(u, self.tiles) * self.tile, self.tile), self.tile)
        target = self.outs[n].at[u // self.tiles, rows]
        return pltpu.make_async_copy(self.staged[n].at[buf], target, self.out_sem.at[n, buf])

    def between(self, step):
        over_rows = (((0,), (0,)), ((), ()))
        rows, gates, ups, tokens, logits = self.held

        @pl.loop(step * self.share, jnp.minimum((step + 1) * self.share, self.units))
        def _(u):
            e = u // self.tiles
            buf = lax.rem(u, 2)

            @pl.when(lax.rem(u, self.tiles) == 0)
            def _():
                for n in range(3):
                    self.fetch(n, e).wait()

            @pl.when(u >= 2)
            def _():
                self.put(0, u - 2, buf).wait()
                self.put(1, u - 2, buf).wait()

            cols = pl.ds(pl.multiple_of(lax.rem(u, self.tiles) * self.tile, self.tile), self.tile)
            left = rows[e, :, cols]
            for n, right in ((0, gates), (1, ups)):
                self.staged[n][buf] = lax.dot_general(
                    left, right[e], over_rows, preferred_element_type=F32
                ).astype(BF)
                self.put(n, u, buf).start()

        @pl.when(step == 0)
        def _():
            self.logits().wait()
            total_ref = self.outs[2]
            total_ref[...] = jnp.zeros_like(total_ref)
            block = 512
            pairs = self.ins[3].shape[0] // 2

            @pl.loop(0, pairs)
            def _(q):
                self.pair(q).wait()

                @pl.when(q + 1 < pairs)
                def _():
                    self.pair(q + 1).start()

                buf = lax.rem(q, 2)

                @pl.loop(0, self.width // block)
                def _(n):
                    cols = pl.ds(pl.multiple_of(n * block, block), block)
                    total = total_ref[:, cols]
                    for j in range(2):
                        total += jnp.dot(
                            logits[2 * q + j], tokens[buf, j, :, cols], preferred_element_type=F32
                        )
                    total_ref[:, cols] = total

    def finish(self):
        for u in (self.units - 2, self.units - 1):
            for n in range(2):
                self.put(n, u, u % 2).wait()


def turn_kernel(
    count,
    seq_count,
    x_ref,
    parts_ref,
    in0,
    in1,
    in2,
    in3,
    in4,
    o_ref,
    sum_ref,
    out0,
    out1,
    out2,
    hold,
    send,
    recv,
    one,
    held0,
    held1,
    held2,
    held3,
    held4,
    staged0,
    staged1,
    in_sem,
    out_sem,
    own,
    sib,
    inbox,
    *sems,
):
    places = where_am_i()
    here = lax.axis_index("seq")
    line = LineScatter(count, places, [parts_ref], [0], ([own], [sib], [inbox]), sems)
    grads = GateUpGrads(
        (in0, in1, in2, in3, in4),
        (out0, out1, out2),
        ((held0, held1, held2, held3, held4), (staged0, staged1), in_sem, out_sem),
        count - 1,
    )
    line.begin_loads()
    take = pltpu.make_async_copy(x_ref, hold, one)
    take.start()
    grads.begin()
    greet(count, places, seq_count)
    for d in range(1, seq_count):
        peer = lax.rem(here + d, seq_count)
        remote(x_ref, o_ref.at[here], send.at[d - 1], recv.at[d - 1], seq=peer).start()
    line.begin()
    take.wait()
    put = pltpu.make_async_copy(hold, o_ref.at[here], one)
    put.start()

    def after(a, q):
        out = pltpu.make_async_copy(own.at[q], sum_ref, sems[6].at[0, q])
        out.start()
        out.wait()

    line.run(after, grads.between)
    grads.finish()
    put.wait()
    for d in range(1, seq_count):
        origin = lax.rem(here + seq_count - d, seq_count)
        remote(x_ref, o_ref.at[origin], send.at[d - 1], recv.at[d - 1], seq=origin).wait()
    line.finish()


def turn_back(block, parts, expert_in, d_gate, d_up, h2_all, logits, seq_count, shards, collective):
    count = shards // 2
    part = parts.shape[1:]
    model_width = part[1]
    local_experts, slots, hidden = d_gate.shape
    tile = 512
    grad = jax.ShapeDtypeStruct((local_experts, model_width, hidden), BF)
    anywhere = pl.BlockSpec(memory_space=ANY)
    return pl.pallas_call(
        partial(turn_kernel, count, seq_count),
        out_shape=[
            jax.ShapeDtypeStruct((seq_count,) + block.shape, block.dtype),
            jax.ShapeDtypeStruct(part, parts.dtype),
            grad,
            grad,
            jax.ShapeDtypeStruct((logits.shape[1], model_width), F32),
        ],
        in_specs=[anywhere] * 7,
        out_specs=[anywhere] * 4 + [pl.BlockSpec(memory_space=pltpu.VMEM)],
        scratch_shapes=[
            pltpu.VMEM(block.shape, block.dtype),
            DMA((seq_count - 1,)),
            DMA((seq_count - 1,)),
            DMA,
        ]
        + [pltpu.VMEM(x.shape, BF) for x in (expert_in, d_gate, d_up)]
        + [pltpu.VMEM((2, 2) + h2_all.shape[1:], BF), pltpu.VMEM(logits.shape, BF)]
        + [pltpu.VMEM((2, tile, hidden), BF)] * 2
        + [DMA((5, max(2, local_experts))), DMA((2, 2))]
        + [pltpu.VMEM((count,) + part, BF)] * 2
        + [pltpu.VMEM((count + 1,) + part, BF)]
        + [DMA((1, count))] * 7,
        compiler_params=pltpu.CompilerParams(
            collective_id=collective, has_side_effects=True, vmem_limit_bytes=60 << 20
        ),
        cost_estimate=pl.CostEstimate(flops=60_000_000_000, bytes_accessed=200_000_000, transcendentals=0),
        name="turn_back",
    )(block, parts, expert_in, d_gate, d_up, h2_all, logits)


def half_sign(shape):
    lane = lax.broadcasted_iota(jnp.int32, shape, 1)
    return jnp.where(lane < shape[1] // 2, -1.0, 1.0)


def turn(value):
    return pltpu.roll(value, value.shape[1] // 2, 1)


def block_probs(q_rows, keys, doc_col, doc_row, start, scale_by):
    end = keys.shape[0]
    scores = (
        lax.dot_general(q_rows, keys, (((1,), (1,)), ((), ())), preferred_element_type=F32) * scale_by
    )
    shape = scores.shape
    query_pos = start + lax.broadcasted_iota(jnp.int32, shape, 0)
    key_pos = lax.broadcasted_iota(jnp.int32, shape, 1)
    allowed = (doc_col == doc_row) & (key_pos <= query_pos)
    scores = jnp.where(allowed, scores, MASKED_OUT)
    weights = jnp.exp(scores - jnp.max(scores, axis=-1, keepdims=True))
    return weights * (1.0 / jnp.sum(weights, axis=-1, keepdims=True))


def attend_kernel(
    row_block, q_raw, k_raw, v_ref, rq, rk, gq, gk, cos, sin, doc_col, doc_row, o_ref, q_out, k_out
):
    seq_len = q_raw.shape[0]
    sign = half_sign(cos.shape)

    def rotated(raw, scale, gain):
        value = raw[...] * scale[...] * gain[...]
        return (value * cos[...] + turn(value) * (sin[...] * sign)).astype(BF)

    q_out[...] = rotated(q_raw, rq, gq)
    k_out[...] = rotated(k_raw, rk, gk)
    scale_by = HEAD ** (-0.5)
    for start in range(0, seq_len, row_block):
        end = start + row_block
        probs = block_probs(
            q_out[start:end, :], k_out[:end, :], doc_col[start:end, :], doc_row[:, :end], start, scale_by
        )
        o_ref[start:end, :] = jnp.dot(
            probs.astype(BF), v_ref[:end, :], preferred_element_type=F32
        ).astype(BF)


def attend(q_raw, k_raw, values, rq, rk, gq, gk, cos, sin, doc_col, doc_row):
    seq_len, width = q_raw.shape
    head = pl.BlockSpec((seq_len, HEAD), lambda h: (0, h))
    gain = pl.BlockSpec((1, HEAD), lambda h: (0, h))

    def whole(x):
        return pl.BlockSpec(x.shape, lambda h: (0, 0))

    out = jax.ShapeDtypeStruct((seq_len, width), BF)
    return pl.pallas_call(
        partial(attend_kernel, 256),
        grid=(width // HEAD,),
        out_shape=[out, out, out],
        in_specs=[head, head, head, whole(rq), whole(rk), gain, gain, whole(cos), whole(sin)]
        + [whole(doc_col), whole(doc_row)],
        out_specs=[head, head, head],
        compiler_params=pltpu.CompilerParams(vmem_limit_bytes=48 << 20),
        name="attend",
    )(q_raw, k_raw, values, rq, rk, gq, gk, cos, sin, doc_col, doc_row)


def attend_back_kernel(
    row_block,
    q_low,
    k_low,
    v_ref,
    do_ref,
    q_raw,
    k_raw,
    rq,
    rk,
    gq,
    gk,
    cos,
    sin,
    doc_col,
    doc_row,
    uq_ref,
    uk_ref,
    dv_ref,
    dots,
    gain_q,
    gain_k,
    dq_acc,
    dk_acc,
    dv_acc,
):
    seq_len = q_low.shape[0]
    scale_by = HEAD ** (-0.5)
    dk_acc[...] = jnp.zeros_like(dk_acc)
    dv_acc[...] = jnp.zeros_like(dv_acc)
    for start in range(0, seq_len, row_block):
        end = start + row_block
        rows = slice(start, end)
        probs = block_probs(
            q_low[rows, :], k_low[:end, :], doc_col[rows, :], doc_row[:, :end], start, scale_by
        )
        grad_rows = do_ref[rows, :]
        grad_probs = lax.dot_general(
            grad_rows, v_ref[:end, :], (((1,), (1,)), ((), ())), preferred_element_type=F32
        )
        centre = jnp.sum(probs * grad_probs, axis=-1, keepdims=True)
        grad_scores = (probs * (grad_probs - centre)).astype(BF)
        dq_acc[rows, :] = jnp.dot(grad_scores, k_low[:end, :], preferred_element_type=F32)
        over_rows = (((0,), (0,)), ((), ()))
        dk_acc[:end, :] += lax.dot_general(
            grad_scores, q_low[rows, :], over_rows, preferred_element_type=F32
        )
        dv_acc[:end, :] += lax.dot_general(
            probs.astype(BF), grad_rows, over_rows, preferred_element_type=F32
        )
    dv_ref[...] = dv_acc[...].astype(BF)
    sign = half_sign(cos.shape)

    def unrotated(acc, raw, scale, gain, u_ref, gain_ref, lane):
        low = (acc[...] * scale_by).astype(BF).astype(F32)
        back = low * cos[...] - turn(low * sin[...]) * sign
        gain_ref[...] = jnp.sum(back * raw[...] * scale[...], axis=0, keepdims=True)
        u = back * gain[...]
        u_ref[...] = u
        dot = jnp.sum(u * raw[...], axis=1, keepdims=True)

        @pl.when(pl.program_id(0) == 0)
        def _():
            dots[:, lane : lane + 1] = dot

        @pl.when(pl.program_id(0) > 0)
        def _():
            dots[:, lane : lane + 1] += dot

    unrotated(dq_acc, q_raw, rq, gq, uq_ref, gain_q, 0)
    unrotated(dk_acc, k_raw, rk, gk, uk_ref, gain_k, 1)


def attend_back(q_low, k_low, values, d_heads, q_raw, k_raw, rq, rk, gq, gk, cos, sin, doc_col, doc_row):
    seq_len, width = q_raw.shape
    head = pl.BlockSpec((seq_len, HEAD), lambda h: (0, h))
    gain = pl.BlockSpec((1, HEAD), lambda h: (0, h))

    def whole(x):
        return pl.BlockSpec(x.shape, lambda h: (0, 0))

    wide = jax.ShapeDtypeStruct((seq_len, width), F32)
    row = jax.ShapeDtypeStruct((1, width), F32)
    return pl.pallas_call(
        partial(attend_back_kernel, 256),
        grid=(width // HEAD,),
        out_shape=[
            wide,
            wide,
            jax.ShapeDtypeStruct((seq_len, width), BF),
            jax.ShapeDtypeStruct((seq_len, 2), F32),
            row,
            row,
        ],
        in_specs=[head] * 6
        + [whole(rq), whole(rk), gain, gain, whole(cos), whole(sin), whole(doc_col), whole(doc_row)],
        out_specs=[head, head, head, pl.BlockSpec((seq_len, 2), lambda h: (0, 0)), gain, gain],
        scratch_shapes=[pltpu.VMEM((seq_len, HEAD), F32)] * 3,
        compiler_params=pltpu.CompilerParams(vmem_limit_bytes=56 << 20),
        name="attend_back",
    )(q_low, k_low, values, d_heads, q_raw, k_raw, rq, rk, gq, gk, cos, sin, doc_col, doc_row)


def experts_in_kernel(
    count,
    cap,
    h2_ref,
    dy_ref,
    targets,
    router_t,
    wg_ref,
    wu_ref,
    h2_out,
    x_out,
    y_out,
    act_out,
    by_up_out,
    by_gate_out,
    gate_slots,
    probs_out,
    h2,
    wg,
    wu,
    dy,
    xs,
    ys,
    acts,
    by_up,
    by_gate,
    s0,
    s1,
    s2,
    recv,
    w_sem,
    dy_sem,
    h_sem,
    out_sem,
):
    places = where_am_i()
    i, p, sib = places
    local_experts, model_width, hidden = wg_ref.shape
    tokens = h2_ref.shape[0]
    experts = router_t.shape[0]
    own_in = pltpu.make_async_copy(h2_ref, h2.at[i], h_sem.at[0])
    own_in.start()

    def fetch(q, buf):
        src = dy_ref.at[pl.ds(2 * q, 2)]
        return pltpu.make_async_copy(src, dy.at[buf], dy_sem.at[buf])

    fetch(p, 0).start()
    for e in range(local_experts):
        pltpu.make_async_copy(wg_ref.at[e], wg.at[e], w_sem.at[0, e]).start()
        pltpu.make_async_copy(wu_ref.at[e], wu.at[e], w_sem.at[1, e]).start()
    greet(count, places)
    own_in.wait()
    line = LineGather(count, places, [h2], [0], s0, s1, s2, recv)
    line.first(0)
    staged = ((xs, x_out), (ys, y_out), (acts, act_out), (by_up, by_up_out), (by_gate, by_gate_out))

    def store(n, e, q):
        rows = pl.ds(pl.multiple_of(q * 2 * cap, 2 * cap), 2 * cap)
        return pltpu.make_async_copy(staged[n][0].at[e], staged[n][1].at[e, rows], out_sem.at[n, e])

    def keep(q):
        src = h2.at[pl.ds(2 * q, 2)]
        return pltpu.make_async_copy(src, h2_out.at[pl.ds(2 * q, 2)], h_sem.at[1])

    slot_rows = lax.broadcasted_iota(jnp.int32, (local_experts * cap, tokens), 0)
    expert_rows = lax.broadcasted_iota(jnp.int32, (experts, tokens), 0)

    @pl.loop(0, count)
    def _(k):
        q = chunk_order(k, p, count)
        buf = k % 2

        @pl.when(k > 0)
        def _():
            line.forward(k)

        line.copy(0, 2 * q + lax.rem(sib, 2), 2, 0, sib).wait_recv()
        fetch(q, buf).wait()

        @pl.when(k + 1 < count)
        def _():
            fetch(chunk_order(k + 1, p, count), 1 - buf).start()

        @pl.when(k > 0)
        def _():
            for n in range(5):
                for e in range(local_experts):
                    store(n, e, q).wait()
            keep(q).wait()

        keep(q).start()
        picks = []
        for j in range(2):
            slot = 2 * q + j
            tokens_j = h2[slot]
            logits = lax.dot_general(
                router_t[...], tokens_j, (((1,), (1,)), ((), ())), preferred_element_type=F32
            )
            shifted = jnp.exp(logits - jnp.max(logits, axis=0, keepdims=True))
            probs = shifted / jnp.sum(shifted, axis=0, keepdims=True)
            probs_out[slot] = probs
            pick = None
            for e in range(local_experts):
                mask = slot_rows == targets[slot, e : e + 1, :]
                gate = jnp.sum(
                    jnp.where(expert_rows == i * local_experts + e, probs, 0.0), axis=0, keepdims=True
                )
                part = slice(e * cap, (e + 1) * cap)
                gate_slots[e, q, j * cap : (j + 1) * cap, :] = jnp.sum(
                    jnp.where(mask[part], gate, 0.0), axis=1, keepdims=True
                )
                pick = mask if pick is None else pick | mask
            picks.append(jnp.where(pick, 1.0, 0.0).astype(BF))

        block = 512

        @pl.loop(0, model_width // block)
        def _(n):
            cols = pl.ds(pl.multiple_of(n * block, block), block)
            for source, target in ((0, xs), (1, ys)):
                got = []
                for j in range(2):
                    rows = h2[2 * q + j, :, cols] if source == 0 else dy[buf, j, :, cols]
                    got.append(jnp.dot(picks[j], rows, preferred_element_type=F32))
                for e in range(local_experts):
                    part = slice(e * cap, (e + 1) * cap)
                    target[e, :, cols] = jnp.concatenate([got[0][part], got[1][part]], axis=0).astype(BF)

        for e in range(local_experts):
            store(0, e, q).start()
            store(1, e, q).start()

            @pl.when(k == 0)
            def _():
                pltpu.make_async_copy(wg_ref.at[e], wg.at[e], w_sem.at[0, e]).wait()
                pltpu.make_async_copy(wu_ref.at[e], wu.at[e], w_sem.at[1, e]).wait()

            wide = 256

            @pl.loop(0, hidden // wide)
            def _(n):
                cols = pl.ds(pl.multiple_of(n * wide, wide), wide)
                gate = jnp.dot(xs[e], wg[e, :, cols], preferred_element_type=F32)
                up = jnp.dot(xs[e], wu[e, :, cols], preferred_element_type=F32)
                sigmoid = 1.0 / (1.0 + jnp.exp(-gate))
                silu = gate * sigmoid
                acts[e, :, cols] = (silu * up).astype(BF)
                by_up[e, :, cols] = silu.astype(BF)
                by_gate[e, :, cols] = (up * sigmoid * (1.0 + gate * (1.0 - sigmoid))).astype(BF)

            for n in (2, 3, 4):
                store(n, e, q).start()

    for n in range(5):
        for e in range(local_experts):
            store(n, e, 0).wait()
    keep(0).wait()
    sends_done(line)


def sends_done(line):
    i, p, sib = line.places
    count = line.count
    line.copy(0, i, 2, 0, sib).wait_send()

    @pl.when(p < count - 1)
    def _():
        line.copy(0, i, 0, 0, i + 2).wait_send()

    @pl.when(p > 0)
    def _():
        line.copy(0, i, 1, 0, i - 2).wait_send()

    for t in range(1, count):

        @pl.when(p - t >= 0)
        def _():
            slot = i - 2 * t

            @pl.when(p < count - 1)
            def _():
                line.copy(0, slot, 0, t, i + 2).wait_send()

            line.copy(0, slot, 2, t, sib).wait_send()

        @pl.when(p + t < count)
        def _():
            slot = i + 2 * t

            @pl.when(p > 0)
            def _():
                line.copy(0, slot, 1, t, i - 2).wait_send()

            line.copy(0, slot, 2, count + t, sib).wait_send()


def experts_in(h2, dy_all, targets, router_t, w_gate, w_up, collective):
    shards, tokens, model_width = dy_all.shape
    local_experts, _, hidden = w_gate.shape
    experts = router_t.shape[0]
    count = shards // 2
    wide = jax.ShapeDtypeStruct((local_experts, count * 2 * CAP, model_width), BF)
    thin = jax.ShapeDtypeStruct((local_experts, count * 2 * CAP, hidden), BF)
    anywhere = pl.BlockSpec(memory_space=ANY)
    vmem = pl.BlockSpec(memory_space=pltpu.VMEM)
    return pl.pallas_call(
        partial(experts_in_kernel, count, CAP),
        out_shape=[
            jax.ShapeDtypeStruct((shards, tokens, model_width), BF),
            wide,
            wide,
            thin,
            thin,
            thin,
            jax.ShapeDtypeStruct((local_experts, count, 2 * CAP, 1), F32),
            jax.ShapeDtypeStruct((shards, experts, tokens), F32),
        ],
        in_specs=[anywhere, anywhere, vmem, vmem, anywhere, anywhere],
        out_specs=[anywhere] * 6 + [vmem, vmem],
        scratch_shapes=[
            pltpu.VMEM((shards, tokens, model_width), BF),
            pltpu.VMEM(w_gate.shape, BF),
            pltpu.VMEM(w_up.shape, BF),
            pltpu.VMEM((2, 2, tokens, model_width), BF),
        ]
        + [pltpu.VMEM((local_experts, 2 * CAP, model_width), BF)] * 2
        + [pltpu.VMEM((local_experts, 2 * CAP, hidden), BF)] * 3
        + line_sems(1, count)
        + [DMA((2, local_experts)), DMA((2,)), DMA((2,)), DMA((5, local_experts))],
        compiler_params=pltpu.CompilerParams(
            collective_id=collective, has_side_effects=True, vmem_limit_bytes=60 << 20
        ),
        name="experts_in",
    )(h2, dy_all, targets, router_t, w_gate, w_up)


class StagedScatter(LineScatter):
    def __init__(self, count, places, stage, bufs, sems):
        super().__init__(count, places, [None], [0], bufs, sems)
        self.stage = stage

    def to_sib(self, a, q):
        sib = self.places[2]
        return remote(self.stage, self.sib[a].at[q], self.sems[2].at[a, q], self.sems[5].at[a, q], fsdp=sib)

    def ready(self, a, q):
        self.to_sib(a, q).wait_recv()

    def finish(self):
        i, p, sib = self.places
        for q in range(self.count):

            @pl.when(q > p)
            def _():
                self.right(0, q).wait_send()

            @pl.when(q < p)
            def _():
                self.left(0, q).wait_send()


def experts_out_kernel(
    count,
    cap,
    y_in,
    act_in,
    by_up_in,
    by_gate_in,
    gate_slots,
    targets,
    targets_t,
    probs_ref,
    router_t,
    wg_in,
    wu_in,
    wd_in,
    gated_out,
    d_gate_out,
    d_up_out,
    parts_out,
    logit_ref,
    sum_ref,
    g_down_out,
    wg,
    wu,
    wd,
    ys,
    acts,
    by_ups,
    by_gates,
    gated,
    d_gate,
    d_up,
    parts,
    stage,
    own,
    sibling,
    inbox,
    w_sem,
    in_sem,
    out_sem,
    part_sem,
    down_sem,
    *rest,
):
    sems = rest[:7]
    room_gated, room_y = rest[7:] if len(rest) > 7 else (wg, wu)
    places = where_am_i()
    i, p, sib = places
    core = lax.rem(i, 2)
    local_experts, hidden, model_width = wd_in.shape
    tokens = targets.shape[2]
    experts = router_t.shape[0]
    first = i * local_experts
    over_lanes = (((1,), (1,)), ((), ()))
    line = StagedScatter(count, places, stage, ([own], [sibling], [inbox]), sems)
    weights = ((wd_in, wd), (wg_in, wg), (wu_in, wu))
    inputs = ((y_in, ys), (act_in, acts), (by_up_in, by_ups), (by_gate_in, by_gates))
    results = ((gated, gated_out), (d_gate, d_gate_out), (d_up, d_up_out))

    def weight(n):
        return pltpu.make_async_copy(weights[n][0], weights[n][1], w_sem.at[n])

    def rows_of(q):
        return pl.ds(pl.multiple_of(q * 2 * cap, 2 * cap), 2 * cap)

    def fetch(n, q, buf):
        src = inputs[n][0].at[:, rows_of(q)]
        return pltpu.make_async_copy(src, inputs[n][1].at[buf], in_sem.at[n, buf])

    def store(n, q):
        return pltpu.make_async_copy(results[n][0], results[n][1].at[:, rows_of(q)], out_sem.at[n])

    def put(q):
        return pltpu.make_async_copy(parts, parts_out.at[pl.ds(2 * q, 2)], part_sem)

    def order(k):
        return chunk_order(count - 1 - k, p, count)

    weight(0).start()
    for n in range(4):
        fetch(n, order(0), 0).start()
    weight(1).start()
    weight(2).start()
    greet(count, places)
    slot_rows = lax.broadcasted_iota(jnp.int32, (local_experts * cap, tokens), 0)
    slot_lanes = lax.broadcasted_iota(jnp.int32, (tokens, local_experts * cap), 1)
    expert_rows = lax.broadcasted_iota(jnp.int32, (experts, tokens), 0)

    def compute(k):
        q = order(k)
        buf = lax.rem(k, 2)
        for n in range(4):
            fetch(n, q, buf).wait()

        @pl.when(k + 1 < count)
        def _():
            for n in range(4):
                fetch(n, order(k + 1), 1 - buf).start()

        @pl.when(k > 0)
        def _():
            for n in range(3):
                store(n, q).wait()
            put(q).wait()
            line.to_sib(0, order(k - 1)).wait_send()

        @pl.when(k == 0)
        def _():
            weight(0).wait()

        dots = []
        for e in range(local_experts):
            wide = 256

            def step(n, dot):
                cols = pl.ds(pl.multiple_of(n * wide, wide), wide)
                grad_act = lax.dot_general(
                    ys[buf, e], wd[e, cols, :], over_lanes, preferred_element_type=F32
                )
                act = acts[buf, e, :, cols].astype(F32)
                gate = gate_slots[e, q]
                dot = dot + jnp.sum(act * grad_act, axis=1, keepdims=True)
                grad_act = grad_act * gate
                gated[e, :, cols] = (act * gate).astype(BF)
                d_up[e, :, cols] = (grad_act * by_ups[buf, e, :, cols].astype(F32)).astype(BF)
                d_gate[e, :, cols] = (grad_act * by_gates[buf, e, :, cols].astype(F32)).astype(BF)
                return dot

            dots.append(lax.fori_loop(0, hidden // wide, step, jnp.zeros((2 * cap, 1), F32)))
        for n in range(3):
            store(n, q).start()

        picks, logits_low = [], []
        for j in range(2):
            slot = 2 * q + j
            grad_probs = jnp.zeros((experts, tokens), F32)
            pick = None
            for e in range(local_experts):
                part = slice(e * cap, (e + 1) * cap)
                mask = (slot_rows == targets[slot, e : e + 1, :])[part]
                row = jnp.sum(jnp.where(mask, dots[e][j * cap : (j + 1) * cap], 0.0), axis=0, keepdims=True)
                grad_probs = jnp.where(expert_rows == first + e, row, grad_probs)
                hit = slot_lanes == targets_t[slot, :, e : e + 1]
                pick = hit if pick is None else pick | hit
            probs = probs_ref[slot]
            grad_logits = probs * (grad_probs - jnp.sum(probs * grad_probs, axis=0, keepdims=True))
            logit_ref[slot] = grad_logits.astype(BF)
            picks.append(jnp.where(pick, 1.0, 0.0).astype(BF))
            logits_low.append(grad_logits.T.astype(BF))

        @pl.when(k == 0)
        def _():
            weight(1).wait()
            weight(2).wait()

        block = 512

        @pl.loop(0, model_width // block)
        def _(n):
            cols = pl.ds(pl.multiple_of(n * block, block), block)
            outs, grads = [], []
            for e in range(local_experts):
                outs.append(jnp.dot(gated[e], wd[e, :, cols], preferred_element_type=F32))
                grads.append(
                    lax.dot_general(d_gate[e], wg[e, cols, :], over_lanes, preferred_element_type=F32)
                    + lax.dot_general(d_up[e], wu[e, cols, :], over_lanes, preferred_element_type=F32)
                )
            for j in range(2):
                part = slice(j * cap, (j + 1) * cap)
                mine = jnp.concatenate([value[part] for value in outs], axis=0).astype(BF)
                back = jnp.concatenate([value[part] for value in grads], axis=0).astype(BF)
                parts[j, :, cols] = jnp.dot(picks[j], mine, preferred_element_type=F32).astype(BF)
                total = (
                    jnp.dot(picks[j], back, preferred_element_type=F32)
                    + jnp.dot(logits_low[j], router_t[:, cols], preferred_element_type=F32)
                ).astype(BF)

                @pl.when(core == j)
                def _():
                    own[q, :, cols] = total

                @pl.when(core != j)
                def _():
                    stage[:, cols] = total

        line.to_sib(0, q).start()
        put(q).start()

    @pl.loop(0, 1)
    def _(k):
        compute(k)

    def after(a, q):
        out = pltpu.make_async_copy(own.at[q], sum_ref, part_sem)
        out.start()
        out.wait()

    def down_grads():
        slots = count * 2 * cap
        tile = 256
        tiles = hidden // tile
        spans = model_width // hidden

        def load_gated(e):
            return pltpu.make_async_copy(
                gated_out.at[e], room_gated.at[e, pl.ds(0, slots)], down_sem.at[0, e]
            )

        def load_y(e, span):
            src = y_in.at[e, :, pl.ds(span * hidden, hidden)]
            return pltpu.make_async_copy(src, room_y.at[e, pl.ds(0, slots)], down_sem.at[1, e])

        def put_grad(e, span, n, buf):
            part = (d_gate, d_up)[buf].at[0, pl.ds(0, tile)]
            rows = pl.ds(pl.multiple_of(n * tile, tile), tile)
            target = g_down_out.at[e, rows, pl.ds(span * hidden, hidden)]
            return pltpu.make_async_copy(part, target, out_sem.at[buf])

        for e in range(local_experts):
            load_gated(e).start()
            load_y(e, 0).start()
        for span in range(spans):
            for e in range(local_experts):
                if span == 0:
                    load_gated(e).wait()
                load_y(e, span).wait()

                @pl.loop(0, tiles // 2)
                def _(m):
                    for buf in range(2):
                        n = 2 * m + buf

                        def wait_last():
                            put_grad(e, span, n, buf).wait()

                        if span + e > 0:
                            wait_last()
                        else:
                            pl.when(m > 0)(wait_last)
                        cols = pl.ds(pl.multiple_of(n * tile, tile), tile)
                        (d_gate, d_up)[buf][0, 0:tile, :] = lax.dot_general(
                            room_gated[e, 0:slots, cols],
                            room_y[e, 0:slots, :],
                            (((0,), (0,)), ((), ())),
                            preferred_element_type=F32,
                        ).astype(BF)
                        put_grad(e, span, n, buf).start()

                if span + 1 < spans:
                    load_y(e, span + 1).start()
        for buf in range(2):
            put_grad(0, 0, 0, buf).wait()

    def between(step):
        compute(step + 1)

        @pl.when(step == count - 2)
        def _():
            for n in range(3):
                store(n, 0).wait()
            put(0).wait()
            line.to_sib(0, order(count - 1)).wait_send()
            down_grads()

    line.run(lambda a, q: None, between)
    after(0, p)
    line.finish()


def experts_out(
    grads, act, by_up, by_gate, gate_slots, targets, targets_t, probs, router_t, w_gate, w_up, w_down, collective
):
    local_experts, _, model_width = grads.shape
    hidden = act.shape[2]
    shards, experts, tokens = probs.shape
    count = shards // 2
    anywhere = pl.BlockSpec(memory_space=ANY)
    vmem = pl.BlockSpec(memory_space=pltpu.VMEM)
    thin = jax.ShapeDtypeStruct(act.shape, BF)
    extra = [] if act.shape[1] <= model_width else [pltpu.VMEM(act.shape, BF)] * 2
    return pl.pallas_call(
        partial(experts_out_kernel, count, CAP),
        out_shape=[
            thin,
            thin,
            thin,
            jax.ShapeDtypeStruct((shards, tokens, model_width), BF),
            jax.ShapeDtypeStruct(probs.shape, BF),
            jax.ShapeDtypeStruct((tokens, model_width), BF),
            jax.ShapeDtypeStruct(w_down.shape, BF),
        ],
        in_specs=[anywhere] * 4 + [vmem] * 5 + [anywhere] * 3,
        out_specs=[anywhere] * 4 + [vmem, anywhere, anywhere],
        scratch_shapes=[pltpu.VMEM(x.shape, BF) for x in (w_gate, w_up, w_down)]
        + [pltpu.VMEM((2, local_experts, 2 * CAP, model_width), BF)]
        + [pltpu.VMEM((2, local_experts, 2 * CAP, hidden), BF)] * 3
        + [pltpu.VMEM((local_experts, 2 * CAP, hidden), BF)] * 3
        + [
            pltpu.VMEM((2, tokens, model_width), BF),
            pltpu.VMEM((tokens, model_width), BF),
            pltpu.VMEM((count, tokens, model_width), BF),
            pltpu.VMEM((count, tokens, model_width), BF),
            pltpu.VMEM((count + 1, tokens, model_width), BF),
            DMA((3,)),
            DMA((4, 2)),
            DMA((3,)),
            DMA,
            DMA((2, local_experts)),
        ]
        + [DMA((1, count))] * 7
        + extra,
        compiler_params=pltpu.CompilerParams(
            collective_id=collective, has_side_effects=True, vmem_limit_bytes=63 << 20
        ),
        name="experts_out",
    )(grads, act, by_up, by_gate, gate_slots, targets, targets_t, probs, router_t, w_gate, w_up, w_down)


def rope_tables(positions, head_dim):
    half_dim = head_dim // 2
    inverse = ROPE_BASE ** (-(jnp.arange(half_dim, dtype=F32) * 2.0 / head_dim))
    angles = positions.astype(F32)[:, None] * inverse[None, :]
    angles = jnp.concatenate([angles, angles], axis=-1)
    return (jnp.cos(angles), jnp.sin(angles))


def dot(left, right, sides=(1, 0), out=F32):
    return lax.dot_general(
        left, right, (((sides[0],), (sides[1],)), ((), ())), preferred_element_type=F32
    ).astype(out)


def inverse_rms(rows):
    return lax.rsqrt(jnp.mean(rows * rows, axis=-1, keepdims=True) + EPSILON)


def on_device(
    inputs,
    out_grad,
    doc_ids,
    routes,
    w_query,
    w_key,
    w_value,
    w_output,
    w_router,
    attn_gain,
    ffn_gain,
    query_gain,
    key_gain,
    w_gate,
    w_up,
    w_down,
):
    seq_count = lax.axis_size("seq")
    shards = lax.axis_size("fsdp")
    tok_rows, model_width = inputs.shape[1:]
    seq_len = tok_rows * seq_count
    rows = w_query.shape[0]
    width = model_width // seq_count
    local_experts = w_gate.shape[0]
    experts = w_router.shape[1]
    top_k = routes.shape[2]
    lanes = 128

    small = jnp.concatenate(
        [
            w_router,
            attn_gain[:, None],
            ffn_gain[:, None],
            jnp.zeros((rows, lanes - experts - 2), BF),
        ],
        axis=1,
    )
    gains = jnp.pad(jnp.stack([query_gain, key_gain]), ((0, 14), (0, lanes - rows)))
    routes_flat = routes.reshape(tok_rows * top_k // lanes, lanes)
    wq, wk, wv, wo, small_all, gains_all, routes_all, x_all = gather_start(
        (w_query, w_key, w_value, w_output, small, gains, routes_flat, inputs[0]), seq_count, shards, 0
    )
    x_all = x_all.reshape(seq_len, model_width)
    full_gate = lax.all_gather(w_gate, "seq", axis=1, tiled=True)
    full_up = lax.all_gather(w_up, "seq", axis=1, tiled=True)
    full_down = lax.all_gather(w_down, "seq", axis=1, tiled=True)

    wq = wq.reshape(model_width, width)
    wk = wk.reshape(model_width, width)
    wv = wv.reshape(model_width, width)
    wo = wo.reshape(width, model_width)
    small_all = small_all.reshape(model_width, lanes)
    w_r = small_all[:, :experts]
    gain_a = small_all[:, experts].astype(F32)
    gain_f = small_all[:, experts + 1].astype(F32)
    gq = gains_all[:, 0, :rows].reshape(1, width).astype(F32)
    gk = gains_all[:, 1, :rows].reshape(1, width).astype(F32)

    x_float = x_all.astype(F32)
    h1 = (x_float * inverse_rms(x_float) * gain_a).astype(BF)
    q_raw = dot(h1, wq)
    k_raw = dot(h1, wk)
    values = dot(h1, wv, out=BF)
    squares = jnp.stack([jnp.sum(q_raw * q_raw, axis=1), jnp.sum(k_raw * k_raw, axis=1)])
    squares = seq_sum(squares, seq_count, 1)
    scales = lax.rsqrt(squares / model_width + EPSILON)
    rq, rk = scales[0][:, None], scales[1][:, None]
    cos, sin = rope_tables(jnp.arange(seq_len, dtype=jnp.int32), HEAD)
    doc_row = doc_ids
    doc_col = doc_ids.reshape(seq_len, 1)
    attended, q_low, k_low = attend(q_raw, k_raw, values, rq, rk, gq, gk, cos, sin, doc_col, doc_row)
    projected = dot(attended, wo, out=BF).reshape(seq_count, tok_rows, model_width)
    rows_in = inputs[0].astype(F32)
    grad_rows = out_grad[0].astype(F32)
    summed, dy_all = middle(projected, out_grad[0], shards, 2)
    x_mid = rows_in + summed
    scale_f = inverse_rms(x_mid)
    h2 = (x_mid * scale_f * gain_f).astype(BF)

    routes_all = routes_all.reshape(shards, tok_rows, top_k)
    local_ids = lax.axis_index("fsdp") * local_experts + jnp.arange(local_experts, dtype=jnp.int32)
    chosen = jnp.any(routes_all[:, None] == local_ids[None, :, None, None], axis=3)
    slot = jnp.cumsum(chosen.astype(jnp.int32), axis=2) - 1
    slot = slot + CAP * jnp.arange(local_experts, dtype=jnp.int32)[None, :, None]
    targets = jnp.where(chosen, slot, -1)
    targets_t = jnp.swapaxes(targets, 1, 2)
    router_t = w_r.T
    h2_all, expert_in, grad_slots, act, by_up, by_gate, gate_slots, gate_probs = experts_in(
        h2, dy_all, targets, router_t, full_gate, full_up, 3
    )
    gated, d_gate, d_up, out_parts, grad_logits, grad_h2, g_down = experts_out(
        grad_slots,
        act,
        by_up,
        by_gate,
        gate_slots,
        targets,
        targets_t,
        gate_probs,
        router_t,
        full_gate,
        full_up,
        full_down,
        4,
    )

    def spread(part):
        return lax.psum_scatter(part, "seq", scatter_dimension=1, tiled=True)

    g_down = spread(g_down)
    grad_h2 = grad_h2.astype(F32)

    u_rows = gain_f * grad_h2
    grad_mid = (
        grad_rows
        + scale_f * u_rows
        - x_mid * scale_f**3 * jnp.mean(u_rows * x_mid, axis=-1, keepdims=True)
    )
    ffn_part = jnp.sum(grad_h2 * x_mid * scale_f, axis=0)

    d_attn, out_sum, g_gate, g_up, router_part = turn_back(
        grad_mid.astype(BF),
        out_parts,
        expert_in,
        d_gate,
        d_up,
        h2_all,
        grad_logits,
        seq_count,
        shards,
        5,
    )
    g_gate = spread(g_gate)
    g_up = spread(g_up)
    d_attn = d_attn.reshape(seq_len, model_width)
    result = x_mid + out_sum.astype(F32)
    d_heads = dot(d_attn, wo, (1, 1), BF)
    u_q, u_k, dv_low, dots, gain_q_part, gain_k_part = attend_back(
        q_low, k_low, values, d_heads, q_raw, k_raw, rq, rk, gq, gk, cos, sin, doc_col, doc_row
    )
    dots, g_down = lax.optimization_barrier((dots, g_down))
    dots = seq_sum(dots.T, seq_count, 6) / model_width

    def norm_back(u, raw, scale, product):
        return (scale * u - raw * (scale**3 * product[:, None])).astype(BF)

    dq_low = norm_back(u_q, q_raw, rq, dots[0])
    dk_low = norm_back(u_k, k_raw, rk, dots[1])
    grad_h1 = dot(dq_low, wq, (1, 1)) + dot(dk_low, wk, (1, 1)) + dot(dv_low, wv, (1, 1))
    grad_h1 = grad_h1.astype(BF).reshape(seq_count, tok_rows, model_width)

    sheet = (seq_count, shards, rows, width)
    small_part = jnp.concatenate(
        [router_part.T, ffn_part[:, None], jnp.zeros((model_width, lanes - experts - 1), F32)], axis=1
    ).reshape(seq_count, shards, rows, lanes)
    gains_part = jnp.stack([gain_q_part.reshape(shards, rows), gain_k_part.reshape(shards, rows)], axis=1)
    gains_part = jnp.pad(gains_part, ((0, 0), (0, 6), (0, lanes - rows)))
    g_query, g_key, g_value, g_output, g_small, g_gains, grad_h1 = scatter_end(
        (
            dot(h1, dq_low, (0, 0), BF).reshape(sheet),
            dot(h1, dk_low, (0, 0), BF).reshape(sheet),
            dot(h1, dv_low, (0, 0), BF).reshape(sheet),
            dot(attended, d_attn, (0, 0), BF).reshape(shards, rows, model_width),
            small_part,
            gains_part,
        ),
        grad_h1,
        seq_count,
        shards,
        8,
    )
    g_query, g_key, g_value = (g_query.astype(F32), g_key.astype(F32), g_value.astype(F32))

    scale_a = inverse_rms(rows_in)
    u_rows = gain_a * grad_h1
    input_grad = (
        grad_mid
        + scale_a * u_rows
        - rows_in * scale_a**3 * jnp.mean(u_rows * rows_in, axis=-1, keepdims=True)
    )
    pairs = (
        w_query.astype(F32) * g_query + w_key.astype(F32) * g_key + w_value.astype(F32) * g_value
    )
    g_attn_gain = jnp.sum(pairs, axis=1) / attn_gain.astype(F32)

    return (
        result.astype(BF)[None],
        input_grad[None],
        g_query,
        g_key,
        g_value,
        g_output.astype(F32),
        g_small[:, :experts],
        g_attn_gain,
        g_small[:, experts],
        g_gains[0, :rows],
        g_gains[1, :rows],
        g_gate.astype(F32),
        g_up.astype(F32),
        g_down.astype(F32),
    )


def solution(mesh):
    rows = P("fsdp", "seq", None)
    sheet = P(("seq", "fsdp"), None)
    line = P(("seq", "fsdp"))
    return jax.shard_map(
        on_device,
        mesh=mesh,
        in_specs=(rows, rows, P("fsdp", None), rows) + (sheet,) * 5 + (line,) * 4 + (rows,) * 3,
        out_specs=(rows, rows) + (sheet,) * 5 + (line,) * 4 + (rows,) * 3,
        check_vma=False,
    )
```

```python
from functools import partial

import jax
import jax.numpy as jnp
from jax import lax
from jax.experimental import pallas as pl
from jax.experimental.pallas import tpu as pltpu
from jax.sharding import PartitionSpec as P

CAP = 136
HEAD = 128
EPSILON = 1e-05
ROPE_BASE = 10000.0
MASKED_OUT = -1e30
ANY = pl.ANY
MESH = pl.DeviceIdType.MESH
DMA = pltpu.SemaphoreType.DMA
BF = jnp.bfloat16
F32 = jnp.float32


def remote(src, dst, send, recv, **where):
    return pltpu.make_async_remote_copy(
        src_ref=src, dst_ref=dst, send_sem=send, recv_sem=recv, device_id=where, device_id_type=MESH
    )


def greet(count, places, seq_count=1):
    i, p, sib = places
    barrier = pltpu.get_barrier_semaphore()
    pl.semaphore_signal(barrier, inc=1, device_id={"fsdp": sib}, device_id_type=MESH)
    here = lax.axis_index("seq")
    for d in range(1, seq_count):
        peer = lax.rem(here + d, seq_count)
        pl.semaphore_signal(barrier, inc=1, device_id={"seq": peer}, device_id_type=MESH)

    @pl.when(p > 0)
    def _():
        pl.semaphore_signal(barrier, inc=1, device_id={"fsdp": i - 2}, device_id_type=MESH)

    @pl.when(p < count - 1)
    def _():
        pl.semaphore_signal(barrier, inc=1, device_id={"fsdp": i + 2}, device_id_type=MESH)

    last = count - 1
    pl.semaphore_wait(barrier, seq_count + (p + last) // count + (last - p + last) // count)


def slot_of(ref, axis, index):
    return ref.at[index] if axis == 0 else ref.at[:, index]


class LineGather:
    def __init__(self, count, places, refs, axes, send_r, send_l, send_s, recv):
        self.count, self.places = count, places
        self.refs, self.axes = refs, axes
        self.sems = (send_r, send_l, send_s, recv)

    def copy(self, a, slot, kind, t, device):
        send = self.sems[kind].at[a, t]
        ref = slot_of(self.refs[a], self.axes[a], slot)
        return remote(ref, ref, send, self.sems[3].at[a, slot], fsdp=device)

    def first(self, a):
        i, p, sib = self.places

        @pl.when(p < self.count - 1)
        def _():
            self.copy(a, i, 0, 0, i + 2).start()

        @pl.when(p > 0)
        def _():
            self.copy(a, i, 1, 0, i - 2).start()

        self.copy(a, i, 2, 0, sib).start()

    def forward(self, t):
        i, p, sib = self.places
        count = self.count
        for a in range(len(self.refs)):

            @pl.when(p - t >= 0)
            def _():
                slot = i - 2 * t
                self.copy(a, slot, 0, t, sib).wait_recv()

                @pl.when(p < count - 1)
                def _():
                    self.copy(a, slot, 0, t, i + 2).start()

                self.copy(a, slot, 2, t, sib).start()

            @pl.when(p + t < count)
            def _():
                slot = i + 2 * t
                self.copy(a, slot, 1, t, sib).wait_recv()

                @pl.when(p > 0)
                def _():
                    self.copy(a, slot, 1, t, i - 2).start()

                self.copy(a, slot, 2, count + t, sib).start()

    def finish(self):
        i, p, sib = self.places
        count = self.count
        for a in range(len(self.refs)):
            for q in range(count):
                self.copy(a, 2 * q + lax.rem(sib, 2), 2, 0, sib).wait_recv()
            self.copy(a, i, 2, 0, sib).wait_send()

            @pl.when(p < count - 1)
            def _():
                self.copy(a, i, 0, 0, i + 2).wait_send()

            @pl.when(p > 0)
            def _():
                self.copy(a, i, 1, 0, i - 2).wait_send()

            for t in range(1, count):

                @pl.when(p - t >= 0)
                def _():
                    slot = i - 2 * t

                    @pl.when(p < count - 1)
                    def _():
                        self.copy(a, slot, 0, t, i + 2).wait_send()

                    self.copy(a, slot, 2, t, sib).wait_send()

                @pl.when(p + t < count)
                def _():
                    slot = i + 2 * t

                    @pl.when(p > 0)
                    def _():
                        self.copy(a, slot, 1, t, i - 2).wait_send()

                    self.copy(a, slot, 2, count + t, sib).wait_send()


def line_sems(arrays, count):
    return [DMA((arrays, count)), DMA((arrays, count)), DMA((arrays, 2 * count)), DMA((arrays, 2 * count))]


def where_am_i():
    i = lax.axis_index("fsdp")
    p = i // 2
    c = i % 2
    return i, p, 2 * p + 1 - c


def start_kernel(count, seq_count, *refs):
    wq, wk, wv, wo, small, gains, routes, rows = refs[:8]
    outs = refs[8:15]
    rows_out = refs[15]
    holds = refs[16:24]
    send_x, recv_x, local, send_r, send_l, send_s, recv, send_y, recv_y = refs[24:]
    places = where_am_i()
    i = places[0]
    here = lax.axis_index("seq")
    width = wq.shape[1] // seq_count

    def columns(ref, peer):
        return ref.at[:, pl.ds(pl.multiple_of(peer * width, width), width)]

    own = [columns(wq, here), columns(wk, here), columns(wv, here), wo, small, gains, routes, rows]
    for a in range(8):
        pltpu.make_async_copy(own[a], holds[a], local.at[a]).start()
    greet(count, places, seq_count)

    def piece(a, d):
        peer = lax.rem(here + d, seq_count)
        src = small if a == 4 else columns((wq, wk, wv)[a], peer)
        slot = 3 if a == 4 else a
        return remote(
            src, outs[a].at[here, i], send_x.at[slot, d - 1], recv_x.at[slot, d - 1], seq=peer
        )

    def arrived(a, d):
        origin = lax.rem(here + seq_count - d, seq_count)
        slot = 3 if a == 4 else a
        return remote(
            outs[a].at[origin, i],
            outs[a].at[origin, i],
            send_x.at[slot, d - 1],
            recv_x.at[slot, d - 1],
            seq=origin,
        )

    for a in (4, 0, 1, 2):
        for d in range(1, seq_count):
            piece(a, d).start()
    gather = SeqGather(seq_count, rows, rows_out, send_y, recv_y)
    gather.begin()
    axes = [1, 1, 1, 0, 1, 0, 0]
    for a in (3, 5, 6, 4, 0, 1, 2):
        pltpu.make_async_copy(own[a], holds[a], local.at[a]).wait()
        target = outs[a].at[here, i] if axes[a] == 1 else outs[a].at[i]
        pltpu.make_async_copy(holds[a], target, local.at[a]).start()
    line = LineGather(count, places, outs, axes, send_r, send_l, send_s, recv)
    for a in (5, 6, 4, 0, 1, 2, 3):
        target = outs[a].at[here, i] if axes[a] == 1 else outs[a].at[i]
        pltpu.make_async_copy(holds[a], target, local.at[a]).wait()
        if axes[a] == 1:
            for d in range(1, seq_count):
                arrived(a, d).wait_recv()
        line.first(a)
    pltpu.make_async_copy(rows, holds[7], local.at[7]).wait()
    pltpu.make_async_copy(holds[7], rows_out.at[here], local.at[7]).start()
    for t in range(1, count):
        line.forward(t)
        if t == 1:
            gather.relay()
    line.finish()
    pltpu.make_async_copy(holds[7], rows_out.at[here], local.at[7]).wait()
    gather.finish()
    for a in (4, 0, 1, 2):
        for d in range(1, seq_count):
            piece(a, d).wait_send()


def gather_start(arrays, seq_count, shards, collective):
    count = shards // 2
    wq, wk, wv, wo, small, gains, routes, tokens = arrays
    rows, model_width = wq.shape
    width = model_width // seq_count
    sheet = jax.ShapeDtypeStruct((seq_count, shards, rows, width), BF)
    shapes = [
        sheet,
        sheet,
        sheet,
        jax.ShapeDtypeStruct((shards,) + wo.shape, BF),
        jax.ShapeDtypeStruct((seq_count, shards) + small.shape, BF),
        jax.ShapeDtypeStruct((shards,) + gains.shape, BF),
        jax.ShapeDtypeStruct((shards,) + routes.shape, jnp.int32),
        jax.ShapeDtypeStruct((seq_count,) + tokens.shape, BF),
    ]
    holds = [pltpu.VMEM((rows, width), BF)] * 3 + [
        pltpu.VMEM(wo.shape, BF),
        pltpu.VMEM(small.shape, BF),
        pltpu.VMEM(gains.shape, BF),
        pltpu.VMEM(routes.shape, jnp.int32),
        pltpu.VMEM(tokens.shape, BF),
    ]
    return pl.pallas_call(
        partial(start_kernel, count, seq_count),
        out_shape=shapes,
        in_specs=[pl.BlockSpec(memory_space=ANY)] * 8,
        out_specs=[pl.BlockSpec(memory_space=ANY)] * 8,
        scratch_shapes=holds
        + [DMA((4, seq_count - 1)), DMA((4, seq_count - 1)), DMA((8,))]
        + line_sems(7, count)
        + seq_gather_sems(seq_count),
        compiler_params=pltpu.CompilerParams(collective_id=collective, has_side_effects=True),
        name="gather_start",
    )(*arrays)


def chunk_order(k, p, count):
    near = jnp.minimum(p, count - 1 - p)
    step = (k + 1) // 2
    both = jnp.where(k % 2 == 1, p - step, p + step)
    return jnp.where(k <= 2 * near, both, jnp.where(p < count - 1 - p, k, count - 1 - k))


class LineScatter:
    def __init__(self, count, places, sources, axes, bufs, sems):
        self.count, self.places = count, places
        self.sources, self.axes = sources, axes
        self.own, self.sib, self.inbox = bufs
        self.sems = sems

    def load(self, a, q):
        i = self.places[0]
        src = slot_of(self.sources[a], self.axes[a], 2 * q + lax.rem(i, 2))
        return pltpu.make_async_copy(src, self.own[a].at[q], self.sems[6].at[a, q])

    def to_sib(self, a, q):
        sib = self.places[2]
        src = slot_of(self.sources[a], self.axes[a], 2 * q + lax.rem(sib, 2))
        return remote(src, self.sib[a].at[q], self.sems[2].at[a, q], self.sems[5].at[a, q], fsdp=sib)

    def right(self, a, q):
        i = self.places[0]
        return remote(
            self.own[a].at[q], self.inbox[a].at[q], self.sems[0].at[a, q], self.sems[3].at[a, q], fsdp=i + 2
        )

    def left(self, a, q):
        i, p, sib = self.places
        slot = jnp.where(q == p - 1, self.count, q)
        return remote(
            self.own[a].at[q], self.inbox[a].at[slot], self.sems[1].at[a, q], self.sems[4].at[a, q], fsdp=i - 2
        )

    def begin_loads(self):
        for k in range(self.count):
            q = chunk_order(self.count - 1 - k, self.places[1], self.count)
            for a in range(len(self.sources)):
                self.load(a, q).start()

    def begin(self):
        for k in range(self.count):
            q = chunk_order(self.count - 1 - k, self.places[1], self.count)
            for a in range(len(self.sources)):
                self.to_sib(a, q).start()

    def add(self, a, q, others):
        own = self.own[a]
        lead = own.shape[1:-2]
        rows, width = own.shape[-2:]
        step = rows
        while step * width > 65536 and step % 16 == 0:
            step //= 2

        def strip(index):
            total = own[index].astype(F32) + self.sib[a][index].astype(F32)
            for slot in others:
                total += self.inbox[a][(slot,) + index[1:]].astype(F32)
            own[index] = total.astype(own.dtype)

        def rows_of(prefix):
            if step == rows:
                strip(prefix)
                return

            @pl.loop(0, rows // step)
            def _(k):
                strip(prefix + (pl.ds(pl.multiple_of(k * step, step), step),))

        if lead:
            for b in range(lead[0]):
                rows_of((q, b))
        else:
            rows_of((q,))

    def ready(self, a, q):
        self.load(a, q).wait()
        self.to_sib(a, q).wait_recv()

    def run(self, after, between=None):
        i, p, sib = self.places
        count = self.count
        arrays = range(len(self.sources))

        @pl.loop(0, count - 1)
        def _(step):
            @pl.when(step >= p)
            def _():
                q = count - 1 - (step - p)
                for a in arrays:
                    self.ready(a, q)

                    @pl.when(p > 0)
                    def _():
                        self.right(a, q).wait_recv()
                        self.add(a, q, [q])

                    @pl.when(p == 0)
                    def _():
                        self.add(a, q, [])

                    self.right(a, q).start()

            @pl.when(step >= count - 1 - p)
            def _():
                q = step - (count - 1 - p)
                for a in arrays:
                    self.ready(a, q)

                    @pl.when(p < count - 1)
                    def _():
                        self.left(a, q).wait_recv()
                        self.add(a, q, [q])

                    @pl.when(p == count - 1)
                    def _():
                        self.add(a, q, [])

                    self.left(a, q).start()

            if between is not None:
                between(step)

        for a in arrays:
            self.ready(a, p)

            @pl.when(p > 0)
            def _():
                self.right(a, p).wait_recv()

            @pl.when(p < count - 1)
            def _():
                self.left(a, p).wait_recv()

            @pl.when(p == 0)
            def _():
                self.add(a, p, [count])

            @pl.when(p == count - 1)
            def _():
                self.add(a, p, [p])

            @pl.when((p > 0) & (p < count - 1))
            def _():
                self.add(a, p, [p, count])

            after(a, p)

    def finish(self):
        i, p, sib = self.places
        for a in range(len(self.sources)):
            for q in range(self.count):
                self.to_sib(a, q).wait_send()

                @pl.when(q > p)
                def _():
                    self.right(a, q).wait_send()

                @pl.when(q < p)
                def _():
                    self.left(a, q).wait_send()


def end_kernel(count, seq_count, *refs):
    sources = refs[:6]
    rows_ref = refs[6]
    outs = refs[7:13]
    sum_ref = refs[13]
    bufs = tuple(refs[14 + 6 * k : 20 + 6 * k] for k in range(3))
    landing = refs[32]
    sems = refs[33:40]
    send_x, recv_x, local = refs[40:43]
    seq = SeqScatter(seq_count, rows_ref, *refs[43:48])
    places = where_am_i()
    here = lax.axis_index("seq")
    width = sources[0].shape[3]
    line = LineScatter(count, places, sources, [1, 1, 1, 0, 1, 0], bufs, sems)
    line.begin_loads()
    seq.begin_loads()
    greet(count, places, seq_count)
    seq.begin()
    line.begin()
    own = bufs[0]

    def at_home(a, block):
        if a == 4:
            return landing.at[block]
        start = pl.multiple_of(block * width, width)
        return outs[a].at[:, pl.ds(start, width)]

    def piece(a, q, d):
        peer = lax.rem(here + d, seq_count)
        slot = 3 if a == 4 else a
        return remote(
            own[a].at[q, peer], at_home(a, here), send_x.at[slot, d - 1], recv_x.at[slot, d - 1], seq=peer
        )

    def arrived(a, d):
        origin = lax.rem(here + seq_count - d, seq_count)
        slot = 3 if a == 4 else a
        return remote(
            at_home(a, origin), at_home(a, origin), send_x.at[slot, d - 1], recv_x.at[slot, d - 1], seq=origin
        )

    def after(a, q):
        if a in (3, 5):
            pltpu.make_async_copy(own[a].at[q], outs[a], local.at[a]).start()
        else:
            for d in range(1, seq_count):
                piece(a, q, d).start()
            pltpu.make_async_copy(own[a].at[q, here], at_home(a, here), local.at[a]).start()

    def between(step):
        @pl.when(step == 0)
        def _():
            seq.relay()

    line.run(after, between)
    seq.total(sum_ref)
    for q in range(count):

        @pl.when(q == places[1])
        def _():
            for a in range(6):
                if a in (3, 5):
                    pltpu.make_async_copy(own[a].at[q], outs[a], local.at[a]).wait()
                else:
                    pltpu.make_async_copy(own[a].at[q, here], at_home(a, here), local.at[a]).wait()
                    for d in range(1, seq_count):
                        piece(a, q, d).wait_send()
                        arrived(a, d).wait_recv()

    total = landing[0]
    for block in range(1, seq_count):
        total += landing[block]
    landing[0] = total
    last = pltpu.make_async_copy(landing.at[0], outs[4], local.at[4])
    last.start()
    last.wait()
    line.finish()
    seq.finish()


def scatter_end(arrays, row_blocks, seq_count, shards, collective):
    count = shards // 2
    gq, gk, gv, go, small, gains = arrays
    rows, width = gq.shape[2:]
    home = jax.ShapeDtypeStruct((rows, width * seq_count), BF)
    shapes = [
        home,
        home,
        home,
        jax.ShapeDtypeStruct(go.shape[1:], BF),
        jax.ShapeDtypeStruct(small.shape[2:], F32),
        jax.ShapeDtypeStruct(gains.shape[1:], F32),
        jax.ShapeDtypeStruct(row_blocks.shape[1:], F32),
    ]
    blocks, inboxes = [], []
    for a in range(6):
        shape = arrays[a].shape
        block = (shape[0],) + shape[2:] if a in (0, 1, 2, 4) else shape[1:]
        blocks.append(pltpu.VMEM((count,) + block, arrays[a].dtype))
        inboxes.append(pltpu.VMEM((count + 1,) + block, arrays[a].dtype))
    return pl.pallas_call(
        partial(end_kernel, count, seq_count),
        out_shape=shapes,
        in_specs=[pl.BlockSpec(memory_space=ANY)] * 7,
        out_specs=[pl.BlockSpec(memory_space=ANY)] * 6 + [pl.BlockSpec(memory_space=pltpu.VMEM)],
        scratch_shapes=blocks * 2
        + inboxes
        + [pltpu.VMEM((seq_count,) + small.shape[2:], F32)]
        + [DMA((6, count))] * 7
        + [DMA((4, seq_count - 1)), DMA((4, seq_count - 1)), DMA((6,))]
        + seq_scatter_scratch(row_blocks.shape[1:], row_blocks.dtype, seq_count),
        compiler_params=pltpu.CompilerParams(
            collective_id=collective, has_side_effects=True, vmem_limit_bytes=62 << 20
        ),
        name="scatter_end",
    )(*arrays, row_blocks)


def greet_seq(seq_count):
    here = lax.axis_index("seq")
    barrier = pltpu.get_barrier_semaphore()
    for d in range(1, seq_count):
        peer = lax.rem(here + d, seq_count)
        pl.semaphore_signal(barrier, inc=1, device_id={"seq": peer}, device_id_type=MESH)
    pl.semaphore_wait(barrier, seq_count - 1)
    return here


class SeqScatter:
    def __init__(self, seq_count, x_ref, own, inbox, send, recv, local):
        here = lax.axis_index("seq")
        self.own, self.inbox, self.local, self.count = own, inbox, local, seq_count
        self.take = pltpu.make_async_copy(x_ref.at[here], own, local.at[0])
        rows = own.shape[0]
        self.half = rows // 2
        low, high = pl.ds(0, self.half), pl.ds(self.half, self.half)
        if seq_count != 4:
            self.copies = []
            for d in range(1, seq_count):
                peer = lax.rem(here + d, seq_count)
                self.copies.append(
                    remote(x_ref.at[peer], inbox.at[d - 1], send.at[d - 1], recv.at[d - 1], seq=peer)
                )
            return
        beside = here + 1 - 2 * lax.rem(here, 2)
        across = lax.rem(here + 2, 4)
        corner = 3 - here
        self.loads = [
            pltpu.make_async_copy(x_ref.at[across, low], inbox.at[3, low], local.at[1]),
            pltpu.make_async_copy(x_ref.at[beside, high], inbox.at[3, high], local.at[2]),
        ]
        plans = (
            (x_ref.at[corner, low], inbox.at[2, low], beside),
            (x_ref.at[corner, high], inbox.at[2, high], across),
            (x_ref.at[beside, low], inbox.at[0, low], beside),
            (x_ref.at[across, high], inbox.at[1, high], across),
            (inbox.at[3, low], inbox.at[1, low], across),
            (inbox.at[3, high], inbox.at[0, high], beside),
        )
        self.copies = [
            remote(src, dst, send.at[n], recv.at[n], seq=peer) for n, (src, dst, peer) in enumerate(plans)
        ]

    def begin_loads(self):
        self.take.start()
        if self.count == 4:
            for load in self.loads:
                load.start()

    def begin(self):
        for copy in self.copies[:4] if self.count == 4 else self.copies:
            copy.start()

    def strips(self, start, rows, body):
        step = min(32, rows)

        @pl.loop(0, rows // step)
        def _(k):
            body(pl.ds(pl.multiple_of(start + k * step, step), step))

    def relay(self):
        if self.count != 4:
            return
        inbox = self.inbox

        def add(strip):
            inbox[3, strip, :] = (
                inbox[3, strip, :].astype(F32) + inbox[2, strip, :].astype(F32)
            ).astype(inbox.dtype)

        for n, start in ((0, 0), (1, self.half)):
            self.loads[n].wait()
            self.copies[n].wait_recv()
            self.strips(start, self.half, add)
            self.copies[4 + n].start()

    def total(self, o_ref):
        self.take.wait()
        for copy in self.copies[2:] if self.count == 4 else self.copies:
            copy.wait_recv()
        parts = 2 if self.count == 4 else self.count - 1

        def add(strip):
            total = self.own[strip, :].astype(F32)
            for d in range(parts):
                total += self.inbox[d, strip, :].astype(F32)
            o_ref[strip, :] = total

        self.strips(0, self.own.shape[0], add)

    def finish(self):
        for copy in self.copies:
            copy.wait_send()


def seq_scatter_scratch(block, dtype, seq_count):
    boxes = 4 if seq_count == 4 else seq_count - 1
    copies = 6 if seq_count == 4 else seq_count - 1
    return [
        pltpu.VMEM(block, dtype),
        pltpu.VMEM((boxes,) + block, dtype),
        DMA((copies,)),
        DMA((copies,)),
        DMA((3,)),
    ]


class SeqGather:
    def __init__(self, seq_count, x_ref, o_ref, send, recv):
        here = lax.axis_index("seq")
        self.count = seq_count
        rows = x_ref.shape[0]
        low, high = pl.ds(0, rows // 2), pl.ds(rows // 2, rows // 2)
        if seq_count != 4:
            peers = [lax.rem(here + d, seq_count) for d in range(1, seq_count)]
            origins = [lax.rem(here + seq_count - d, seq_count) for d in range(1, seq_count)]
            out = [(x_ref, o_ref.at[here], peer) for peer in peers]
            landed = [o_ref.at[origin] for origin in origins]
        else:
            beside = here + 1 - 2 * lax.rem(here, 2)
            across = lax.rem(here + 2, 4)
            corner = 3 - here
            out = [
                (x_ref, o_ref.at[here], beside),
                (x_ref, o_ref.at[here], across),
                (o_ref.at[across, low], o_ref.at[across, low], beside),
                (o_ref.at[beside, high], o_ref.at[beside, high], across),
            ]
            landed = [o_ref.at[beside], o_ref.at[across], o_ref.at[corner, low], o_ref.at[corner, high]]
        self.sends = [
            remote(src, dst, send.at[n], recv.at[n], seq=peer) for n, (src, dst, peer) in enumerate(out)
        ]
        self.lands = [
            remote(ref, ref, send.at[n], recv.at[n], seq=out[n][2]) for n, ref in enumerate(landed)
        ]

    def begin(self):
        for copy in self.sends[:2] if self.count == 4 else self.sends:
            copy.start()

    def relay(self):
        if self.count == 4:
            for n in (0, 1):
                self.lands[n].wait_recv()
            for n in (2, 3):
                self.sends[n].start()

    def finish(self):
        for n, copy in enumerate(self.lands):
            if self.count != 4 or n > 1:
                copy.wait_recv()
        for copy in self.sends:
            copy.wait_send()


def seq_gather_sems(seq_count):
    copies = 4 if seq_count == 4 else seq_count - 1
    return [DMA((copies,)), DMA((copies,))]


def middle_kernel(
    count, seq_count, x_ref, dy_ref, o_ref, all_ref, own, inbox, xs, xr, xl, hold, s0, s1, s2, recv, local
):
    places = where_am_i()
    i = places[0]
    seq = SeqScatter(seq_count, x_ref, own, inbox, xs, xr, xl)
    seq.begin_loads()
    take = pltpu.make_async_copy(dy_ref, hold, local.at[0])
    take.start()
    greet(count, places, seq_count)
    seq.begin()
    take.wait()
    put = pltpu.make_async_copy(hold, all_ref.at[i], local.at[1])
    put.start()
    put.wait()
    line = LineGather(count, places, [all_ref], [0], s0, s1, s2, recv)
    line.first(0)
    for t in range(1, count):
        line.forward(t)
        if t == 1:
            seq.relay()
    seq.total(o_ref)
    line.finish()
    seq.finish()


def middle(blocks, dy, shards, collective):
    count = shards // 2
    seq_count = blocks.shape[0]
    block = blocks.shape[1:]
    return pl.pallas_call(
        partial(middle_kernel, count, seq_count),
        out_shape=[
            jax.ShapeDtypeStruct(block, F32),
            jax.ShapeDtypeStruct((shards,) + dy.shape, dy.dtype),
        ],
        in_specs=[pl.BlockSpec(memory_space=ANY)] * 2,
        out_specs=[pl.BlockSpec(memory_space=pltpu.VMEM), pl.BlockSpec(memory_space=ANY)],
        scratch_shapes=seq_scatter_scratch(block, blocks.dtype, seq_count)
        + [pltpu.VMEM(dy.shape, dy.dtype)]
        + line_sems(1, count)
        + [DMA((2,))],
        compiler_params=pltpu.CompilerParams(
            collective_id=collective, has_side_effects=True, vmem_limit_bytes=32 << 20
        ),
        name="middle",
    )(blocks, dy)


def seq_sum_kernel(seq_count, x_ref, o_ref, inbox, send, recv):
    here = greet_seq(seq_count)
    copies = []
    for d in range(1, seq_count):
        peer = lax.rem(here + d, seq_count)
        copies.append(remote(x_ref, inbox.at[d - 1], send.at[d - 1], recv.at[d - 1], seq=peer))
    for copy in copies:
        copy.start()
    for copy in copies:
        copy.wait_recv()
    total = x_ref[...]
    for d in range(seq_count - 1):
        total += inbox[d]
    o_ref[...] = total
    for copy in copies:
        copy.wait_send()


def seq_sum(value, seq_count, collective):
    return pl.pallas_call(
        partial(seq_sum_kernel, seq_count),
        out_shape=jax.ShapeDtypeStruct(value.shape, F32),
        in_specs=[pl.BlockSpec(memory_space=pltpu.VMEM)],
        out_specs=pl.BlockSpec(memory_space=pltpu.VMEM),
        scratch_shapes=[
            pltpu.VMEM((seq_count - 1,) + value.shape, F32),
            DMA((seq_count - 1,)),
            DMA((seq_count - 1,)),
        ],
        compiler_params=pltpu.CompilerParams(collective_id=collective, has_side_effects=True),
        name="seq_sum",
    )(value)


class RouterGrad:
    def __init__(self, tokens_in, logits_in, out, tokens, logits, sems):
        self.tokens_in, self.logits_in, self.out = tokens_in, logits_in, out
        self.tokens, self.logits, self.sems = tokens, logits, sems

    def take(self):
        return pltpu.make_async_copy(self.logits_in, self.logits, self.sems.at[2])

    def pair(self, q):
        buf = lax.rem(q, 2)
        src = self.tokens_in.at[pl.ds(2 * q, 2)]
        return pltpu.make_async_copy(src, self.tokens.at[buf], self.sems.at[buf])

    def begin(self):
        self.take().start()
        self.pair(0).start()

    def run(self):
        self.take().wait()
        self.out[...] = jnp.zeros_like(self.out)
        width = self.out.shape[1]
        block = 512
        pairs = self.tokens_in.shape[0] // 2

        @pl.loop(0, pairs)
        def _(q):
            self.pair(q).wait()

            @pl.when(q + 1 < pairs)
            def _():
                self.pair(q + 1).start()

            buf = lax.rem(q, 2)

            @pl.loop(0, width // block)
            def _(n):
                cols = pl.ds(pl.multiple_of(n * block, block), block)
                total = self.out[:, cols]
                for j in range(2):
                    total += jnp.dot(
                        self.logits[2 * q + j], self.tokens[buf, j, :, cols], preferred_element_type=F32
                    )
                self.out[:, cols] = total


def turn_kernel(
    count,
    seq_count,
    x_ref,
    parts_ref,
    left_ref,
    right_ref,
    h2_ref,
    logits_ref,
    o_ref,
    sum_ref,
    grad_ref,
    router_ref,
    hold,
    send,
    recv,
    one,
    tiles_in,
    held,
    staged,
    outer_sem,
    tokens,
    logits,
    router_sem,
    own,
    sib,
    inbox,
    *sems,
):
    places = where_am_i()
    here = lax.axis_index("seq")
    line = LineScatter(count, places, [parts_ref], [0], ([own], [sib], [inbox]), sems)
    grads = OuterGrads(left_ref, right_ref, grad_ref, (tiles_in, held, staged, outer_sem), count - 1)
    router = RouterGrad(h2_ref, logits_ref, router_ref, tokens, logits, router_sem)
    line.begin_loads()
    take = pltpu.make_async_copy(x_ref, hold, one)
    take.start()
    grads.begin()
    router.begin()
    greet(count, places, seq_count)
    rows = SeqGather(seq_count, x_ref, o_ref, send, recv)
    rows.begin()
    line.begin()
    take.wait()
    put = pltpu.make_async_copy(hold, o_ref.at[here], one)
    put.start()

    def after(a, q):
        out = pltpu.make_async_copy(own.at[q], sum_ref, sems[6].at[0, q])
        out.start()
        out.wait()

    def between(step):
        @pl.when(step == 1)
        def _():
            rows.relay()

        grads.between(step)

        @pl.when(step == 0)
        def _():
            router.run()

    line.run(after, between)
    grads.finish()
    put.wait()
    rows.finish()
    line.finish()


def turn_back(block, parts, expert_in, d_up, h2_all, logits, seq_count, shards, collective):
    count = shards // 2
    part = parts.shape[1:]
    model_width = part[1]
    local_experts, slots, hidden = d_up.shape
    anywhere = pl.BlockSpec(memory_space=ANY)
    return pl.pallas_call(
        partial(turn_kernel, count, seq_count),
        out_shape=[
            jax.ShapeDtypeStruct((seq_count,) + block.shape, block.dtype),
            jax.ShapeDtypeStruct(part, parts.dtype),
            jax.ShapeDtypeStruct((local_experts, model_width, hidden), BF),
            jax.ShapeDtypeStruct((logits.shape[1], model_width), F32),
        ],
        in_specs=[anywhere] * 6,
        out_specs=[anywhere] * 3 + [pl.BlockSpec(memory_space=pltpu.VMEM)],
        scratch_shapes=[pltpu.VMEM(block.shape, block.dtype)]
        + seq_gather_sems(seq_count)
        + [DMA]
        + outer_scratch(d_up, 512)
        + [
            pltpu.VMEM((2, 2) + h2_all.shape[1:], BF),
            pltpu.VMEM(logits.shape, BF),
            DMA((3,)),
        ]
        + [pltpu.VMEM((count,) + part, BF)] * 2
        + [pltpu.VMEM((count + 1,) + part, BF)]
        + [DMA((1, count))] * 7,
        compiler_params=pltpu.CompilerParams(
            collective_id=collective, has_side_effects=True, vmem_limit_bytes=60 << 20
        ),
        cost_estimate=pl.CostEstimate(flops=60_000_000_000, bytes_accessed=200_000_000, transcendentals=0),
        name="turn_back",
    )(block, parts, expert_in, d_up, h2_all, logits)


def half_sign(shape):
    lane = lax.broadcasted_iota(jnp.int32, shape, 1)
    return jnp.where(lane < shape[1] // 2, -1.0, 1.0)


def turn(value):
    return pltpu.roll(value, value.shape[1] // 2, 1)


def block_probs(q_rows, keys, doc_col, doc_row, start, scale_by):
    end = keys.shape[0]
    scores = (
        lax.dot_general(q_rows, keys, (((1,), (1,)), ((), ())), preferred_element_type=F32) * scale_by
    )
    shape = scores.shape
    query_pos = start + lax.broadcasted_iota(jnp.int32, shape, 0)
    key_pos = lax.broadcasted_iota(jnp.int32, shape, 1)
    allowed = (doc_col == doc_row) & (key_pos <= query_pos)
    scores = jnp.where(allowed, scores, MASKED_OUT)
    weights = jnp.exp(scores - jnp.max(scores, axis=-1, keepdims=True))
    return weights * (1.0 / jnp.sum(weights, axis=-1, keepdims=True))


def attend_kernel(
    row_block, q_raw, k_raw, v_ref, rq, rk, gq, gk, cos, sin, doc_col, doc_row, o_ref, q_out, k_out
):
    seq_len = q_raw.shape[0]
    sign = half_sign(cos.shape)

    def rotated(raw, scale, gain):
        value = raw[...] * scale[...] * gain[...]
        return (value * cos[...] + turn(value) * (sin[...] * sign)).astype(BF)

    q_out[...] = rotated(q_raw, rq, gq)
    k_out[...] = rotated(k_raw, rk, gk)
    scale_by = HEAD ** (-0.5)
    for start in range(0, seq_len, row_block):
        end = start + row_block
        probs = block_probs(
            q_out[start:end, :], k_out[:end, :], doc_col[start:end, :], doc_row[:, :end], start, scale_by
        )
        o_ref[start:end, :] = jnp.dot(
            probs.astype(BF), v_ref[:end, :], preferred_element_type=F32
        ).astype(BF)


def attend(q_raw, k_raw, values, rq, rk, gq, gk, cos, sin, doc_col, doc_row):
    seq_len, width = q_raw.shape
    head = pl.BlockSpec((seq_len, HEAD), lambda h: (0, h))
    gain = pl.BlockSpec((1, HEAD), lambda h: (0, h))

    def whole(x):
        return pl.BlockSpec(x.shape, lambda h: (0, 0))

    out = jax.ShapeDtypeStruct((seq_len, width), BF)
    return pl.pallas_call(
        partial(attend_kernel, 256),
        grid=(width // HEAD,),
        out_shape=[out, out, out],
        in_specs=[head, head, head, whole(rq), whole(rk), gain, gain, whole(cos), whole(sin)]
        + [whole(doc_col), whole(doc_row)],
        out_specs=[head, head, head],
        compiler_params=pltpu.CompilerParams(vmem_limit_bytes=48 << 20),
        name="attend",
    )(q_raw, k_raw, values, rq, rk, gq, gk, cos, sin, doc_col, doc_row)


def attend_back_kernel(
    row_block,
    q_low,
    k_low,
    v_ref,
    do_ref,
    q_raw,
    k_raw,
    rq,
    rk,
    gq,
    gk,
    cos,
    sin,
    doc_col,
    doc_row,
    uq_ref,
    uk_ref,
    dv_ref,
    dots,
    gain_q,
    gain_k,
    dq_acc,
    dk_acc,
    dv_acc,
):
    seq_len = q_low.shape[0]
    scale_by = HEAD ** (-0.5)
    dk_acc[...] = jnp.zeros_like(dk_acc)
    dv_acc[...] = jnp.zeros_like(dv_acc)
    for start in range(0, seq_len, row_block):
        end = start + row_block
        rows = slice(start, end)
        probs = block_probs(
            q_low[rows, :], k_low[:end, :], doc_col[rows, :], doc_row[:, :end], start, scale_by
        )
        grad_rows = do_ref[rows, :]
        grad_probs = lax.dot_general(
            grad_rows, v_ref[:end, :], (((1,), (1,)), ((), ())), preferred_element_type=F32
        )
        centre = jnp.sum(probs * grad_probs, axis=-1, keepdims=True)
        grad_scores = (probs * (grad_probs - centre)).astype(BF)
        dq_acc[rows, :] = jnp.dot(grad_scores, k_low[:end, :], preferred_element_type=F32)
        over_rows = (((0,), (0,)), ((), ()))
        dk_acc[:end, :] += lax.dot_general(
            grad_scores, q_low[rows, :], over_rows, preferred_element_type=F32
        )
        dv_acc[:end, :] += lax.dot_general(
            probs.astype(BF), grad_rows, over_rows, preferred_element_type=F32
        )
    dv_ref[...] = dv_acc[...].astype(BF)
    sign = half_sign(cos.shape)

    def unrotated(acc, raw, scale, gain, u_ref, gain_ref, lane):
        low = (acc[...] * scale_by).astype(BF).astype(F32)
        back = low * cos[...] - turn(low * sin[...]) * sign
        gain_ref[...] = jnp.sum(back * raw[...] * scale[...], axis=0, keepdims=True)
        u = back * gain[...]
        u_ref[...] = u
        dot = jnp.sum(u * raw[...], axis=1, keepdims=True)

        @pl.when(pl.program_id(0) == 0)
        def _():
            dots[:, lane : lane + 1] = dot

        @pl.when(pl.program_id(0) > 0)
        def _():
            dots[:, lane : lane + 1] += dot

    unrotated(dq_acc, q_raw, rq, gq, uq_ref, gain_q, 0)
    unrotated(dk_acc, k_raw, rk, gk, uk_ref, gain_k, 1)


def attend_back(q_low, k_low, values, d_heads, q_raw, k_raw, rq, rk, gq, gk, cos, sin, doc_col, doc_row):
    seq_len, width = q_raw.shape
    head = pl.BlockSpec((seq_len, HEAD), lambda h: (0, h))
    gain = pl.BlockSpec((1, HEAD), lambda h: (0, h))

    def whole(x):
        return pl.BlockSpec(x.shape, lambda h: (0, 0))

    wide = jax.ShapeDtypeStruct((seq_len, width), F32)
    row = jax.ShapeDtypeStruct((1, width), F32)
    return pl.pallas_call(
        partial(attend_back_kernel, 256),
        grid=(width // HEAD,),
        out_shape=[
            wide,
            wide,
            jax.ShapeDtypeStruct((seq_len, width), BF),
            jax.ShapeDtypeStruct((seq_len, 2), F32),
            row,
            row,
        ],
        in_specs=[head] * 6
        + [whole(rq), whole(rk), gain, gain, whole(cos), whole(sin), whole(doc_col), whole(doc_row)],
        out_specs=[head, head, head, pl.BlockSpec((seq_len, 2), lambda h: (0, 0)), gain, gain],
        scratch_shapes=[pltpu.VMEM((seq_len, HEAD), F32)] * 3,
        compiler_params=pltpu.CompilerParams(vmem_limit_bytes=56 << 20),
        name="attend_back",
    )(q_low, k_low, values, d_heads, q_raw, k_raw, rq, rk, gq, gk, cos, sin, doc_col, doc_row)


def experts_in_kernel(
    count,
    cap,
    h2_ref,
    dy_ref,
    targets,
    router_t,
    wg_ref,
    wu_ref,
    h2_out,
    x_out,
    y_out,
    act_out,
    by_up_out,
    by_gate_out,
    gate_slots,
    probs_out,
    h2,
    wg,
    wu,
    dy,
    xs,
    ys,
    acts,
    by_up,
    by_gate,
    s0,
    s1,
    s2,
    recv,
    w_sem,
    dy_sem,
    h_sem,
    out_sem,
):
    places = where_am_i()
    i, p, sib = places
    local_experts, model_width, hidden = wg_ref.shape
    tokens = h2_ref.shape[0]
    experts = router_t.shape[0]
    own_in = pltpu.make_async_copy(h2_ref, h2.at[i], h_sem.at[0])
    own_in.start()

    def fetch(q, buf):
        src = dy_ref.at[pl.ds(2 * q, 2)]
        return pltpu.make_async_copy(src, dy.at[buf], dy_sem.at[buf])

    fetch(p, 0).start()
    for e in range(local_experts):
        pltpu.make_async_copy(wg_ref.at[e], wg.at[e], w_sem.at[0, e]).start()
        pltpu.make_async_copy(wu_ref.at[e], wu.at[e], w_sem.at[1, e]).start()
    greet(count, places)
    own_in.wait()
    line = LineGather(count, places, [h2], [0], s0, s1, s2, recv)
    line.first(0)
    staged = ((xs, x_out), (ys, y_out), (acts, act_out), (by_up, by_up_out), (by_gate, by_gate_out))

    def store(n, e, q):
        rows = pl.ds(pl.multiple_of(q * 2 * cap, 2 * cap), 2 * cap)
        return pltpu.make_async_copy(staged[n][0].at[e], staged[n][1].at[e, rows], out_sem.at[n, e])

    def keep(q):
        src = h2.at[pl.ds(2 * q, 2)]
        return pltpu.make_async_copy(src, h2_out.at[pl.ds(2 * q, 2)], h_sem.at[1])

    slot_rows = lax.broadcasted_iota(jnp.int32, (local_experts * cap, tokens), 0)
    expert_rows = lax.broadcasted_iota(jnp.int32, (experts, tokens), 0)

    @pl.loop(0, count)
    def _(k):
        q = chunk_order(k, p, count)
        buf = k % 2

        @pl.when(k > 0)
        def _():
            line.forward(k)

        line.copy(0, 2 * q + lax.rem(sib, 2), 2, 0, sib).wait_recv()
        fetch(q, buf).wait()

        @pl.when(k + 1 < count)
        def _():
            fetch(chunk_order(k + 1, p, count), 1 - buf).start()

        @pl.when(k > 0)
        def _():
            for n in range(5):
                for e in range(local_experts):
                    store(n, e, q).wait()
            keep(q).wait()

        keep(q).start()
        picks = []
        for j in range(2):
            slot = 2 * q + j
            tokens_j = h2[slot]
            logits = lax.dot_general(
                router_t[...], tokens_j, (((1,), (1,)), ((), ())), preferred_element_type=F32
            )
            shifted = jnp.exp(logits - jnp.max(logits, axis=0, keepdims=True))
            probs = shifted / jnp.sum(shifted, axis=0, keepdims=True)
            probs_out[slot] = probs
            pick = None
            for e in range(local_experts):
                mask = slot_rows == targets[slot, e : e + 1, :]
                gate = jnp.sum(
                    jnp.where(expert_rows == i * local_experts + e, probs, 0.0), axis=0, keepdims=True
                )
                part = slice(e * cap, (e + 1) * cap)
                gate_slots[e, q, j * cap : (j + 1) * cap, :] = jnp.sum(
                    jnp.where(mask[part], gate, 0.0), axis=1, keepdims=True
                )
                pick = mask if pick is None else pick | mask
            picks.append(jnp.where(pick, 1.0, 0.0).astype(BF))

        block = 512

        @pl.loop(0, model_width // block)
        def _(n):
            cols = pl.ds(pl.multiple_of(n * block, block), block)
            for source, target in ((0, xs), (1, ys)):
                got = []
                for j in range(2):
                    rows = h2[2 * q + j, :, cols] if source == 0 else dy[buf, j, :, cols]
                    got.append(jnp.dot(picks[j], rows, preferred_element_type=F32))
                for e in range(local_experts):
                    part = slice(e * cap, (e + 1) * cap)
                    target[e, :, cols] = jnp.concatenate([got[0][part], got[1][part]], axis=0).astype(BF)

        for e in range(local_experts):
            store(0, e, q).start()
            store(1, e, q).start()

            @pl.when(k == 0)
            def _():
                pltpu.make_async_copy(wg_ref.at[e], wg.at[e], w_sem.at[0, e]).wait()
                pltpu.make_async_copy(wu_ref.at[e], wu.at[e], w_sem.at[1, e]).wait()

            wide = 256

            @pl.loop(0, hidden // wide)
            def _(n):
                cols = pl.ds(pl.multiple_of(n * wide, wide), wide)
                gate = jnp.dot(xs[e], wg[e, :, cols], preferred_element_type=F32)
                up = jnp.dot(xs[e], wu[e, :, cols], preferred_element_type=F32)
                sigmoid = 1.0 / (1.0 + jnp.exp(-gate))
                silu = gate * sigmoid
                acts[e, :, cols] = (silu * up).astype(BF)
                by_up[e, :, cols] = silu.astype(BF)
                by_gate[e, :, cols] = (up * sigmoid * (1.0 + gate * (1.0 - sigmoid))).astype(BF)

            for n in (2, 3, 4):
                store(n, e, q).start()

    for n in range(5):
        for e in range(local_experts):
            store(n, e, 0).wait()
    keep(0).wait()
    sends_done(line)


def sends_done(line):
    i, p, sib = line.places
    count = line.count
    line.copy(0, i, 2, 0, sib).wait_send()

    @pl.when(p < count - 1)
    def _():
        line.copy(0, i, 0, 0, i + 2).wait_send()

    @pl.when(p > 0)
    def _():
        line.copy(0, i, 1, 0, i - 2).wait_send()

    for t in range(1, count):

        @pl.when(p - t >= 0)
        def _():
            slot = i - 2 * t

            @pl.when(p < count - 1)
            def _():
                line.copy(0, slot, 0, t, i + 2).wait_send()

            line.copy(0, slot, 2, t, sib).wait_send()

        @pl.when(p + t < count)
        def _():
            slot = i + 2 * t

            @pl.when(p > 0)
            def _():
                line.copy(0, slot, 1, t, i - 2).wait_send()

            line.copy(0, slot, 2, count + t, sib).wait_send()


def experts_in(h2, dy_all, targets, router_t, w_gate, w_up, collective):
    shards, tokens, model_width = dy_all.shape
    local_experts, _, hidden = w_gate.shape
    experts = router_t.shape[0]
    count = shards // 2
    wide = jax.ShapeDtypeStruct((local_experts, count * 2 * CAP, model_width), BF)
    thin = jax.ShapeDtypeStruct((local_experts, count * 2 * CAP, hidden), BF)
    anywhere = pl.BlockSpec(memory_space=ANY)
    vmem = pl.BlockSpec(memory_space=pltpu.VMEM)
    return pl.pallas_call(
        partial(experts_in_kernel, count, CAP),
        out_shape=[
            jax.ShapeDtypeStruct((shards, tokens, model_width), BF),
            wide,
            wide,
            thin,
            thin,
            thin,
            jax.ShapeDtypeStruct((local_experts, count, 2 * CAP, 1), F32),
            jax.ShapeDtypeStruct((shards, experts, tokens), F32),
        ],
        in_specs=[anywhere, anywhere, vmem, vmem, anywhere, anywhere],
        out_specs=[anywhere] * 6 + [vmem, vmem],
        scratch_shapes=[
            pltpu.VMEM((shards, tokens, model_width), BF),
            pltpu.VMEM(w_gate.shape, BF),
            pltpu.VMEM(w_up.shape, BF),
            pltpu.VMEM((2, 2, tokens, model_width), BF),
        ]
        + [pltpu.VMEM((local_experts, 2 * CAP, model_width), BF)] * 2
        + [pltpu.VMEM((local_experts, 2 * CAP, hidden), BF)] * 3
        + line_sems(1, count)
        + [DMA((2, local_experts)), DMA((2,)), DMA((2,)), DMA((5, local_experts))],
        compiler_params=pltpu.CompilerParams(
            collective_id=collective, has_side_effects=True, vmem_limit_bytes=60 << 20
        ),
        name="experts_in",
    )(h2, dy_all, targets, router_t, w_gate, w_up)


def experts_mid_kernel(
    cap,
    y_in,
    act_in,
    by_up_in,
    by_gate_in,
    gate_slots,
    wd_in,
    gated_out,
    d_gate_out,
    d_up_out,
    dots_ref,
    g_down_out,
    wd,
    ys,
    acts,
    by_ups,
    by_gates,
    gated,
    d_gate,
    d_up,
    staged,
    in_sem,
    out_sem,
    grad_sem,
):
    local_experts, hidden, model_width = wd_in.shape
    count = gate_slots.shape[1]
    slots = ys.shape[1]
    over_lanes = (((1,), (1,)), ((), ()))
    over_rows = (((0,), (0,)), ((), ()))
    inputs = ((wd_in, wd), (y_in, ys), (act_in, acts), (by_up_in, by_ups), (by_gate_in, by_gates))
    results = ((gated, gated_out), (d_gate, d_gate_out), (d_up, d_up_out))
    wide = 256
    tile = staged.shape[1]

    def fetch(n, e):
        return pltpu.make_async_copy(inputs[n][0].at[e], inputs[n][1].at[e], in_sem.at[n, e])

    def store(n, e):
        return pltpu.make_async_copy(results[n][0].at[e], results[n][1].at[e], out_sem.at[n, e])

    def put_grad(e, n, buf):
        rows = pl.ds(pl.multiple_of(n * tile, tile), tile)
        return pltpu.make_async_copy(staged.at[buf], g_down_out.at[e, rows], grad_sem.at[buf])

    for e in range(local_experts):
        for n in range(5):
            fetch(n, e).start()
    for e in range(local_experts):
        for n in range(5):
            fetch(n, e).wait()
        gate = jnp.concatenate([gate_slots[e, q] for q in range(count)], axis=0)

        def step(n, dot):
            cols = pl.ds(pl.multiple_of(n * wide, wide), wide)
            grad_act = lax.dot_general(ys[e], wd[e, cols, :], over_lanes, preferred_element_type=F32)
            act = acts[e, :, cols].astype(F32)
            dot = dot + jnp.sum(act * grad_act, axis=1, keepdims=True)
            grad_act = grad_act * gate
            gated[e, :, cols] = (act * gate).astype(BF)
            d_up[e, :, cols] = (grad_act * by_ups[e, :, cols].astype(F32)).astype(BF)
            d_gate[e, :, cols] = (grad_act * by_gates[e, :, cols].astype(F32)).astype(BF)
            return dot

        dot = lax.fori_loop(0, hidden // wide, step, jnp.zeros((slots, 1), F32))
        for q in range(count):
            dots_ref[e, q] = dot[2 * cap * q : 2 * cap * (q + 1)]
        for n in range(3):
            store(n, e).start()

        @pl.loop(0, hidden // tile // 2)
        def _(m):
            for buf in range(2):
                n = 2 * m + buf

                def wait_last():
                    put_grad(e, n, buf).wait()

                if e > 0:
                    wait_last()
                else:
                    pl.when(m > 0)(wait_last)
                cols = pl.ds(pl.multiple_of(n * tile, tile), tile)
                staged[buf] = lax.dot_general(
                    gated[e, :, cols], ys[e], over_rows, preferred_element_type=F32
                ).astype(BF)
                put_grad(e, n, buf).start()

    for buf in range(2):
        put_grad(0, 0, buf).wait()
    for e in range(local_experts):
        for n in range(3):
            store(n, e).wait()


def experts_mid(grads, act, by_up, by_gate, gate_slots, w_down):
    local_experts, slots, model_width = grads.shape
    anywhere = pl.BlockSpec(memory_space=ANY)
    vmem = pl.BlockSpec(memory_space=pltpu.VMEM)
    thin = jax.ShapeDtypeStruct(act.shape, BF)
    return pl.pallas_call(
        partial(experts_mid_kernel, CAP),
        out_shape=[
            thin,
            thin,
            thin,
            jax.ShapeDtypeStruct(gate_slots.shape, F32),
            jax.ShapeDtypeStruct(w_down.shape, BF),
        ],
        in_specs=[anywhere] * 4 + [vmem, anywhere],
        out_specs=[anywhere] * 3 + [vmem, anywhere],
        scratch_shapes=[pltpu.VMEM(w_down.shape, BF), pltpu.VMEM(grads.shape, BF)]
        + [pltpu.VMEM(act.shape, BF)] * 6
        + [
            pltpu.VMEM((2, 256, model_width), BF),
            DMA((5, local_experts)),
            DMA((3, local_experts)),
            DMA((2,)),
        ],
        compiler_params=pltpu.CompilerParams(vmem_limit_bytes=60 << 20),
        cost_estimate=pl.CostEstimate(flops=18_000_000_000, bytes_accessed=60_000_000, transcendentals=0),
        name="experts_mid",
    )(grads, act, by_up, by_gate, gate_slots, w_down)


class StagedScatter(LineScatter):
    def __init__(self, count, places, stage, bufs, sems):
        super().__init__(count, places, [None], [0], bufs, sems)
        self.stage = stage

    def to_sib(self, a, q):
        sib = self.places[2]
        return remote(self.stage, self.sib[a].at[q], self.sems[2].at[a, q], self.sems[5].at[a, q], fsdp=sib)

    def ready(self, a, q):
        self.to_sib(a, q).wait_recv()

    def finish(self):
        i, p, sib = self.places
        for q in range(self.count):

            @pl.when(q > p)
            def _():
                self.right(0, q).wait_send()

            @pl.when(q < p)
            def _():
                self.left(0, q).wait_send()


class OuterGrads:
    def __init__(self, left, right, out, scratch, steps):
        self.left, self.right, self.out = left, right, out
        self.tiles_in, self.held, self.staged, self.sems = scratch
        self.experts, self.width, self.hidden = out.shape
        self.tile = self.staged.shape[1]
        self.tiles = self.width // self.tile
        self.units = self.experts * self.tiles
        self.share = -(-self.units // steps)

    def span(self, u):
        start = lax.rem(u, self.tiles) * self.tile
        return pl.ds(pl.multiple_of(start, self.tile), self.tile)

    def fetch(self, u):
        src = self.left.at[u // self.tiles, :, self.span(u)]
        return pltpu.make_async_copy(src, self.tiles_in.at[lax.rem(u, 2)], self.sems.at[0, lax.rem(u, 2)])

    def put(self, u):
        buf = lax.rem(u, 2)
        target = self.out.at[u // self.tiles, self.span(u)]
        return pltpu.make_async_copy(self.staged.at[buf], target, self.sems.at[1, buf])

    def hold(self):
        return pltpu.make_async_copy(self.right, self.held, self.sems.at[2, 0])

    def begin(self):
        self.hold().start()
        self.fetch(0).start()

    def between(self, step):
        @pl.loop(step * self.share, jnp.minimum((step + 1) * self.share, self.units))
        def _(u):
            @pl.when(u == 0)
            def _():
                self.hold().wait()

            self.fetch(u).wait()

            @pl.when(u + 1 < self.units)
            def _():
                self.fetch(u + 1).start()

            @pl.when(u >= 2)
            def _():
                self.put(u - 2).wait()

            buf = lax.rem(u, 2)
            self.staged[buf] = lax.dot_general(
                self.tiles_in[buf],
                self.held[u // self.tiles],
                (((0,), (0,)), ((), ())),
                preferred_element_type=F32,
            ).astype(BF)
            self.put(u).start()

    def finish(self):
        self.put(self.units - 2).wait()
        self.put(self.units - 1).wait()


def outer_scratch(right, tile):
    slots, hidden = right.shape[1:]
    return [
        pltpu.VMEM((2, slots, tile), BF),
        pltpu.VMEM(right.shape, BF),
        pltpu.VMEM((2, tile, hidden), BF),
        DMA((3, 2)),
    ]


def experts_out_kernel(
    count,
    cap,
    x_in,
    gated_in,
    d_gate_in,
    d_up_in,
    dots,
    targets,
    targets_t,
    probs_ref,
    router_t,
    wg_in,
    wu_in,
    wd_in,
    parts_out,
    logit_ref,
    sum_ref,
    g_gate_out,
    wg,
    wu,
    wd,
    gated,
    d_gate,
    d_up,
    parts,
    stage,
    own,
    sibling,
    inbox,
    w_sem,
    in_sem,
    part_sem,
    tiles_in,
    held,
    staged,
    outer_sem,
    *sems,
):
    places = where_am_i()
    i, p, sib = places
    core = lax.rem(i, 2)
    local_experts, hidden, model_width = wd_in.shape
    tokens = targets.shape[2]
    experts = router_t.shape[0]
    first = i * local_experts
    over_lanes = (((1,), (1,)), ((), ()))
    line = StagedScatter(count, places, stage, ([own], [sibling], [inbox]), sems)
    grads_of = OuterGrads(x_in, d_gate_in, g_gate_out, (tiles_in, held, staged, outer_sem), count - 1)
    weights = ((wd_in, wd), (wg_in, wg), (wu_in, wu))
    inputs = ((gated_in, gated), (d_gate_in, d_gate), (d_up_in, d_up))

    def weight(n):
        return pltpu.make_async_copy(weights[n][0], weights[n][1], w_sem.at[n])

    def fetch(n, q, buf):
        rows = pl.ds(pl.multiple_of(q * 2 * cap, 2 * cap), 2 * cap)
        return pltpu.make_async_copy(inputs[n][0].at[:, rows], inputs[n][1].at[buf], in_sem.at[n, buf])

    def put(q):
        return pltpu.make_async_copy(parts, parts_out.at[pl.ds(2 * q, 2)], part_sem)

    def order(k):
        return chunk_order(count - 1 - k, p, count)

    for n in range(3):
        fetch(n, order(0), 0).start()
    for n in range(3):
        weight(n).start()
    grads_of.begin()
    greet(count, places)
    slot_rows = lax.broadcasted_iota(jnp.int32, (local_experts * cap, tokens), 0)
    slot_lanes = lax.broadcasted_iota(jnp.int32, (tokens, local_experts * cap), 1)
    expert_rows = lax.broadcasted_iota(jnp.int32, (experts, tokens), 0)

    def compute(k):
        q = order(k)
        buf = lax.rem(k, 2)
        picks, logits_low = [], []
        for j in range(2):
            slot = 2 * q + j
            grad_probs = jnp.zeros((experts, tokens), F32)
            pick = None
            for e in range(local_experts):
                part = slice(e * cap, (e + 1) * cap)
                mask = (slot_rows == targets[slot, e : e + 1, :])[part]
                dot = dots[e, q, j * cap : (j + 1) * cap, :]
                row = jnp.sum(jnp.where(mask, dot, 0.0), axis=0, keepdims=True)
                grad_probs = jnp.where(expert_rows == first + e, row, grad_probs)
                hit = slot_lanes == targets_t[slot, :, e : e + 1]
                pick = hit if pick is None else pick | hit
            probs = probs_ref[slot]
            grad_logits = probs * (grad_probs - jnp.sum(probs * grad_probs, axis=0, keepdims=True))
            logit_ref[slot] = grad_logits.astype(BF)
            picks.append(jnp.where(pick, 1.0, 0.0).astype(BF))
            logits_low.append(grad_logits.T.astype(BF))
        for n in range(3):
            fetch(n, q, buf).wait()

        @pl.when(k + 1 < count)
        def _():
            for n in range(3):
                fetch(n, order(k + 1), 1 - buf).start()

        @pl.when(k > 0)
        def _():
            put(q).wait()
            line.to_sib(0, order(k - 1)).wait_send()

        @pl.when(k == 0)
        def _():
            for n in range(3):
                weight(n).wait()

        block = 512

        @pl.loop(0, model_width // block)
        def _(n):
            cols = pl.ds(pl.multiple_of(n * block, block), block)
            outs, grads = [], []
            for e in range(local_experts):
                outs.append(jnp.dot(gated[buf, e], wd[e, :, cols], preferred_element_type=F32))
                grads.append(
                    lax.dot_general(d_gate[buf, e], wg[e, cols, :], over_lanes, preferred_element_type=F32)
                    + lax.dot_general(d_up[buf, e], wu[e, cols, :], over_lanes, preferred_element_type=F32)
                )
            for j in range(2):
                part = slice(j * cap, (j + 1) * cap)
                mine = jnp.concatenate([value[part] for value in outs], axis=0).astype(BF)
                back = jnp.concatenate([value[part] for value in grads], axis=0).astype(BF)
                parts[j, :, cols] = jnp.dot(picks[j], mine, preferred_element_type=F32).astype(BF)
                total = (
                    jnp.dot(picks[j], back, preferred_element_type=F32)
                    + jnp.dot(logits_low[j], router_t[:, cols], preferred_element_type=F32)
                ).astype(BF)

                @pl.when(core == j)
                def _():
                    own[q, :, cols] = total

                @pl.when(core != j)
                def _():
                    stage[:, cols] = total

        line.to_sib(0, q).start()
        put(q).start()

    @pl.loop(0, 1)
    def _(k):
        compute(k)

    def between(step):
        compute(step + 1)
        grads_of.between(step)

    line.run(lambda a, q: None, between)
    grads_of.finish()
    put(0).wait()
    line.to_sib(0, order(count - 1)).wait_send()
    out = pltpu.make_async_copy(own.at[p], sum_ref, part_sem)
    out.start()
    out.wait()
    line.finish()


def experts_out(
    expert_in, gated, d_gate, d_up, dots, targets, targets_t, probs, router_t, w_gate, w_up, w_down, collective
):
    local_experts, slots, model_width = expert_in.shape
    hidden = gated.shape[2]
    shards, experts, tokens = probs.shape
    count = shards // 2
    anywhere = pl.BlockSpec(memory_space=ANY)
    vmem = pl.BlockSpec(memory_space=pltpu.VMEM)
    return pl.pallas_call(
        partial(experts_out_kernel, count, CAP),
        out_shape=[
            jax.ShapeDtypeStruct((shards, tokens, model_width), BF),
            jax.ShapeDtypeStruct(probs.shape, BF),
            jax.ShapeDtypeStruct((tokens, model_width), BF),
            jax.ShapeDtypeStruct(w_gate.shape, BF),
        ],
        in_specs=[anywhere] * 4 + [vmem] * 5 + [anywhere] * 3,
        out_specs=[anywhere, vmem, anywhere, anywhere],
        scratch_shapes=[pltpu.VMEM(x.shape, BF) for x in (w_gate, w_up, w_down)]
        + [pltpu.VMEM((2, local_experts, 2 * CAP, hidden), BF)] * 3
        + [
            pltpu.VMEM((2, tokens, model_width), BF),
            pltpu.VMEM((tokens, model_width), BF),
            pltpu.VMEM((count, tokens, model_width), BF),
            pltpu.VMEM((count, tokens, model_width), BF),
            pltpu.VMEM((count + 1, tokens, model_width), BF),
            DMA((3,)),
            DMA((3, 2)),
            DMA,
        ]
        + outer_scratch(d_gate, 256)
        + [DMA((1, count))] * 7,
        compiler_params=pltpu.CompilerParams(
            collective_id=collective, has_side_effects=True, vmem_limit_bytes=63 << 20
        ),
        cost_estimate=pl.CostEstimate(flops=60_000_000_000, bytes_accessed=200_000_000, transcendentals=0),
        name="experts_out",
    )(expert_in, gated, d_gate, d_up, dots, targets, targets_t, probs, router_t, w_gate, w_up, w_down)


def rope_tables(positions, head_dim):
    half_dim = head_dim // 2
    inverse = ROPE_BASE ** (-(jnp.arange(half_dim, dtype=F32) * 2.0 / head_dim))
    angles = positions.astype(F32)[:, None] * inverse[None, :]
    angles = jnp.concatenate([angles, angles], axis=-1)
    return (jnp.cos(angles), jnp.sin(angles))


def dot(left, right, sides=(1, 0), out=F32):
    return lax.dot_general(
        left, right, (((sides[0],), (sides[1],)), ((), ())), preferred_element_type=F32
    ).astype(out)


def inverse_rms(rows):
    return lax.rsqrt(jnp.mean(rows * rows, axis=-1, keepdims=True) + EPSILON)


def on_device(
    inputs,
    out_grad,
    doc_ids,
    routes,
    w_query,
    w_key,
    w_value,
    w_output,
    w_router,
    attn_gain,
    ffn_gain,
    query_gain,
    key_gain,
    w_gate,
    w_up,
    w_down,
):
    seq_count = lax.axis_size("seq")
    shards = lax.axis_size("fsdp")
    tok_rows, model_width = inputs.shape[1:]
    seq_len = tok_rows * seq_count
    rows = w_query.shape[0]
    width = model_width // seq_count
    local_experts = w_gate.shape[0]
    experts = w_router.shape[1]
    top_k = routes.shape[2]
    lanes = 128

    small = jnp.concatenate(
        [
            w_router,
            attn_gain[:, None],
            ffn_gain[:, None],
            jnp.zeros((rows, lanes - experts - 2), BF),
        ],
        axis=1,
    )
    gains = jnp.pad(jnp.stack([query_gain, key_gain]), ((0, 14), (0, lanes - rows)))
    routes_flat = routes.reshape(tok_rows * top_k // lanes, lanes)
    wq, wk, wv, wo, small_all, gains_all, routes_all, x_all = gather_start(
        (w_query, w_key, w_value, w_output, small, gains, routes_flat, inputs[0]), seq_count, shards, 0
    )
    x_all = x_all.reshape(seq_len, model_width)
    full_gate = lax.all_gather(w_gate, "seq", axis=1, tiled=True)
    full_up = lax.all_gather(w_up, "seq", axis=1, tiled=True)
    full_down = lax.all_gather(w_down, "seq", axis=1, tiled=True)

    wq = wq.reshape(model_width, width)
    wk = wk.reshape(model_width, width)
    wv = wv.reshape(model_width, width)
    wo = wo.reshape(width, model_width)
    small_all = small_all.reshape(model_width, lanes)
    w_r = small_all[:, :experts]
    gain_a = small_all[:, experts].astype(F32)
    gain_f = small_all[:, experts + 1].astype(F32)
    gq = gains_all[:, 0, :rows].reshape(1, width).astype(F32)
    gk = gains_all[:, 1, :rows].reshape(1, width).astype(F32)

    x_float = x_all.astype(F32)
    h1 = (x_float * inverse_rms(x_float) * gain_a).astype(BF)
    q_raw = dot(h1, wq)
    k_raw = dot(h1, wk)
    values = dot(h1, wv, out=BF)
    squares = jnp.stack([jnp.sum(q_raw * q_raw, axis=1), jnp.sum(k_raw * k_raw, axis=1)])
    squares = seq_sum(squares, seq_count, 1)
    scales = lax.rsqrt(squares / model_width + EPSILON)
    rq, rk = scales[0][:, None], scales[1][:, None]
    cos, sin = rope_tables(jnp.arange(seq_len, dtype=jnp.int32), HEAD)
    doc_row = doc_ids
    doc_col = doc_ids.reshape(seq_len, 1)
    attended, q_low, k_low = attend(q_raw, k_raw, values, rq, rk, gq, gk, cos, sin, doc_col, doc_row)
    projected = dot(attended, wo, out=BF).reshape(seq_count, tok_rows, model_width)
    rows_in = inputs[0].astype(F32)
    grad_rows = out_grad[0].astype(F32)
    summed, dy_all = middle(projected, out_grad[0], shards, 2)
    x_mid = rows_in + summed
    scale_f = inverse_rms(x_mid)
    h2 = (x_mid * scale_f * gain_f).astype(BF)

    routes_all = routes_all.reshape(shards, tok_rows, top_k)
    local_ids = lax.axis_index("fsdp") * local_experts + jnp.arange(local_experts, dtype=jnp.int32)
    chosen = jnp.any(routes_all[:, None] == local_ids[None, :, None, None], axis=3)
    slot = jnp.cumsum(chosen.astype(jnp.int32), axis=2) - 1
    slot = slot + CAP * jnp.arange(local_experts, dtype=jnp.int32)[None, :, None]
    targets = jnp.where(chosen, slot, -1)
    targets_t = jnp.swapaxes(targets, 1, 2)
    router_t = w_r.T
    h2_all, expert_in, grad_slots, act, by_up, by_gate, gate_slots, gate_probs = experts_in(
        h2, dy_all, targets, router_t, full_gate, full_up, 3
    )
    gated, d_gate, d_up, dots_slots, g_down = experts_mid(
        grad_slots, act, by_up, by_gate, gate_slots, full_down
    )
    out_parts, grad_logits, grad_h2, g_gate = experts_out(
        expert_in,
        gated,
        d_gate,
        d_up,
        dots_slots,
        targets,
        targets_t,
        gate_probs,
        router_t,
        full_gate,
        full_up,
        full_down,
        4,
    )

    def spread(part):
        return lax.psum_scatter(part, "seq", scatter_dimension=1, tiled=True)

    g_down = spread(g_down)
    g_gate = spread(g_gate)
    grad_h2 = grad_h2.astype(F32)

    u_rows = gain_f * grad_h2
    grad_mid = (
        grad_rows
        + scale_f * u_rows
        - x_mid * scale_f**3 * jnp.mean(u_rows * x_mid, axis=-1, keepdims=True)
    )
    ffn_part = jnp.sum(grad_h2 * x_mid * scale_f, axis=0)

    d_attn, out_sum, g_up, router_part = turn_back(
        grad_mid.astype(BF), out_parts, expert_in, d_up, h2_all, grad_logits, seq_count, shards, 5
    )
    g_up = spread(g_up)
    d_attn = d_attn.reshape(seq_len, model_width)
    result = x_mid + out_sum.astype(F32)
    d_heads = dot(d_attn, wo, (1, 1), BF)
    u_q, u_k, dv_low, dots, gain_q_part, gain_k_part = attend_back(
        q_low, k_low, values, d_heads, q_raw, k_raw, rq, rk, gq, gk, cos, sin, doc_col, doc_row
    )
    dots, g_down, g_gate = lax.optimization_barrier((dots, g_down, g_gate))
    dots = seq_sum(dots.T, seq_count, 6) / model_width

    def norm_back(u, raw, scale, product):
        return (scale * u - raw * (scale**3 * product[:, None])).astype(BF)

    dq_low = norm_back(u_q, q_raw, rq, dots[0])
    dk_low = norm_back(u_k, k_raw, rk, dots[1])
    grad_h1 = dot(dq_low, wq, (1, 1)) + dot(dk_low, wk, (1, 1)) + dot(dv_low, wv, (1, 1))
    grad_h1 = grad_h1.astype(BF).reshape(seq_count, tok_rows, model_width)

    sheet = (seq_count, shards, rows, width)
    small_part = jnp.concatenate(
        [router_part.T, ffn_part[:, None], jnp.zeros((model_width, lanes - experts - 1), F32)], axis=1
    ).reshape(seq_count, shards, rows, lanes)
    gains_part = jnp.stack([gain_q_part.reshape(shards, rows), gain_k_part.reshape(shards, rows)], axis=1)
    gains_part = jnp.pad(gains_part, ((0, 0), (0, 6), (0, lanes - rows)))
    g_query, g_key, g_value, g_output, g_small, g_gains, grad_h1 = scatter_end(
        (
            dot(h1, dq_low, (0, 0), BF).reshape(sheet),
            dot(h1, dk_low, (0, 0), BF).reshape(sheet),
            dot(h1, dv_low, (0, 0), BF).reshape(sheet),
            dot(attended, d_attn, (0, 0), BF).reshape(shards, rows, model_width),
            small_part,
            gains_part,
        ),
        grad_h1,
        seq_count,
        shards,
        8,
    )
    g_query, g_key, g_value = (g_query.astype(F32), g_key.astype(F32), g_value.astype(F32))

    scale_a = inverse_rms(rows_in)
    u_rows = gain_a * grad_h1
    input_grad = (
        grad_mid
        + scale_a * u_rows
        - rows_in * scale_a**3 * jnp.mean(u_rows * rows_in, axis=-1, keepdims=True)
    )
    pairs = (
        w_query.astype(F32) * g_query + w_key.astype(F32) * g_key + w_value.astype(F32) * g_value
    )
    g_attn_gain = jnp.sum(pairs, axis=1) / attn_gain.astype(F32)

    return (
        result.astype(BF)[None],
        input_grad[None],
        g_query,
        g_key,
        g_value,
        g_output.astype(F32),
        g_small[:, :experts],
        g_attn_gain,
        g_small[:, experts],
        g_gains[0, :rows],
        g_gains[1, :rows],
        g_gate.astype(F32),
        g_up.astype(F32),
        g_down.astype(F32),
    )


def solution(mesh):
    rows = P("fsdp", "seq", None)
    sheet = P(("seq", "fsdp"), None)
    line = P(("seq", "fsdp"))
    return jax.shard_map(
        on_device,
        mesh=mesh,
        in_specs=(rows, rows, P("fsdp", None), rows) + (sheet,) * 5 + (line,) * 4 + (rows,) * 3,
        out_specs=(rows, rows) + (sheet,) * 5 + (line,) * 4 + (rows,) * 3,
        check_vma=False,
    )
```

```python
from functools import partial

import jax
import jax.numpy as jnp
import numpy as np
from jax import lax
from jax.experimental import pallas as pl
from jax.experimental.pallas import tpu as pltpu
from jax.sharding import PartitionSpec as P

CAP = 136
HEAD = 128
EPSILON = 1e-05
ROPE_BASE = 10000.0
MASKED_OUT = -1e30
ANY = pl.ANY
MESH = pl.DeviceIdType.MESH
DMA = pltpu.SemaphoreType.DMA
BF = jnp.bfloat16
F32 = jnp.float32


def remote(src, dst, send, recv, **where):
    return pltpu.make_async_remote_copy(
        src_ref=src, dst_ref=dst, send_sem=send, recv_sem=recv, device_id=where, device_id_type=MESH
    )


def greet(count, places, seq_count=1):
    i, p, sib = places
    barrier = pltpu.get_barrier_semaphore()
    pl.semaphore_signal(barrier, inc=1, device_id={"fsdp": sib}, device_id_type=MESH)
    here = lax.axis_index("seq")
    for d in range(1, seq_count):
        peer = lax.rem(here + d, seq_count)
        pl.semaphore_signal(barrier, inc=1, device_id={"seq": peer}, device_id_type=MESH)

    @pl.when(p > 0)
    def _():
        pl.semaphore_signal(barrier, inc=1, device_id={"fsdp": i - 2}, device_id_type=MESH)

    @pl.when(p < count - 1)
    def _():
        pl.semaphore_signal(barrier, inc=1, device_id={"fsdp": i + 2}, device_id_type=MESH)

    last = count - 1
    pl.semaphore_wait(barrier, seq_count + (p + last) // count + (last - p + last) // count)


def slot_of(ref, axis, index):
    return ref.at[index] if axis == 0 else ref.at[:, index]


class LineGather:
    def __init__(self, count, places, refs, axes, send_r, send_l, send_s, recv):
        self.count, self.places = count, places
        self.refs, self.axes = refs, axes
        self.sems = (send_r, send_l, send_s, recv)

    def copy(self, a, slot, kind, t, device):
        send = self.sems[kind].at[a, t]
        ref = slot_of(self.refs[a], self.axes[a], slot)
        return remote(ref, ref, send, self.sems[3].at[a, slot], fsdp=device)

    def first(self, a):
        i, p, sib = self.places

        @pl.when(p < self.count - 1)
        def _():
            self.copy(a, i, 0, 0, i + 2).start()

        @pl.when(p > 0)
        def _():
            self.copy(a, i, 1, 0, i - 2).start()

        self.copy(a, i, 2, 0, sib).start()

    def forward(self, t):
        i, p, sib = self.places
        count = self.count
        for a in range(len(self.refs)):

            @pl.when(p - t >= 0)
            def _():
                slot = i - 2 * t
                self.copy(a, slot, 0, t, sib).wait_recv()

                @pl.when(p < count - 1)
                def _():
                    self.copy(a, slot, 0, t, i + 2).start()

                self.copy(a, slot, 2, t, sib).start()

            @pl.when(p + t < count)
            def _():
                slot = i + 2 * t
                self.copy(a, slot, 1, t, sib).wait_recv()

                @pl.when(p > 0)
                def _():
                    self.copy(a, slot, 1, t, i - 2).start()

                self.copy(a, slot, 2, count + t, sib).start()

    def finish(self):
        i, p, sib = self.places
        count = self.count
        for a in range(len(self.refs)):
            for q in range(count):
                self.copy(a, 2 * q + lax.rem(sib, 2), 2, 0, sib).wait_recv()
            self.copy(a, i, 2, 0, sib).wait_send()

            @pl.when(p < count - 1)
            def _():
                self.copy(a, i, 0, 0, i + 2).wait_send()

            @pl.when(p > 0)
            def _():
                self.copy(a, i, 1, 0, i - 2).wait_send()

            for t in range(1, count):

                @pl.when(p - t >= 0)
                def _():
                    slot = i - 2 * t

                    @pl.when(p < count - 1)
                    def _():
                        self.copy(a, slot, 0, t, i + 2).wait_send()

                    self.copy(a, slot, 2, t, sib).wait_send()

                @pl.when(p + t < count)
                def _():
                    slot = i + 2 * t

                    @pl.when(p > 0)
                    def _():
                        self.copy(a, slot, 1, t, i - 2).wait_send()

                    self.copy(a, slot, 2, count + t, sib).wait_send()


def line_sems(arrays, count):
    return [DMA((arrays, count)), DMA((arrays, count)), DMA((arrays, 2 * count)), DMA((arrays, 2 * count))]


def where_am_i():
    i = lax.axis_index("fsdp")
    p = i // 2
    c = i % 2
    return i, p, 2 * p + 1 - c


def start_kernel(count, seq_count, *refs):
    wq, wk, wv, small, gains, routes, wo, rows = refs[:8]
    outs = refs[8:15]
    rows_out = refs[15]
    holds = refs[16:24]
    send_x, recv_x, local, send_r, send_l, send_s, recv, send_y, recv_y = refs[24:]
    places = where_am_i()
    i = places[0]
    here = lax.axis_index("seq")
    width = wq.shape[1] // seq_count

    def columns(ref, peer):
        return ref.at[:, pl.ds(pl.multiple_of(peer * width, width), width)]

    own = [columns(wq, here), columns(wk, here), columns(wv, here), small, gains, routes, wo, rows]
    for a in range(8):
        pltpu.make_async_copy(own[a], holds[a], local.at[a]).start()
    greet(count, places, seq_count)

    def piece(a, d):
        peer = lax.rem(here + d, seq_count)
        src = small if a == 3 else columns((wq, wk, wv)[a], peer)
        return remote(src, outs[a].at[here, i], send_x.at[a, d - 1], recv_x.at[a, d - 1], seq=peer)

    def arrived(a, d):
        origin = lax.rem(here + seq_count - d, seq_count)
        ref = outs[a].at[origin, i]
        return remote(ref, ref, send_x.at[a, d - 1], recv_x.at[a, d - 1], seq=origin)

    for a in (3, 0, 1, 2):
        for d in range(1, seq_count):
            piece(a, d).start()
    gather = SeqGather(seq_count, rows, rows_out, send_y, recv_y)
    gather.begin()
    axes = [1, 1, 1, 1, 0, 0, 0]

    def target(a):
        return outs[a].at[here, i] if axes[a] == 1 else outs[a].at[i]

    for a in (4, 5, 6, 3, 0, 1, 2):
        pltpu.make_async_copy(own[a], holds[a], local.at[a]).wait()
        pltpu.make_async_copy(holds[a], target(a), local.at[a]).start()
    line = LineGather(count, places, outs, axes, send_r, send_l, send_s, recv)
    for a in (4, 5, 6, 3, 0, 1, 2):
        pltpu.make_async_copy(holds[a], target(a), local.at[a]).wait()
        if axes[a] == 1:
            for d in range(1, seq_count):
                arrived(a, d).wait_recv()
        line.first(a)
    pltpu.make_async_copy(rows, holds[7], local.at[7]).wait()
    pltpu.make_async_copy(holds[7], rows_out.at[here], local.at[7]).start()
    for t in range(1, count):
        line.forward(t)
        if t == 1:
            gather.relay()
    line.finish()
    pltpu.make_async_copy(holds[7], rows_out.at[here], local.at[7]).wait()
    gather.finish()
    for a in (3, 0, 1, 2):
        for d in range(1, seq_count):
            piece(a, d).wait_send()


def gather_start(arrays, seq_count, shards, collective):
    count = shards // 2
    wq, wk, wv, small, gains, routes, wo, tokens = arrays
    rows, model_width = wq.shape
    width = model_width // seq_count
    sheet = jax.ShapeDtypeStruct((seq_count, shards, rows, width), BF)
    shapes = [
        sheet,
        sheet,
        sheet,
        jax.ShapeDtypeStruct((seq_count, shards) + small.shape, BF),
        jax.ShapeDtypeStruct((shards,) + gains.shape, BF),
        jax.ShapeDtypeStruct((shards,) + routes.shape, jnp.int32),
        jax.ShapeDtypeStruct((shards,) + wo.shape, BF),
        jax.ShapeDtypeStruct((seq_count,) + tokens.shape, BF),
    ]
    holds = [pltpu.VMEM((rows, width), BF)] * 3 + [
        pltpu.VMEM(small.shape, BF),
        pltpu.VMEM(gains.shape, BF),
        pltpu.VMEM(routes.shape, jnp.int32),
        pltpu.VMEM(wo.shape, BF),
        pltpu.VMEM(tokens.shape, BF),
    ]
    return pl.pallas_call(
        partial(start_kernel, count, seq_count),
        out_shape=shapes,
        in_specs=[pl.BlockSpec(memory_space=ANY)] * 8,
        out_specs=[pl.BlockSpec(memory_space=ANY)] * 8,
        scratch_shapes=holds
        + [DMA((4, seq_count - 1)), DMA((4, seq_count - 1)), DMA((8,))]
        + line_sems(7, count)
        + seq_gather_sems(seq_count),
        compiler_params=pltpu.CompilerParams(collective_id=collective, has_side_effects=True),
        name="gather_start",
    )(*arrays)


def chunk_order(k, p, count):
    near = jnp.minimum(p, count - 1 - p)
    step = (k + 1) // 2
    both = jnp.where(k % 2 == 1, p - step, p + step)
    return jnp.where(k <= 2 * near, both, jnp.where(p < count - 1 - p, k, count - 1 - k))


class LineScatter:
    def __init__(self, count, places, sources, axes, bufs, sems):
        self.count, self.places = count, places
        self.sources, self.axes = sources, axes
        self.own, self.sib, self.inbox = bufs
        self.sems = sems

    def load(self, a, q):
        i = self.places[0]
        src = slot_of(self.sources[a], self.axes[a], 2 * q + lax.rem(i, 2))
        return pltpu.make_async_copy(src, self.own[a].at[q], self.sems[6].at[a, q])

    def to_sib(self, a, q):
        sib = self.places[2]
        src = slot_of(self.sources[a], self.axes[a], 2 * q + lax.rem(sib, 2))
        return remote(src, self.sib[a].at[q], self.sems[2].at[a, q], self.sems[5].at[a, q], fsdp=sib)

    def right(self, a, q):
        i = self.places[0]
        return remote(
            self.own[a].at[q], self.inbox[a].at[q], self.sems[0].at[a, q], self.sems[3].at[a, q], fsdp=i + 2
        )

    def left(self, a, q):
        i, p, sib = self.places
        slot = jnp.where(q == p - 1, self.count, q)
        return remote(
            self.own[a].at[q], self.inbox[a].at[slot], self.sems[1].at[a, q], self.sems[4].at[a, q], fsdp=i - 2
        )

    def begin_loads(self):
        for k in range(self.count):
            q = chunk_order(self.count - 1 - k, self.places[1], self.count)
            for a in range(len(self.sources)):
                self.load(a, q).start()

    def begin(self):
        for k in range(self.count):
            q = chunk_order(self.count - 1 - k, self.places[1], self.count)
            for a in range(len(self.sources)):
                self.to_sib(a, q).start()

    def add(self, a, q, others):
        own = self.own[a]
        lead = own.shape[1:-2]
        rows, width = own.shape[-2:]
        step = rows
        while step * width > 65536 and step % 16 == 0:
            step //= 2

        def strip(index):
            total = own[index].astype(F32) + self.sib[a][index].astype(F32)
            for slot in others:
                total += self.inbox[a][(slot,) + index[1:]].astype(F32)
            own[index] = total.astype(own.dtype)

        def rows_of(prefix):
            if step == rows:
                strip(prefix)
                return

            @pl.loop(0, rows // step)
            def _(k):
                strip(prefix + (pl.ds(pl.multiple_of(k * step, step), step),))

        if lead:
            for b in range(lead[0]):
                rows_of((q, b))
        else:
            rows_of((q,))

    def ready(self, a, q):
        self.load(a, q).wait()
        self.to_sib(a, q).wait_recv()

    def event(self, step):
        i, p, sib = self.places
        count = self.count
        arrays = range(len(self.sources))

        @pl.when(step >= p)
        def _():
            q = count - 1 - (step - p)
            for a in arrays:
                self.ready(a, q)

                @pl.when(p > 0)
                def _():
                    self.right(a, q).wait_recv()
                    self.add(a, q, [q])

                @pl.when(p == 0)
                def _():
                    self.add(a, q, [])

                self.right(a, q).start()

        @pl.when(step >= count - 1 - p)
        def _():
            q = step - (count - 1 - p)
            for a in arrays:
                self.ready(a, q)

                @pl.when(p < count - 1)
                def _():
                    self.left(a, q).wait_recv()
                    self.add(a, q, [q])

                @pl.when(p == count - 1)
                def _():
                    self.add(a, q, [])

                self.left(a, q).start()

    def final(self, after):
        i, p, sib = self.places
        count = self.count
        for a in range(len(self.sources)):
            self.ready(a, p)

            @pl.when(p > 0)
            def _():
                self.right(a, p).wait_recv()

            @pl.when(p < count - 1)
            def _():
                self.left(a, p).wait_recv()

            @pl.when(p == 0)
            def _():
                self.add(a, p, [count])

            @pl.when(p == count - 1)
            def _():
                self.add(a, p, [p])

            @pl.when((p > 0) & (p < count - 1))
            def _():
                self.add(a, p, [p, count])

            after(a, p)

    def run(self, after, between=None):
        @pl.loop(0, self.count - 1)
        def _(step):
            self.event(step)
            if between is not None:
                between(step)

        self.final(after)

    def finish(self):
        i, p, sib = self.places
        for a in range(len(self.sources)):
            for q in range(self.count):
                self.to_sib(a, q).wait_send()

                @pl.when(q > p)
                def _():
                    self.right(a, q).wait_send()

                @pl.when(q < p)
                def _():
                    self.left(a, q).wait_send()


def end_kernel(count, seq_count, *refs):
    sources = refs[:6]
    factors = refs[6:12]
    outs = refs[12:18]
    sum_ref = refs[18]
    bufs = tuple(refs[19 + 6 * k : 25 + 6 * k] for k in range(3))
    landing = refs[37]
    sems = refs[38:45]
    send_x, recv_x, local = refs[45:48]
    held = refs[48:54]
    rows_ref, factor_sem = refs[54:56]
    seq = SeqScatter(seq_count, rows_ref, *refs[56:61])
    places = where_am_i()
    here = lax.axis_index("seq")
    width = sources[0].shape[3]
    line = LineScatter(count, places, sources, [1, 1, 1, 0, 1, 0], bufs, sems)
    line.begin_loads()
    for n in range(6):
        pltpu.make_async_copy(factors[n], held[n], factor_sem.at[n]).start()
    greet(count, places, seq_count)
    line.begin()
    own = bufs[0]

    def at_home(a, block):
        if a == 4:
            return landing.at[block]
        start = pl.multiple_of(block * width, width)
        return outs[a].at[:, pl.ds(start, width)]

    def piece(a, q, d):
        peer = lax.rem(here + d, seq_count)
        slot = 3 if a == 4 else a
        return remote(
            own[a].at[q, peer], at_home(a, here), send_x.at[slot, d - 1], recv_x.at[slot, d - 1], seq=peer
        )

    def arrived(a, d):
        origin = lax.rem(here + seq_count - d, seq_count)
        slot = 3 if a == 4 else a
        return remote(
            at_home(a, origin), at_home(a, origin), send_x.at[slot, d - 1], recv_x.at[slot, d - 1], seq=origin
        )

    def after(a, q):
        if a in (3, 5):
            pltpu.make_async_copy(own[a].at[q], outs[a], local.at[a]).start()
        else:
            for d in range(1, seq_count):
                piece(a, q, d).start()
            pltpu.make_async_copy(own[a].at[q, here], at_home(a, here), local.at[a]).start()

    def back_rows():
        for n in range(6):
            pltpu.make_async_copy(factors[n], held[n], factor_sem.at[n]).wait()
        tokens, model_width = rows_ref.shape[1:]
        tile = 512
        tiles = model_width // tile

        @pl.loop(0, seq_count * tiles)
        def _(u):
            block = u // tiles
            strip = pl.ds(pl.multiple_of(block * tokens, tokens), tokens)
            cols = pl.ds(pl.multiple_of(lax.rem(u, tiles) * tile, tile), tile)
            total = jnp.zeros((tokens, tile), F32)
            for n in range(3):
                total += lax.dot_general(
                    held[n][strip, :], held[3 + n][cols, :], (((1,), (1,)), ((), ())), preferred_element_type=F32
                )
            rows_ref[block, :, cols] = total.astype(BF)

        seq.begin_loads()
        seq.begin()

    def between(step):
        pl.when(step == 0)(back_rows)

        @pl.when(step == 1)
        def _():
            seq.relay()

    line.run(after, between)
    seq.total(sum_ref)
    for q in range(count):

        @pl.when(q == places[1])
        def _():
            for a in range(6):
                if a in (3, 5):
                    pltpu.make_async_copy(own[a].at[q], outs[a], local.at[a]).wait()
                else:
                    pltpu.make_async_copy(own[a].at[q, here], at_home(a, here), local.at[a]).wait()
                    for d in range(1, seq_count):
                        piece(a, q, d).wait_send()
                        arrived(a, d).wait_recv()

    total = landing[0]
    for block in range(1, seq_count):
        total += landing[block]
    landing[0] = total
    last = pltpu.make_async_copy(landing.at[0], outs[4], local.at[4])
    last.start()
    last.wait()
    line.finish()
    seq.finish()


def scatter_end(arrays, factors, seq_count, shards, collective):
    count = shards // 2
    gq, gk, gv, go, small, gains = arrays
    rows, width = gq.shape[2:]
    tokens, model_width = factors[0].shape[0] // seq_count, factors[3].shape[0]
    home = jax.ShapeDtypeStruct((rows, width * seq_count), BF)
    shapes = [
        home,
        home,
        home,
        jax.ShapeDtypeStruct(go.shape[1:], BF),
        jax.ShapeDtypeStruct(small.shape[2:], F32),
        jax.ShapeDtypeStruct(gains.shape[1:], F32),
        jax.ShapeDtypeStruct((tokens, model_width), F32),
    ]
    blocks, inboxes = [], []
    for a in range(6):
        shape = arrays[a].shape
        block = (shape[0],) + shape[2:] if a in (0, 1, 2, 4) else shape[1:]
        blocks.append(pltpu.VMEM((count,) + block, arrays[a].dtype))
        inboxes.append(pltpu.VMEM((count + 1,) + block, arrays[a].dtype))
    return pl.pallas_call(
        partial(end_kernel, count, seq_count),
        out_shape=shapes,
        in_specs=[pl.BlockSpec(memory_space=ANY)] * 12,
        out_specs=[pl.BlockSpec(memory_space=ANY)] * 6 + [pl.BlockSpec(memory_space=pltpu.VMEM)],
        scratch_shapes=blocks * 2
        + inboxes
        + [pltpu.VMEM((seq_count,) + small.shape[2:], F32)]
        + [DMA((6, count))] * 7
        + [DMA((4, seq_count - 1)), DMA((4, seq_count - 1)), DMA((6,))]
        + [pltpu.VMEM(x.shape, BF) for x in factors]
        + [pltpu.VMEM((seq_count, tokens, model_width), BF), DMA((6,))]
        + seq_scatter_scratch((tokens, model_width), BF, seq_count),
        compiler_params=pltpu.CompilerParams(
            collective_id=collective, has_side_effects=True, vmem_limit_bytes=62 << 20
        ),
        name="scatter_end",
    )(*arrays, *factors)


def greet_seq(seq_count):
    here = lax.axis_index("seq")
    barrier = pltpu.get_barrier_semaphore()
    for d in range(1, seq_count):
        peer = lax.rem(here + d, seq_count)
        pl.semaphore_signal(barrier, inc=1, device_id={"seq": peer}, device_id_type=MESH)
    pl.semaphore_wait(barrier, seq_count - 1)
    return here


class SeqScatter:
    def __init__(self, seq_count, x_ref, own, inbox, send, recv, local):
        here = lax.axis_index("seq")
        self.own, self.inbox, self.local, self.count = own, inbox, local, seq_count
        self.take = pltpu.make_async_copy(x_ref.at[here], own, local.at[0])
        rows = own.shape[0]
        self.half = rows // 2
        low, high = pl.ds(0, self.half), pl.ds(self.half, self.half)
        if seq_count != 4:
            self.copies = []
            for d in range(1, seq_count):
                peer = lax.rem(here + d, seq_count)
                self.copies.append(
                    remote(x_ref.at[peer], inbox.at[d - 1], send.at[d - 1], recv.at[d - 1], seq=peer)
                )
            return
        beside = here + 1 - 2 * lax.rem(here, 2)
        across = lax.rem(here + 2, 4)
        corner = 3 - here
        self.loads = [
            pltpu.make_async_copy(x_ref.at[across, low], inbox.at[3, low], local.at[1]),
            pltpu.make_async_copy(x_ref.at[beside, high], inbox.at[3, high], local.at[2]),
        ]
        plans = (
            (x_ref.at[corner, low], inbox.at[2, low], beside),
            (x_ref.at[corner, high], inbox.at[2, high], across),
            (x_ref.at[beside, low], inbox.at[0, low], beside),
            (x_ref.at[across, high], inbox.at[1, high], across),
            (inbox.at[3, low], inbox.at[1, low], across),
            (inbox.at[3, high], inbox.at[0, high], beside),
        )
        self.copies = [
            remote(src, dst, send.at[n], recv.at[n], seq=peer) for n, (src, dst, peer) in enumerate(plans)
        ]

    def begin_loads(self):
        self.take.start()
        if self.count == 4:
            for load in self.loads:
                load.start()

    def begin(self):
        for copy in self.copies[:4] if self.count == 4 else self.copies:
            copy.start()

    def strips(self, start, rows, body):
        step = min(32, rows)

        @pl.loop(0, rows // step)
        def _(k):
            body(pl.ds(pl.multiple_of(start + k * step, step), step))

    def relay(self):
        if self.count != 4:
            return
        inbox = self.inbox

        def add(strip):
            inbox[3, strip, :] = (
                inbox[3, strip, :].astype(F32) + inbox[2, strip, :].astype(F32)
            ).astype(inbox.dtype)

        for n, start in ((0, 0), (1, self.half)):
            self.loads[n].wait()
            self.copies[n].wait_recv()
            self.strips(start, self.half, add)
            self.copies[4 + n].start()

    def total(self, o_ref):
        self.take.wait()
        for copy in self.copies[2:] if self.count == 4 else self.copies:
            copy.wait_recv()
        parts = 2 if self.count == 4 else self.count - 1

        def add(strip):
            total = self.own[strip, :].astype(F32)
            for d in range(parts):
                total += self.inbox[d, strip, :].astype(F32)
            o_ref[strip, :] = total

        self.strips(0, self.own.shape[0], add)

    def finish(self):
        for copy in self.copies:
            copy.wait_send()


def seq_scatter_scratch(block, dtype, seq_count):
    boxes = 4 if seq_count == 4 else seq_count - 1
    copies = 6 if seq_count == 4 else seq_count - 1
    return [
        pltpu.VMEM(block, dtype),
        pltpu.VMEM((boxes,) + block, dtype),
        DMA((copies,)),
        DMA((copies,)),
        DMA((3,)),
    ]


class SeqGather:
    def __init__(self, seq_count, x_ref, o_ref, send, recv):
        here = lax.axis_index("seq")
        self.count = seq_count
        rows = x_ref.shape[0]
        low, high = pl.ds(0, rows // 2), pl.ds(rows // 2, rows // 2)
        if seq_count != 4:
            peers = [lax.rem(here + d, seq_count) for d in range(1, seq_count)]
            origins = [lax.rem(here + seq_count - d, seq_count) for d in range(1, seq_count)]
            out = [(x_ref, o_ref.at[here], peer) for peer in peers]
            landed = [o_ref.at[origin] for origin in origins]
        else:
            beside = here + 1 - 2 * lax.rem(here, 2)
            across = lax.rem(here + 2, 4)
            corner = 3 - here
            out = [
                (x_ref, o_ref.at[here], beside),
                (x_ref, o_ref.at[here], across),
                (o_ref.at[across, low], o_ref.at[across, low], beside),
                (o_ref.at[beside, high], o_ref.at[beside, high], across),
            ]
            landed = [o_ref.at[beside], o_ref.at[across], o_ref.at[corner, low], o_ref.at[corner, high]]
        self.sends = [
            remote(src, dst, send.at[n], recv.at[n], seq=peer) for n, (src, dst, peer) in enumerate(out)
        ]
        self.lands = [
            remote(ref, ref, send.at[n], recv.at[n], seq=out[n][2]) for n, ref in enumerate(landed)
        ]

    def begin(self):
        for copy in self.sends[:2] if self.count == 4 else self.sends:
            copy.start()

    def relay(self):
        if self.count == 4:
            for n in (0, 1):
                self.lands[n].wait_recv()
            for n in (2, 3):
                self.sends[n].start()

    def finish(self):
        for n, copy in enumerate(self.lands):
            if self.count != 4 or n > 1:
                copy.wait_recv()
        for copy in self.sends:
            copy.wait_send()


def seq_gather_sems(seq_count):
    copies = 4 if seq_count == 4 else seq_count - 1
    return [DMA((copies,)), DMA((copies,))]


def slot_targets(first, local_experts, cap, routes, targets, targets_t):
    shards, top_k, tokens = routes.shape
    earlier = lax.broadcasted_iota(jnp.int32, (tokens, tokens), 0)
    later = lax.broadcasted_iota(jnp.int32, (tokens, tokens), 1)
    upto = jnp.where(earlier <= later, 1.0, 0.0).astype(BF)
    row = lax.broadcasted_iota(jnp.int32, (8, tokens), 0)
    for j in range(shards):
        named = routes[j]
        chosen = jnp.zeros((8, tokens), F32)
        for e in range(local_experts):
            hit = jnp.max(jnp.where(named == first + e, 1.0, 0.0), axis=0, keepdims=True)
            chosen = jnp.where(row == e, hit, chosen)
        place = jnp.dot(chosen.astype(BF), upto, preferred_element_type=F32) - 1.0
        slot = jnp.where(chosen > 0.5, place + (cap * row).astype(F32), -1.0)
        targets[j] = slot[0:local_experts].astype(jnp.int32)
        targets_t[j] = slot.T[:, 0:local_experts].astype(jnp.int32)


def middle_kernel(
    count,
    seq_count,
    cap,
    x_ref,
    dy_ref,
    routes,
    o_ref,
    all_ref,
    targets,
    targets_t,
    own,
    inbox,
    xs,
    xr,
    xl,
    hold,
    s0,
    s1,
    s2,
    recv,
    local,
):
    places = where_am_i()
    i = places[0]
    seq = SeqScatter(seq_count, x_ref, own, inbox, xs, xr, xl)
    seq.begin_loads()
    take = pltpu.make_async_copy(dy_ref, hold, local.at[0])
    take.start()
    greet(count, places, seq_count)
    seq.begin()
    take.wait()
    put = pltpu.make_async_copy(hold, all_ref.at[i], local.at[1])
    put.start()
    put.wait()
    line = LineGather(count, places, [all_ref], [0], s0, s1, s2, recv)
    line.first(0)
    local_experts = targets.shape[1]
    slot_targets(i * local_experts, local_experts, cap, routes, targets, targets_t)
    for t in range(1, count):
        line.forward(t)
        if t == 1:
            seq.relay()
    seq.total(o_ref)
    line.finish()
    seq.finish()


def middle(blocks, dy, routes, local_experts, collective):
    shards, _, tokens = routes.shape
    count = shards // 2
    seq_count = blocks.shape[0]
    block = blocks.shape[1:]
    anywhere = pl.BlockSpec(memory_space=ANY)
    vmem = pl.BlockSpec(memory_space=pltpu.VMEM)
    return pl.pallas_call(
        partial(middle_kernel, count, seq_count, CAP),
        out_shape=[
            jax.ShapeDtypeStruct(block, F32),
            jax.ShapeDtypeStruct((shards,) + dy.shape, dy.dtype),
            jax.ShapeDtypeStruct((shards, local_experts, tokens), jnp.int32),
            jax.ShapeDtypeStruct((shards, tokens, local_experts), jnp.int32),
        ],
        in_specs=[anywhere, anywhere, vmem],
        out_specs=[vmem, anywhere, vmem, vmem],
        scratch_shapes=seq_scatter_scratch(block, blocks.dtype, seq_count)
        + [pltpu.VMEM(dy.shape, dy.dtype)]
        + line_sems(1, count)
        + [DMA((2,))],
        compiler_params=pltpu.CompilerParams(
            collective_id=collective, has_side_effects=True, vmem_limit_bytes=32 << 20
        ),
        name="middle",
    )(blocks, dy, routes)


class RouterGrad:
    def __init__(self, tokens_in, logits_in, gain_row, out, tokens, logits, total, sems):
        self.tokens_in, self.logits_in, self.out = tokens_in, logits_in, out
        self.tokens, self.logits, self.sems = tokens, logits, sems
        self.gain_row, self.total = gain_row, total

    def take(self):
        return pltpu.make_async_copy(self.logits_in, self.logits, self.sems.at[2])

    def pair(self, q):
        buf = lax.rem(q, 2)
        src = self.tokens_in.at[pl.ds(2 * q, 2)]
        return pltpu.make_async_copy(src, self.tokens.at[buf], self.sems.at[buf])

    def begin(self):
        self.take().start()
        self.pair(0).start()

    def run(self):
        self.take().wait()
        self.total[...] = jnp.zeros_like(self.total)
        experts, width = self.total.shape
        block = 512
        pairs = self.tokens_in.shape[0] // 2

        @pl.loop(0, pairs)
        def _(q):
            self.pair(q).wait()

            @pl.when(q + 1 < pairs)
            def _():
                self.pair(q + 1).start()

            buf = lax.rem(q, 2)

            @pl.loop(0, width // block)
            def _(n):
                cols = pl.ds(pl.multiple_of(n * block, block), block)
                total = self.total[:, cols]
                for j in range(2):
                    total += jnp.dot(
                        self.logits[2 * q + j], self.tokens[buf, j, :, cols], preferred_element_type=F32
                    )
                self.total[:, cols] = total

        lanes = self.out.shape[1]

        @pl.loop(0, width // block)
        def _(n):
            cols = pl.ds(pl.multiple_of(n * block, block), block)
            gain = jnp.broadcast_to(self.gain_row[:, cols], (8, block))
            rest = jnp.zeros((lanes - experts - 8, block), F32)
            self.out[cols, :] = jnp.concatenate([self.total[:, cols], gain, rest], axis=0).T


def turn_kernel(
    count,
    seq_count,
    x_ref,
    parts_ref,
    left_ref,
    right0,
    right1,
    h2_ref,
    logits_ref,
    gain_row,
    o_ref,
    sum_ref,
    grad_ref,
    router_ref,
    hold,
    send,
    recv,
    one,
    tiles_in,
    held,
    staged,
    outer_sem,
    tokens,
    logits,
    router_sum,
    router_sem,
    own,
    sib,
    inbox,
    *sems,
):
    places = where_am_i()
    here = lax.axis_index("seq")
    line = LineScatter(count, places, [parts_ref], [0], ([own], [sib], [inbox]), sems)
    grads = OuterGrads(left_ref, (right0, right1), grad_ref, (tiles_in, held, staged, outer_sem), count - 1)
    router = RouterGrad(h2_ref, logits_ref, gain_row, router_ref, tokens, logits, router_sum, router_sem)
    line.begin_loads()
    take = pltpu.make_async_copy(x_ref, hold, one)
    take.start()
    grads.begin()
    router.begin()
    greet(count, places, seq_count)
    rows = SeqGather(seq_count, x_ref, o_ref, send, recv)
    rows.begin()
    line.begin()
    take.wait()
    put = pltpu.make_async_copy(hold, o_ref.at[here], one)
    put.start()

    def after(a, q):
        out = pltpu.make_async_copy(own.at[q], sum_ref, sems[6].at[0, q])
        out.start()
        out.wait()

    def between(step):
        @pl.when(step == 1)
        def _():
            rows.relay()

        grads.between(step)
        pl.when(step == 0)(router.run)

    line.run(after, between)
    grads.finish()
    put.wait()
    rows.finish()
    line.finish()


def turn_back(block, parts, expert_in, d_gate, d_up, h2_all, logits, gain_row, seq_count, shards, collective):
    count = shards // 2
    part = parts.shape[1:]
    model_width = block.shape[1]
    anywhere = pl.BlockSpec(memory_space=ANY)
    return pl.pallas_call(
        partial(turn_kernel, count, seq_count),
        out_shape=[
            jax.ShapeDtypeStruct((seq_count,) + block.shape, block.dtype),
            jax.ShapeDtypeStruct(part, parts.dtype),
            jax.ShapeDtypeStruct((d_gate.shape[0], model_width, 2 * d_gate.shape[2]), BF),
            jax.ShapeDtypeStruct((model_width, 128), F32),
        ],
        in_specs=[anywhere] * 7 + [pl.BlockSpec(memory_space=pltpu.VMEM)],
        out_specs=[anywhere] * 3 + [pl.BlockSpec(memory_space=pltpu.VMEM)],
        scratch_shapes=[pltpu.VMEM(block.shape, block.dtype)]
        + seq_gather_sems(seq_count)
        + [DMA]
        + outer_scratch(d_up, 512, 2)
        + [
            pltpu.VMEM((2, 2) + h2_all.shape[1:], BF),
            pltpu.VMEM(logits.shape, BF),
            pltpu.VMEM((logits.shape[1], model_width), F32),
            DMA((3,)),
        ]
        + [pltpu.VMEM((count,) + part, BF)] * 2
        + [pltpu.VMEM((count + 1,) + part, BF)]
        + [DMA((1, count))] * 7,
        compiler_params=pltpu.CompilerParams(
            collective_id=collective, has_side_effects=True, vmem_limit_bytes=60 << 20
        ),
        cost_estimate=pl.CostEstimate(flops=60_000_000_000, bytes_accessed=200_000_000, transcendentals=0),
        name="turn_back",
    )(block, parts, expert_in, d_gate, d_up, h2_all, logits, gain_row)


def half_sign(shape):
    lane = lax.broadcasted_iota(jnp.int32, shape, 1)
    return jnp.where(lane < shape[1] // 2, -1.0, 1.0)


def turn(value):
    return pltpu.roll(value, value.shape[1] // 2, 1)


def block_probs(q_rows, keys, doc_col, doc_row, start, scale_by):
    end = keys.shape[0]
    scores = (
        lax.dot_general(q_rows, keys, (((1,), (1,)), ((), ())), preferred_element_type=F32) * scale_by
    )
    shape = scores.shape
    query_pos = start + lax.broadcasted_iota(jnp.int32, shape, 0)
    key_pos = lax.broadcasted_iota(jnp.int32, shape, 1)
    allowed = (doc_col == doc_row) & (key_pos <= query_pos)
    scores = jnp.where(allowed, scores, MASKED_OUT)
    weights = jnp.exp(scores - jnp.max(scores, axis=-1, keepdims=True))
    return weights * (1.0 / jnp.sum(weights, axis=-1, keepdims=True))


class SeqSum:
    def __init__(self, seq_count, sheet, inbox, send, recv):
        here = lax.axis_index("seq")
        self.sheet, self.inbox = sheet, inbox
        self.copies = []
        for d in range(1, seq_count):
            peer = lax.rem(here + d, seq_count)
            self.copies.append(remote(sheet, inbox.at[d - 1], send.at[d - 1], recv.at[d - 1], seq=peer))

    def begin(self):
        for copy in self.copies:
            copy.start()

    def total(self):
        for copy in self.copies:
            copy.wait_recv()
        total = self.sheet[...]
        for d in range(len(self.copies)):
            total += self.inbox[d]
        for copy in self.copies:
            copy.wait_send()
        return total


def attend_kernel(
    seq_count,
    row_block,
    model_width,
    q_raw,
    k_raw,
    v_ref,
    squares,
    gq,
    gk,
    cos,
    sin,
    doc_col,
    doc_row,
    o_ref,
    q_out,
    k_out,
    scales,
    inbox,
    send,
    recv,
):
    seq_len = q_raw.shape[0]

    @pl.when(pl.program_id(0) == 0)
    def _():
        greet_seq(seq_count)
        sums = SeqSum(seq_count, squares, inbox, send, recv)
        sums.begin()
        scales[...] = lax.rsqrt(sums.total() / model_width + EPSILON).T

    sign = half_sign(cos.shape)

    def rotated(raw, lane, gain):
        value = raw[...] * scales[:, lane : lane + 1] * gain[...]
        return (value * cos[...] + turn(value) * (sin[...] * sign)).astype(BF)

    q_out[...] = rotated(q_raw, 0, gq)
    k_out[...] = rotated(k_raw, 1, gk)
    scale_by = HEAD ** (-0.5)
    for start in range(0, seq_len, row_block):
        end = start + row_block
        probs = block_probs(
            q_out[start:end, :], k_out[:end, :], doc_col[start:end, :], doc_row[:, :end], start, scale_by
        )
        o_ref[start:end, :] = jnp.dot(
            probs.astype(BF), v_ref[:end, :], preferred_element_type=F32
        ).astype(BF)


def attend(q_raw, k_raw, values, squares, gq, gk, cos, sin, doc_col, doc_row, model_width, seq_count, collective):
    seq_len, width = q_raw.shape
    head = pl.BlockSpec((seq_len, HEAD), lambda h: (0, h))
    gain = pl.BlockSpec((1, HEAD), lambda h: (0, h))

    def whole(shape):
        return pl.BlockSpec(shape, lambda h: (0, 0))

    out = jax.ShapeDtypeStruct((seq_len, width), BF)
    return pl.pallas_call(
        partial(attend_kernel, seq_count, 256, model_width),
        grid=(width // HEAD,),
        out_shape=[
            out,
            out,
            out,
            jax.ShapeDtypeStruct((seq_len, 8), F32),
        ],
        in_specs=[head, head, head, whole(squares.shape), gain, gain, whole(cos.shape), whole(sin.shape)]
        + [whole(doc_col.shape), whole(doc_row.shape)],
        out_specs=[head, head, head, whole((seq_len, 8))],
        scratch_shapes=[
            pltpu.VMEM((seq_count - 1,) + squares.shape, F32),
            DMA((seq_count - 1,)),
            DMA((seq_count - 1,)),
        ],
        compiler_params=pltpu.CompilerParams(
            collective_id=collective, has_side_effects=True, vmem_limit_bytes=48 << 20
        ),
        name="attend",
    )(q_raw, k_raw, values, squares, gq, gk, cos, sin, doc_col, doc_row)


def attend_back_kernel(
    count,
    seq_count,
    heads,
    row_block,
    model_width,
    q_low,
    k_low,
    v_ref,
    do_ref,
    q_raw,
    k_raw,
    scales,
    gq,
    gk,
    cos,
    sin,
    doc_col,
    doc_row,
    parts_ref,
    dq_ref,
    dk_ref,
    dv_ref,
    gain_ref,
    sum_ref,
    dq_acc,
    dk_acc,
    dv_acc,
    uq,
    uk,
    dots,
    sheet,
    inbox,
    send,
    recv,
    own,
    sib,
    landed,
    *sems,
):
    seq_len = q_low.shape[0]
    head = pl.program_id(0)
    scale_by = HEAD ** (-0.5)
    places = where_am_i()
    line = LineScatter(count, places, [parts_ref], [0], ([own], [sib], [landed]), sems)

    @pl.when(head == 0)
    def _():
        line.begin_loads()
        greet(count, places, seq_count)
        line.begin()
        dots[...] = jnp.zeros_like(dots)

    dk_acc[...] = jnp.zeros_like(dk_acc)
    dv_acc[...] = jnp.zeros_like(dv_acc)
    for start in range(0, seq_len, row_block):
        end = start + row_block
        rows = slice(start, end)
        probs = block_probs(
            q_low[rows, :], k_low[:end, :], doc_col[rows, :], doc_row[:, :end], start, scale_by
        )
        grad_rows = do_ref[rows, :]
        grad_probs = lax.dot_general(
            grad_rows, v_ref[:end, :], (((1,), (1,)), ((), ())), preferred_element_type=F32
        )
        centre = jnp.sum(probs * grad_probs, axis=-1, keepdims=True)
        grad_scores = (probs * (grad_probs - centre)).astype(BF)
        dq_acc[rows, :] = jnp.dot(grad_scores, k_low[:end, :], preferred_element_type=F32)
        over_rows = (((0,), (0,)), ((), ()))
        dk_acc[:end, :] += lax.dot_general(
            grad_scores, q_low[rows, :], over_rows, preferred_element_type=F32
        )
        dv_acc[:end, :] += lax.dot_general(
            probs.astype(BF), grad_rows, over_rows, preferred_element_type=F32
        )
        if start == row_block:

            @pl.when(head == 0)
            def _():
                line.event(0)

    dv_ref[...] = dv_acc[...].astype(BF)
    sign = half_sign(cos.shape)
    cols = pl.ds(pl.multiple_of(head * HEAD, HEAD), HEAD)
    blocks, _, lanes = gain_ref.shape
    rows = HEAD // blocks

    def unrotated(acc, raw, gain, u_ref, lane):
        low = (acc[...] * scale_by).astype(BF).astype(F32)
        back = low * cos[...] - turn(low * sin[...]) * sign
        value = raw[:, cols]
        grad_gain = jnp.sum(back * value * scales[:, lane : lane + 1], axis=0, keepdims=True)
        u = back * gain[...]
        u_ref[:, cols] = u
        dots[:, lane : lane + 1] += jnp.sum(u * value, axis=1, keepdims=True)
        return grad_gain

    grads = (unrotated(dq_acc, q_raw, gq, uq, 0), unrotated(dk_acc, k_raw, gk, uk, 1))
    which = lax.broadcasted_iota(jnp.int32, (8, lanes), 0)
    both = jnp.where(which == 0, grads[0], jnp.where(which == 1, grads[1], 0.0))
    for block in range(blocks):
        gain_ref[block] = both if block == 0 else pltpu.roll(both, lanes - block * rows, 1)

    for step in range(1, count - 1):

        @pl.when(head == min(step, heads - 1))
        def _():
            line.event(step)

    @pl.when(head == heads - 1)
    def _():
        sheet[...] = dots[...].T
        sums = SeqSum(seq_count, sheet, inbox, send, recv)
        sums.begin()
        dots[...] = sums.total().T / model_width
        strip = 128

        @pl.loop(0, seq_len // strip)
        def _(n):
            part = pl.ds(pl.multiple_of(n * strip, strip), strip)
            for lane, u_ref, raw, out in ((0, uq, q_raw, dq_ref), (1, uk, k_raw, dk_ref)):
                scale = scales[part, lane : lane + 1]
                product = dots[part, lane : lane + 1]
                out[part, :] = (
                    scale * u_ref[part, :] - raw[part, :] * (scale * scale * scale * product)
                ).astype(BF)

        def after(a, q):
            out = pltpu.make_async_copy(own.at[q], sum_ref, sems[6].at[0, q])
            out.start()
            out.wait()

        line.final(after)
        line.finish()


def attend_back(
    q_low,
    k_low,
    values,
    d_heads,
    q_raw,
    k_raw,
    scales,
    gq,
    gk,
    cos,
    sin,
    doc_col,
    doc_row,
    parts,
    rows,
    model_width,
    seq_count,
    collective,
):
    seq_len, width = q_raw.shape
    heads = width // HEAD
    blocks = HEAD // rows
    shards = parts.shape[0]
    count = shards // 2
    part = parts.shape[1:]
    head = pl.BlockSpec((seq_len, HEAD), lambda h: (0, h))
    gain = pl.BlockSpec((1, HEAD), lambda h: (0, h))

    def whole(shape):
        return pl.BlockSpec(shape, lambda h: (0, 0))

    def once(x):
        return pl.BlockSpec(x.shape, lambda h: (0, 0), pipeline_mode=pl.Buffered(1))

    out = jax.ShapeDtypeStruct((seq_len, width), BF)
    return pl.pallas_call(
        partial(attend_back_kernel, count, seq_count, heads, 256, model_width),
        grid=(heads,),
        out_shape=[
            out,
            out,
            out,
            jax.ShapeDtypeStruct((width // rows, 8, HEAD), F32),
            jax.ShapeDtypeStruct(part, BF),
        ],
        in_specs=[head] * 4
        + [once(q_raw), once(k_raw), once(scales), gain, gain, once(cos), once(sin)]
        + [once(doc_col), once(doc_row), pl.BlockSpec(memory_space=ANY)],
        out_specs=[
            whole((seq_len, width)),
            whole((seq_len, width)),
            head,
            pl.BlockSpec((blocks, 8, HEAD), lambda h: (h, 0, 0)),
            pl.BlockSpec(memory_space=ANY),
        ],
        scratch_shapes=[pltpu.VMEM((seq_len, HEAD), F32)] * 3
        + [pltpu.VMEM((seq_len, width), F32)] * 2
        + [
            pltpu.VMEM((seq_len, 8), F32),
            pltpu.VMEM((8, seq_len), F32),
            pltpu.VMEM((seq_count - 1, 8, seq_len), F32),
            DMA((seq_count - 1,)),
            DMA((seq_count - 1,)),
        ]
        + [pltpu.VMEM((count,) + part, BF)] * 2
        + [pltpu.VMEM((count + 1,) + part, BF)]
        + [DMA((1, count))] * 7,
        compiler_params=pltpu.CompilerParams(
            collective_id=collective, has_side_effects=True, vmem_limit_bytes=60 << 20
        ),
        name="attend_back",
    )(q_low, k_low, values, d_heads, q_raw, k_raw, scales, gq, gk, cos, sin, doc_col, doc_row, parts)


def experts_in_kernel(
    count,
    cap,
    h2_ref,
    dy_ref,
    targets,
    router_t,
    wgu_ref,
    h2_out,
    x_out,
    y_out,
    act_out,
    by_up_out,
    by_gate_out,
    gate_slots,
    probs_out,
    h2,
    wgu,
    dy,
    xs,
    ys,
    acts,
    by_up,
    by_gate,
    s0,
    s1,
    s2,
    recv,
    w_sem,
    dy_sem,
    h_sem,
    out_sem,
):
    places = where_am_i()
    i, p, sib = places
    local_experts, model_width, hidden = wgu_ref.shape
    hidden = hidden // 2
    tokens = h2_ref.shape[0]
    experts = router_t.shape[0]
    own_in = pltpu.make_async_copy(h2_ref, h2.at[i], h_sem.at[0])
    own_in.start()

    def fetch(q, buf):
        src = dy_ref.at[pl.ds(2 * q, 2)]
        return pltpu.make_async_copy(src, dy.at[buf], dy_sem.at[buf])

    fetch(p, 0).start()
    for e in range(local_experts):
        pltpu.make_async_copy(wgu_ref.at[e], wgu.at[e], w_sem.at[e]).start()
    greet(count, places)
    own_in.wait()
    line = LineGather(count, places, [h2], [0], s0, s1, s2, recv)
    line.first(0)
    staged = ((xs, x_out), (ys, y_out), (acts, act_out), (by_up, by_up_out), (by_gate, by_gate_out))

    def store(n, e, q):
        rows = pl.ds(pl.multiple_of(q * 2 * cap, 2 * cap), 2 * cap)
        return pltpu.make_async_copy(staged[n][0].at[e], staged[n][1].at[e, rows], out_sem.at[n, e])

    def keep(q):
        src = h2.at[pl.ds(2 * q, 2)]
        return pltpu.make_async_copy(src, h2_out.at[pl.ds(2 * q, 2)], h_sem.at[1])

    slot_rows = lax.broadcasted_iota(jnp.int32, (local_experts * cap, tokens), 0)
    expert_rows = lax.broadcasted_iota(jnp.int32, (experts, tokens), 0)

    @pl.loop(0, count)
    def _(k):
        q = chunk_order(k, p, count)
        buf = k % 2

        @pl.when(k > 0)
        def _():
            line.forward(k)

        line.copy(0, 2 * q + lax.rem(sib, 2), 2, 0, sib).wait_recv()
        fetch(q, buf).wait()

        @pl.when(k + 1 < count)
        def _():
            fetch(chunk_order(k + 1, p, count), 1 - buf).start()

        @pl.when(k > 0)
        def _():
            for n in range(5):
                for e in range(local_experts):
                    store(n, e, q).wait()
            keep(q).wait()

        keep(q).start()
        picks = []
        for j in range(2):
            slot = 2 * q + j
            tokens_j = h2[slot]
            logits = lax.dot_general(
                router_t[...], tokens_j, (((1,), (1,)), ((), ())), preferred_element_type=F32
            )
            shifted = jnp.exp(logits - jnp.max(logits, axis=0, keepdims=True))
            probs = shifted / jnp.sum(shifted, axis=0, keepdims=True)
            probs_out[slot] = probs
            pick = None
            for e in range(local_experts):
                mask = slot_rows == targets[slot, e : e + 1, :]
                gate = jnp.sum(
                    jnp.where(expert_rows == i * local_experts + e, probs, 0.0), axis=0, keepdims=True
                )
                part = slice(e * cap, (e + 1) * cap)
                gate_slots[e, q, j * cap : (j + 1) * cap, :] = jnp.sum(
                    jnp.where(mask[part], gate, 0.0), axis=1, keepdims=True
                )
                pick = mask if pick is None else pick | mask
            picks.append(jnp.where(pick, 1.0, 0.0).astype(BF))

        block = 512

        @pl.loop(0, model_width // block)
        def _(n):
            cols = pl.ds(pl.multiple_of(n * block, block), block)
            for source, target in ((0, xs), (1, ys)):
                got = []
                for j in range(2):
                    rows = h2[2 * q + j, :, cols] if source == 0 else dy[buf, j, :, cols]
                    got.append(jnp.dot(picks[j], rows, preferred_element_type=F32))
                for e in range(local_experts):
                    part = slice(e * cap, (e + 1) * cap)
                    target[e, :, cols] = jnp.concatenate([got[0][part], got[1][part]], axis=0).astype(BF)

        for e in range(local_experts):
            store(0, e, q).start()
            store(1, e, q).start()

            @pl.when(k == 0)
            def _():
                pltpu.make_async_copy(wgu_ref.at[e], wgu.at[e], w_sem.at[e]).wait()

            wide = 256

            @pl.loop(0, hidden // wide)
            def _(n):
                cols = pl.ds(pl.multiple_of(n * wide, wide), wide)
                beyond = pl.ds(pl.multiple_of(hidden + n * wide, wide), wide)
                gate = jnp.dot(xs[e], wgu[e, :, cols], preferred_element_type=F32)
                up = jnp.dot(xs[e], wgu[e, :, beyond], preferred_element_type=F32)
                sigmoid = 1.0 / (1.0 + jnp.exp(-gate))
                silu = gate * sigmoid
                acts[e, :, cols] = (silu * up).astype(BF)
                by_up[e, :, cols] = silu.astype(BF)
                by_gate[e, :, cols] = (up * sigmoid * (1.0 + gate * (1.0 - sigmoid))).astype(BF)

            for n in (2, 3, 4):
                store(n, e, q).start()

    for n in range(5):
        for e in range(local_experts):
            store(n, e, 0).wait()
    keep(0).wait()
    sends_done(line)


def sends_done(line):
    i, p, sib = line.places
    count = line.count
    line.copy(0, i, 2, 0, sib).wait_send()

    @pl.when(p < count - 1)
    def _():
        line.copy(0, i, 0, 0, i + 2).wait_send()

    @pl.when(p > 0)
    def _():
        line.copy(0, i, 1, 0, i - 2).wait_send()

    for t in range(1, count):

        @pl.when(p - t >= 0)
        def _():
            slot = i - 2 * t

            @pl.when(p < count - 1)
            def _():
                line.copy(0, slot, 0, t, i + 2).wait_send()

            line.copy(0, slot, 2, t, sib).wait_send()

        @pl.when(p + t < count)
        def _():
            slot = i + 2 * t

            @pl.when(p > 0)
            def _():
                line.copy(0, slot, 1, t, i - 2).wait_send()

            line.copy(0, slot, 2, count + t, sib).wait_send()


def experts_in(h2, dy_all, targets, router_t, w_gate_up, collective):
    shards, tokens, model_width = dy_all.shape
    local_experts, _, hidden = w_gate_up.shape
    hidden = hidden // 2
    experts = router_t.shape[0]
    count = shards // 2
    wide = jax.ShapeDtypeStruct((local_experts, count * 2 * CAP, model_width), BF)
    thin = jax.ShapeDtypeStruct((local_experts, count * 2 * CAP, hidden), BF)
    anywhere = pl.BlockSpec(memory_space=ANY)
    vmem = pl.BlockSpec(memory_space=pltpu.VMEM)
    return pl.pallas_call(
        partial(experts_in_kernel, count, CAP),
        out_shape=[
            jax.ShapeDtypeStruct((shards, tokens, model_width), BF),
            wide,
            wide,
            thin,
            thin,
            thin,
            jax.ShapeDtypeStruct((local_experts, count, 2 * CAP, 1), F32),
            jax.ShapeDtypeStruct((shards, experts, tokens), F32),
        ],
        in_specs=[anywhere, anywhere, vmem, vmem, anywhere],
        out_specs=[anywhere] * 6 + [vmem, vmem],
        scratch_shapes=[
            pltpu.VMEM((shards, tokens, model_width), BF),
            pltpu.VMEM(w_gate_up.shape, BF),
            pltpu.VMEM((2, 2, tokens, model_width), BF),
        ]
        + [pltpu.VMEM((local_experts, 2 * CAP, model_width), BF)] * 2
        + [pltpu.VMEM((local_experts, 2 * CAP, hidden), BF)] * 3
        + line_sems(1, count)
        + [DMA((local_experts,)), DMA((2,)), DMA((2,)), DMA((5, local_experts))],
        compiler_params=pltpu.CompilerParams(
            collective_id=collective, has_side_effects=True, vmem_limit_bytes=60 << 20
        ),
        name="experts_in",
    )(h2, dy_all, targets, router_t, w_gate_up)


def experts_mid_kernel(
    cap,
    y_in,
    act_in,
    by_up_in,
    by_gate_in,
    gate_slots,
    wd_in,
    gated_out,
    d_gate_out,
    d_up_out,
    dots_ref,
    g_down_out,
    wd,
    ys,
    acts,
    by_ups,
    by_gates,
    gated,
    d_gate,
    d_up,
    staged,
    in_sem,
    out_sem,
    grad_sem,
):
    local_experts, hidden, model_width = wd_in.shape
    count = gate_slots.shape[1]
    slots = ys.shape[1]
    over_lanes = (((1,), (1,)), ((), ()))
    over_rows = (((0,), (0,)), ((), ()))
    inputs = ((wd_in, wd), (y_in, ys), (act_in, acts), (by_up_in, by_ups), (by_gate_in, by_gates))
    results = ((gated, gated_out), (d_gate, d_gate_out), (d_up, d_up_out))
    wide = 256
    tile = staged.shape[1]

    def fetch(n, e):
        return pltpu.make_async_copy(inputs[n][0].at[e], inputs[n][1].at[e], in_sem.at[n, e])

    def store(n, e):
        return pltpu.make_async_copy(results[n][0].at[e], results[n][1].at[e], out_sem.at[n, e])

    def put_grad(e, n, buf):
        rows = pl.ds(pl.multiple_of(n * tile, tile), tile)
        return pltpu.make_async_copy(staged.at[buf], g_down_out.at[e, rows], grad_sem.at[buf])

    for e in range(local_experts):
        for n in range(5):
            fetch(n, e).start()
    for e in range(local_experts):
        for n in range(5):
            fetch(n, e).wait()
        gate = jnp.concatenate([gate_slots[e, q] for q in range(count)], axis=0)

        def step(n, dot):
            cols = pl.ds(pl.multiple_of(n * wide, wide), wide)
            grad_act = lax.dot_general(ys[e], wd[e, cols, :], over_lanes, preferred_element_type=F32)
            act = acts[e, :, cols].astype(F32)
            dot = dot + jnp.sum(act * grad_act, axis=1, keepdims=True)
            grad_act = grad_act * gate
            gated[e, :, cols] = (act * gate).astype(BF)
            d_up[e, :, cols] = (grad_act * by_ups[e, :, cols].astype(F32)).astype(BF)
            d_gate[e, :, cols] = (grad_act * by_gates[e, :, cols].astype(F32)).astype(BF)
            return dot

        dot = lax.fori_loop(0, hidden // wide, step, jnp.zeros((slots, 1), F32))
        for q in range(count):
            dots_ref[e, q] = dot[2 * cap * q : 2 * cap * (q + 1)]
        for n in range(3):
            store(n, e).start()

        @pl.loop(0, hidden // tile // 2)
        def _(m):
            for buf in range(2):
                n = 2 * m + buf

                def wait_last():
                    put_grad(e, n, buf).wait()

                if e > 0:
                    wait_last()
                else:
                    pl.when(m > 0)(wait_last)
                cols = pl.ds(pl.multiple_of(n * tile, tile), tile)
                staged[buf] = lax.dot_general(
                    gated[e, :, cols], ys[e], over_rows, preferred_element_type=F32
                ).astype(BF)
                put_grad(e, n, buf).start()

    for buf in range(2):
        put_grad(0, 0, buf).wait()
    for e in range(local_experts):
        for n in range(3):
            store(n, e).wait()


def experts_mid(grads, act, by_up, by_gate, gate_slots, w_down):
    local_experts, slots, model_width = grads.shape
    anywhere = pl.BlockSpec(memory_space=ANY)
    vmem = pl.BlockSpec(memory_space=pltpu.VMEM)
    thin = jax.ShapeDtypeStruct(act.shape, BF)
    return pl.pallas_call(
        partial(experts_mid_kernel, CAP),
        out_shape=[
            thin,
            thin,
            thin,
            jax.ShapeDtypeStruct(gate_slots.shape, F32),
            jax.ShapeDtypeStruct(w_down.shape, BF),
        ],
        in_specs=[anywhere] * 4 + [vmem, anywhere],
        out_specs=[anywhere] * 3 + [vmem, anywhere],
        scratch_shapes=[pltpu.VMEM(w_down.shape, BF), pltpu.VMEM(grads.shape, BF)]
        + [pltpu.VMEM(act.shape, BF)] * 6
        + [
            pltpu.VMEM((2, 256, model_width), BF),
            DMA((5, local_experts)),
            DMA((3, local_experts)),
            DMA((2,)),
        ],
        compiler_params=pltpu.CompilerParams(vmem_limit_bytes=60 << 20),
        cost_estimate=pl.CostEstimate(flops=18_000_000_000, bytes_accessed=60_000_000, transcendentals=0),
        name="experts_mid",
    )(grads, act, by_up, by_gate, gate_slots, w_down)


class StagedScatter(LineScatter):
    def __init__(self, count, places, stage, bufs, sems):
        super().__init__(count, places, [None], [0], bufs, sems)
        self.stage = stage

    def to_sib(self, a, q):
        sib = self.places[2]
        return remote(self.stage, self.sib[a].at[q], self.sems[2].at[a, q], self.sems[5].at[a, q], fsdp=sib)

    def ready(self, a, q):
        self.to_sib(a, q).wait_recv()

    def finish(self):
        i, p, sib = self.places
        for q in range(self.count):

            @pl.when(q > p)
            def _():
                self.right(0, q).wait_send()

            @pl.when(q < p)
            def _():
                self.left(0, q).wait_send()


class OuterGrads:
    def __init__(self, left, rights, out, scratch, steps):
        self.left, self.rights, self.out = left, rights, out
        self.tiles_in, self.held, self.staged, self.sems = scratch
        self.experts, self.width, _ = out.shape
        self.hidden = rights[0].shape[2]
        self.tile = self.staged.shape[1]
        self.tiles = self.width // self.tile
        self.units = self.experts * self.tiles
        self.share = -(-self.units // steps)

    def span(self, u):
        start = lax.rem(u, self.tiles) * self.tile
        return pl.ds(pl.multiple_of(start, self.tile), self.tile)

    def fetch(self, u):
        src = self.left.at[u // self.tiles, :, self.span(u)]
        return pltpu.make_async_copy(src, self.tiles_in.at[lax.rem(u, 2)], self.sems.at[0, lax.rem(u, 2)])

    def put(self, u):
        buf = lax.rem(u, 2)
        target = self.out.at[u // self.tiles, self.span(u)]
        return pltpu.make_async_copy(self.staged.at[buf], target, self.sems.at[1, buf])

    def hold(self, n):
        return pltpu.make_async_copy(self.rights[n], self.held.at[n], self.sems.at[2, n])

    def begin(self):
        for n in range(len(self.rights)):
            self.hold(n).start()
        self.fetch(0).start()

    def between(self, step):
        @pl.loop(step * self.share, jnp.minimum((step + 1) * self.share, self.units))
        def _(u):
            @pl.when(u == 0)
            def _():
                for n in range(len(self.rights)):
                    self.hold(n).wait()

            self.fetch(u).wait()

            @pl.when(u + 1 < self.units)
            def _():
                self.fetch(u + 1).start()

            @pl.when(u >= 2)
            def _():
                self.put(u - 2).wait()

            buf = lax.rem(u, 2)
            for n in range(len(self.rights)):
                self.staged[buf, :, n * self.hidden : (n + 1) * self.hidden] = lax.dot_general(
                    self.tiles_in[buf],
                    self.held[n, u // self.tiles],
                    (((0,), (0,)), ((), ())),
                    preferred_element_type=F32,
                ).astype(BF)
            self.put(u).start()

    def finish(self):
        self.put(self.units - 2).wait()
        self.put(self.units - 1).wait()


def outer_scratch(right, tile, factors):
    slots, hidden = right.shape[1:]
    return [
        pltpu.VMEM((2, slots, tile), BF),
        pltpu.VMEM((factors,) + right.shape, BF),
        pltpu.VMEM((2, tile, factors * hidden), BF),
        DMA((3, 2)),
    ]


def experts_out_kernel(
    count,
    cap,
    gated_in,
    d_gate_in,
    d_up_in,
    dots,
    targets,
    targets_t,
    probs_ref,
    router_t,
    wgu_in,
    wd_in,
    parts_a,
    parts_b,
    logit_ref,
    sum_ref,
    wgu,
    wd,
    gated,
    d_gate,
    d_up,
    parts,
    stage,
    own,
    sibling,
    inbox,
    w_sem,
    in_sem,
    part_sem,
    *sems,
):
    places = where_am_i()
    i, p, sib = places
    core = lax.rem(i, 2)
    local_experts, hidden, model_width = wd_in.shape
    tokens = targets.shape[2]
    experts = router_t.shape[0]
    first = i * local_experts
    over_lanes = (((1,), (1,)), ((), ()))
    line = StagedScatter(count, places, stage, ([own], [sibling], [inbox]), sems)
    weights = ((wgu_in, wgu), (wd_in, wd))
    inputs = ((gated_in, gated), (d_gate_in, d_gate), (d_up_in, d_up))

    def weight(n):
        return pltpu.make_async_copy(weights[n][0], weights[n][1], w_sem.at[n])

    def fetch(n, q, buf):
        rows = pl.ds(pl.multiple_of(q * 2 * cap, 2 * cap), 2 * cap)
        return pltpu.make_async_copy(inputs[n][0].at[:, rows], inputs[n][1].at[buf], in_sem.at[n, buf])

    first_part = parts_a.shape[2]

    def put(n, q):
        src = parts.at[:, :, pl.ds(n * first_part, (parts_a, parts_b)[n].shape[2])]
        return pltpu.make_async_copy(src, (parts_a, parts_b)[n].at[pl.ds(2 * q, 2)], part_sem.at[n])

    def order(k):
        return chunk_order(count - 1 - k, p, count)

    for n in range(3):
        fetch(n, order(0), 0).start()
    for n in range(2):
        weight(n).start()
    greet(count, places)
    slot_rows = lax.broadcasted_iota(jnp.int32, (local_experts * cap, tokens), 0)
    slot_lanes = lax.broadcasted_iota(jnp.int32, (tokens, local_experts * cap), 1)
    expert_rows = lax.broadcasted_iota(jnp.int32, (experts, tokens), 0)

    def compute(k):
        q = order(k)
        buf = lax.rem(k, 2)
        picks, logits_low = [], []
        for j in range(2):
            slot = 2 * q + j
            grad_probs = jnp.zeros((experts, tokens), F32)
            pick = None
            for e in range(local_experts):
                part = slice(e * cap, (e + 1) * cap)
                mask = (slot_rows == targets[slot, e : e + 1, :])[part]
                dot = dots[e, q, j * cap : (j + 1) * cap, :]
                row = jnp.sum(jnp.where(mask, dot, 0.0), axis=0, keepdims=True)
                grad_probs = jnp.where(expert_rows == first + e, row, grad_probs)
                hit = slot_lanes == targets_t[slot, :, e : e + 1]
                pick = hit if pick is None else pick | hit
            probs = probs_ref[slot]
            grad_logits = probs * (grad_probs - jnp.sum(probs * grad_probs, axis=0, keepdims=True))
            logit_ref[slot] = grad_logits.astype(BF)
            picks.append(jnp.where(pick, 1.0, 0.0).astype(BF))
            logits_low.append(grad_logits.T.astype(BF))
        for n in range(3):
            fetch(n, q, buf).wait()

        @pl.when(k + 1 < count)
        def _():
            for n in range(3):
                fetch(n, order(k + 1), 1 - buf).start()

        @pl.when(k > 0)
        def _():
            line.to_sib(0, order(k - 1)).wait_send()

        @pl.when(k == 0)
        def _():
            weight(0).wait()

        block = 512

        @pl.loop(0, model_width // block)
        def _(n):
            cols = pl.ds(pl.multiple_of(n * block, block), block)
            grads = []
            for e in range(local_experts):
                grads.append(
                    lax.dot_general(
                        d_gate[buf, e], wgu[e, cols, 0:hidden], over_lanes, preferred_element_type=F32
                    )
                    + lax.dot_general(
                        d_up[buf, e], wgu[e, cols, hidden:], over_lanes, preferred_element_type=F32
                    )
                )
            for j in range(2):
                part = slice(j * cap, (j + 1) * cap)
                back = jnp.concatenate([value[part] for value in grads], axis=0).astype(BF)
                total = (
                    jnp.dot(picks[j], back, preferred_element_type=F32)
                    + jnp.dot(logits_low[j], router_t[:, cols], preferred_element_type=F32)
                ).astype(BF)

                @pl.when(core == j)
                def _():
                    own[q, :, cols] = total

                @pl.when(core != j)
                def _():
                    stage[:, cols] = total

        line.to_sib(0, q).start()

        @pl.when(k > 0)
        def _():
            put(0, q).wait()
            put(1, q).wait()

        @pl.when(k == 0)
        def _():
            weight(1).wait()

        @pl.loop(0, model_width // block)
        def _(n):
            cols = pl.ds(pl.multiple_of(n * block, block), block)
            outs = []
            for e in range(local_experts):
                outs.append(jnp.dot(gated[buf, e], wd[e, :, cols], preferred_element_type=F32))
            for j in range(2):
                part = slice(j * cap, (j + 1) * cap)
                mine = jnp.concatenate([value[part] for value in outs], axis=0).astype(BF)
                parts[j, :, cols] = jnp.dot(picks[j], mine, preferred_element_type=F32).astype(BF)

        put(0, q).start()
        put(1, q).start()

    @pl.loop(0, 1)
    def _(k):
        compute(k)

    line.run(lambda a, q: None, lambda step: compute(step + 1))
    put(0, 0).wait()
    put(1, 0).wait()
    line.to_sib(0, order(count - 1)).wait_send()
    out = pltpu.make_async_copy(own.at[p], sum_ref, part_sem.at[0])
    out.start()
    out.wait()
    line.finish()


def experts_out(
    gated, d_gate, d_up, dots, targets, targets_t, probs, router_t, w_gate_up, w_down, collective
):
    local_experts, slots, hidden = gated.shape
    model_width = router_t.shape[1]
    shards, experts, tokens = probs.shape
    count = shards // 2
    anywhere = pl.BlockSpec(memory_space=ANY)
    vmem = pl.BlockSpec(memory_space=pltpu.VMEM)
    return pl.pallas_call(
        partial(experts_out_kernel, count, CAP),
        out_shape=[
            jax.ShapeDtypeStruct((shards, tokens, model_width // 8 * 5), BF),
            jax.ShapeDtypeStruct((shards, tokens, model_width // 8 * 3), BF),
            jax.ShapeDtypeStruct(probs.shape, BF),
            jax.ShapeDtypeStruct((tokens, model_width), BF),
        ],
        in_specs=[anywhere] * 3 + [vmem] * 5 + [anywhere] * 2,
        out_specs=[anywhere, anywhere, vmem, anywhere],
        scratch_shapes=[pltpu.VMEM(x.shape, BF) for x in (w_gate_up, w_down)]
        + [pltpu.VMEM((2, local_experts, 2 * CAP, hidden), BF)] * 3
        + [
            pltpu.VMEM((2, tokens, model_width), BF),
            pltpu.VMEM((tokens, model_width), BF),
            pltpu.VMEM((count, tokens, model_width), BF),
            pltpu.VMEM((count, tokens, model_width), BF),
            pltpu.VMEM((count + 1, tokens, model_width), BF),
            DMA((2,)),
            DMA((3, 2)),
            DMA((2,)),
        ]
        + [DMA((1, count))] * 7,
        compiler_params=pltpu.CompilerParams(
            collective_id=collective, has_side_effects=True, vmem_limit_bytes=67_043_328
        ),
        cost_estimate=pl.CostEstimate(flops=60_000_000_000, bytes_accessed=200_000_000, transcendentals=0),
        name="experts_out",
    )(gated, d_gate, d_up, dots, targets, targets_t, probs, router_t, w_gate_up, w_down)


def rope_tables(seq_len, head_dim):
    half_dim = head_dim // 2
    inverse = np.float32(ROPE_BASE) ** (-(np.arange(half_dim, dtype=np.float32) * 2.0 / head_dim))
    angles = np.arange(seq_len, dtype=np.float32)[:, None] * inverse.astype(np.float32)[None, :]
    angles = np.concatenate([angles, angles], axis=-1).astype(np.float64)
    return (np.cos(angles).astype(np.float32), np.sin(angles).astype(np.float32))


def dot(left, right, sides=(1, 0), out=F32):
    return lax.dot_general(
        left, right, (((sides[0],), (sides[1],)), ((), ())), preferred_element_type=F32
    ).astype(out)


def inverse_rms(rows):
    return lax.rsqrt(jnp.mean(rows * rows, axis=-1, keepdims=True) + EPSILON)


def on_device(
    inputs,
    out_grad,
    doc_ids,
    routes,
    w_query,
    w_key,
    w_value,
    w_output,
    w_router,
    attn_gain,
    ffn_gain,
    query_gain,
    key_gain,
    w_gate,
    w_up,
    w_down,
):
    seq_count = lax.axis_size("seq")
    shards = lax.axis_size("fsdp")
    tok_rows, model_width = inputs.shape[1:]
    seq_len = tok_rows * seq_count
    rows = w_query.shape[0]
    width = model_width // seq_count
    local_experts = w_gate.shape[0]
    experts = w_router.shape[1]
    top_k = routes.shape[2]
    lanes = 128

    small = jnp.concatenate(
        [
            w_router,
            attn_gain[:, None],
            ffn_gain[:, None],
            jnp.zeros((rows, lanes - experts - 2), BF),
        ],
        axis=1,
    )
    gains = jnp.pad(jnp.stack([query_gain, key_gain]), ((0, 14), (0, lanes - rows)))
    wq, wk, wv, small_all, gains_all, routes_all, wo, x_all = gather_start(
        (w_query, w_key, w_value, small, gains, routes[0].T, w_output, inputs[0]), seq_count, shards, 0
    )
    x_all = x_all.reshape(seq_len, model_width)
    gate_up = jnp.concatenate([w_gate, w_up], axis=2)
    full_gate_up = lax.all_gather(gate_up, "seq", axis=1, tiled=True)
    full_down = lax.all_gather(w_down, "seq", axis=1, tiled=True)

    wq = wq.reshape(model_width, width)
    wk = wk.reshape(model_width, width)
    wv = wv.reshape(model_width, width)
    small_all = small_all.reshape(model_width, lanes)
    w_r = small_all[:, :experts]
    gain_a = small_all[:, experts].astype(F32)
    gain_f = small_all[:, experts + 1].astype(F32)
    gq = gains_all[:, 0, :rows].reshape(1, width).astype(F32)
    gk = gains_all[:, 1, :rows].reshape(1, width).astype(F32)

    x_float = x_all.astype(F32)
    h1 = (x_float * inverse_rms(x_float) * gain_a).astype(BF)
    q_raw = dot(h1, wq)
    k_raw = dot(h1, wk)
    values = dot(h1, wv, out=BF)
    squares = jnp.stack(
        [jnp.sum(q_raw * q_raw, axis=1), jnp.sum(k_raw * k_raw, axis=1)]
        + [jnp.ones((seq_len,), F32)] * 6
    )
    cos, sin = rope_tables(seq_len, HEAD)
    doc_row = doc_ids
    doc_col = doc_ids.reshape(seq_len, 1)
    attended, q_low, k_low, scales = attend(
        q_raw, k_raw, values, squares, gq, gk, cos, sin, doc_col, doc_row, model_width, seq_count, 1
    )
    wo = wo.reshape(width, model_width)
    projected = dot(attended, wo, out=BF).reshape(seq_count, tok_rows, model_width)
    rows_in = inputs[0].astype(F32)
    grad_rows = out_grad[0].astype(F32)
    summed, dy_all, targets, targets_t = middle(projected, out_grad[0], routes_all, local_experts, 2)
    x_mid = rows_in + summed
    scale_f = inverse_rms(x_mid)
    h2 = (x_mid * scale_f * gain_f).astype(BF)

    router_t = w_r.T
    h2_all, expert_in, grad_slots, act, by_up, by_gate, gate_slots, gate_probs = experts_in(
        h2, dy_all, targets, router_t, full_gate_up, 3
    )
    gated, d_gate, d_up, dots_slots, g_down = experts_mid(
        grad_slots, act, by_up, by_gate, gate_slots, full_down
    )
    parts_a, parts_b, grad_logits, grad_h2 = experts_out(
        gated,
        d_gate,
        d_up,
        dots_slots,
        targets,
        targets_t,
        gate_probs,
        router_t,
        full_gate_up,
        full_down,
        4,
    )

    def spread(part):
        return lax.psum_scatter(part, "seq", scatter_dimension=1, tiled=True)

    g_down = spread(g_down)
    grad_h2, g_down = lax.optimization_barrier((grad_h2, g_down))
    grad_h2 = grad_h2.astype(F32)

    u_rows = gain_f * grad_h2
    grad_mid = (
        grad_rows
        + scale_f * u_rows
        - x_mid * scale_f**3 * jnp.mean(u_rows * x_mid, axis=-1, keepdims=True)
    )
    ffn_part = jnp.sum(grad_h2 * x_mid * scale_f, axis=0)

    d_attn, sum_a, g_gate_up, small_part = turn_back(
        grad_mid.astype(BF),
        parts_a,
        expert_in,
        d_gate,
        d_up,
        h2_all,
        grad_logits,
        ffn_part[None],
        seq_count,
        shards,
        5,
    )
    g_gate_up = spread(g_gate_up)
    d_attn = d_attn.reshape(seq_len, model_width)
    d_heads = dot(d_attn, wo, (1, 1), BF)
    dq_low, dk_low, dv_low, gains_part, sum_b = attend_back(
        q_low,
        k_low,
        values,
        d_heads,
        q_raw,
        k_raw,
        scales,
        gq,
        gk,
        cos,
        sin,
        doc_col,
        doc_row,
        parts_b,
        rows,
        model_width,
        seq_count,
        6,
    )
    result = x_mid + jnp.concatenate([sum_a, sum_b], axis=1).astype(F32)

    sheet = (seq_count, shards, rows, width)
    g_query, g_key, g_value, g_output, g_small, g_gains, grad_h1 = scatter_end(
        (
            dot(h1, dq_low, (0, 0), BF).reshape(sheet),
            dot(h1, dk_low, (0, 0), BF).reshape(sheet),
            dot(h1, dv_low, (0, 0), BF).reshape(sheet),
            dot(attended, d_attn, (0, 0), BF).reshape(shards, rows, model_width),
            small_part.reshape(seq_count, shards, rows, lanes),
            gains_part,
        ),
        (dq_low, dk_low, dv_low, wq, wk, wv),
        seq_count,
        shards,
        7,
    )
    g_query, g_key, g_value = (g_query.astype(F32), g_key.astype(F32), g_value.astype(F32))

    scale_a = inverse_rms(rows_in)
    u_rows = gain_a * grad_h1
    input_grad = (
        grad_mid
        + scale_a * u_rows
        - rows_in * scale_a**3 * jnp.mean(u_rows * rows_in, axis=-1, keepdims=True)
    )
    pairs = (
        w_query.astype(F32) * g_query + w_key.astype(F32) * g_key + w_value.astype(F32) * g_value
    )
    g_attn_gain = jnp.sum(pairs, axis=1) / attn_gain.astype(F32)

    return (
        result.astype(BF)[None],
        input_grad[None],
        g_query,
        g_key,
        g_value,
        g_output.astype(F32),
        g_small[:, :experts],
        g_attn_gain,
        g_small[:, experts],
        g_gains[0, :rows],
        g_gains[1, :rows],
        g_gate_up[:, :, : g_gate_up.shape[2] // 2].astype(F32),
        g_gate_up[:, :, g_gate_up.shape[2] // 2 :].astype(F32),
        g_down.astype(F32),
    )


def solution(mesh):
    rows = P("fsdp", "seq", None)
    sheet = P(("seq", "fsdp"), None)
    line = P(("seq", "fsdp"))
    return jax.shard_map(
        on_device,
        mesh=mesh,
        in_specs=(rows, rows, P("fsdp", None), rows) + (sheet,) * 5 + (line,) * 4 + (rows,) * 3,
        out_specs=(rows, rows) + (sheet,) * 5 + (line,) * 4 + (rows,) * 3,
        check_vma=False,
    )
```

```python
from functools import partial

import jax
import jax.numpy as jnp
import numpy as np
from jax import lax
from jax.experimental import pallas as pl
from jax.experimental.pallas import tpu as pltpu
from jax.sharding import PartitionSpec as P

CAP = 136
HEAD = 128
EPSILON = 1e-05
ROPE_BASE = 10000.0
MASKED_OUT = -1e30
ANY = pl.ANY
MESH = pl.DeviceIdType.MESH
DMA = pltpu.SemaphoreType.DMA
BF = jnp.bfloat16
F32 = jnp.float32


def remote(src, dst, send, recv, **where):
    return pltpu.make_async_remote_copy(
        src_ref=src, dst_ref=dst, send_sem=send, recv_sem=recv, device_id=where, device_id_type=MESH
    )


def greet(count, places, seq_count=1):
    i, p, sib = places
    barrier = pltpu.get_barrier_semaphore()
    pl.semaphore_signal(barrier, inc=1, device_id={"fsdp": sib}, device_id_type=MESH)
    here = lax.axis_index("seq")
    for d in range(1, seq_count):
        peer = lax.rem(here + d, seq_count)
        pl.semaphore_signal(barrier, inc=1, device_id={"seq": peer}, device_id_type=MESH)

    @pl.when(p > 0)
    def _():
        pl.semaphore_signal(barrier, inc=1, device_id={"fsdp": i - 2}, device_id_type=MESH)

    @pl.when(p < count - 1)
    def _():
        pl.semaphore_signal(barrier, inc=1, device_id={"fsdp": i + 2}, device_id_type=MESH)

    last = count - 1
    pl.semaphore_wait(barrier, seq_count + (p + last) // count + (last - p + last) // count)


def slot_of(ref, axis, index):
    return ref.at[index] if axis == 0 else ref.at[:, index]


class LineGather:
    def __init__(self, count, places, refs, axes, send_r, send_l, send_s, recv):
        self.count, self.places = count, places
        self.refs, self.axes = refs, axes
        self.sems = (send_r, send_l, send_s, recv)

    def copy(self, a, slot, kind, t, device):
        send = self.sems[kind].at[a, t]
        ref = slot_of(self.refs[a], self.axes[a], slot)
        return remote(ref, ref, send, self.sems[3].at[a, slot], fsdp=device)

    def first(self, a):
        i, p, sib = self.places

        @pl.when(p < self.count - 1)
        def _():
            self.copy(a, i, 0, 0, i + 2).start()

        @pl.when(p > 0)
        def _():
            self.copy(a, i, 1, 0, i - 2).start()

        self.copy(a, i, 2, 0, sib).start()

    def forward(self, t):
        i, p, sib = self.places
        count = self.count
        for a in range(len(self.refs)):

            @pl.when(p - t >= 0)
            def _():
                slot = i - 2 * t
                self.copy(a, slot, 0, t, sib).wait_recv()

                @pl.when(p < count - 1)
                def _():
                    self.copy(a, slot, 0, t, i + 2).start()

                self.copy(a, slot, 2, t, sib).start()

            @pl.when(p + t < count)
            def _():
                slot = i + 2 * t
                self.copy(a, slot, 1, t, sib).wait_recv()

                @pl.when(p > 0)
                def _():
                    self.copy(a, slot, 1, t, i - 2).start()

                self.copy(a, slot, 2, count + t, sib).start()

    def finish(self):
        i, p, sib = self.places
        count = self.count
        for a in range(len(self.refs)):
            for q in range(count):
                self.copy(a, 2 * q + lax.rem(sib, 2), 2, 0, sib).wait_recv()
            self.copy(a, i, 2, 0, sib).wait_send()

            @pl.when(p < count - 1)
            def _():
                self.copy(a, i, 0, 0, i + 2).wait_send()

            @pl.when(p > 0)
            def _():
                self.copy(a, i, 1, 0, i - 2).wait_send()

            for t in range(1, count):

                @pl.when(p - t >= 0)
                def _():
                    slot = i - 2 * t

                    @pl.when(p < count - 1)
                    def _():
                        self.copy(a, slot, 0, t, i + 2).wait_send()

                    self.copy(a, slot, 2, t, sib).wait_send()

                @pl.when(p + t < count)
                def _():
                    slot = i + 2 * t

                    @pl.when(p > 0)
                    def _():
                        self.copy(a, slot, 1, t, i - 2).wait_send()

                    self.copy(a, slot, 2, count + t, sib).wait_send()


def line_sems(arrays, count):
    return [DMA((arrays, count)), DMA((arrays, count)), DMA((arrays, 2 * count)), DMA((arrays, 2 * count))]


def where_am_i():
    i = lax.axis_index("fsdp")
    p = i // 2
    c = i % 2
    return i, p, 2 * p + 1 - c


def start_kernel(count, seq_count, *refs):
    wq, wk, wv, small, gains, routes, wo, rows = refs[:8]
    outs = refs[8:15]
    rows_out = refs[15]
    holds = refs[16:24]
    send_x, recv_x, local, send_r, send_l, send_s, recv, send_y, recv_y = refs[24:]
    places = where_am_i()
    i = places[0]
    here = lax.axis_index("seq")
    width = wq.shape[1] // seq_count

    def columns(ref, peer):
        return ref.at[:, pl.ds(pl.multiple_of(peer * width, width), width)]

    own = [columns(wq, here), columns(wk, here), columns(wv, here), small, gains, routes, wo, rows]
    for a in range(8):
        pltpu.make_async_copy(own[a], holds[a], local.at[a]).start()
    greet(count, places, seq_count)

    def piece(a, d):
        peer = lax.rem(here + d, seq_count)
        src = small if a == 3 else columns((wq, wk, wv)[a], peer)
        return remote(src, outs[a].at[here, i], send_x.at[a, d - 1], recv_x.at[a, d - 1], seq=peer)

    def arrived(a, d):
        origin = lax.rem(here + seq_count - d, seq_count)
        ref = outs[a].at[origin, i]
        return remote(ref, ref, send_x.at[a, d - 1], recv_x.at[a, d - 1], seq=origin)

    for a in (3, 0, 1, 2):
        for d in range(1, seq_count):
            piece(a, d).start()
    gather = SeqGather(seq_count, rows, rows_out, send_y, recv_y)
    gather.begin()
    axes = [1, 1, 1, 1, 0, 0, 0]

    def target(a):
        return outs[a].at[here, i] if axes[a] == 1 else outs[a].at[i]

    for a in (4, 5, 6, 3, 0, 1, 2):
        pltpu.make_async_copy(own[a], holds[a], local.at[a]).wait()
        pltpu.make_async_copy(holds[a], target(a), local.at[a]).start()
    line = LineGather(count, places, outs, axes, send_r, send_l, send_s, recv)
    for a in (4, 5, 6, 3, 0, 1, 2):
        pltpu.make_async_copy(holds[a], target(a), local.at[a]).wait()
        if axes[a] == 1:
            for d in range(1, seq_count):
                arrived(a, d).wait_recv()
        line.first(a)
    pltpu.make_async_copy(rows, holds[7], local.at[7]).wait()
    pltpu.make_async_copy(holds[7], rows_out.at[here], local.at[7]).start()
    for t in range(1, count):
        line.forward(t)
        if t == 1:
            gather.relay()
    line.finish()
    pltpu.make_async_copy(holds[7], rows_out.at[here], local.at[7]).wait()
    gather.finish()
    for a in (3, 0, 1, 2):
        for d in range(1, seq_count):
            piece(a, d).wait_send()


def gather_start(arrays, seq_count, shards, collective):
    count = shards // 2
    wq, wk, wv, small, gains, routes, wo, tokens = arrays
    rows, model_width = wq.shape
    width = model_width // seq_count
    sheet = jax.ShapeDtypeStruct((seq_count, shards, rows, width), BF)
    shapes = [
        sheet,
        sheet,
        sheet,
        jax.ShapeDtypeStruct((seq_count, shards) + small.shape, BF),
        jax.ShapeDtypeStruct((shards,) + gains.shape, BF),
        jax.ShapeDtypeStruct((shards,) + routes.shape, jnp.int32),
        jax.ShapeDtypeStruct((shards,) + wo.shape, BF),
        jax.ShapeDtypeStruct((seq_count,) + tokens.shape, BF),
    ]
    holds = [pltpu.VMEM((rows, width), BF)] * 3 + [
        pltpu.VMEM(small.shape, BF),
        pltpu.VMEM(gains.shape, BF),
        pltpu.VMEM(routes.shape, jnp.int32),
        pltpu.VMEM(wo.shape, BF),
        pltpu.VMEM(tokens.shape, BF),
    ]
    return pl.pallas_call(
        partial(start_kernel, count, seq_count),
        out_shape=shapes,
        in_specs=[pl.BlockSpec(memory_space=ANY)] * 8,
        out_specs=[pl.BlockSpec(memory_space=ANY)] * 8,
        scratch_shapes=holds
        + [DMA((4, seq_count - 1)), DMA((4, seq_count - 1)), DMA((8,))]
        + line_sems(7, count)
        + seq_gather_sems(seq_count),
        compiler_params=pltpu.CompilerParams(collective_id=collective, has_side_effects=True),
        name="gather_start",
    )(*arrays)


def chunk_order(k, p, count):
    near = jnp.minimum(p, count - 1 - p)
    step = (k + 1) // 2
    both = jnp.where(k % 2 == 1, p - step, p + step)
    return jnp.where(k <= 2 * near, both, jnp.where(p < count - 1 - p, k, count - 1 - k))


class LineScatter:
    def __init__(self, count, places, sources, axes, bufs, sems):
        self.count, self.places = count, places
        self.sources, self.axes = sources, axes
        self.own, self.sib, self.inbox = bufs
        self.sems = sems

    def view(self, a, ref):
        return ref

    def load(self, a, q):
        i = self.places[0]
        src = slot_of(self.sources[a], self.axes[a], 2 * q + lax.rem(i, 2))
        return pltpu.make_async_copy(self.view(a, src), self.view(a, self.own[a].at[q]), self.sems[6].at[a, q])

    def to_sib(self, a, q):
        sib = self.places[2]
        src = slot_of(self.sources[a], self.axes[a], 2 * q + lax.rem(sib, 2))
        dst = self.view(a, self.sib[a].at[q])
        return remote(self.view(a, src), dst, self.sems[2].at[a, q], self.sems[5].at[a, q], fsdp=sib)

    def right(self, a, q):
        i = self.places[0]
        src, dst = self.view(a, self.own[a].at[q]), self.view(a, self.inbox[a].at[q])
        return remote(src, dst, self.sems[0].at[a, q], self.sems[3].at[a, q], fsdp=i + 2)

    def left(self, a, q):
        i, p, sib = self.places
        slot = jnp.where(q == p - 1, self.count, q)
        src, dst = self.view(a, self.own[a].at[q]), self.view(a, self.inbox[a].at[slot])
        return remote(src, dst, self.sems[1].at[a, q], self.sems[4].at[a, q], fsdp=i - 2)

    def begin_loads(self):
        for k in range(self.count):
            q = chunk_order(self.count - 1 - k, self.places[1], self.count)
            for a in range(len(self.sources)):
                self.load(a, q).start()

    def begin(self):
        for k in range(self.count):
            q = chunk_order(self.count - 1 - k, self.places[1], self.count)
            for a in range(len(self.sources)):
                self.to_sib(a, q).start()

    def add(self, a, q, others):
        own = self.own[a]
        lead = own.shape[1:-2]
        rows, width = own.shape[-2:]
        step = rows
        while step * width > 65536 and step % 16 == 0:
            step //= 2

        def strip(index):
            total = own[index].astype(F32) + self.sib[a][index].astype(F32)
            for slot in others:
                total += self.inbox[a][(slot,) + index[1:]].astype(F32)
            own[index] = total.astype(own.dtype)

        def rows_of(prefix):
            if step == rows:
                strip(prefix)
                return

            @pl.loop(0, rows // step)
            def _(k):
                strip(prefix + (pl.ds(pl.multiple_of(k * step, step), step),))

        if lead:
            for b in range(lead[0]):
                rows_of((q, b))
        else:
            rows_of((q,))

    def ready(self, a, q):
        self.load(a, q).wait()
        self.to_sib(a, q).wait_recv()

    def event(self, step):
        i, p, sib = self.places
        count = self.count
        arrays = range(len(self.sources))

        @pl.when(step >= p)
        def _():
            q = count - 1 - (step - p)
            for a in arrays:
                self.ready(a, q)

                @pl.when(p > 0)
                def _():
                    self.right(a, q).wait_recv()
                    self.add(a, q, [q])

                @pl.when(p == 0)
                def _():
                    self.add(a, q, [])

                self.right(a, q).start()

        @pl.when(step >= count - 1 - p)
        def _():
            q = step - (count - 1 - p)
            for a in arrays:
                self.ready(a, q)

                @pl.when(p < count - 1)
                def _():
                    self.left(a, q).wait_recv()
                    self.add(a, q, [q])

                @pl.when(p == count - 1)
                def _():
                    self.add(a, q, [])

                self.left(a, q).start()

    def final(self, after):
        i, p, sib = self.places
        count = self.count
        for a in range(len(self.sources)):
            self.ready(a, p)

            @pl.when(p > 0)
            def _():
                self.right(a, p).wait_recv()

            @pl.when(p < count - 1)
            def _():
                self.left(a, p).wait_recv()

            @pl.when(p == 0)
            def _():
                self.add(a, p, [count])

            @pl.when(p == count - 1)
            def _():
                self.add(a, p, [p])

            @pl.when((p > 0) & (p < count - 1))
            def _():
                self.add(a, p, [p, count])

            after(a, p)

    def run(self, after, between=None):
        @pl.loop(0, self.count - 1)
        def _(step):
            self.event(step)
            if between is not None:
                between(step)

        self.final(after)

    def finish(self):
        i, p, sib = self.places
        for a in range(len(self.sources)):
            for q in range(self.count):
                self.to_sib(a, q).wait_send()

                @pl.when(q > p)
                def _():
                    self.right(a, q).wait_send()

                @pl.when(q < p)
                def _():
                    self.left(a, q).wait_send()


class SplitScatter(LineScatter):
    def __init__(self, count, places, source, bufs, sems):
        super().__init__(count, places, [source] * 2, [0] * 2, tuple([buf] * 2 for buf in bufs), sems)
        self.half = bufs[0].shape[-1] // 2

    def cols(self, a):
        return pl.ds(a * self.half, self.half)

    def view(self, a, ref):
        return ref.at[:, self.cols(a)]

    def add(self, a, q, others):
        own = self.own[a]
        rows = own.shape[1]
        step = rows
        while step * self.half > 65536 and step % 16 == 0:
            step //= 2

        @pl.loop(0, rows // step)
        def _(k):
            index = (pl.ds(pl.multiple_of(k * step, step), step), self.cols(a))
            total = own[(q,) + index].astype(F32) + self.sib[a][(q,) + index].astype(F32)
            for slot in others:
                total += self.inbox[a][(slot,) + index].astype(F32)
            own[(q,) + index] = total.astype(own.dtype)


def end_kernel(count, seq_count, *refs):
    sources = refs[:6]
    factors = refs[6:12]
    outs = refs[12:18]
    sum_ref = refs[18]
    bufs = tuple(refs[19 + 6 * k : 25 + 6 * k] for k in range(3))
    landing = refs[37]
    sems = refs[38:45]
    send_x, recv_x, local = refs[45:48]
    held = refs[48:54]
    rows_ref, factor_sem = refs[54:56]
    seq = SeqScatter(seq_count, rows_ref, *refs[56:61])
    places = where_am_i()
    here = lax.axis_index("seq")
    width = sources[0].shape[3]
    line = LineScatter(count, places, sources, [1, 1, 1, 0, 1, 0], bufs, sems)
    line.begin_loads()
    for n in range(6):
        pltpu.make_async_copy(factors[n], held[n], factor_sem.at[n]).start()
    greet(count, places, seq_count)
    line.begin()
    own = bufs[0]

    def at_home(a, block):
        if a == 4:
            return landing.at[block]
        start = pl.multiple_of(block * width, width)
        return outs[a].at[:, pl.ds(start, width)]

    def piece(a, q, d):
        peer = lax.rem(here + d, seq_count)
        slot = 3 if a == 4 else a
        return remote(
            own[a].at[q, peer], at_home(a, here), send_x.at[slot, d - 1], recv_x.at[slot, d - 1], seq=peer
        )

    def arrived(a, d):
        origin = lax.rem(here + seq_count - d, seq_count)
        slot = 3 if a == 4 else a
        return remote(
            at_home(a, origin), at_home(a, origin), send_x.at[slot, d - 1], recv_x.at[slot, d - 1], seq=origin
        )

    def after(a, q):
        if a in (3, 5):
            pltpu.make_async_copy(own[a].at[q], outs[a], local.at[a]).start()
        else:
            for d in range(1, seq_count):
                piece(a, q, d).start()
            pltpu.make_async_copy(own[a].at[q, here], at_home(a, here), local.at[a]).start()

    def back_rows():
        for n in range(6):
            pltpu.make_async_copy(factors[n], held[n], factor_sem.at[n]).wait()
        tokens, model_width = rows_ref.shape[1:]
        tile = 512
        tiles = model_width // tile

        @pl.loop(0, seq_count * tiles)
        def _(u):
            block = u // tiles
            strip = pl.ds(pl.multiple_of(block * tokens, tokens), tokens)
            cols = pl.ds(pl.multiple_of(lax.rem(u, tiles) * tile, tile), tile)
            total = jnp.zeros((tokens, tile), F32)
            for n in range(3):
                total += lax.dot_general(
                    held[n][strip, :], held[3 + n][cols, :], (((1,), (1,)), ((), ())), preferred_element_type=F32
                )
            rows_ref[block, :, cols] = total.astype(BF)

        seq.begin_loads()
        seq.begin()

    def between(step):
        pl.when(step == 0)(back_rows)

        @pl.when(step == 1)
        def _():
            seq.relay()

    line.run(after, between)
    seq.total(sum_ref)
    for q in range(count):

        @pl.when(q == places[1])
        def _():
            for a in range(6):
                if a in (3, 5):
                    pltpu.make_async_copy(own[a].at[q], outs[a], local.at[a]).wait()
                else:
                    pltpu.make_async_copy(own[a].at[q, here], at_home(a, here), local.at[a]).wait()
                    for d in range(1, seq_count):
                        piece(a, q, d).wait_send()
                        arrived(a, d).wait_recv()

    total = landing[0]
    for block in range(1, seq_count):
        total += landing[block]
    landing[0] = total
    last = pltpu.make_async_copy(landing.at[0], outs[4], local.at[4])
    last.start()
    last.wait()
    line.finish()
    seq.finish()


def scatter_end(arrays, factors, seq_count, shards, collective):
    count = shards // 2
    gq, gk, gv, go, small, gains = arrays
    rows, width = gq.shape[2:]
    tokens, model_width = factors[0].shape[0] // seq_count, factors[3].shape[0]
    home = jax.ShapeDtypeStruct((rows, width * seq_count), BF)
    shapes = [
        home,
        home,
        home,
        jax.ShapeDtypeStruct(go.shape[1:], BF),
        jax.ShapeDtypeStruct(small.shape[2:], F32),
        jax.ShapeDtypeStruct(gains.shape[1:], F32),
        jax.ShapeDtypeStruct((tokens, model_width), F32),
    ]
    blocks, inboxes = [], []
    for a in range(6):
        shape = arrays[a].shape
        block = (shape[0],) + shape[2:] if a in (0, 1, 2, 4) else shape[1:]
        blocks.append(pltpu.VMEM((count,) + block, arrays[a].dtype))
        inboxes.append(pltpu.VMEM((count + 1,) + block, arrays[a].dtype))
    return pl.pallas_call(
        partial(end_kernel, count, seq_count),
        out_shape=shapes,
        in_specs=[pl.BlockSpec(memory_space=ANY)] * 12,
        out_specs=[pl.BlockSpec(memory_space=ANY)] * 6 + [pl.BlockSpec(memory_space=pltpu.VMEM)],
        scratch_shapes=blocks * 2
        + inboxes
        + [pltpu.VMEM((seq_count,) + small.shape[2:], F32)]
        + [DMA((6, count))] * 7
        + [DMA((4, seq_count - 1)), DMA((4, seq_count - 1)), DMA((6,))]
        + [pltpu.VMEM(x.shape, BF) for x in factors]
        + [pltpu.VMEM((seq_count, tokens, model_width), BF), DMA((6,))]
        + seq_scatter_scratch((tokens, model_width), BF, seq_count),
        compiler_params=pltpu.CompilerParams(
            collective_id=collective, has_side_effects=True, vmem_limit_bytes=62 << 20
        ),
        name="scatter_end",
    )(*arrays, *factors)


def greet_seq(seq_count):
    here = lax.axis_index("seq")
    barrier = pltpu.get_barrier_semaphore()
    for d in range(1, seq_count):
        peer = lax.rem(here + d, seq_count)
        pl.semaphore_signal(barrier, inc=1, device_id={"seq": peer}, device_id_type=MESH)
    pl.semaphore_wait(barrier, seq_count - 1)
    return here


class SeqScatter:
    def __init__(self, seq_count, x_ref, own, inbox, send, recv, local):
        here = lax.axis_index("seq")
        self.own, self.inbox, self.local, self.count = own, inbox, local, seq_count
        self.take = pltpu.make_async_copy(x_ref.at[here], own, local.at[0])
        rows = own.shape[0]
        self.half = rows // 2
        low, high = pl.ds(0, self.half), pl.ds(self.half, self.half)
        if seq_count != 4:
            self.copies = []
            for d in range(1, seq_count):
                peer = lax.rem(here + d, seq_count)
                self.copies.append(
                    remote(x_ref.at[peer], inbox.at[d - 1], send.at[d - 1], recv.at[d - 1], seq=peer)
                )
            return
        beside = here + 1 - 2 * lax.rem(here, 2)
        across = lax.rem(here + 2, 4)
        corner = 3 - here
        self.loads = [
            pltpu.make_async_copy(x_ref.at[across, low], inbox.at[3, low], local.at[1]),
            pltpu.make_async_copy(x_ref.at[beside, high], inbox.at[3, high], local.at[2]),
        ]
        plans = (
            (x_ref.at[corner, low], inbox.at[2, low], beside),
            (x_ref.at[corner, high], inbox.at[2, high], across),
            (x_ref.at[beside, low], inbox.at[0, low], beside),
            (x_ref.at[across, high], inbox.at[1, high], across),
            (inbox.at[3, low], inbox.at[1, low], across),
            (inbox.at[3, high], inbox.at[0, high], beside),
        )
        self.copies = [
            remote(src, dst, send.at[n], recv.at[n], seq=peer) for n, (src, dst, peer) in enumerate(plans)
        ]

    def begin_loads(self):
        self.take.start()
        if self.count == 4:
            for load in self.loads:
                load.start()

    def begin(self):
        for copy in self.copies[:4] if self.count == 4 else self.copies:
            copy.start()

    def strips(self, start, rows, body):
        step = min(32, rows)

        @pl.loop(0, rows // step)
        def _(k):
            body(pl.ds(pl.multiple_of(start + k * step, step), step))

    def relay(self):
        if self.count != 4:
            return
        inbox = self.inbox

        def add(strip):
            inbox[3, strip, :] = (
                inbox[3, strip, :].astype(F32) + inbox[2, strip, :].astype(F32)
            ).astype(inbox.dtype)

        for n, start in ((0, 0), (1, self.half)):
            self.loads[n].wait()
            self.copies[n].wait_recv()
            self.strips(start, self.half, add)
            self.copies[4 + n].start()

    def total(self, o_ref):
        self.take.wait()
        for copy in self.copies[2:] if self.count == 4 else self.copies:
            copy.wait_recv()
        parts = 2 if self.count == 4 else self.count - 1

        def add(strip):
            total = self.own[strip, :].astype(F32)
            for d in range(parts):
                total += self.inbox[d, strip, :].astype(F32)
            o_ref[strip, :] = total

        self.strips(0, self.own.shape[0], add)

    def finish(self):
        for copy in self.copies:
            copy.wait_send()


def seq_scatter_scratch(block, dtype, seq_count):
    boxes = 4 if seq_count == 4 else seq_count - 1
    copies = 6 if seq_count == 4 else seq_count - 1
    return [
        pltpu.VMEM(block, dtype),
        pltpu.VMEM((boxes,) + block, dtype),
        DMA((copies,)),
        DMA((copies,)),
        DMA((3,)),
    ]


class SeqGather:
    def __init__(self, seq_count, x_ref, o_ref, send, recv):
        here = lax.axis_index("seq")
        self.count = seq_count
        rows = x_ref.shape[0]
        low, high = pl.ds(0, rows // 2), pl.ds(rows // 2, rows // 2)
        if seq_count != 4:
            peers = [lax.rem(here + d, seq_count) for d in range(1, seq_count)]
            origins = [lax.rem(here + seq_count - d, seq_count) for d in range(1, seq_count)]
            out = [(x_ref, o_ref.at[here], peer) for peer in peers]
            landed = [o_ref.at[origin] for origin in origins]
        else:
            beside = here + 1 - 2 * lax.rem(here, 2)
            across = lax.rem(here + 2, 4)
            corner = 3 - here
            out = [
                (x_ref, o_ref.at[here], beside),
                (x_ref, o_ref.at[here], across),
                (o_ref.at[across, low], o_ref.at[across, low], beside),
                (o_ref.at[beside, high], o_ref.at[beside, high], across),
            ]
            landed = [o_ref.at[beside], o_ref.at[across], o_ref.at[corner, low], o_ref.at[corner, high]]
        self.sends = [
            remote(src, dst, send.at[n], recv.at[n], seq=peer) for n, (src, dst, peer) in enumerate(out)
        ]
        self.lands = [
            remote(ref, ref, send.at[n], recv.at[n], seq=out[n][2]) for n, ref in enumerate(landed)
        ]

    def begin(self):
        for copy in self.sends[:2] if self.count == 4 else self.sends:
            copy.start()

    def relay(self):
        if self.count == 4:
            for n in (0, 1):
                self.lands[n].wait_recv()
            for n in (2, 3):
                self.sends[n].start()

    def finish(self):
        for n, copy in enumerate(self.lands):
            if self.count != 4 or n > 1:
                copy.wait_recv()
        for copy in self.sends:
            copy.wait_send()


def seq_gather_sems(seq_count):
    copies = 4 if seq_count == 4 else seq_count - 1
    return [DMA((copies,)), DMA((copies,))]


def slot_targets(first, local_experts, cap, routes, targets, targets_t):
    shards, top_k, tokens = routes.shape
    earlier = lax.broadcasted_iota(jnp.int32, (tokens, tokens), 0)
    later = lax.broadcasted_iota(jnp.int32, (tokens, tokens), 1)
    upto = jnp.where(earlier <= later, 1.0, 0.0).astype(BF)
    row = lax.broadcasted_iota(jnp.int32, (8, tokens), 0)
    for j in range(shards):
        named = routes[j]
        chosen = jnp.zeros((8, tokens), F32)
        for e in range(local_experts):
            hit = jnp.max(jnp.where(named == first + e, 1.0, 0.0), axis=0, keepdims=True)
            chosen = jnp.where(row == e, hit, chosen)
        place = jnp.dot(chosen.astype(BF), upto, preferred_element_type=F32) - 1.0
        slot = jnp.where(chosen > 0.5, place + (cap * row).astype(F32), -1.0)
        targets[j] = slot[0:local_experts].astype(jnp.int32)
        targets_t[j] = slot.T[:, 0:local_experts].astype(jnp.int32)


def middle_kernel(
    count,
    seq_count,
    cap,
    x_ref,
    dy_ref,
    routes,
    o_ref,
    all_ref,
    targets,
    targets_t,
    own,
    inbox,
    xs,
    xr,
    xl,
    hold,
    s0,
    s1,
    s2,
    recv,
    local,
):
    places = where_am_i()
    i = places[0]
    seq = SeqScatter(seq_count, x_ref, own, inbox, xs, xr, xl)
    seq.begin_loads()
    take = pltpu.make_async_copy(dy_ref, hold, local.at[0])
    take.start()
    greet(count, places, seq_count)
    seq.begin()
    take.wait()
    put = pltpu.make_async_copy(hold, all_ref.at[i], local.at[1])
    put.start()
    put.wait()
    line = LineGather(count, places, [all_ref], [0], s0, s1, s2, recv)
    line.first(0)
    local_experts = targets.shape[1]
    slot_targets(i * local_experts, local_experts, cap, routes, targets, targets_t)
    for t in range(1, count):
        line.forward(t)
        if t == 1:
            seq.relay()
    seq.total(o_ref)
    line.finish()
    seq.finish()


def middle(blocks, dy, routes, local_experts, collective):
    shards, _, tokens = routes.shape
    count = shards // 2
    seq_count = blocks.shape[0]
    block = blocks.shape[1:]
    anywhere = pl.BlockSpec(memory_space=ANY)
    vmem = pl.BlockSpec(memory_space=pltpu.VMEM)
    return pl.pallas_call(
        partial(middle_kernel, count, seq_count, CAP),
        out_shape=[
            jax.ShapeDtypeStruct(block, F32),
            jax.ShapeDtypeStruct((shards,) + dy.shape, dy.dtype),
            jax.ShapeDtypeStruct((shards, local_experts, tokens), jnp.int32),
            jax.ShapeDtypeStruct((shards, tokens, local_experts), jnp.int32),
        ],
        in_specs=[anywhere, anywhere, vmem],
        out_specs=[vmem, pl.BlockSpec(memory_space=pltpu.HBM), vmem, vmem],
        scratch_shapes=seq_scatter_scratch(block, blocks.dtype, seq_count)
        + [pltpu.VMEM(dy.shape, dy.dtype)]
        + line_sems(1, count)
        + [DMA((2,))],
        compiler_params=pltpu.CompilerParams(
            collective_id=collective, has_side_effects=True, vmem_limit_bytes=32 << 20
        ),
        name="middle",
    )(blocks, dy, routes)


def turn_kernel(
    count,
    seq_count,
    x_ref,
    parts_ref,
    left_ref,
    right0,
    right1,
    o_ref,
    sum_ref,
    grad_ref,
    hold,
    send,
    recv,
    one,
    tiles_in,
    held,
    staged,
    outer_sem,
    own,
    sib,
    inbox,
    *sems,
):
    places = where_am_i()
    here = lax.axis_index("seq")
    line = SplitScatter(count, places, parts_ref, (own, sib, inbox), sems)
    grads = OuterGrads(left_ref, (right0, right1), grad_ref, (tiles_in, held, staged, outer_sem), count - 1)
    line.begin_loads()
    take = pltpu.make_async_copy(x_ref, hold, one)
    take.start()
    grads.begin()
    greet(count, places, seq_count)
    rows = SeqGather(seq_count, x_ref, o_ref, send, recv)
    rows.begin()
    line.begin()
    take.wait()
    put = pltpu.make_async_copy(hold, o_ref.at[here], one)
    put.start()

    def after(a, q):
        out = pltpu.make_async_copy(line.view(a, own.at[q]), line.view(a, sum_ref), sems[6].at[a, q])
        out.start()
        out.wait()

    def between(step):
        @pl.when(step == 1)
        def _():
            rows.relay()

        grads.between(step)

    line.run(after, between)
    grads.finish()
    put.wait()
    rows.finish()
    line.finish()


def turn_back(block, parts, expert_in, d_gate, d_up, seq_count, shards, collective):
    count = shards // 2
    part = parts.shape[1:]
    model_width = block.shape[1]
    anywhere = pl.BlockSpec(memory_space=ANY)
    return pl.pallas_call(
        partial(turn_kernel, count, seq_count),
        out_shape=[
            jax.ShapeDtypeStruct((seq_count,) + block.shape, block.dtype),
            jax.ShapeDtypeStruct(part, parts.dtype),
            jax.ShapeDtypeStruct((d_gate.shape[0], model_width, 2 * d_gate.shape[2]), BF),
        ],
        in_specs=[anywhere] * 5,
        out_specs=[anywhere] * 3,
        scratch_shapes=[pltpu.VMEM(block.shape, block.dtype)]
        + seq_gather_sems(seq_count)
        + [DMA]
        + outer_scratch(d_up, 512, 2)
        + [pltpu.VMEM((count,) + part, BF)] * 2
        + [pltpu.VMEM((count + 1,) + part, BF)]
        + [DMA((2, count))] * 7,
        compiler_params=pltpu.CompilerParams(
            collective_id=collective, has_side_effects=True, vmem_limit_bytes=60 << 20
        ),
        cost_estimate=pl.CostEstimate(flops=60_000_000_000, bytes_accessed=200_000_000, transcendentals=0),
        name="turn_back",
    )(block, parts, expert_in, d_gate, d_up)


def half_sign(shape):
    lane = lax.broadcasted_iota(jnp.int32, shape, 1)
    return jnp.where(lane < shape[1] // 2, -1.0, 1.0)


def turn(value):
    return pltpu.roll(value, value.shape[1] // 2, 1)


def block_probs(q_rows, keys, doc_col, doc_row, start, scale_by):
    end = keys.shape[0]
    scores = (
        lax.dot_general(q_rows, keys, (((1,), (1,)), ((), ())), preferred_element_type=F32) * scale_by
    )
    shape = scores.shape
    query_pos = start + lax.broadcasted_iota(jnp.int32, shape, 0)
    key_pos = lax.broadcasted_iota(jnp.int32, shape, 1)
    allowed = (doc_col == doc_row) & (key_pos <= query_pos)
    scores = jnp.where(allowed, scores, MASKED_OUT)
    weights = jnp.exp(scores - jnp.max(scores, axis=-1, keepdims=True))
    return weights * (1.0 / jnp.sum(weights, axis=-1, keepdims=True))


class SeqSum:
    def __init__(self, seq_count, sheet, inbox, send, recv):
        here = lax.axis_index("seq")
        self.sheet, self.inbox = sheet, inbox
        self.copies = []
        for d in range(1, seq_count):
            peer = lax.rem(here + d, seq_count)
            self.copies.append(remote(sheet, inbox.at[d - 1], send.at[d - 1], recv.at[d - 1], seq=peer))

    def begin(self):
        for copy in self.copies:
            copy.start()

    def total(self):
        for copy in self.copies:
            copy.wait_recv()
        total = self.sheet[...]
        for d in range(len(self.copies)):
            total += self.inbox[d]
        for copy in self.copies:
            copy.wait_send()
        return total


def attend_kernel(
    seq_count,
    row_block,
    model_width,
    q_raw,
    k_raw,
    v_ref,
    squares,
    gq,
    gk,
    cos,
    sin,
    doc_col,
    doc_row,
    o_ref,
    q_out,
    k_out,
    scales,
    inbox,
    send,
    recv,
):
    seq_len = q_raw.shape[0]

    @pl.when(pl.program_id(0) == 0)
    def _():
        greet_seq(seq_count)
        sums = SeqSum(seq_count, squares, inbox, send, recv)
        sums.begin()
        scales[...] = lax.rsqrt(sums.total() / model_width + EPSILON).T

    sign = half_sign(cos.shape)

    def rotated(raw, lane, gain):
        value = raw[...] * scales[:, lane : lane + 1] * gain[...]
        return (value * cos[...] + turn(value) * (sin[...] * sign)).astype(BF)

    q_out[...] = rotated(q_raw, 0, gq)
    k_out[...] = rotated(k_raw, 1, gk)
    scale_by = HEAD ** (-0.5)
    for start in range(0, seq_len, row_block):
        end = start + row_block
        probs = block_probs(
            q_out[start:end, :], k_out[:end, :], doc_col[start:end, :], doc_row[:, :end], start, scale_by
        )
        o_ref[start:end, :] = jnp.dot(
            probs.astype(BF), v_ref[:end, :], preferred_element_type=F32
        ).astype(BF)


def attend(q_raw, k_raw, values, squares, gq, gk, cos, sin, doc_col, doc_row, model_width, seq_count, collective):
    seq_len, width = q_raw.shape
    head = pl.BlockSpec((seq_len, HEAD), lambda h: (0, h))
    gain = pl.BlockSpec((1, HEAD), lambda h: (0, h))

    def whole(shape):
        return pl.BlockSpec(shape, lambda h: (0, 0))

    out = jax.ShapeDtypeStruct((seq_len, width), BF)
    return pl.pallas_call(
        partial(attend_kernel, seq_count, 256, model_width),
        grid=(width // HEAD,),
        out_shape=[
            out,
            out,
            out,
            jax.ShapeDtypeStruct((seq_len, 8), F32),
        ],
        in_specs=[head, head, head, whole(squares.shape), gain, gain, whole(cos.shape), whole(sin.shape)]
        + [whole(doc_col.shape), whole(doc_row.shape)],
        out_specs=[head, head, head, whole((seq_len, 8))],
        scratch_shapes=[
            pltpu.VMEM((seq_count - 1,) + squares.shape, F32),
            DMA((seq_count - 1,)),
            DMA((seq_count - 1,)),
        ],
        compiler_params=pltpu.CompilerParams(
            collective_id=collective, has_side_effects=True, vmem_limit_bytes=48 << 20
        ),
        name="attend",
    )(q_raw, k_raw, values, squares, gq, gk, cos, sin, doc_col, doc_row)


def attend_back_kernel(
    count,
    seq_count,
    heads,
    row_block,
    model_width,
    q_low,
    k_low,
    v_ref,
    do_ref,
    q_raw,
    k_raw,
    scales,
    gq,
    gk,
    cos,
    sin,
    doc_col,
    doc_row,
    parts_ref,
    dq_ref,
    dk_ref,
    dv_ref,
    gain_ref,
    sum_ref,
    dq_acc,
    dk_acc,
    dv_acc,
    uq,
    uk,
    dots,
    sheet,
    inbox,
    send,
    recv,
    own,
    sib,
    landed,
    *sems,
):
    seq_len = q_low.shape[0]
    head = pl.program_id(0)
    scale_by = HEAD ** (-0.5)
    places = where_am_i()
    line = LineScatter(count, places, [parts_ref], [0], ([own], [sib], [landed]), sems)

    @pl.when(head == 0)
    def _():
        line.begin_loads()
        greet(count, places, seq_count)
        line.begin()
        dots[...] = jnp.zeros_like(dots)

    dk_acc[...] = jnp.zeros_like(dk_acc)
    dv_acc[...] = jnp.zeros_like(dv_acc)
    for start in range(0, seq_len, row_block):
        end = start + row_block
        rows = slice(start, end)
        probs = block_probs(
            q_low[rows, :], k_low[:end, :], doc_col[rows, :], doc_row[:, :end], start, scale_by
        )
        grad_rows = do_ref[rows, :]
        grad_probs = lax.dot_general(
            grad_rows, v_ref[:end, :], (((1,), (1,)), ((), ())), preferred_element_type=F32
        )
        centre = jnp.sum(probs * grad_probs, axis=-1, keepdims=True)
        grad_scores = (probs * (grad_probs - centre)).astype(BF)
        dq_acc[rows, :] = jnp.dot(grad_scores, k_low[:end, :], preferred_element_type=F32)
        over_rows = (((0,), (0,)), ((), ()))
        dk_acc[:end, :] += lax.dot_general(
            grad_scores, q_low[rows, :], over_rows, preferred_element_type=F32
        )
        dv_acc[:end, :] += lax.dot_general(
            probs.astype(BF), grad_rows, over_rows, preferred_element_type=F32
        )
        if start == row_block:

            @pl.when(head == 0)
            def _():
                line.event(0)

    dv_ref[...] = dv_acc[...].astype(BF)
    sign = half_sign(cos.shape)
    cols = pl.ds(pl.multiple_of(head * HEAD, HEAD), HEAD)
    blocks, _, lanes = gain_ref.shape
    rows = HEAD // blocks

    def unrotated(acc, raw, gain, u_ref, lane):
        low = (acc[...] * scale_by).astype(BF).astype(F32)
        back = low * cos[...] - turn(low * sin[...]) * sign
        value = raw[:, cols]
        grad_gain = jnp.sum(back * value * scales[:, lane : lane + 1], axis=0, keepdims=True)
        u = back * gain[...]
        u_ref[:, cols] = u
        dots[:, lane : lane + 1] += jnp.sum(u * value, axis=1, keepdims=True)
        return grad_gain

    grads = (unrotated(dq_acc, q_raw, gq, uq, 0), unrotated(dk_acc, k_raw, gk, uk, 1))
    which = lax.broadcasted_iota(jnp.int32, (8, lanes), 0)
    both = jnp.where(which == 0, grads[0], jnp.where(which == 1, grads[1], 0.0))
    for block in range(blocks):
        gain_ref[block] = both if block == 0 else pltpu.roll(both, lanes - block * rows, 1)

    for step in range(1, count - 1):

        @pl.when(head == min(step, heads - 1))
        def _():
            line.event(step)

    @pl.when(head == heads - 1)
    def _():
        sheet[...] = dots[...].T
        sums = SeqSum(seq_count, sheet, inbox, send, recv)
        sums.begin()
        dots[...] = sums.total().T / model_width
        strip = 128

        @pl.loop(0, seq_len // strip)
        def _(n):
            part = pl.ds(pl.multiple_of(n * strip, strip), strip)
            for lane, u_ref, raw, out in ((0, uq, q_raw, dq_ref), (1, uk, k_raw, dk_ref)):
                scale = scales[part, lane : lane + 1]
                product = dots[part, lane : lane + 1]
                out[part, :] = (
                    scale * u_ref[part, :] - raw[part, :] * (scale * scale * scale * product)
                ).astype(BF)

        def after(a, q):
            out = pltpu.make_async_copy(own.at[q], sum_ref, sems[6].at[0, q])
            out.start()
            out.wait()

        line.final(after)
        line.finish()


def attend_back(
    q_low,
    k_low,
    values,
    d_heads,
    q_raw,
    k_raw,
    scales,
    gq,
    gk,
    cos,
    sin,
    doc_col,
    doc_row,
    parts,
    rows,
    model_width,
    seq_count,
    collective,
):
    seq_len, width = q_raw.shape
    heads = width // HEAD
    blocks = HEAD // rows
    shards = parts.shape[0]
    count = shards // 2
    part = parts.shape[1:]
    head = pl.BlockSpec((seq_len, HEAD), lambda h: (0, h))
    gain = pl.BlockSpec((1, HEAD), lambda h: (0, h))

    def whole(shape):
        return pl.BlockSpec(shape, lambda h: (0, 0))

    def once(x):
        return pl.BlockSpec(x.shape, lambda h: (0, 0), pipeline_mode=pl.Buffered(1))

    out = jax.ShapeDtypeStruct((seq_len, width), BF)
    return pl.pallas_call(
        partial(attend_back_kernel, count, seq_count, heads, 256, model_width),
        grid=(heads,),
        out_shape=[
            out,
            out,
            out,
            jax.ShapeDtypeStruct((width // rows, 8, HEAD), F32),
            jax.ShapeDtypeStruct(part, BF),
        ],
        in_specs=[head] * 4
        + [once(q_raw), once(k_raw), once(scales), gain, gain, once(cos), once(sin)]
        + [once(doc_col), once(doc_row), pl.BlockSpec(memory_space=ANY)],
        out_specs=[
            whole((seq_len, width)),
            whole((seq_len, width)),
            head,
            pl.BlockSpec((blocks, 8, HEAD), lambda h: (h, 0, 0)),
            pl.BlockSpec(memory_space=ANY),
        ],
        scratch_shapes=[pltpu.VMEM((seq_len, HEAD), F32)] * 3
        + [pltpu.VMEM((seq_len, width), F32)] * 2
        + [
            pltpu.VMEM((seq_len, 8), F32),
            pltpu.VMEM((8, seq_len), F32),
            pltpu.VMEM((seq_count - 1, 8, seq_len), F32),
            DMA((seq_count - 1,)),
            DMA((seq_count - 1,)),
        ]
        + [pltpu.VMEM((count,) + part, BF)] * 2
        + [pltpu.VMEM((count + 1,) + part, BF)]
        + [DMA((1, count))] * 7,
        compiler_params=pltpu.CompilerParams(
            collective_id=collective, has_side_effects=True, vmem_limit_bytes=60 << 20
        ),
        name="attend_back",
    )(q_low, k_low, values, d_heads, q_raw, k_raw, scales, gq, gk, cos, sin, doc_col, doc_row, parts)


def experts_in_kernel(
    count,
    cap,
    h2_ref,
    dy_ref,
    targets,
    router_t,
    wgu_ref,
    h2_out,
    x_out,
    y_out,
    act_out,
    by_up_out,
    by_gate_out,
    gate_slots,
    probs_out,
    h2,
    wgu,
    dy,
    xs,
    ys,
    acts,
    by_up,
    by_gate,
    s0,
    s1,
    s2,
    recv,
    w_sem,
    dy_sem,
    h_sem,
    out_sem,
):
    places = where_am_i()
    i, p, sib = places
    local_experts, model_width, hidden = wgu_ref.shape
    hidden = hidden // 2
    tokens = h2_ref.shape[0]
    experts = router_t.shape[0]
    own_in = pltpu.make_async_copy(h2_ref, h2.at[i], h_sem.at[0])
    own_in.start()

    def fetch(q, buf):
        src = dy_ref.at[pl.ds(2 * q, 2)]
        return pltpu.make_async_copy(src, dy.at[buf], dy_sem.at[buf])

    fetch(p, 0).start()
    for e in range(local_experts):
        pltpu.make_async_copy(wgu_ref.at[e], wgu.at[e], w_sem.at[e]).start()
    greet(count, places)
    own_in.wait()
    line = LineGather(count, places, [h2], [0], s0, s1, s2, recv)
    line.first(0)
    staged = ((xs, x_out), (ys, y_out), (acts, act_out), (by_up, by_up_out), (by_gate, by_gate_out))

    def store(n, e, q):
        rows = pl.ds(pl.multiple_of(q * 2 * cap, 2 * cap), 2 * cap)
        return pltpu.make_async_copy(staged[n][0].at[e], staged[n][1].at[e, rows], out_sem.at[n, e])

    def keep(q):
        src = h2.at[pl.ds(2 * q, 2)]
        return pltpu.make_async_copy(src, h2_out.at[pl.ds(2 * q, 2)], h_sem.at[1])

    slot_rows = lax.broadcasted_iota(jnp.int32, (local_experts * cap, tokens), 0)
    expert_rows = lax.broadcasted_iota(jnp.int32, (experts, tokens), 0)

    @pl.loop(0, count)
    def _(k):
        q = chunk_order(k, p, count)
        buf = k % 2

        @pl.when(k > 0)
        def _():
            line.forward(k)

        line.copy(0, 2 * q + lax.rem(sib, 2), 2, 0, sib).wait_recv()
        fetch(q, buf).wait()

        @pl.when(k + 1 < count)
        def _():
            fetch(chunk_order(k + 1, p, count), 1 - buf).start()

        @pl.when(k > 0)
        def _():
            for n in range(5):
                for e in range(local_experts):
                    store(n, e, q).wait()
            keep(q).wait()

        keep(q).start()
        picks = []
        for j in range(2):
            slot = 2 * q + j
            tokens_j = h2[slot]
            logits = lax.dot_general(
                router_t[...], tokens_j, (((1,), (1,)), ((), ())), preferred_element_type=F32
            )
            shifted = jnp.exp(logits - jnp.max(logits, axis=0, keepdims=True))
            probs = shifted / jnp.sum(shifted, axis=0, keepdims=True)
            probs_out[slot] = probs
            pick = None
            for e in range(local_experts):
                mask = slot_rows == targets[slot, e : e + 1, :]
                gate = jnp.sum(
                    jnp.where(expert_rows == i * local_experts + e, probs, 0.0), axis=0, keepdims=True
                )
                part = slice(e * cap, (e + 1) * cap)
                gate_slots[e, q, j * cap : (j + 1) * cap, :] = jnp.sum(
                    jnp.where(mask[part], gate, 0.0), axis=1, keepdims=True
                )
                pick = mask if pick is None else pick | mask
            picks.append(jnp.where(pick, 1.0, 0.0).astype(BF))

        block = 512

        @pl.loop(0, model_width // block)
        def _(n):
            cols = pl.ds(pl.multiple_of(n * block, block), block)
            for source, target in ((0, xs), (1, ys)):
                got = []
                for j in range(2):
                    rows = h2[2 * q + j, :, cols] if source == 0 else dy[buf, j, :, cols]
                    got.append(jnp.dot(picks[j], rows, preferred_element_type=F32))
                for e in range(local_experts):
                    part = slice(e * cap, (e + 1) * cap)
                    target[e, :, cols] = jnp.concatenate([got[0][part], got[1][part]], axis=0).astype(BF)

        for e in range(local_experts):
            store(0, e, q).start()
            store(1, e, q).start()

            @pl.when(k == 0)
            def _():
                pltpu.make_async_copy(wgu_ref.at[e], wgu.at[e], w_sem.at[e]).wait()

            wide = 256

            @pl.loop(0, hidden // wide)
            def _(n):
                cols = pl.ds(pl.multiple_of(n * wide, wide), wide)
                beyond = pl.ds(pl.multiple_of(hidden + n * wide, wide), wide)
                gate = jnp.dot(xs[e], wgu[e, :, cols], preferred_element_type=F32)
                up = jnp.dot(xs[e], wgu[e, :, beyond], preferred_element_type=F32)
                sigmoid = 1.0 / (1.0 + jnp.exp(-gate))
                silu = gate * sigmoid
                acts[e, :, cols] = (silu * up).astype(BF)
                by_up[e, :, cols] = silu.astype(BF)
                by_gate[e, :, cols] = (up * sigmoid * (1.0 + gate * (1.0 - sigmoid))).astype(BF)

            for n in (2, 3, 4):
                store(n, e, q).start()

    for n in range(5):
        for e in range(local_experts):
            store(n, e, 0).wait()
    keep(0).wait()
    sends_done(line)


def sends_done(line):
    i, p, sib = line.places
    count = line.count
    line.copy(0, i, 2, 0, sib).wait_send()

    @pl.when(p < count - 1)
    def _():
        line.copy(0, i, 0, 0, i + 2).wait_send()

    @pl.when(p > 0)
    def _():
        line.copy(0, i, 1, 0, i - 2).wait_send()

    for t in range(1, count):

        @pl.when(p - t >= 0)
        def _():
            slot = i - 2 * t

            @pl.when(p < count - 1)
            def _():
                line.copy(0, slot, 0, t, i + 2).wait_send()

            line.copy(0, slot, 2, t, sib).wait_send()

        @pl.when(p + t < count)
        def _():
            slot = i + 2 * t

            @pl.when(p > 0)
            def _():
                line.copy(0, slot, 1, t, i - 2).wait_send()

            line.copy(0, slot, 2, count + t, sib).wait_send()


def experts_in(h2, dy_all, targets, router_t, w_gate_up, collective):
    shards, tokens, model_width = dy_all.shape
    local_experts, _, hidden = w_gate_up.shape
    hidden = hidden // 2
    experts = router_t.shape[0]
    count = shards // 2
    wide = jax.ShapeDtypeStruct((local_experts, count * 2 * CAP, model_width), BF)
    thin = jax.ShapeDtypeStruct((local_experts, count * 2 * CAP, hidden), BF)
    anywhere = pl.BlockSpec(memory_space=ANY)
    vmem = pl.BlockSpec(memory_space=pltpu.VMEM)
    return pl.pallas_call(
        partial(experts_in_kernel, count, CAP),
        out_shape=[
            jax.ShapeDtypeStruct((shards, tokens, model_width), BF),
            wide,
            wide,
            thin,
            thin,
            thin,
            jax.ShapeDtypeStruct((local_experts, count, 2 * CAP, 1), F32),
            jax.ShapeDtypeStruct((shards, experts, tokens), F32),
        ],
        in_specs=[anywhere, anywhere, vmem, vmem, anywhere],
        out_specs=[anywhere] * 6 + [vmem, vmem],
        scratch_shapes=[
            pltpu.VMEM((shards, tokens, model_width), BF),
            pltpu.VMEM(w_gate_up.shape, BF),
            pltpu.VMEM((2, 2, tokens, model_width), BF),
        ]
        + [pltpu.VMEM((local_experts, 2 * CAP, model_width), BF)] * 2
        + [pltpu.VMEM((local_experts, 2 * CAP, hidden), BF)] * 3
        + line_sems(1, count)
        + [DMA((local_experts,)), DMA((2,)), DMA((2,)), DMA((5, local_experts))],
        compiler_params=pltpu.CompilerParams(
            collective_id=collective, has_side_effects=True, vmem_limit_bytes=60 << 20
        ),
        name="experts_in",
    )(h2, dy_all, targets, router_t, w_gate_up)


def experts_mid_kernel(
    cap,
    y_in,
    act_in,
    by_up_in,
    by_gate_in,
    gate_slots,
    wd_in,
    gated_out,
    d_gate_out,
    d_up_out,
    dots_ref,
    g_down_out,
    wd,
    ys,
    acts,
    by_ups,
    by_gates,
    gated,
    d_gate,
    d_up,
    staged,
    in_sem,
    out_sem,
    grad_sem,
):
    local_experts, hidden, model_width = wd_in.shape
    count = gate_slots.shape[1]
    slots = ys.shape[1]
    over_lanes = (((1,), (1,)), ((), ()))
    over_rows = (((0,), (0,)), ((), ()))
    inputs = ((y_in, ys), (wd_in, wd), (act_in, acts), (by_up_in, by_ups), (by_gate_in, by_gates))
    results = ((gated, gated_out), (d_gate, d_gate_out), (d_up, d_up_out))
    wide = 256
    tile = staged.shape[1]

    def fetch(n, e):
        return pltpu.make_async_copy(inputs[n][0].at[e], inputs[n][1].at[e], in_sem.at[n, e])

    def store(n, e):
        return pltpu.make_async_copy(results[n][0].at[e], results[n][1].at[e], out_sem.at[n, e])

    def put_grad(e, n, buf):
        rows = pl.ds(pl.multiple_of(n * tile, tile), tile)
        return pltpu.make_async_copy(staged.at[buf], g_down_out.at[e, rows], grad_sem.at[buf])

    for e in range(local_experts):
        for n in range(5):
            fetch(n, e).start()
    for e in range(local_experts):
        for n in range(2):
            fetch(n, e).wait()
        gate = jnp.concatenate([gate_slots[e, q] for q in range(count)], axis=0)

        def step(n, dot):
            cols = pl.ds(pl.multiple_of(n * wide, wide), wide)
            grad_act = lax.dot_general(ys[e], wd[e, cols, :], over_lanes, preferred_element_type=F32)

            @pl.when(n == 0)
            def _():
                for kind in range(2, 5):
                    fetch(kind, e).wait()

            act = acts[e, :, cols].astype(F32)
            dot = dot + jnp.sum(act * grad_act, axis=1, keepdims=True)
            grad_act = grad_act * gate
            gated[e, :, cols] = (act * gate).astype(BF)
            d_up[e, :, cols] = (grad_act * by_ups[e, :, cols].astype(F32)).astype(BF)
            d_gate[e, :, cols] = (grad_act * by_gates[e, :, cols].astype(F32)).astype(BF)
            return dot

        dot = lax.fori_loop(0, hidden // wide, step, jnp.zeros((slots, 1), F32))
        for q in range(count):
            dots_ref[e, q] = dot[2 * cap * q : 2 * cap * (q + 1)]
        for n in range(3):
            store(n, e).start()

        @pl.loop(0, hidden // tile // 2)
        def _(m):
            for buf in range(2):
                n = 2 * m + buf

                def wait_last():
                    put_grad(e, n, buf).wait()

                if e > 0:
                    wait_last()
                else:
                    pl.when(m > 0)(wait_last)
                cols = pl.ds(pl.multiple_of(n * tile, tile), tile)
                staged[buf] = lax.dot_general(
                    gated[e, :, cols], ys[e], over_rows, preferred_element_type=F32
                ).astype(BF)
                put_grad(e, n, buf).start()

    for buf in range(2):
        put_grad(0, 0, buf).wait()
    for e in range(local_experts):
        for n in range(3):
            store(n, e).wait()


def experts_mid(grads, act, by_up, by_gate, gate_slots, w_down):
    local_experts, slots, model_width = grads.shape
    anywhere = pl.BlockSpec(memory_space=ANY)
    vmem = pl.BlockSpec(memory_space=pltpu.VMEM)
    thin = jax.ShapeDtypeStruct(act.shape, BF)
    return pl.pallas_call(
        partial(experts_mid_kernel, CAP),
        out_shape=[
            thin,
            thin,
            thin,
            jax.ShapeDtypeStruct(gate_slots.shape, F32),
            jax.ShapeDtypeStruct(w_down.shape, BF),
        ],
        in_specs=[anywhere] * 4 + [vmem, anywhere],
        out_specs=[anywhere] * 3 + [vmem, anywhere],
        scratch_shapes=[pltpu.VMEM(w_down.shape, BF), pltpu.VMEM(grads.shape, BF)]
        + [pltpu.VMEM(act.shape, BF)] * 6
        + [
            pltpu.VMEM((2, 256, model_width), BF),
            DMA((5, local_experts)),
            DMA((3, local_experts)),
            DMA((2,)),
        ],
        compiler_params=pltpu.CompilerParams(vmem_limit_bytes=60 << 20),
        cost_estimate=pl.CostEstimate(flops=18_000_000_000, bytes_accessed=60_000_000, transcendentals=0),
        name="experts_mid",
    )(grads, act, by_up, by_gate, gate_slots, w_down)


class StagedScatter(SplitScatter):
    def __init__(self, count, places, stage, bufs, sems):
        super().__init__(count, places, None, bufs, sems)
        self.stage = stage

    def to_sib(self, a, q):
        sib = self.places[2]
        src, dst = self.view(a, self.stage), self.view(a, self.sib[a].at[q])
        return remote(src, dst, self.sems[2].at[a, q], self.sems[5].at[a, q], fsdp=sib)

    def ready(self, a, q):
        self.to_sib(a, q).wait_recv()

    def finish(self):
        i, p, sib = self.places
        for a in range(2):
            for q in range(self.count):

                @pl.when(q > p)
                def _():
                    self.right(a, q).wait_send()

                @pl.when(q < p)
                def _():
                    self.left(a, q).wait_send()


class OuterGrads:
    def __init__(self, left, rights, out, scratch, steps):
        self.left, self.rights, self.out = left, rights, out
        self.tiles_in, self.held, self.staged, self.sems = scratch
        self.experts, self.width, _ = out.shape
        self.hidden = rights[0].shape[2]
        self.tile = self.staged.shape[1]
        self.tiles = self.width // self.tile
        self.units = self.experts * self.tiles
        self.share = -(-self.units // steps)

    def span(self, u):
        start = lax.rem(u, self.tiles) * self.tile
        return pl.ds(pl.multiple_of(start, self.tile), self.tile)

    def fetch(self, u):
        src = self.left.at[u // self.tiles, :, self.span(u)]
        return pltpu.make_async_copy(src, self.tiles_in.at[lax.rem(u, 2)], self.sems.at[0, lax.rem(u, 2)])

    def put(self, u):
        buf = lax.rem(u, 2)
        target = self.out.at[u // self.tiles, self.span(u)]
        return pltpu.make_async_copy(self.staged.at[buf], target, self.sems.at[1, buf])

    def hold(self, n):
        return pltpu.make_async_copy(self.rights[n], self.held.at[n], self.sems.at[2, n])

    def begin(self):
        for n in range(len(self.rights)):
            self.hold(n).start()
        self.fetch(0).start()

    def between(self, step):
        @pl.loop(step * self.share, jnp.minimum((step + 1) * self.share, self.units))
        def _(u):
            @pl.when(u == 0)
            def _():
                for n in range(len(self.rights)):
                    self.hold(n).wait()

            self.fetch(u).wait()

            @pl.when(u + 1 < self.units)
            def _():
                self.fetch(u + 1).start()

            @pl.when(u >= 2)
            def _():
                self.put(u - 2).wait()

            buf = lax.rem(u, 2)
            for n in range(len(self.rights)):
                self.staged[buf, :, n * self.hidden : (n + 1) * self.hidden] = lax.dot_general(
                    self.tiles_in[buf],
                    self.held[n, u // self.tiles],
                    (((0,), (0,)), ((), ())),
                    preferred_element_type=F32,
                ).astype(BF)
            self.put(u).start()

    def finish(self):
        self.put(self.units - 2).wait()
        self.put(self.units - 1).wait()


def outer_scratch(right, tile, factors):
    slots, hidden = right.shape[1:]
    return [
        pltpu.VMEM((2, slots, tile), BF),
        pltpu.VMEM((factors,) + right.shape, BF),
        pltpu.VMEM((2, tile, factors * hidden), BF),
        DMA((3, 2)),
    ]


def experts_out_kernel(
    count,
    cap,
    gated_in,
    d_gate_in,
    d_up_in,
    dots,
    targets,
    targets_t,
    probs_ref,
    router_t,
    wgu_in,
    wd_in,
    tokens_in,
    x_in,
    dy_in,
    gain_row,
    parts_a,
    parts_b,
    grad_ref,
    low_ref,
    small_ref,
    wgu,
    wd,
    gated,
    d_gate,
    d_up,
    parts,
    stage,
    own,
    sibling,
    inbox,
    w_sem,
    in_sem,
    part_sem,
    held_tokens,
    x_mid,
    dy,
    router_sum,
    row_sem,
    *sems,
):
    places = where_am_i()
    i, p, sib = places
    core = lax.rem(i, 2)
    local_experts, hidden, model_width = wd_in.shape
    tokens = targets.shape[2]
    experts = router_t.shape[0]
    first = i * local_experts
    over_lanes = (((1,), (1,)), ((), ()))
    line = StagedScatter(count, places, stage, (own, sibling, inbox), sems)
    weights = ((wgu_in, wgu), (wd_in, wd))
    inputs = ((gated_in, gated), (d_gate_in, d_gate), (d_up_in, d_up))

    def weight(n):
        return pltpu.make_async_copy(weights[n][0], weights[n][1], w_sem.at[n])

    def fetch(n, q, buf):
        rows = pl.ds(pl.multiple_of(q * 2 * cap, 2 * cap), 2 * cap)
        return pltpu.make_async_copy(inputs[n][0].at[:, rows], inputs[n][1].at[buf], in_sem.at[n, buf])

    first_part = parts_a.shape[2]

    def put(n, q):
        src = parts.at[:, :, pl.ds(n * first_part, (parts_a, parts_b)[n].shape[2])]
        return pltpu.make_async_copy(src, (parts_a, parts_b)[n].at[pl.ds(2 * q, 2)], part_sem.at[n])

    def order(k):
        return chunk_order(count - 1 - k, p, count)

    for n in range(3):
        fetch(n, order(0), 0).start()
    for n in range(2):
        weight(n).start()
    take_x = pltpu.make_async_copy(x_in, x_mid, row_sem.at[0])
    take_dy = pltpu.make_async_copy(dy_in, dy, row_sem.at[1])
    take_x.start()
    take_dy.start()
    router_sum[...] = jnp.zeros_like(router_sum)
    greet(count, places)
    slot_rows = lax.broadcasted_iota(jnp.int32, (local_experts * cap, tokens), 0)
    slot_lanes = lax.broadcasted_iota(jnp.int32, (tokens, local_experts * cap), 1)
    expert_rows = lax.broadcasted_iota(jnp.int32, (experts, tokens), 0)

    def take_tokens(q):
        return pltpu.make_async_copy(tokens_in.at[pl.ds(2 * q, 2)], held_tokens, row_sem.at[2])

    def compute(k):
        q = order(k)
        buf = lax.rem(k, 2)
        take_tokens(q).start()
        picks, logits_low, logits_row = [], [], []
        for j in range(2):
            slot = 2 * q + j
            grad_probs = jnp.zeros((experts, tokens), F32)
            pick = None
            for e in range(local_experts):
                part = slice(e * cap, (e + 1) * cap)
                mask = (slot_rows == targets[slot, e : e + 1, :])[part]
                dot = dots[e, q, j * cap : (j + 1) * cap, :]
                row = jnp.sum(jnp.where(mask, dot, 0.0), axis=0, keepdims=True)
                grad_probs = jnp.where(expert_rows == first + e, row, grad_probs)
                hit = slot_lanes == targets_t[slot, :, e : e + 1]
                pick = hit if pick is None else pick | hit
            probs = probs_ref[slot]
            grad_logits = probs * (grad_probs - jnp.sum(probs * grad_probs, axis=0, keepdims=True))
            logits_row.append(grad_logits.astype(BF))
            picks.append(jnp.where(pick, 1.0, 0.0).astype(BF))
            logits_low.append(grad_logits.T.astype(BF))
        for n in range(3):
            fetch(n, q, buf).wait()

        @pl.when(k + 1 < count)
        def _():
            for n in range(3):
                fetch(n, order(k + 1), 1 - buf).start()

        @pl.when(k > 0)
        def _():
            line.to_sib(0, order(k - 1)).wait_send()
            line.to_sib(1, order(k - 1)).wait_send()

        @pl.when(k == 0)
        def _():
            weight(0).wait()

        block = 512

        @pl.loop(0, model_width // block)
        def _(n):
            cols = pl.ds(pl.multiple_of(n * block, block), block)
            grads = []
            for e in range(local_experts):
                grads.append(
                    lax.dot_general(
                        d_gate[buf, e], wgu[e, cols, 0:hidden], over_lanes, preferred_element_type=F32
                    )
                    + lax.dot_general(
                        d_up[buf, e], wgu[e, cols, hidden:], over_lanes, preferred_element_type=F32
                    )
                )
            for j in range(2):
                part = slice(j * cap, (j + 1) * cap)
                back = jnp.concatenate([value[part] for value in grads], axis=0).astype(BF)
                total = (
                    jnp.dot(picks[j], back, preferred_element_type=F32)
                    + jnp.dot(logits_low[j], router_t[:, cols], preferred_element_type=F32)
                ).astype(BF)

                @pl.when(core == j)
                def _():
                    own[q, :, cols] = total

                @pl.when(core != j)
                def _():
                    stage[:, cols] = total

            @pl.when(n == model_width // block // 2 - 1)
            def _():
                line.to_sib(0, q).start()

        line.to_sib(1, q).start()

        @pl.when(k > 0)
        def _():
            put(0, q).wait()
            put(1, q).wait()

        @pl.when(k == 0)
        def _():
            weight(1).wait()

        take_tokens(q).wait()

        @pl.loop(0, model_width // block)
        def _(n):
            cols = pl.ds(pl.multiple_of(n * block, block), block)
            outs = []
            for e in range(local_experts):
                outs.append(jnp.dot(gated[buf, e], wd[e, :, cols], preferred_element_type=F32))
            for j in range(2):
                part = slice(j * cap, (j + 1) * cap)
                mine = jnp.concatenate([value[part] for value in outs], axis=0).astype(BF)
                parts[j, :, cols] = jnp.dot(picks[j], mine, preferred_element_type=F32).astype(BF)
            total = router_sum[:, cols]
            for j in range(2):
                total += jnp.dot(logits_row[j], held_tokens[j, :, cols], preferred_element_type=F32)
            router_sum[:, cols] = total

        put(0, q).start()
        put(1, q).start()

    @pl.loop(0, 1)
    def _(k):
        compute(k)

    line.run(lambda a, q: None, lambda step: compute(step + 1))
    put(0, 0).wait()
    put(1, 0).wait()
    line.to_sib(0, order(count - 1)).wait_send()
    line.to_sib(1, order(count - 1)).wait_send()
    take_x.wait()
    take_dy.wait()
    strip = 16

    def norm_back(n, total):
        rows = pl.ds(pl.multiple_of(n * strip, strip), strip)
        back = own[p, rows, :].astype(F32)
        x = x_mid[rows, :]
        scale = lax.rsqrt(jnp.mean(x * x, axis=1, keepdims=True) + EPSILON)
        u = gain_row[...] * back
        product = jnp.mean(u * x, axis=1, keepdims=True)
        grad = dy[rows, :].astype(F32) + scale * u - x * (scale * scale * scale * product)
        grad_ref[rows, :] = grad
        low_ref[rows, :] = grad.astype(BF)
        return total + jnp.sum(back * x * scale, axis=0, keepdims=True)

    norm_part = lax.fori_loop(0, tokens // strip, norm_back, jnp.zeros((1, model_width), F32))
    lanes = small_ref.shape[1]
    piece = 512
    for n in range(model_width // piece):
        cols = slice(n * piece, (n + 1) * piece)
        norm = jnp.broadcast_to(norm_part[:, cols], (8, piece))
        rest = jnp.zeros((lanes - experts - 8, piece), F32)
        small_ref[cols, :] = jnp.concatenate([router_sum[:, cols], norm, rest], axis=0).T

    line.finish()


def experts_out(
    gated,
    d_gate,
    d_up,
    dots,
    targets,
    targets_t,
    probs,
    router_t,
    w_gate_up,
    w_down,
    h2_all,
    x_mid,
    dy,
    gain_row,
    collective,
):
    local_experts, slots, hidden = gated.shape
    model_width = router_t.shape[1]
    shards, experts, tokens = probs.shape
    count = shards // 2
    anywhere = pl.BlockSpec(memory_space=ANY)
    vmem = pl.BlockSpec(memory_space=pltpu.VMEM)
    return pl.pallas_call(
        partial(experts_out_kernel, count, CAP),
        out_shape=[
            jax.ShapeDtypeStruct((shards, tokens, model_width // 2), BF),
            jax.ShapeDtypeStruct((shards, tokens, model_width // 2), BF),
            jax.ShapeDtypeStruct((tokens, model_width), F32),
            jax.ShapeDtypeStruct((tokens, model_width), BF),
            jax.ShapeDtypeStruct((model_width, 128), F32),
        ],
        in_specs=[anywhere] * 3 + [vmem] * 5 + [anywhere] * 5 + [vmem],
        out_specs=[anywhere, anywhere, vmem, vmem, vmem],
        scratch_shapes=[pltpu.VMEM(x.shape, BF) for x in (w_gate_up, w_down)]
        + [pltpu.VMEM((2, local_experts, 2 * CAP, hidden), BF)] * 3
        + [
            pltpu.VMEM((2, tokens, model_width), BF),
            pltpu.VMEM((tokens, model_width), BF),
            pltpu.VMEM((count, tokens, model_width), BF),
            pltpu.VMEM((count, tokens, model_width), BF),
            pltpu.VMEM((count + 1, tokens, model_width), BF),
            DMA((2,)),
            DMA((3, 2)),
            DMA((2,)),
            pltpu.VMEM((2, tokens, model_width), BF),
            pltpu.VMEM((tokens, model_width), F32),
            pltpu.VMEM((tokens, model_width), BF),
            pltpu.VMEM((experts, model_width), F32),
            DMA((3,)),
        ]
        + [DMA((2, count))] * 7,
        compiler_params=pltpu.CompilerParams(
            collective_id=collective, has_side_effects=True, vmem_limit_bytes=67_043_328
        ),
        cost_estimate=pl.CostEstimate(flops=60_000_000_000, bytes_accessed=200_000_000, transcendentals=0),
        name="experts_out",
    )(
        gated,
        d_gate,
        d_up,
        dots,
        targets,
        targets_t,
        probs,
        router_t,
        w_gate_up,
        w_down,
        h2_all,
        x_mid,
        dy,
        gain_row,
    )


def rope_tables(seq_len, head_dim):
    half_dim = head_dim // 2
    inverse = np.float32(ROPE_BASE) ** (-(np.arange(half_dim, dtype=np.float32) * 2.0 / head_dim))
    angles = np.arange(seq_len, dtype=np.float32)[:, None] * inverse.astype(np.float32)[None, :]
    angles = np.concatenate([angles, angles], axis=-1).astype(np.float64)
    return (np.cos(angles).astype(np.float32), np.sin(angles).astype(np.float32))


def dot(left, right, sides=(1, 0), out=F32):
    return lax.dot_general(
        left, right, (((sides[0],), (sides[1],)), ((), ())), preferred_element_type=F32
    ).astype(out)


def inverse_rms(rows):
    return lax.rsqrt(jnp.mean(rows * rows, axis=-1, keepdims=True) + EPSILON)


def on_device(
    inputs,
    out_grad,
    doc_ids,
    routes,
    w_query,
    w_key,
    w_value,
    w_output,
    w_router,
    attn_gain,
    ffn_gain,
    query_gain,
    key_gain,
    w_gate,
    w_up,
    w_down,
):
    seq_count = lax.axis_size("seq")
    shards = lax.axis_size("fsdp")
    tok_rows, model_width = inputs.shape[1:]
    seq_len = tok_rows * seq_count
    rows = w_query.shape[0]
    width = model_width // seq_count
    local_experts = w_gate.shape[0]
    experts = w_router.shape[1]
    top_k = routes.shape[2]
    lanes = 128

    small = jnp.concatenate(
        [
            w_router,
            attn_gain[:, None],
            ffn_gain[:, None],
            jnp.zeros((rows, lanes - experts - 2), BF),
        ],
        axis=1,
    )
    gains = jnp.pad(jnp.stack([query_gain, key_gain]), ((0, 14), (0, lanes - rows)))
    wq, wk, wv, small_all, gains_all, routes_all, wo, x_all = gather_start(
        (w_query, w_key, w_value, small, gains, routes[0].T, w_output, inputs[0]), seq_count, shards, 0
    )
    x_all = x_all.reshape(seq_len, model_width)
    gate_up = jnp.concatenate([w_gate, w_up], axis=2)
    full_gate_up = lax.all_gather(gate_up, "seq", axis=1, tiled=True)
    full_down = lax.all_gather(w_down, "seq", axis=1, tiled=True)

    wq = wq.reshape(model_width, width)
    wk = wk.reshape(model_width, width)
    wv = wv.reshape(model_width, width)
    small_all = small_all.reshape(model_width, lanes)
    w_r = small_all[:, :experts]
    gain_a = small_all[:, experts].astype(F32)
    gain_f = small_all[:, experts + 1].astype(F32)
    gq = gains_all[:, 0, :rows].reshape(1, width).astype(F32)
    gk = gains_all[:, 1, :rows].reshape(1, width).astype(F32)

    x_float = x_all.astype(F32)
    h1 = (x_float * inverse_rms(x_float) * gain_a).astype(BF)
    h1 = lax.optimization_barrier(h1)
    q_raw, k_raw = lax.optimization_barrier((dot(h1, wq), dot(h1, wk)))
    values = dot(h1, wv, out=BF)
    squares = jnp.stack(
        [jnp.sum(q_raw * q_raw, axis=1), jnp.sum(k_raw * k_raw, axis=1)]
        + [jnp.ones((seq_len,), F32)] * 6
    )
    cos, sin = rope_tables(seq_len, HEAD)
    doc_row = doc_ids
    doc_col = doc_ids.reshape(seq_len, 1)
    attended, q_low, k_low, scales = attend(
        q_raw, k_raw, values, squares, gq, gk, cos, sin, doc_col, doc_row, model_width, seq_count, 1
    )
    wo = wo.reshape(width, model_width)
    projected = dot(attended, wo, out=BF).reshape(seq_count, tok_rows, model_width)
    rows_in = inputs[0].astype(F32)
    grad_rows = out_grad[0].astype(F32)
    summed, dy_all, targets, targets_t = middle(projected, out_grad[0], routes_all, local_experts, 2)
    x_mid = rows_in + summed
    scale_f = inverse_rms(x_mid)
    h2 = (x_mid * scale_f * gain_f).astype(BF)

    router_t = w_r.T
    h2_all, expert_in, grad_slots, act, by_up, by_gate, gate_slots, gate_probs = experts_in(
        h2, dy_all, targets, router_t, full_gate_up, 3
    )
    gated, d_gate, d_up, dots_slots, g_down = experts_mid(
        grad_slots, act, by_up, by_gate, gate_slots, full_down
    )
    parts_a, parts_b, grad_mid, grad_low, small_part = experts_out(
        gated,
        d_gate,
        d_up,
        dots_slots,
        targets,
        targets_t,
        gate_probs,
        router_t,
        full_gate_up,
        full_down,
        h2_all,
        x_mid,
        out_grad[0],
        gain_f[None],
        4,
    )

    def spread(part):
        return lax.psum_scatter(part, "seq", scatter_dimension=1, tiled=True)

    g_down = spread(g_down)
    grad_low, g_down = lax.optimization_barrier((grad_low, g_down))

    d_attn, sum_a, g_gate_up = turn_back(grad_low, parts_a, expert_in, d_gate, d_up, seq_count, shards, 5)
    g_gate_up = spread(g_gate_up)
    d_attn = d_attn.reshape(seq_len, model_width)
    d_heads = dot(d_attn, wo, (1, 1), BF)
    dq_low, dk_low, dv_low, gains_part, sum_b = attend_back(
        q_low,
        k_low,
        values,
        d_heads,
        q_raw,
        k_raw,
        scales,
        gq,
        gk,
        cos,
        sin,
        doc_col,
        doc_row,
        parts_b,
        rows,
        model_width,
        seq_count,
        6,
    )
    result = x_mid + jnp.concatenate([sum_a, sum_b], axis=1).astype(F32)

    sheet = (seq_count, shards, rows, width)
    g_query, g_key, g_value, g_output, g_small, g_gains, grad_h1 = scatter_end(
        (
            dot(h1, dq_low, (0, 0), BF).reshape(sheet),
            dot(h1, dk_low, (0, 0), BF).reshape(sheet),
            dot(h1, dv_low, (0, 0), BF).reshape(sheet),
            dot(attended, d_attn, (0, 0), BF).reshape(shards, rows, model_width),
            small_part.reshape(seq_count, shards, rows, lanes),
            gains_part,
        ),
        (dq_low, dk_low, dv_low, wq, wk, wv),
        seq_count,
        shards,
        7,
    )
    g_query, g_key, g_value = (g_query.astype(F32), g_key.astype(F32), g_value.astype(F32))

    scale_a = inverse_rms(rows_in)
    u_rows = gain_a * grad_h1
    input_grad = (
        grad_mid
        + scale_a * u_rows
        - rows_in * scale_a**3 * jnp.mean(u_rows * rows_in, axis=-1, keepdims=True)
    )
    pairs = (
        w_query.astype(F32) * g_query + w_key.astype(F32) * g_key + w_value.astype(F32) * g_value
    )
    g_attn_gain = jnp.sum(pairs, axis=1) / attn_gain.astype(F32)

    return (
        result.astype(BF)[None],
        input_grad[None],
        g_query,
        g_key,
        g_value,
        g_output.astype(F32),
        g_small[:, :experts],
        g_attn_gain,
        g_small[:, experts],
        g_gains[0, :rows],
        g_gains[1, :rows],
        g_gate_up[:, :, : g_gate_up.shape[2] // 2].astype(F32),
        g_gate_up[:, :, g_gate_up.shape[2] // 2 :].astype(F32),
        g_down.astype(F32),
    )


def solution(mesh):
    rows = P("fsdp", "seq", None)
    sheet = P(("seq", "fsdp"), None)
    line = P(("seq", "fsdp"))
    return jax.shard_map(
        on_device,
        mesh=mesh,
        in_specs=(rows, rows, P("fsdp", None), rows) + (sheet,) * 5 + (line,) * 4 + (rows,) * 3,
        out_specs=(rows, rows) + (sheet,) * 5 + (line,) * 4 + (rows,) * 3,
        check_vma=False,
    )
```

```python
from functools import partial

import jax
import jax.numpy as jnp
import numpy as np
from jax import lax
from jax.experimental import pallas as pl
from jax.experimental.pallas import tpu as pltpu
from jax.sharding import PartitionSpec as P

CAP = 136
HEAD = 128
EPSILON = 1e-05
ROPE_BASE = 10000.0
MASKED_OUT = -1e30
ANY = pl.ANY
MESH = pl.DeviceIdType.MESH
DMA = pltpu.SemaphoreType.DMA
BF = jnp.bfloat16
F32 = jnp.float32


def remote(src, dst, send, recv, **where):
    return pltpu.make_async_remote_copy(
        src_ref=src, dst_ref=dst, send_sem=send, recv_sem=recv, device_id=where, device_id_type=MESH
    )


def greet(count, places, seq_count=1):
    i, p, sib = places
    barrier = pltpu.get_barrier_semaphore()
    pl.semaphore_signal(barrier, inc=1, device_id={"fsdp": sib}, device_id_type=MESH)
    here = lax.axis_index("seq")
    for d in range(1, seq_count):
        peer = lax.rem(here + d, seq_count)
        pl.semaphore_signal(barrier, inc=1, device_id={"seq": peer}, device_id_type=MESH)

    @pl.when(p > 0)
    def _():
        pl.semaphore_signal(barrier, inc=1, device_id={"fsdp": i - 2}, device_id_type=MESH)

    @pl.when(p < count - 1)
    def _():
        pl.semaphore_signal(barrier, inc=1, device_id={"fsdp": i + 2}, device_id_type=MESH)

    last = count - 1
    pl.semaphore_wait(barrier, seq_count + (p + last) // count + (last - p + last) // count)


def slot_of(ref, axis, index):
    return ref.at[index] if axis == 0 else ref.at[:, index]


class LineGather:
    def __init__(self, count, places, refs, axes, send_r, send_l, send_s, recv):
        self.count, self.places = count, places
        self.refs, self.axes = refs, axes
        self.sems = (send_r, send_l, send_s, recv)

    def copy(self, a, slot, kind, t, device):
        send = self.sems[kind].at[a, t]
        ref = slot_of(self.refs[a], self.axes[a], slot)
        return remote(ref, ref, send, self.sems[3].at[a, slot], fsdp=device)

    def first(self, a):
        i, p, sib = self.places

        @pl.when(p < self.count - 1)
        def _():
            self.copy(a, i, 0, 0, i + 2).start()

        @pl.when(p > 0)
        def _():
            self.copy(a, i, 1, 0, i - 2).start()

        self.copy(a, i, 2, 0, sib).start()

    def forward(self, t):
        i, p, sib = self.places
        count = self.count
        for a in range(len(self.refs)):

            @pl.when(p - t >= 0)
            def _():
                slot = i - 2 * t
                self.copy(a, slot, 0, t, sib).wait_recv()

                @pl.when(p < count - 1)
                def _():
                    self.copy(a, slot, 0, t, i + 2).start()

                self.copy(a, slot, 2, t, sib).start()

            @pl.when(p + t < count)
            def _():
                slot = i + 2 * t
                self.copy(a, slot, 1, t, sib).wait_recv()

                @pl.when(p > 0)
                def _():
                    self.copy(a, slot, 1, t, i - 2).start()

                self.copy(a, slot, 2, count + t, sib).start()

    def finish(self):
        i, p, sib = self.places
        count = self.count
        for a in range(len(self.refs)):
            for q in range(count):
                self.copy(a, 2 * q + lax.rem(sib, 2), 2, 0, sib).wait_recv()
            self.copy(a, i, 2, 0, sib).wait_send()

            @pl.when(p < count - 1)
            def _():
                self.copy(a, i, 0, 0, i + 2).wait_send()

            @pl.when(p > 0)
            def _():
                self.copy(a, i, 1, 0, i - 2).wait_send()

            for t in range(1, count):

                @pl.when(p - t >= 0)
                def _():
                    slot = i - 2 * t

                    @pl.when(p < count - 1)
                    def _():
                        self.copy(a, slot, 0, t, i + 2).wait_send()

                    self.copy(a, slot, 2, t, sib).wait_send()

                @pl.when(p + t < count)
                def _():
                    slot = i + 2 * t

                    @pl.when(p > 0)
                    def _():
                        self.copy(a, slot, 1, t, i - 2).wait_send()

                    self.copy(a, slot, 2, count + t, sib).wait_send()


def line_sems(arrays, count):
    return [DMA((arrays, count)), DMA((arrays, count)), DMA((arrays, 2 * count)), DMA((arrays, 2 * count))]


def where_am_i():
    i = lax.axis_index("fsdp")
    p = i // 2
    c = i % 2
    return i, p, 2 * p + 1 - c


def start_kernel(count, seq_count, *refs):
    wq, wk, wv, small, gains, routes, wo, rows = refs[:8]
    outs = refs[8:15]
    rows_out = refs[15]
    holds = refs[16:24]
    send_x, recv_x, local, send_r, send_l, send_s, recv, send_y, recv_y = refs[24:]
    places = where_am_i()
    i = places[0]
    here = lax.axis_index("seq")
    width = wq.shape[1] // seq_count

    def columns(ref, peer):
        return ref.at[:, pl.ds(pl.multiple_of(peer * width, width), width)]

    own = [columns(wq, here), columns(wk, here), columns(wv, here), small, gains, routes, wo, rows]
    for a in range(8):
        pltpu.make_async_copy(own[a], holds[a], local.at[a]).start()
    greet(count, places, seq_count)

    def piece(a, d):
        peer = lax.rem(here + d, seq_count)
        src = small if a == 3 else columns((wq, wk, wv)[a], peer)
        return remote(src, outs[a].at[here, i], send_x.at[a, d - 1], recv_x.at[a, d - 1], seq=peer)

    def arrived(a, d):
        origin = lax.rem(here + seq_count - d, seq_count)
        ref = outs[a].at[origin, i]
        return remote(ref, ref, send_x.at[a, d - 1], recv_x.at[a, d - 1], seq=origin)

    for a in (3, 0, 1, 2):
        for d in range(1, seq_count):
            piece(a, d).start()
    gather = SeqGather(seq_count, rows, rows_out, send_y, recv_y)
    gather.begin()
    axes = [1, 1, 1, 1, 0, 0, 0]

    def target(a):
        return outs[a].at[here, i] if axes[a] == 1 else outs[a].at[i]

    for a in (4, 5, 6, 3, 0, 1, 2):
        pltpu.make_async_copy(own[a], holds[a], local.at[a]).wait()
        pltpu.make_async_copy(holds[a], target(a), local.at[a]).start()
    line = LineGather(count, places, outs, axes, send_r, send_l, send_s, recv)
    for a in (4, 5, 6, 3, 0, 1, 2):
        pltpu.make_async_copy(holds[a], target(a), local.at[a]).wait()
        if axes[a] == 1:
            for d in range(1, seq_count):
                arrived(a, d).wait_recv()
        line.first(a)
    pltpu.make_async_copy(rows, holds[7], local.at[7]).wait()
    pltpu.make_async_copy(holds[7], rows_out.at[here], local.at[7]).start()
    for t in range(1, count):
        line.forward(t)
        if t == 1:
            gather.relay()
    line.finish()
    pltpu.make_async_copy(holds[7], rows_out.at[here], local.at[7]).wait()
    gather.finish()
    for a in (3, 0, 1, 2):
        for d in range(1, seq_count):
            piece(a, d).wait_send()


def gather_start(arrays, seq_count, shards, collective):
    count = shards // 2
    wq, wk, wv, small, gains, routes, wo, tokens = arrays
    rows, model_width = wq.shape
    width = model_width // seq_count
    sheet = jax.ShapeDtypeStruct((seq_count, shards, rows, width), BF)
    shapes = [
        sheet,
        sheet,
        sheet,
        jax.ShapeDtypeStruct((seq_count, shards) + small.shape, BF),
        jax.ShapeDtypeStruct((shards,) + gains.shape, BF),
        jax.ShapeDtypeStruct((shards,) + routes.shape, jnp.int32),
        jax.ShapeDtypeStruct((shards,) + wo.shape, BF),
        jax.ShapeDtypeStruct((seq_count,) + tokens.shape, BF),
    ]
    holds = [pltpu.VMEM((rows, width), BF)] * 3 + [
        pltpu.VMEM(small.shape, BF),
        pltpu.VMEM(gains.shape, BF),
        pltpu.VMEM(routes.shape, jnp.int32),
        pltpu.VMEM(wo.shape, BF),
        pltpu.VMEM(tokens.shape, BF),
    ]
    return pl.pallas_call(
        partial(start_kernel, count, seq_count),
        out_shape=shapes,
        in_specs=[pl.BlockSpec(memory_space=ANY)] * 8,
        out_specs=[pl.BlockSpec(memory_space=ANY)] * 8,
        scratch_shapes=holds
        + [DMA((4, seq_count - 1)), DMA((4, seq_count - 1)), DMA((8,))]
        + line_sems(7, count)
        + seq_gather_sems(seq_count),
        compiler_params=pltpu.CompilerParams(collective_id=collective, has_side_effects=True),
        name="gather_start",
    )(*arrays)


def chunk_order(k, p, count):
    near = jnp.minimum(p, count - 1 - p)
    step = (k + 1) // 2
    both = jnp.where(k % 2 == 1, p - step, p + step)
    return jnp.where(k <= 2 * near, both, jnp.where(p < count - 1 - p, k, count - 1 - k))


class LineScatter:
    def __init__(self, count, places, sources, axes, bufs, sems):
        self.count, self.places = count, places
        self.sources, self.axes = sources, axes
        self.own, self.sib, self.inbox = bufs
        self.sems = sems

    def view(self, a, ref):
        return ref

    def load(self, a, q):
        i = self.places[0]
        src = slot_of(self.sources[a], self.axes[a], 2 * q + lax.rem(i, 2))
        return pltpu.make_async_copy(self.view(a, src), self.view(a, self.own[a].at[q]), self.sems[6].at[a, q])

    def to_sib(self, a, q):
        sib = self.places[2]
        src = slot_of(self.sources[a], self.axes[a], 2 * q + lax.rem(sib, 2))
        dst = self.view(a, self.sib[a].at[q])
        return remote(self.view(a, src), dst, self.sems[2].at[a, q], self.sems[5].at[a, q], fsdp=sib)

    def right(self, a, q):
        i = self.places[0]
        src, dst = self.view(a, self.own[a].at[q]), self.view(a, self.inbox[a].at[q])
        return remote(src, dst, self.sems[0].at[a, q], self.sems[3].at[a, q], fsdp=i + 2)

    def left(self, a, q):
        i, p, sib = self.places
        slot = jnp.where(q == p - 1, self.count, q)
        src, dst = self.view(a, self.own[a].at[q]), self.view(a, self.inbox[a].at[slot])
        return remote(src, dst, self.sems[1].at[a, q], self.sems[4].at[a, q], fsdp=i - 2)

    def begin_loads(self):
        for k in range(self.count):
            q = chunk_order(self.count - 1 - k, self.places[1], self.count)
            for a in range(len(self.sources)):
                self.load(a, q).start()

    def begin(self):
        for k in range(self.count):
            q = chunk_order(self.count - 1 - k, self.places[1], self.count)
            for a in range(len(self.sources)):
                self.to_sib(a, q).start()

    def add(self, a, q, others):
        own = self.own[a]
        lead = own.shape[1:-2]
        rows, width = own.shape[-2:]
        step = rows
        while step * width > 65536 and step % 16 == 0:
            step //= 2

        def strip(index):
            total = own[index].astype(F32) + self.sib[a][index].astype(F32)
            for slot in others:
                total += self.inbox[a][(slot,) + index[1:]].astype(F32)
            own[index] = total.astype(own.dtype)

        def rows_of(prefix):
            if step == rows:
                strip(prefix)
                return

            @pl.loop(0, rows // step)
            def _(k):
                strip(prefix + (pl.ds(pl.multiple_of(k * step, step), step),))

        if lead:
            for b in range(lead[0]):
                rows_of((q, b))
        else:
            rows_of((q,))

    def ready(self, a, q):
        self.load(a, q).wait()
        self.to_sib(a, q).wait_recv()

    def event(self, step):
        i, p, sib = self.places
        count = self.count
        arrays = range(len(self.sources))

        @pl.when(step >= p)
        def _():
            q = count - 1 - (step - p)
            for a in arrays:
                self.ready(a, q)

                @pl.when(p > 0)
                def _():
                    self.right(a, q).wait_recv()
                    self.add(a, q, [q])

                @pl.when(p == 0)
                def _():
                    self.add(a, q, [])

                self.right(a, q).start()

        @pl.when(step >= count - 1 - p)
        def _():
            q = step - (count - 1 - p)
            for a in arrays:
                self.ready(a, q)

                @pl.when(p < count - 1)
                def _():
                    self.left(a, q).wait_recv()
                    self.add(a, q, [q])

                @pl.when(p == count - 1)
                def _():
                    self.add(a, q, [])

                self.left(a, q).start()

    def final(self, after):
        i, p, sib = self.places
        count = self.count
        for a in range(len(self.sources)):
            self.ready(a, p)

            @pl.when(p > 0)
            def _():
                self.right(a, p).wait_recv()

            @pl.when(p < count - 1)
            def _():
                self.left(a, p).wait_recv()

            @pl.when(p == 0)
            def _():
                self.add(a, p, [count])

            @pl.when(p == count - 1)
            def _():
                self.add(a, p, [p])

            @pl.when((p > 0) & (p < count - 1))
            def _():
                self.add(a, p, [p, count])

            after(a, p)

    def run(self, after, between=None):
        @pl.loop(0, self.count - 1)
        def _(step):
            self.event(step)
            if between is not None:
                between(step)

        self.final(after)

    def finish(self):
        i, p, sib = self.places
        for a in range(len(self.sources)):
            for q in range(self.count):
                self.to_sib(a, q).wait_send()

                @pl.when(q > p)
                def _():
                    self.right(a, q).wait_send()

                @pl.when(q < p)
                def _():
                    self.left(a, q).wait_send()


class SplitScatter(LineScatter):
    def __init__(self, count, places, source, bufs, sems):
        super().__init__(count, places, [source] * 2, [0] * 2, tuple([buf] * 2 for buf in bufs), sems)
        self.half = bufs[0].shape[-1] // 2

    def cols(self, a):
        return pl.ds(a * self.half, self.half)

    def view(self, a, ref):
        return ref.at[:, self.cols(a)]

    def add(self, a, q, others):
        own = self.own[a]
        rows = own.shape[1]
        step = rows
        while step * self.half > 65536 and step % 16 == 0:
            step //= 2

        @pl.loop(0, rows // step)
        def _(k):
            index = (pl.ds(pl.multiple_of(k * step, step), step), self.cols(a))
            total = own[(q,) + index].astype(F32) + self.sib[a][(q,) + index].astype(F32)
            for slot in others:
                total += self.inbox[a][(slot,) + index].astype(F32)
            own[(q,) + index] = total.astype(own.dtype)


def end_kernel(count, seq_count, *refs):
    sources = refs[:6]
    factors = refs[6:12]
    outs = refs[12:18]
    sum_ref = refs[18]
    bufs = tuple(refs[19 + 6 * k : 25 + 6 * k] for k in range(3))
    landing = refs[37]
    sems = refs[38:45]
    send_x, recv_x, local = refs[45:48]
    held = refs[48:54]
    rows_ref, factor_sem = refs[54:56]
    seq = SeqScatter(seq_count, rows_ref, *refs[56:61])
    places = where_am_i()
    here = lax.axis_index("seq")
    width = sources[0].shape[3]
    line = LineScatter(count, places, sources, [1, 1, 1, 0, 1, 0], bufs, sems)
    line.begin_loads()
    for n in range(6):
        pltpu.make_async_copy(factors[n], held[n], factor_sem.at[n]).start()
    greet(count, places, seq_count)
    line.begin()
    own = bufs[0]

    def at_home(a, block):
        if a == 4:
            return landing.at[block]
        start = pl.multiple_of(block * width, width)
        return outs[a].at[:, pl.ds(start, width)]

    def piece(a, q, d):
        peer = lax.rem(here + d, seq_count)
        slot = 3 if a == 4 else a
        return remote(
            own[a].at[q, peer], at_home(a, here), send_x.at[slot, d - 1], recv_x.at[slot, d - 1], seq=peer
        )

    def arrived(a, d):
        origin = lax.rem(here + seq_count - d, seq_count)
        slot = 3 if a == 4 else a
        return remote(
            at_home(a, origin), at_home(a, origin), send_x.at[slot, d - 1], recv_x.at[slot, d - 1], seq=origin
        )

    def after(a, q):
        if a in (3, 5):
            pltpu.make_async_copy(own[a].at[q], outs[a], local.at[a]).start()
        else:
            for d in range(1, seq_count):
                piece(a, q, d).start()
            pltpu.make_async_copy(own[a].at[q, here], at_home(a, here), local.at[a]).start()

    def back_rows():
        for n in range(6):
            pltpu.make_async_copy(factors[n], held[n], factor_sem.at[n]).wait()
        tokens, model_width = rows_ref.shape[1:]
        tile = 512
        tiles = model_width // tile

        @pl.loop(0, seq_count * tiles)
        def _(u):
            block = u // tiles
            strip = pl.ds(pl.multiple_of(block * tokens, tokens), tokens)
            cols = pl.ds(pl.multiple_of(lax.rem(u, tiles) * tile, tile), tile)
            total = jnp.zeros((tokens, tile), F32)
            for n in range(3):
                total += lax.dot_general(
                    held[n][strip, :], held[3 + n][cols, :], (((1,), (1,)), ((), ())), preferred_element_type=F32
                )
            rows_ref[block, :, cols] = total.astype(BF)

        seq.begin_loads()
        seq.begin()

    def between(step):
        @pl.when(step == 1)
        def _():
            seq.relay()

    back_rows()
    line.run(after, between)
    seq.total(sum_ref)
    for q in range(count):

        @pl.when(q == places[1])
        def _():
            for a in range(6):
                if a in (3, 5):
                    pltpu.make_async_copy(own[a].at[q], outs[a], local.at[a]).wait()
                else:
                    pltpu.make_async_copy(own[a].at[q, here], at_home(a, here), local.at[a]).wait()
                    for d in range(1, seq_count):
                        piece(a, q, d).wait_send()
                        arrived(a, d).wait_recv()

    total = landing[0]
    for block in range(1, seq_count):
        total += landing[block]
    landing[0] = total
    last = pltpu.make_async_copy(landing.at[0], outs[4], local.at[4])
    last.start()
    last.wait()
    line.finish()
    seq.finish()


def scatter_end(arrays, factors, seq_count, shards, collective):
    count = shards // 2
    gq, gk, gv, go, small, gains = arrays
    rows, width = gq.shape[2:]
    tokens, model_width = factors[0].shape[0] // seq_count, factors[3].shape[0]
    home = jax.ShapeDtypeStruct((rows, width * seq_count), BF)
    shapes = [
        home,
        home,
        home,
        jax.ShapeDtypeStruct(go.shape[1:], BF),
        jax.ShapeDtypeStruct(small.shape[2:], F32),
        jax.ShapeDtypeStruct(gains.shape[1:], F32),
        jax.ShapeDtypeStruct((tokens, model_width), F32),
    ]
    blocks, inboxes = [], []
    for a in range(6):
        shape = arrays[a].shape
        block = (shape[0],) + shape[2:] if a in (0, 1, 2, 4) else shape[1:]
        blocks.append(pltpu.VMEM((count,) + block, arrays[a].dtype))
        inboxes.append(pltpu.VMEM((count + 1,) + block, arrays[a].dtype))
    return pl.pallas_call(
        partial(end_kernel, count, seq_count),
        out_shape=shapes,
        in_specs=[pl.BlockSpec(memory_space=ANY)] * 12,
        out_specs=[pl.BlockSpec(memory_space=ANY)] * 6 + [pl.BlockSpec(memory_space=pltpu.VMEM)],
        scratch_shapes=blocks * 2
        + inboxes
        + [pltpu.VMEM((seq_count,) + small.shape[2:], F32)]
        + [DMA((6, count))] * 7
        + [DMA((4, seq_count - 1)), DMA((4, seq_count - 1)), DMA((6,))]
        + [pltpu.VMEM(x.shape, BF) for x in factors]
        + [pltpu.VMEM((seq_count, tokens, model_width), BF), DMA((6,))]
        + seq_scatter_scratch((tokens, model_width), BF, seq_count),
        compiler_params=pltpu.CompilerParams(
            collective_id=collective, has_side_effects=True, vmem_limit_bytes=62 << 20
        ),
        name="scatter_end",
    )(*arrays, *factors)


def greet_seq(seq_count):
    here = lax.axis_index("seq")
    barrier = pltpu.get_barrier_semaphore()
    for d in range(1, seq_count):
        peer = lax.rem(here + d, seq_count)
        pl.semaphore_signal(barrier, inc=1, device_id={"seq": peer}, device_id_type=MESH)
    pl.semaphore_wait(barrier, seq_count - 1)
    return here


class SeqScatter:
    def __init__(self, seq_count, x_ref, own, inbox, send, recv, local):
        here = lax.axis_index("seq")
        self.own, self.inbox, self.local, self.count = own, inbox, local, seq_count
        self.take = pltpu.make_async_copy(x_ref.at[here], own, local.at[0])
        rows = own.shape[0]
        self.half = rows // 2
        low, high = pl.ds(0, self.half), pl.ds(self.half, self.half)
        if seq_count != 4:
            self.copies = []
            for d in range(1, seq_count):
                peer = lax.rem(here + d, seq_count)
                self.copies.append(
                    remote(x_ref.at[peer], inbox.at[d - 1], send.at[d - 1], recv.at[d - 1], seq=peer)
                )
            return
        beside = here + 1 - 2 * lax.rem(here, 2)
        across = lax.rem(here + 2, 4)
        corner = 3 - here
        self.loads = [
            pltpu.make_async_copy(x_ref.at[across, low], inbox.at[3, low], local.at[1]),
            pltpu.make_async_copy(x_ref.at[beside, high], inbox.at[3, high], local.at[2]),
        ]
        plans = (
            (x_ref.at[corner, low], inbox.at[2, low], beside),
            (x_ref.at[corner, high], inbox.at[2, high], across),
            (x_ref.at[beside, low], inbox.at[0, low], beside),
            (x_ref.at[across, high], inbox.at[1, high], across),
            (inbox.at[3, low], inbox.at[1, low], across),
            (inbox.at[3, high], inbox.at[0, high], beside),
        )
        self.copies = [
            remote(src, dst, send.at[n], recv.at[n], seq=peer) for n, (src, dst, peer) in enumerate(plans)
        ]

    def begin_loads(self):
        self.take.start()
        if self.count == 4:
            for load in self.loads:
                load.start()

    def begin(self):
        for copy in self.copies[:4] if self.count == 4 else self.copies:
            copy.start()

    def strips(self, start, rows, body):
        step = min(32, rows)

        @pl.loop(0, rows // step)
        def _(k):
            body(pl.ds(pl.multiple_of(start + k * step, step), step))

    def relay(self):
        if self.count != 4:
            return
        inbox = self.inbox

        def add(strip):
            inbox[3, strip, :] = (
                inbox[3, strip, :].astype(F32) + inbox[2, strip, :].astype(F32)
            ).astype(inbox.dtype)

        for n, start in ((0, 0), (1, self.half)):
            self.loads[n].wait()
            self.copies[n].wait_recv()
            self.strips(start, self.half, add)
            self.copies[4 + n].start()

    def total(self, o_ref):
        self.take.wait()
        for copy in self.copies[2:] if self.count == 4 else self.copies:
            copy.wait_recv()
        parts = 2 if self.count == 4 else self.count - 1

        def add(strip):
            total = self.own[strip, :].astype(F32)
            for d in range(parts):
                total += self.inbox[d, strip, :].astype(F32)
            o_ref[strip, :] = total

        self.strips(0, self.own.shape[0], add)

    def finish(self):
        for copy in self.copies:
            copy.wait_send()


def seq_scatter_scratch(block, dtype, seq_count):
    boxes = 4 if seq_count == 4 else seq_count - 1
    copies = 6 if seq_count == 4 else seq_count - 1
    return [
        pltpu.VMEM(block, dtype),
        pltpu.VMEM((boxes,) + block, dtype),
        DMA((copies,)),
        DMA((copies,)),
        DMA((3,)),
    ]


class SeqGather:
    def __init__(self, seq_count, x_ref, o_ref, send, recv):
        here = lax.axis_index("seq")
        self.count = seq_count
        rows = x_ref.shape[0]
        low, high = pl.ds(0, rows // 2), pl.ds(rows // 2, rows // 2)
        if seq_count != 4:
            peers = [lax.rem(here + d, seq_count) for d in range(1, seq_count)]
            origins = [lax.rem(here + seq_count - d, seq_count) for d in range(1, seq_count)]
            out = [(x_ref, o_ref.at[here], peer) for peer in peers]
            landed = [o_ref.at[origin] for origin in origins]
        else:
            beside = here + 1 - 2 * lax.rem(here, 2)
            across = lax.rem(here + 2, 4)
            corner = 3 - here
            out = [
                (x_ref, o_ref.at[here], beside),
                (x_ref, o_ref.at[here], across),
                (o_ref.at[across, low], o_ref.at[across, low], beside),
                (o_ref.at[beside, high], o_ref.at[beside, high], across),
            ]
            landed = [o_ref.at[beside], o_ref.at[across], o_ref.at[corner, low], o_ref.at[corner, high]]
        self.sends = [
            remote(src, dst, send.at[n], recv.at[n], seq=peer) for n, (src, dst, peer) in enumerate(out)
        ]
        self.lands = [
            remote(ref, ref, send.at[n], recv.at[n], seq=out[n][2]) for n, ref in enumerate(landed)
        ]

    def begin(self):
        for copy in self.sends[:2] if self.count == 4 else self.sends:
            copy.start()

    def relay(self):
        if self.count == 4:
            for n in (0, 1):
                self.lands[n].wait_recv()
            for n in (2, 3):
                self.sends[n].start()

    def finish(self):
        for n, copy in enumerate(self.lands):
            if self.count != 4 or n > 1:
                copy.wait_recv()
        for copy in self.sends:
            copy.wait_send()


def seq_gather_sems(seq_count):
    copies = 4 if seq_count == 4 else seq_count - 1
    return [DMA((copies,)), DMA((copies,))]


def slot_targets(first, local_experts, cap, routes, targets, targets_t):
    shards, top_k, tokens = routes.shape
    earlier = lax.broadcasted_iota(jnp.int32, (tokens, tokens), 0)
    later = lax.broadcasted_iota(jnp.int32, (tokens, tokens), 1)
    upto = jnp.where(earlier <= later, 1.0, 0.0).astype(BF)
    row = lax.broadcasted_iota(jnp.int32, (8, tokens), 0)
    for j in range(shards):
        named = routes[j]
        chosen = jnp.zeros((8, tokens), F32)
        for e in range(local_experts):
            hit = jnp.max(jnp.where(named == first + e, 1.0, 0.0), axis=0, keepdims=True)
            chosen = jnp.where(row == e, hit, chosen)
        place = jnp.dot(chosen.astype(BF), upto, preferred_element_type=F32) - 1.0
        slot = jnp.where(chosen > 0.5, place + (cap * row).astype(F32), -1.0)
        targets[j] = slot[0:local_experts].astype(jnp.int32)
        targets_t[j] = slot.T[:, 0:local_experts].astype(jnp.int32)


def middle_kernel(
    count,
    seq_count,
    cap,
    x_ref,
    dy_ref,
    routes,
    o_ref,
    all_ref,
    targets,
    targets_t,
    own,
    inbox,
    xs,
    xr,
    xl,
    hold,
    s0,
    s1,
    s2,
    recv,
    local,
):
    places = where_am_i()
    i = places[0]
    seq = SeqScatter(seq_count, x_ref, own, inbox, xs, xr, xl)
    seq.begin_loads()
    take = pltpu.make_async_copy(dy_ref, hold, local.at[0])
    take.start()
    greet(count, places, seq_count)
    seq.begin()
    take.wait()
    put = pltpu.make_async_copy(hold, all_ref.at[i], local.at[1])
    put.start()
    put.wait()
    line = LineGather(count, places, [all_ref], [0], s0, s1, s2, recv)
    line.first(0)
    local_experts = targets.shape[1]
    slot_targets(i * local_experts, local_experts, cap, routes, targets, targets_t)
    for t in range(1, count):
        line.forward(t)
        if t == 1:
            seq.relay()
    seq.total(o_ref)
    line.finish()
    seq.finish()


def middle(blocks, dy, routes, local_experts, collective):
    shards, _, tokens = routes.shape
    count = shards // 2
    seq_count = blocks.shape[0]
    block = blocks.shape[1:]
    anywhere = pl.BlockSpec(memory_space=ANY)
    vmem = pl.BlockSpec(memory_space=pltpu.VMEM)
    return pl.pallas_call(
        partial(middle_kernel, count, seq_count, CAP),
        out_shape=[
            jax.ShapeDtypeStruct(block, F32),
            jax.ShapeDtypeStruct((shards,) + dy.shape, dy.dtype),
            jax.ShapeDtypeStruct((shards, local_experts, tokens), jnp.int32),
            jax.ShapeDtypeStruct((shards, tokens, local_experts), jnp.int32),
        ],
        in_specs=[anywhere, anywhere, vmem],
        out_specs=[vmem, pl.BlockSpec(memory_space=pltpu.HBM), vmem, vmem],
        scratch_shapes=seq_scatter_scratch(block, blocks.dtype, seq_count)
        + [pltpu.VMEM(dy.shape, dy.dtype)]
        + line_sems(1, count)
        + [DMA((2,))],
        compiler_params=pltpu.CompilerParams(
            collective_id=collective, has_side_effects=True, vmem_limit_bytes=32 << 20
        ),
        name="middle",
    )(blocks, dy, routes)


def turn_kernel(
    count,
    seq_count,
    x_ref,
    parts_ref,
    left_ref,
    right0,
    right1,
    o_ref,
    sum_ref,
    grad_ref,
    hold,
    send,
    recv,
    one,
    tiles_in,
    held,
    staged,
    outer_sem,
    own,
    sib,
    inbox,
    *sems,
):
    places = where_am_i()
    here = lax.axis_index("seq")
    line = SplitScatter(count, places, parts_ref, (own, sib, inbox), sems)
    grads = OuterGrads(left_ref, (right0, right1), grad_ref, (tiles_in, held, staged, outer_sem), count - 1)
    line.begin_loads()
    take = pltpu.make_async_copy(x_ref, hold, one)
    take.start()
    grads.begin()
    greet(count, places, seq_count)
    rows = SeqGather(seq_count, x_ref, o_ref, send, recv)
    rows.begin()
    line.begin()
    take.wait()
    put = pltpu.make_async_copy(hold, o_ref.at[here], one)
    put.start()

    def after(a, q):
        out = pltpu.make_async_copy(line.view(a, own.at[q]), line.view(a, sum_ref), sems[6].at[a, q])
        out.start()
        out.wait()

    def between(step):
        grads.between(step)

        @pl.when(step == 1)
        def _():
            rows.relay()

    line.run(after, between)
    grads.finish()
    put.wait()
    rows.finish()
    line.finish()


def turn_back(block, parts, expert_in, d_gate, d_up, seq_count, shards, collective):
    count = shards // 2
    part = parts.shape[1:]
    model_width = block.shape[1]
    anywhere = pl.BlockSpec(memory_space=ANY)
    return pl.pallas_call(
        partial(turn_kernel, count, seq_count),
        out_shape=[
            jax.ShapeDtypeStruct((seq_count,) + block.shape, block.dtype),
            jax.ShapeDtypeStruct(part, parts.dtype),
            jax.ShapeDtypeStruct((d_gate.shape[0], model_width, 2 * d_gate.shape[2]), BF),
        ],
        in_specs=[anywhere] * 5,
        out_specs=[anywhere] * 3,
        scratch_shapes=[pltpu.VMEM(block.shape, block.dtype)]
        + seq_gather_sems(seq_count)
        + [DMA]
        + outer_scratch(d_up, 512, 2)
        + [pltpu.VMEM((count,) + part, BF)] * 2
        + [pltpu.VMEM((count + 1,) + part, BF)]
        + [DMA((2, count))] * 7,
        compiler_params=pltpu.CompilerParams(
            collective_id=collective, has_side_effects=True, vmem_limit_bytes=60 << 20
        ),
        cost_estimate=pl.CostEstimate(flops=60_000_000_000, bytes_accessed=200_000_000, transcendentals=0),
        name="turn_back",
    )(block, parts, expert_in, d_gate, d_up)


def half_sign(shape):
    lane = lax.broadcasted_iota(jnp.int32, shape, 1)
    return jnp.where(lane < shape[1] // 2, -1.0, 1.0)


def turn(value):
    return pltpu.roll(value, value.shape[1] // 2, 1)


def block_probs(q_rows, keys, doc_col, doc_row, start, scale_by):
    end = keys.shape[0]
    scores = (
        lax.dot_general(q_rows, keys, (((1,), (1,)), ((), ())), preferred_element_type=F32) * scale_by
    )
    shape = scores.shape
    query_pos = start + lax.broadcasted_iota(jnp.int32, shape, 0)
    key_pos = lax.broadcasted_iota(jnp.int32, shape, 1)
    allowed = (doc_col == doc_row) & (key_pos <= query_pos)
    scores = jnp.where(allowed, scores, MASKED_OUT)
    weights = jnp.exp(scores - jnp.max(scores, axis=-1, keepdims=True))
    return weights * (1.0 / jnp.sum(weights, axis=-1, keepdims=True))


class SeqSum:
    def __init__(self, seq_count, sheet, inbox, send, recv):
        here = lax.axis_index("seq")
        self.sheet, self.inbox = sheet, inbox
        self.copies = []
        for d in range(1, seq_count):
            peer = lax.rem(here + d, seq_count)
            self.copies.append(remote(sheet, inbox.at[d - 1], send.at[d - 1], recv.at[d - 1], seq=peer))

    def begin(self):
        for copy in self.copies:
            copy.start()

    def total(self):
        for copy in self.copies:
            copy.wait_recv()
        total = self.sheet[...]
        for d in range(len(self.copies)):
            total += self.inbox[d]
        for copy in self.copies:
            copy.wait_send()
        return total


def attend_kernel(
    seq_count,
    row_block,
    model_width,
    q_raw,
    k_raw,
    v_ref,
    squares,
    gq,
    gk,
    cos,
    sin,
    doc_col,
    doc_row,
    o_ref,
    q_out,
    k_out,
    scales,
    inbox,
    send,
    recv,
):
    seq_len = q_raw.shape[0]

    @pl.when(pl.program_id(0) == 0)
    def _():
        greet_seq(seq_count)
        sums = SeqSum(seq_count, squares, inbox, send, recv)
        sums.begin()
        scales[...] = lax.rsqrt(sums.total() / model_width + EPSILON).T

    sign = half_sign(cos.shape)

    def rotated(raw, lane, gain):
        value = raw[...] * scales[:, lane : lane + 1] * gain[...]
        return (value * cos[...] + turn(value) * (sin[...] * sign)).astype(BF)

    q_out[...] = rotated(q_raw, 0, gq)
    k_out[...] = rotated(k_raw, 1, gk)
    scale_by = HEAD ** (-0.5)
    for start in range(0, seq_len, row_block):
        end = start + row_block
        probs = block_probs(
            q_out[start:end, :], k_out[:end, :], doc_col[start:end, :], doc_row[:, :end], start, scale_by
        )
        o_ref[start:end, :] = jnp.dot(
            probs.astype(BF), v_ref[:end, :], preferred_element_type=F32
        ).astype(BF)


def attend(q_raw, k_raw, values, squares, gq, gk, cos, sin, doc_col, doc_row, model_width, seq_count, collective):
    seq_len, width = q_raw.shape
    head = pl.BlockSpec((seq_len, HEAD), lambda h: (0, h))
    gain = pl.BlockSpec((1, HEAD), lambda h: (0, h))

    def whole(shape):
        return pl.BlockSpec(shape, lambda h: (0, 0))

    out = jax.ShapeDtypeStruct((seq_len, width), BF)
    return pl.pallas_call(
        partial(attend_kernel, seq_count, 256, model_width),
        grid=(width // HEAD,),
        out_shape=[
            out,
            out,
            out,
            jax.ShapeDtypeStruct((seq_len, 8), F32),
        ],
        in_specs=[head, head, head, whole(squares.shape), gain, gain, whole(cos.shape), whole(sin.shape)]
        + [whole(doc_col.shape), whole(doc_row.shape)],
        out_specs=[head, head, head, whole((seq_len, 8))],
        scratch_shapes=[
            pltpu.VMEM((seq_count - 1,) + squares.shape, F32),
            DMA((seq_count - 1,)),
            DMA((seq_count - 1,)),
        ],
        compiler_params=pltpu.CompilerParams(
            collective_id=collective, has_side_effects=True, vmem_limit_bytes=48 << 20
        ),
        name="attend",
    )(q_raw, k_raw, values, squares, gq, gk, cos, sin, doc_col, doc_row)


def attend_back_kernel(
    count,
    seq_count,
    heads,
    row_block,
    model_width,
    q_low,
    k_low,
    v_ref,
    do_ref,
    q_raw,
    k_raw,
    scales,
    gq,
    gk,
    cos,
    sin,
    doc_col,
    doc_row,
    parts_ref,
    dq_ref,
    dk_ref,
    dv_ref,
    gain_ref,
    sum_ref,
    dq_acc,
    dk_acc,
    dv_acc,
    uq,
    uk,
    dots,
    sheet,
    inbox,
    send,
    recv,
    own,
    sib,
    landed,
    *sems,
):
    seq_len = q_low.shape[0]
    head = pl.program_id(0)
    scale_by = HEAD ** (-0.5)
    places = where_am_i()
    line = LineScatter(count, places, [parts_ref], [0], ([own], [sib], [landed]), sems)

    @pl.when(head == 0)
    def _():
        line.begin_loads()
        greet(count, places, seq_count)
        line.begin()
        dots[...] = jnp.zeros_like(dots)

    dk_acc[...] = jnp.zeros_like(dk_acc)
    dv_acc[...] = jnp.zeros_like(dv_acc)
    for start in range(0, seq_len, row_block):
        end = start + row_block
        rows = slice(start, end)
        probs = block_probs(
            q_low[rows, :], k_low[:end, :], doc_col[rows, :], doc_row[:, :end], start, scale_by
        )
        grad_rows = do_ref[rows, :]
        grad_probs = lax.dot_general(
            grad_rows, v_ref[:end, :], (((1,), (1,)), ((), ())), preferred_element_type=F32
        )
        centre = jnp.sum(probs * grad_probs, axis=-1, keepdims=True)
        grad_scores = (probs * (grad_probs - centre)).astype(BF)
        dq_acc[rows, :] = jnp.dot(grad_scores, k_low[:end, :], preferred_element_type=F32)
        over_rows = (((0,), (0,)), ((), ()))
        dk_acc[:end, :] += lax.dot_general(
            grad_scores, q_low[rows, :], over_rows, preferred_element_type=F32
        )
        dv_acc[:end, :] += lax.dot_general(
            probs.astype(BF), grad_rows, over_rows, preferred_element_type=F32
        )
        if start == row_block:

            @pl.when(head == 0)
            def _():
                line.event(0)

    dv_ref[...] = dv_acc[...].astype(BF)
    sign = half_sign(cos.shape)
    cols = pl.ds(pl.multiple_of(head * HEAD, HEAD), HEAD)
    blocks, _, lanes = gain_ref.shape
    rows = HEAD // blocks

    def unrotated(acc, raw, gain, u_ref, lane):
        low = (acc[...] * scale_by).astype(BF).astype(F32)
        back = low * cos[...] - turn(low * sin[...]) * sign
        value = raw[:, cols]
        grad_gain = jnp.sum(back * value * scales[:, lane : lane + 1], axis=0, keepdims=True)
        u = back * gain[...]
        u_ref[:, cols] = u
        dots[:, lane : lane + 1] += jnp.sum(u * value, axis=1, keepdims=True)
        return grad_gain

    grads = (unrotated(dq_acc, q_raw, gq, uq, 0), unrotated(dk_acc, k_raw, gk, uk, 1))
    which = lax.broadcasted_iota(jnp.int32, (8, lanes), 0)
    both = jnp.where(which == 0, grads[0], jnp.where(which == 1, grads[1], 0.0))
    for block in range(blocks):
        gain_ref[block] = both if block == 0 else pltpu.roll(both, lanes - block * rows, 1)

    for step in range(1, count - 1):

        @pl.when(head == min(step, heads - 1))
        def _():
            line.event(step)

    @pl.when(head == heads - 1)
    def _():
        sheet[...] = dots[...].T
        sums = SeqSum(seq_count, sheet, inbox, send, recv)
        sums.begin()
        dots[...] = sums.total().T / model_width
        strip = 128

        @pl.loop(0, seq_len // strip)
        def _(n):
            part = pl.ds(pl.multiple_of(n * strip, strip), strip)
            for lane, u_ref, raw, out in ((0, uq, q_raw, dq_ref), (1, uk, k_raw, dk_ref)):
                scale = scales[part, lane : lane + 1]
                product = dots[part, lane : lane + 1]
                out[part, :] = (
                    scale * u_ref[part, :] - raw[part, :] * (scale * scale * scale * product)
                ).astype(BF)

        def after(a, q):
            out = pltpu.make_async_copy(own.at[q], sum_ref, sems[6].at[0, q])
            out.start()
            out.wait()

        line.final(after)
        line.finish()


def attend_back(
    q_low,
    k_low,
    values,
    d_heads,
    q_raw,
    k_raw,
    scales,
    gq,
    gk,
    cos,
    sin,
    doc_col,
    doc_row,
    parts,
    rows,
    model_width,
    seq_count,
    collective,
):
    seq_len, width = q_raw.shape
    heads = width // HEAD
    blocks = HEAD // rows
    shards = parts.shape[0]
    count = shards // 2
    part = parts.shape[1:]
    head = pl.BlockSpec((seq_len, HEAD), lambda h: (0, h))
    gain = pl.BlockSpec((1, HEAD), lambda h: (0, h))

    def whole(shape):
        return pl.BlockSpec(shape, lambda h: (0, 0))

    def once(x):
        return pl.BlockSpec(x.shape, lambda h: (0, 0), pipeline_mode=pl.Buffered(1))

    out = jax.ShapeDtypeStruct((seq_len, width), BF)
    return pl.pallas_call(
        partial(attend_back_kernel, count, seq_count, heads, 256, model_width),
        grid=(heads,),
        out_shape=[
            out,
            out,
            out,
            jax.ShapeDtypeStruct((width // rows, 8, HEAD), F32),
            jax.ShapeDtypeStruct(part, BF),
        ],
        in_specs=[head] * 4
        + [once(q_raw), once(k_raw), once(scales), gain, gain, once(cos), once(sin)]
        + [once(doc_col), once(doc_row), pl.BlockSpec(memory_space=ANY)],
        out_specs=[
            whole((seq_len, width)),
            whole((seq_len, width)),
            head,
            pl.BlockSpec((blocks, 8, HEAD), lambda h: (h, 0, 0)),
            pl.BlockSpec(memory_space=ANY),
        ],
        scratch_shapes=[pltpu.VMEM((seq_len, HEAD), F32)] * 3
        + [pltpu.VMEM((seq_len, width), F32)] * 2
        + [
            pltpu.VMEM((seq_len, 8), F32),
            pltpu.VMEM((8, seq_len), F32),
            pltpu.VMEM((seq_count - 1, 8, seq_len), F32),
            DMA((seq_count - 1,)),
            DMA((seq_count - 1,)),
        ]
        + [pltpu.VMEM((count,) + part, BF)] * 2
        + [pltpu.VMEM((count + 1,) + part, BF)]
        + [DMA((1, count))] * 7,
        compiler_params=pltpu.CompilerParams(
            collective_id=collective, has_side_effects=True, vmem_limit_bytes=60 << 20
        ),
        name="attend_back",
    )(q_low, k_low, values, d_heads, q_raw, k_raw, scales, gq, gk, cos, sin, doc_col, doc_row, parts)


def experts_in_kernel(
    count,
    cap,
    h2_ref,
    dy_ref,
    targets,
    router_t,
    wgu_ref,
    h2_out,
    x_out,
    y_out,
    act_out,
    by_up_out,
    by_gate_out,
    gate_slots,
    probs_out,
    h2,
    wgu,
    dy,
    xs,
    ys,
    acts,
    by_up,
    by_gate,
    s0,
    s1,
    s2,
    recv,
    w_sem,
    dy_sem,
    h_sem,
    out_sem,
):
    places = where_am_i()
    i, p, sib = places
    local_experts, model_width, hidden = wgu_ref.shape
    hidden = hidden // 2
    tokens = h2_ref.shape[0]
    experts = router_t.shape[0]
    own_in = pltpu.make_async_copy(h2_ref, h2.at[i], h_sem.at[0])
    own_in.start()

    def fetch(q, buf):
        src = dy_ref.at[pl.ds(2 * q, 2)]
        return pltpu.make_async_copy(src, dy.at[buf], dy_sem.at[buf])

    fetch(p, 0).start()
    for e in range(local_experts):
        pltpu.make_async_copy(wgu_ref.at[e], wgu.at[e], w_sem.at[e]).start()
    greet(count, places)
    own_in.wait()
    line = LineGather(count, places, [h2], [0], s0, s1, s2, recv)
    line.first(0)
    staged = ((xs, x_out), (ys, y_out), (acts, act_out), (by_up, by_up_out), (by_gate, by_gate_out))

    def store(n, e, q):
        rows = pl.ds(pl.multiple_of(q * 2 * cap, 2 * cap), 2 * cap)
        return pltpu.make_async_copy(staged[n][0].at[e], staged[n][1].at[e, rows], out_sem.at[n, e])

    def keep(q):
        src = h2.at[pl.ds(2 * q, 2)]
        return pltpu.make_async_copy(src, h2_out.at[pl.ds(2 * q, 2)], h_sem.at[1])

    slot_rows = lax.broadcasted_iota(jnp.int32, (local_experts * cap, tokens), 0)
    expert_rows = lax.broadcasted_iota(jnp.int32, (experts, tokens), 0)

    @pl.loop(0, count)
    def _(k):
        q = chunk_order(k, p, count)
        buf = k % 2

        @pl.when(k > 0)
        def _():
            line.forward(k)

        line.copy(0, 2 * q + lax.rem(sib, 2), 2, 0, sib).wait_recv()
        fetch(q, buf).wait()

        @pl.when(k + 1 < count)
        def _():
            fetch(chunk_order(k + 1, p, count), 1 - buf).start()

        @pl.when(k > 0)
        def _():
            for n in range(5):
                for e in range(local_experts):
                    store(n, e, q).wait()
            keep(q).wait()

        keep(q).start()
        picks = []
        for j in range(2):
            slot = 2 * q + j
            tokens_j = h2[slot]
            logits = lax.dot_general(
                router_t[...], tokens_j, (((1,), (1,)), ((), ())), preferred_element_type=F32
            )
            shifted = jnp.exp(logits - jnp.max(logits, axis=0, keepdims=True))
            probs = shifted / jnp.sum(shifted, axis=0, keepdims=True)
            probs_out[slot] = probs
            pick = None
            for e in range(local_experts):
                mask = slot_rows == targets[slot, e : e + 1, :]
                gate = jnp.sum(
                    jnp.where(expert_rows == i * local_experts + e, probs, 0.0), axis=0, keepdims=True
                )
                part = slice(e * cap, (e + 1) * cap)
                gate_slots[e, q, j * cap : (j + 1) * cap, :] = jnp.sum(
                    jnp.where(mask[part], gate, 0.0), axis=1, keepdims=True
                )
                pick = mask if pick is None else pick | mask
            picks.append(jnp.where(pick, 1.0, 0.0).astype(BF))

        block = 512

        @pl.loop(0, model_width // block)
        def _(n):
            cols = pl.ds(pl.multiple_of(n * block, block), block)
            for source, target in ((0, xs), (1, ys)):
                got = []
                for j in range(2):
                    rows = h2[2 * q + j, :, cols] if source == 0 else dy[buf, j, :, cols]
                    got.append(jnp.dot(picks[j], rows, preferred_element_type=F32))
                for e in range(local_experts):
                    part = slice(e * cap, (e + 1) * cap)
                    target[e, :, cols] = jnp.concatenate([got[0][part], got[1][part]], axis=0).astype(BF)

        for e in range(local_experts):
            store(0, e, q).start()
            store(1, e, q).start()

            @pl.when(k == 0)
            def _():
                pltpu.make_async_copy(wgu_ref.at[e], wgu.at[e], w_sem.at[e]).wait()

            wide = 256

            @pl.loop(0, hidden // wide)
            def _(n):
                cols = pl.ds(pl.multiple_of(n * wide, wide), wide)
                beyond = pl.ds(pl.multiple_of(hidden + n * wide, wide), wide)
                gate = jnp.dot(xs[e], wgu[e, :, cols], preferred_element_type=F32)
                up = jnp.dot(xs[e], wgu[e, :, beyond], preferred_element_type=F32)
                sigmoid = 1.0 / (1.0 + jnp.exp(-gate))
                silu = gate * sigmoid
                acts[e, :, cols] = (silu * up).astype(BF)
                by_up[e, :, cols] = silu.astype(BF)
                by_gate[e, :, cols] = (up * sigmoid * (1.0 + gate * (1.0 - sigmoid))).astype(BF)

            for n in (2, 3, 4):
                store(n, e, q).start()

    for n in range(5):
        for e in range(local_experts):
            store(n, e, 0).wait()
    keep(0).wait()
    sends_done(line)


def sends_done(line):
    i, p, sib = line.places
    count = line.count
    line.copy(0, i, 2, 0, sib).wait_send()

    @pl.when(p < count - 1)
    def _():
        line.copy(0, i, 0, 0, i + 2).wait_send()

    @pl.when(p > 0)
    def _():
        line.copy(0, i, 1, 0, i - 2).wait_send()

    for t in range(1, count):

        @pl.when(p - t >= 0)
        def _():
            slot = i - 2 * t

            @pl.when(p < count - 1)
            def _():
                line.copy(0, slot, 0, t, i + 2).wait_send()

            line.copy(0, slot, 2, t, sib).wait_send()

        @pl.when(p + t < count)
        def _():
            slot = i + 2 * t

            @pl.when(p > 0)
            def _():
                line.copy(0, slot, 1, t, i - 2).wait_send()

            line.copy(0, slot, 2, count + t, sib).wait_send()


def experts_in(h2, dy_all, targets, router_t, w_gate_up, collective):
    shards, tokens, model_width = dy_all.shape
    local_experts, _, hidden = w_gate_up.shape
    hidden = hidden // 2
    experts = router_t.shape[0]
    count = shards // 2
    wide = jax.ShapeDtypeStruct((local_experts, count * 2 * CAP, model_width), BF)
    thin = jax.ShapeDtypeStruct((local_experts, count * 2 * CAP, hidden), BF)
    anywhere = pl.BlockSpec(memory_space=ANY)
    vmem = pl.BlockSpec(memory_space=pltpu.VMEM)
    return pl.pallas_call(
        partial(experts_in_kernel, count, CAP),
        out_shape=[
            jax.ShapeDtypeStruct((shards, tokens, model_width), BF),
            wide,
            wide,
            thin,
            thin,
            thin,
            jax.ShapeDtypeStruct((local_experts, count, 2 * CAP, 1), F32),
            jax.ShapeDtypeStruct((shards, experts, tokens), F32),
        ],
        in_specs=[anywhere, anywhere, vmem, vmem, anywhere],
        out_specs=[anywhere] * 6 + [vmem, vmem],
        scratch_shapes=[
            pltpu.VMEM((shards, tokens, model_width), BF),
            pltpu.VMEM(w_gate_up.shape, BF),
            pltpu.VMEM((2, 2, tokens, model_width), BF),
        ]
        + [pltpu.VMEM((local_experts, 2 * CAP, model_width), BF)] * 2
        + [pltpu.VMEM((local_experts, 2 * CAP, hidden), BF)] * 3
        + line_sems(1, count)
        + [DMA((local_experts,)), DMA((2,)), DMA((2,)), DMA((5, local_experts))],
        compiler_params=pltpu.CompilerParams(
            collective_id=collective, has_side_effects=True, vmem_limit_bytes=60 << 20
        ),
        name="experts_in",
    )(h2, dy_all, targets, router_t, w_gate_up)


def experts_mid_kernel(
    cap,
    y_in,
    act_in,
    by_up_in,
    by_gate_in,
    gate_slots,
    wd_in,
    gated_out,
    d_gate_out,
    d_up_out,
    dots_ref,
    g_down_out,
    wd,
    ys,
    acts,
    by_ups,
    by_gates,
    gated,
    d_gate,
    d_up,
    staged,
    in_sem,
    out_sem,
    grad_sem,
):
    local_experts, hidden, model_width = wd_in.shape
    count = gate_slots.shape[1]
    slots = ys.shape[1]
    over_lanes = (((1,), (1,)), ((), ()))
    over_rows = (((0,), (0,)), ((), ()))
    inputs = ((y_in, ys), (wd_in, wd), (act_in, acts), (by_up_in, by_ups), (by_gate_in, by_gates))
    results = ((gated, gated_out), (d_gate, d_gate_out), (d_up, d_up_out))
    wide = 256
    tile = staged.shape[1]

    def fetch(n, e):
        return pltpu.make_async_copy(inputs[n][0].at[e], inputs[n][1].at[e], in_sem.at[n, e])

    def store(n, e):
        return pltpu.make_async_copy(results[n][0].at[e], results[n][1].at[e], out_sem.at[n, e])

    def put_grad(e, n, buf):
        rows = pl.ds(pl.multiple_of(n * tile, tile), tile)
        return pltpu.make_async_copy(staged.at[buf], g_down_out.at[e, rows], grad_sem.at[buf])

    for e in range(local_experts):
        for n in range(5):
            fetch(n, e).start()
    @pl.loop(0, local_experts)
    def _(e):
        for n in range(2):
            fetch(n, e).wait()
        gate = jnp.concatenate([gate_slots[e, q] for q in range(count)], axis=0)

        def step(n, dot):
            cols = pl.ds(pl.multiple_of(n * wide, wide), wide)
            grad_act = lax.dot_general(ys[e], wd[e, cols, :], over_lanes, preferred_element_type=F32)

            @pl.when(n == 0)
            def _():
                for kind in range(2, 5):
                    fetch(kind, e).wait()

            act = acts[e, :, cols].astype(F32)
            dot = dot + jnp.sum(act * grad_act, axis=1, keepdims=True)
            grad_act = grad_act * gate
            gated[e, :, cols] = (act * gate).astype(BF)
            d_up[e, :, cols] = (grad_act * by_ups[e, :, cols].astype(F32)).astype(BF)
            d_gate[e, :, cols] = (grad_act * by_gates[e, :, cols].astype(F32)).astype(BF)
            return dot

        dot = lax.fori_loop(0, hidden // wide, step, jnp.zeros((slots, 1), F32))
        for q in range(count):
            dots_ref[e, q] = dot[2 * cap * q : 2 * cap * (q + 1)]
        for n in range(3):
            store(n, e).start()

        @pl.loop(0, hidden // tile // 2)
        def _(m):
            for buf in range(2):
                n = 2 * m + buf

                @pl.when((m > 0) | (e > 0))
                def _():
                    put_grad(e, n, buf).wait()

                cols = pl.ds(pl.multiple_of(n * tile, tile), tile)
                staged[buf] = lax.dot_general(
                    gated[e, :, cols], ys[e], over_rows, preferred_element_type=F32
                ).astype(BF)
                put_grad(e, n, buf).start()

    for buf in range(2):
        put_grad(0, 0, buf).wait()
    for e in range(local_experts):
        for n in range(3):
            store(n, e).wait()


def experts_mid(grads, act, by_up, by_gate, gate_slots, w_down):
    local_experts, slots, model_width = grads.shape
    anywhere = pl.BlockSpec(memory_space=ANY)
    vmem = pl.BlockSpec(memory_space=pltpu.VMEM)
    thin = jax.ShapeDtypeStruct(act.shape, BF)
    return pl.pallas_call(
        partial(experts_mid_kernel, CAP),
        out_shape=[
            thin,
            thin,
            thin,
            jax.ShapeDtypeStruct(gate_slots.shape, F32),
            jax.ShapeDtypeStruct(w_down.shape, BF),
        ],
        in_specs=[anywhere] * 4 + [vmem, anywhere],
        out_specs=[anywhere] * 3 + [vmem, anywhere],
        scratch_shapes=[pltpu.VMEM(w_down.shape, BF), pltpu.VMEM(grads.shape, BF)]
        + [pltpu.VMEM(act.shape, BF)] * 6
        + [
            pltpu.VMEM((2, 256, model_width), BF),
            DMA((5, local_experts)),
            DMA((3, local_experts)),
            DMA((2,)),
        ],
        compiler_params=pltpu.CompilerParams(vmem_limit_bytes=60 << 20),
        cost_estimate=pl.CostEstimate(flops=18_000_000_000, bytes_accessed=60_000_000, transcendentals=0),
        name="experts_mid",
    )(grads, act, by_up, by_gate, gate_slots, w_down)


class StagedScatter(SplitScatter):
    def __init__(self, count, places, stage, bufs, sems):
        super().__init__(count, places, None, bufs, sems)
        self.stage = stage

    def to_sib(self, a, q):
        sib = self.places[2]
        src, dst = self.view(a, self.stage), self.view(a, self.sib[a].at[q])
        return remote(src, dst, self.sems[2].at[a, q], self.sems[5].at[a, q], fsdp=sib)

    def ready(self, a, q):
        self.to_sib(a, q).wait_recv()

    def finish(self):
        i, p, sib = self.places
        for a in range(2):
            for q in range(self.count):

                @pl.when(q > p)
                def _():
                    self.right(a, q).wait_send()

                @pl.when(q < p)
                def _():
                    self.left(a, q).wait_send()


class OuterGrads:
    def __init__(self, left, rights, out, scratch, steps):
        self.left, self.rights, self.out = left, rights, out
        self.tiles_in, self.held, self.staged, self.sems = scratch
        self.experts, self.width, _ = out.shape
        self.hidden = rights[0].shape[2]
        self.tile = self.staged.shape[1]
        self.tiles = self.width // self.tile
        self.units = self.experts * self.tiles
        self.share = -(-self.units // steps)

    def span(self, u):
        start = lax.rem(u, self.tiles) * self.tile
        return pl.ds(pl.multiple_of(start, self.tile), self.tile)

    def fetch(self, u):
        src = self.left.at[u // self.tiles, :, self.span(u)]
        return pltpu.make_async_copy(src, self.tiles_in.at[lax.rem(u, 2)], self.sems.at[0, lax.rem(u, 2)])

    def put(self, u):
        buf = lax.rem(u, 2)
        target = self.out.at[u // self.tiles, self.span(u)]
        return pltpu.make_async_copy(self.staged.at[buf], target, self.sems.at[1, buf])

    def hold(self, n):
        return pltpu.make_async_copy(self.rights[n], self.held.at[n], self.sems.at[2, n])

    def begin(self):
        for n in range(len(self.rights)):
            self.hold(n).start()
        self.fetch(0).start()

    def between(self, step):
        @pl.loop(step * self.share, jnp.minimum((step + 1) * self.share, self.units))
        def _(u):
            @pl.when(u == 0)
            def _():
                for n in range(len(self.rights)):
                    self.hold(n).wait()

            self.fetch(u).wait()

            @pl.when(u + 1 < self.units)
            def _():
                self.fetch(u + 1).start()

            @pl.when(u >= 2)
            def _():
                self.put(u - 2).wait()

            buf = lax.rem(u, 2)
            for n in range(len(self.rights)):
                self.staged[buf, :, n * self.hidden : (n + 1) * self.hidden] = lax.dot_general(
                    self.tiles_in[buf],
                    self.held[n, u // self.tiles],
                    (((0,), (0,)), ((), ())),
                    preferred_element_type=F32,
                ).astype(BF)
            self.put(u).start()

    def finish(self):
        self.put(self.units - 2).wait()
        self.put(self.units - 1).wait()


def outer_scratch(right, tile, factors):
    slots, hidden = right.shape[1:]
    return [
        pltpu.VMEM((2, slots, tile), BF),
        pltpu.VMEM((factors,) + right.shape, BF),
        pltpu.VMEM((2, tile, factors * hidden), BF),
        DMA((3, 2)),
    ]


def experts_out_kernel(
    count,
    cap,
    gated_in,
    d_gate_in,
    d_up_in,
    dots,
    targets,
    targets_t,
    probs_ref,
    router_t,
    wgu_in,
    wd_in,
    tokens_in,
    x_in,
    dy_in,
    gain_row,
    parts_a,
    parts_b,
    grad_ref,
    low_ref,
    small_ref,
    wgu,
    wd,
    gated,
    d_gate,
    d_up,
    parts,
    stage,
    own,
    sibling,
    inbox,
    w_sem,
    in_sem,
    part_sem,
    held_tokens,
    x_mid,
    dy,
    router_sum,
    row_sem,
    *sems,
):
    places = where_am_i()
    i, p, sib = places
    core = lax.rem(i, 2)
    local_experts, hidden, model_width = wd_in.shape
    tokens = targets.shape[2]
    experts = router_t.shape[0]
    first = i * local_experts
    over_lanes = (((1,), (1,)), ((), ()))
    line = StagedScatter(count, places, stage, (own, sibling, inbox), sems)
    block = 512
    take_down = pltpu.make_async_copy(wd_in, wd, w_sem.at[model_width // block])
    inputs = ((gated_in, gated), (d_gate_in, d_gate), (d_up_in, d_up))

    def weight(n):
        rows = pl.ds(pl.multiple_of(n * block, block), block)
        return pltpu.make_async_copy(wgu_in.at[:, rows], wgu.at[:, rows], w_sem.at[n])

    def fetch(n, q, buf):
        rows = pl.ds(pl.multiple_of(q * 2 * cap, 2 * cap), 2 * cap)
        return pltpu.make_async_copy(inputs[n][0].at[:, rows], inputs[n][1].at[buf], in_sem.at[n, buf])

    first_part = parts_a.shape[2]

    def put(n, q):
        src = parts.at[:, :, pl.ds(n * first_part, (parts_a, parts_b)[n].shape[2])]
        return pltpu.make_async_copy(src, (parts_a, parts_b)[n].at[pl.ds(2 * q, 2)], part_sem.at[n])

    def order(k):
        return chunk_order(count - 1 - k, p, count)

    for n in range(3):
        fetch(n, order(0), 0).start()
    for n in range(model_width // block):
        weight(n).start()
    take_down.start()
    take_x = pltpu.make_async_copy(x_in, x_mid, row_sem.at[0])
    take_dy = pltpu.make_async_copy(dy_in, dy, row_sem.at[1])
    take_x.start()
    take_dy.start()
    router_sum[...] = jnp.zeros_like(router_sum)
    greet(count, places)
    slot_rows = lax.broadcasted_iota(jnp.int32, (local_experts * cap, tokens), 0)
    slot_lanes = lax.broadcasted_iota(jnp.int32, (tokens, local_experts * cap), 1)
    expert_rows = lax.broadcasted_iota(jnp.int32, (experts, tokens), 0)

    def take_tokens(q):
        return pltpu.make_async_copy(tokens_in.at[pl.ds(2 * q, 2)], held_tokens, row_sem.at[2])

    def compute(k):
        q = order(k)
        buf = lax.rem(k, 2)
        take_tokens(q).start()
        picks, logits_low, logits_row = [], [], []
        for j in range(2):
            slot = 2 * q + j
            grad_probs = jnp.zeros((experts, tokens), F32)
            pick = None
            for e in range(local_experts):
                part = slice(e * cap, (e + 1) * cap)
                mask = (slot_rows == targets[slot, e : e + 1, :])[part]
                dot = dots[e, q, j * cap : (j + 1) * cap, :]
                row = jnp.sum(jnp.where(mask, dot, 0.0), axis=0, keepdims=True)
                grad_probs = jnp.where(expert_rows == first + e, row, grad_probs)
                hit = slot_lanes == targets_t[slot, :, e : e + 1]
                pick = hit if pick is None else pick | hit
            probs = probs_ref[slot]
            grad_logits = probs * (grad_probs - jnp.sum(probs * grad_probs, axis=0, keepdims=True))
            logits_row.append(grad_logits.astype(BF))
            picks.append(jnp.where(pick, 1.0, 0.0).astype(BF))
            logits_low.append(grad_logits.T.astype(BF))
        for n in range(3):
            fetch(n, q, buf).wait()

        @pl.when(k + 1 < count)
        def _():
            for n in range(3):
                fetch(n, order(k + 1), 1 - buf).start()

        @pl.when(k > 0)
        def _():
            line.to_sib(0, order(k - 1)).wait_send()
            line.to_sib(1, order(k - 1)).wait_send()

        @pl.loop(0, model_width // block)
        def _(n):
            cols = pl.ds(pl.multiple_of(n * block, block), block)

            @pl.when(k == 0)
            def _():
                weight(n).wait()

            grads = []
            for e in range(local_experts):
                grads.append(
                    lax.dot_general(
                        d_gate[buf, e], wgu[e, cols, 0:hidden], over_lanes, preferred_element_type=F32
                    )
                    + lax.dot_general(
                        d_up[buf, e], wgu[e, cols, hidden:], over_lanes, preferred_element_type=F32
                    )
                )
            for j in range(2):
                part = slice(j * cap, (j + 1) * cap)
                back = jnp.concatenate([value[part] for value in grads], axis=0).astype(BF)
                total = (
                    jnp.dot(picks[j], back, preferred_element_type=F32)
                    + jnp.dot(logits_low[j], router_t[:, cols], preferred_element_type=F32)
                ).astype(BF)

                @pl.when(core == j)
                def _():
                    own[q, :, cols] = total

                @pl.when(core != j)
                def _():
                    stage[:, cols] = total

            @pl.when(n == model_width // block // 2 - 1)
            def _():
                line.to_sib(0, q).start()

        line.to_sib(1, q).start()

        @pl.when(k > 0)
        def _():
            put(0, q).wait()
            put(1, q).wait()

        @pl.when(k == 0)
        def _():
            take_down.wait()

        take_tokens(q).wait()

        @pl.loop(0, model_width // block)
        def _(n):
            cols = pl.ds(pl.multiple_of(n * block, block), block)
            outs = []
            for e in range(local_experts):
                outs.append(jnp.dot(gated[buf, e], wd[e, :, cols], preferred_element_type=F32))
            for j in range(2):
                part = slice(j * cap, (j + 1) * cap)
                mine = jnp.concatenate([value[part] for value in outs], axis=0).astype(BF)
                parts[j, :, cols] = jnp.dot(picks[j], mine, preferred_element_type=F32).astype(BF)
            total = router_sum[:, cols]
            for j in range(2):
                total += jnp.dot(logits_row[j], held_tokens[j, :, cols], preferred_element_type=F32)
            router_sum[:, cols] = total

        put(0, q).start()
        put(1, q).start()

    @pl.loop(0, count)
    def _(k):
        compute(k)

        @pl.when(k < count - 1)
        def _():
            line.event(k)

    line.final(lambda a, q: None)
    put(0, 0).wait()
    put(1, 0).wait()
    line.to_sib(0, order(count - 1)).wait_send()
    line.to_sib(1, order(count - 1)).wait_send()
    take_x.wait()
    take_dy.wait()
    strip = 16

    def norm_back(n, total):
        rows = pl.ds(pl.multiple_of(n * strip, strip), strip)
        back = own[p, rows, :].astype(F32)
        x = x_mid[rows, :]
        scale = lax.rsqrt(jnp.mean(x * x, axis=1, keepdims=True) + EPSILON)
        u = gain_row[...] * back
        product = jnp.mean(u * x, axis=1, keepdims=True)
        grad = dy[rows, :].astype(F32) + scale * u - x * (scale * scale * scale * product)
        grad_ref[rows, :] = grad
        low_ref[rows, :] = grad.astype(BF)
        return total + jnp.sum(back * x * scale, axis=0, keepdims=True)

    norm_part = lax.fori_loop(0, tokens // strip, norm_back, jnp.zeros((1, model_width), F32))
    lanes = small_ref.shape[1]
    piece = 512
    for n in range(model_width // piece):
        cols = slice(n * piece, (n + 1) * piece)
        norm = jnp.broadcast_to(norm_part[:, cols], (8, piece))
        rest = jnp.zeros((lanes - experts - 8, piece), F32)
        small_ref[cols, :] = jnp.concatenate([router_sum[:, cols], norm, rest], axis=0).T

    line.finish()


def experts_out(
    gated,
    d_gate,
    d_up,
    dots,
    targets,
    targets_t,
    probs,
    router_t,
    w_gate_up,
    w_down,
    h2_all,
    x_mid,
    dy,
    gain_row,
    collective,
):
    local_experts, slots, hidden = gated.shape
    model_width = router_t.shape[1]
    shards, experts, tokens = probs.shape
    count = shards // 2
    anywhere = pl.BlockSpec(memory_space=ANY)
    vmem = pl.BlockSpec(memory_space=pltpu.VMEM)
    return pl.pallas_call(
        partial(experts_out_kernel, count, CAP),
        out_shape=[
            jax.ShapeDtypeStruct((shards, tokens, model_width // 2), BF),
            jax.ShapeDtypeStruct((shards, tokens, model_width // 2), BF),
            jax.ShapeDtypeStruct((tokens, model_width), F32),
            jax.ShapeDtypeStruct((tokens, model_width), BF),
            jax.ShapeDtypeStruct((model_width, 128), F32),
        ],
        in_specs=[anywhere] * 3 + [vmem] * 5 + [anywhere] * 5 + [vmem],
        out_specs=[anywhere, anywhere, vmem, vmem, vmem],
        scratch_shapes=[pltpu.VMEM(x.shape, BF) for x in (w_gate_up, w_down)]
        + [pltpu.VMEM((2, local_experts, 2 * CAP, hidden), BF)] * 3
        + [
            pltpu.VMEM((2, tokens, model_width), BF),
            pltpu.VMEM((tokens, model_width), BF),
            pltpu.VMEM((count, tokens, model_width), BF),
            pltpu.VMEM((count, tokens, model_width), BF),
            pltpu.VMEM((count + 1, tokens, model_width), BF),
            DMA((model_width // 512 + 1,)),
            DMA((3, 2)),
            DMA((2,)),
            pltpu.VMEM((2, tokens, model_width), BF),
            pltpu.VMEM((tokens, model_width), F32),
            pltpu.VMEM((tokens, model_width), BF),
            pltpu.VMEM((experts, model_width), F32),
            DMA((3,)),
        ]
        + [DMA((2, count))] * 7,
        compiler_params=pltpu.CompilerParams(
            collective_id=collective, has_side_effects=True, vmem_limit_bytes=67_043_328
        ),
        cost_estimate=pl.CostEstimate(flops=60_000_000_000, bytes_accessed=200_000_000, transcendentals=0),
        name="experts_out",
    )(
        gated,
        d_gate,
        d_up,
        dots,
        targets,
        targets_t,
        probs,
        router_t,
        w_gate_up,
        w_down,
        h2_all,
        x_mid,
        dy,
        gain_row,
    )


def rope_tables(seq_len, head_dim):
    half_dim = head_dim // 2
    inverse = np.float32(ROPE_BASE) ** (-(np.arange(half_dim, dtype=np.float32) * 2.0 / head_dim))
    angles = np.arange(seq_len, dtype=np.float32)[:, None] * inverse.astype(np.float32)[None, :]
    angles = np.concatenate([angles, angles], axis=-1).astype(np.float64)
    return (np.cos(angles).astype(np.float32), np.sin(angles).astype(np.float32))


def dot(left, right, sides=(1, 0), out=F32):
    return lax.dot_general(
        left, right, (((sides[0],), (sides[1],)), ((), ())), preferred_element_type=F32
    ).astype(out)


def inverse_rms(rows):
    return lax.rsqrt(jnp.mean(rows * rows, axis=-1, keepdims=True) + EPSILON)


def on_device(
    inputs,
    out_grad,
    doc_ids,
    routes,
    w_query,
    w_key,
    w_value,
    w_output,
    w_router,
    attn_gain,
    ffn_gain,
    query_gain,
    key_gain,
    w_gate,
    w_up,
    w_down,
):
    seq_count = lax.axis_size("seq")
    shards = lax.axis_size("fsdp")
    tok_rows, model_width = inputs.shape[1:]
    seq_len = tok_rows * seq_count
    rows = w_query.shape[0]
    width = model_width // seq_count
    local_experts = w_gate.shape[0]
    experts = w_router.shape[1]
    top_k = routes.shape[2]
    lanes = 128

    small = jnp.concatenate(
        [
            w_router,
            attn_gain[:, None],
            ffn_gain[:, None],
            jnp.zeros((rows, lanes - experts - 2), BF),
        ],
        axis=1,
    )
    gains = jnp.pad(jnp.stack([query_gain, key_gain]), ((0, 14), (0, lanes - rows)))
    wq, wk, wv, small_all, gains_all, routes_all, wo, x_all = gather_start(
        (w_query, w_key, w_value, small, gains, routes[0].T, w_output, inputs[0]), seq_count, shards, 0
    )
    x_all = x_all.reshape(seq_len, model_width)
    gate_up = jnp.concatenate([w_gate, w_up], axis=2)
    full_gate_up = lax.all_gather(gate_up, "seq", axis=1, tiled=True)
    full_down = lax.all_gather(w_down, "seq", axis=1, tiled=True)

    wq = wq.reshape(model_width, width)
    wk = wk.reshape(model_width, width)
    wv = wv.reshape(model_width, width)
    small_all = small_all.reshape(model_width, lanes)
    w_r = small_all[:, :experts]
    gain_a = small_all[:, experts].astype(F32)
    gain_f = small_all[:, experts + 1].astype(F32)
    gq = gains_all[:, 0, :rows].reshape(1, width).astype(F32)
    gk = gains_all[:, 1, :rows].reshape(1, width).astype(F32)

    x_float = x_all.astype(F32)
    h1 = (x_float * inverse_rms(x_float) * gain_a).astype(BF)
    h1 = lax.optimization_barrier(h1)
    q_raw, k_raw = lax.optimization_barrier((dot(h1, wq), dot(h1, wk)))
    values = dot(h1, wv, out=BF)
    squares = jnp.stack(
        [jnp.sum(q_raw * q_raw, axis=1), jnp.sum(k_raw * k_raw, axis=1)]
        + [jnp.ones((seq_len,), F32)] * 6
    )
    cos, sin = rope_tables(seq_len, HEAD)
    doc_row = doc_ids
    doc_col = doc_ids.reshape(seq_len, 1)
    attended, q_low, k_low, scales = attend(
        q_raw, k_raw, values, squares, gq, gk, cos, sin, doc_col, doc_row, model_width, seq_count, 1
    )
    wo = wo.reshape(width, model_width)
    projected = dot(attended, wo, out=BF).reshape(seq_count, tok_rows, model_width)
    rows_in = inputs[0].astype(F32)
    grad_rows = out_grad[0].astype(F32)
    summed, dy_all, targets, targets_t = middle(projected, out_grad[0], routes_all, local_experts, 2)
    x_mid = rows_in + summed
    scale_f = inverse_rms(x_mid)
    h2 = (x_mid * scale_f * gain_f).astype(BF)

    router_t = w_r.T
    h2_all, expert_in, grad_slots, act, by_up, by_gate, gate_slots, gate_probs = experts_in(
        h2, dy_all, targets, router_t, full_gate_up, 3
    )
    gated, d_gate, d_up, dots_slots, g_down = experts_mid(
        grad_slots, act, by_up, by_gate, gate_slots, full_down
    )
    parts_a, parts_b, grad_mid, grad_low, small_part = experts_out(
        gated,
        d_gate,
        d_up,
        dots_slots,
        targets,
        targets_t,
        gate_probs,
        router_t,
        full_gate_up,
        full_down,
        h2_all,
        x_mid,
        out_grad[0],
        gain_f[None],
        4,
    )

    def spread(part):
        return lax.psum_scatter(part, "seq", scatter_dimension=1, tiled=True)

    g_down = spread(g_down)
    grad_low, g_down = lax.optimization_barrier((grad_low, g_down))

    d_attn, sum_a, g_gate_up = turn_back(grad_low, parts_a, expert_in, d_gate, d_up, seq_count, shards, 5)
    g_gate_up = spread(g_gate_up)
    d_attn = d_attn.reshape(seq_len, model_width)
    d_heads = dot(d_attn, wo, (1, 1), BF)
    dq_low, dk_low, dv_low, gains_part, sum_b = attend_back(
        q_low,
        k_low,
        values,
        d_heads,
        q_raw,
        k_raw,
        scales,
        gq,
        gk,
        cos,
        sin,
        doc_col,
        doc_row,
        parts_b,
        rows,
        model_width,
        seq_count,
        6,
    )
    result = x_mid + jnp.concatenate([sum_a, sum_b], axis=1).astype(F32)

    sheet = (seq_count, shards, rows, width)
    g_query, g_key, g_value, g_output, g_small, g_gains, grad_h1 = scatter_end(
        (
            dot(h1, dq_low, (0, 0), BF).reshape(sheet),
            dot(h1, dk_low, (0, 0), BF).reshape(sheet),
            dot(h1, dv_low, (0, 0), BF).reshape(sheet),
            dot(attended, d_attn, (0, 0), BF).reshape(shards, rows, model_width),
            small_part.reshape(seq_count, shards, rows, lanes),
            gains_part,
        ),
        (dq_low, dk_low, dv_low, wq, wk, wv),
        seq_count,
        shards,
        7,
    )
    g_query, g_key, g_value = (g_query.astype(F32), g_key.astype(F32), g_value.astype(F32))

    scale_a = inverse_rms(rows_in)
    u_rows = gain_a * grad_h1
    input_grad = (
        grad_mid
        + scale_a * u_rows
        - rows_in * scale_a**3 * jnp.mean(u_rows * rows_in, axis=-1, keepdims=True)
    )
    pairs = (
        w_query.astype(F32) * g_query + w_key.astype(F32) * g_key + w_value.astype(F32) * g_value
    )
    g_attn_gain = jnp.sum(pairs, axis=1) / attn_gain.astype(F32)

    return (
        result.astype(BF)[None],
        input_grad[None],
        g_query,
        g_key,
        g_value,
        g_output.astype(F32),
        g_small[:, :experts],
        g_attn_gain,
        g_small[:, experts],
        g_gains[0, :rows],
        g_gains[1, :rows],
        g_gate_up[:, :, : g_gate_up.shape[2] // 2].astype(F32),
        g_gate_up[:, :, g_gate_up.shape[2] // 2 :].astype(F32),
        g_down.astype(F32),
    )


def solution(mesh):
    rows = P("fsdp", "seq", None)
    sheet = P(("seq", "fsdp"), None)
    line = P(("seq", "fsdp"))
    return jax.shard_map(
        on_device,
        mesh=mesh,
        in_specs=(rows, rows, P("fsdp", None), rows) + (sheet,) * 5 + (line,) * 4 + (rows,) * 3,
        out_specs=(rows, rows) + (sheet,) * 5 + (line,) * 4 + (rows,) * 3,
        check_vma=False,
    )
```

```python
from functools import partial

import jax
import jax.numpy as jnp
import numpy as np
from jax import lax
from jax.experimental import pallas as pl
from jax.experimental.pallas import tpu as pltpu
from jax.sharding import PartitionSpec as P

CAP = 136
HEAD = 128
EPSILON = 1e-05
ROPE_BASE = 10000.0
MASKED_OUT = -1e30
ANY = pl.ANY
MESH = pl.DeviceIdType.MESH
DMA = pltpu.SemaphoreType.DMA
BF = jnp.bfloat16
F32 = jnp.float32


def remote(src, dst, send, recv, **where):
    return pltpu.make_async_remote_copy(
        src_ref=src, dst_ref=dst, send_sem=send, recv_sem=recv, device_id=where, device_id_type=MESH
    )


def greet(count, places, seq_count=1):
    i, p, sib = places
    barrier = pltpu.get_barrier_semaphore()
    pl.semaphore_signal(barrier, inc=1, device_id={"fsdp": sib}, device_id_type=MESH)
    here = lax.axis_index("seq")
    for d in range(1, seq_count):
        peer = lax.rem(here + d, seq_count)
        pl.semaphore_signal(barrier, inc=1, device_id={"seq": peer}, device_id_type=MESH)

    @pl.when(p > 0)
    def _():
        pl.semaphore_signal(barrier, inc=1, device_id={"fsdp": i - 2}, device_id_type=MESH)

    @pl.when(p < count - 1)
    def _():
        pl.semaphore_signal(barrier, inc=1, device_id={"fsdp": i + 2}, device_id_type=MESH)

    last = count - 1
    pl.semaphore_wait(barrier, seq_count + (p + last) // count + (last - p + last) // count)


def slot_of(ref, axis, index):
    return ref.at[index] if axis == 0 else ref.at[:, index]


class LineGather:
    def __init__(self, count, places, refs, axes, send_r, send_l, send_s, recv):
        self.count, self.places = count, places
        self.refs, self.axes = refs, axes
        self.sems = (send_r, send_l, send_s, recv)

    def copy(self, a, slot, kind, t, device):
        send = self.sems[kind].at[a, t]
        ref = slot_of(self.refs[a], self.axes[a], slot)
        return remote(ref, ref, send, self.sems[3].at[a, slot], fsdp=device)

    def first(self, a):
        i, p, sib = self.places

        @pl.when(p < self.count - 1)
        def _():
            self.copy(a, i, 0, 0, i + 2).start()

        @pl.when(p > 0)
        def _():
            self.copy(a, i, 1, 0, i - 2).start()

        self.copy(a, i, 2, 0, sib).start()

    def forward(self, t):
        i, p, sib = self.places
        count = self.count
        for a in range(len(self.refs)):

            @pl.when(p - t >= 0)
            def _():
                slot = i - 2 * t
                self.copy(a, slot, 0, t, sib).wait_recv()

                @pl.when(p < count - 1)
                def _():
                    self.copy(a, slot, 0, t, i + 2).start()

                self.copy(a, slot, 2, t, sib).start()

            @pl.when(p + t < count)
            def _():
                slot = i + 2 * t
                self.copy(a, slot, 1, t, sib).wait_recv()

                @pl.when(p > 0)
                def _():
                    self.copy(a, slot, 1, t, i - 2).start()

                self.copy(a, slot, 2, count + t, sib).start()

    def finish(self):
        i, p, sib = self.places
        count = self.count
        for a in range(len(self.refs)):
            for q in range(count):
                self.copy(a, 2 * q + lax.rem(sib, 2), 2, 0, sib).wait_recv()
            self.copy(a, i, 2, 0, sib).wait_send()

            @pl.when(p < count - 1)
            def _():
                self.copy(a, i, 0, 0, i + 2).wait_send()

            @pl.when(p > 0)
            def _():
                self.copy(a, i, 1, 0, i - 2).wait_send()

            for t in range(1, count):

                @pl.when(p - t >= 0)
                def _():
                    slot = i - 2 * t

                    @pl.when(p < count - 1)
                    def _():
                        self.copy(a, slot, 0, t, i + 2).wait_send()

                    self.copy(a, slot, 2, t, sib).wait_send()

                @pl.when(p + t < count)
                def _():
                    slot = i + 2 * t

                    @pl.when(p > 0)
                    def _():
                        self.copy(a, slot, 1, t, i - 2).wait_send()

                    self.copy(a, slot, 2, count + t, sib).wait_send()


def line_sems(arrays, count):
    return [DMA((arrays, count)), DMA((arrays, count)), DMA((arrays, 2 * count)), DMA((arrays, 2 * count))]


def where_am_i():
    i = lax.axis_index("fsdp")
    p = i // 2
    c = i % 2
    return i, p, 2 * p + 1 - c


def start_kernel(count, seq_count, *refs):
    wq, wk, wv, small, gains, routes, wo, rows = refs[:8]
    outs = refs[8:15]
    rows_out = refs[15]
    holds = refs[16:24]
    send_x, recv_x, local, send_r, send_l, send_s, recv, send_y, recv_y = refs[24:]
    places = where_am_i()
    i = places[0]
    here = lax.axis_index("seq")
    width = wq.shape[1] // seq_count

    def columns(ref, peer):
        return ref.at[:, pl.ds(pl.multiple_of(peer * width, width), width)]

    own = [columns(wq, here), columns(wk, here), columns(wv, here), small, gains, routes, wo, rows]
    for a in range(8):
        pltpu.make_async_copy(own[a], holds[a], local.at[a]).start()
    greet(count, places, seq_count)

    def piece(a, d):
        peer = lax.rem(here + d, seq_count)
        src = small if a == 3 else columns((wq, wk, wv)[a], peer)
        return remote(src, outs[a].at[here, i], send_x.at[a, d - 1], recv_x.at[a, d - 1], seq=peer)

    def arrived(a, d):
        origin = lax.rem(here + seq_count - d, seq_count)
        ref = outs[a].at[origin, i]
        return remote(ref, ref, send_x.at[a, d - 1], recv_x.at[a, d - 1], seq=origin)

    for a in (3, 0, 1, 2):
        for d in range(1, seq_count):
            piece(a, d).start()
    gather = SeqGather(seq_count, rows, rows_out, send_y, recv_y)
    gather.begin()
    axes = [1, 1, 1, 1, 0, 0, 0]

    def target(a):
        return outs[a].at[here, i] if axes[a] == 1 else outs[a].at[i]

    for a in (4, 5, 6, 3, 0, 1, 2):
        pltpu.make_async_copy(own[a], holds[a], local.at[a]).wait()
        pltpu.make_async_copy(holds[a], target(a), local.at[a]).start()
    line = LineGather(count, places, outs, axes, send_r, send_l, send_s, recv)
    for a in (4, 5, 6, 3, 0, 1, 2):
        pltpu.make_async_copy(holds[a], target(a), local.at[a]).wait()
        if axes[a] == 1:
            for d in range(1, seq_count):
                arrived(a, d).wait_recv()
        line.first(a)
    pltpu.make_async_copy(rows, holds[7], local.at[7]).wait()
    pltpu.make_async_copy(holds[7], rows_out.at[here], local.at[7]).start()
    for t in range(1, count):
        line.forward(t)
        if t == 1:
            gather.relay()
    line.finish()
    pltpu.make_async_copy(holds[7], rows_out.at[here], local.at[7]).wait()
    gather.finish()
    for a in (3, 0, 1, 2):
        for d in range(1, seq_count):
            piece(a, d).wait_send()


def gather_start(arrays, seq_count, shards, collective):
    count = shards // 2
    wq, wk, wv, small, gains, routes, wo, tokens = arrays
    rows, model_width = wq.shape
    width = model_width // seq_count
    sheet = jax.ShapeDtypeStruct((seq_count, shards, rows, width), BF)
    shapes = [
        sheet,
        sheet,
        sheet,
        jax.ShapeDtypeStruct((seq_count, shards) + small.shape, BF),
        jax.ShapeDtypeStruct((shards,) + gains.shape, BF),
        jax.ShapeDtypeStruct((shards,) + routes.shape, jnp.int32),
        jax.ShapeDtypeStruct((shards,) + wo.shape, BF),
        jax.ShapeDtypeStruct((seq_count,) + tokens.shape, BF),
    ]
    holds = [pltpu.VMEM((rows, width), BF)] * 3 + [
        pltpu.VMEM(small.shape, BF),
        pltpu.VMEM(gains.shape, BF),
        pltpu.VMEM(routes.shape, jnp.int32),
        pltpu.VMEM(wo.shape, BF),
        pltpu.VMEM(tokens.shape, BF),
    ]
    return pl.pallas_call(
        partial(start_kernel, count, seq_count),
        out_shape=shapes,
        in_specs=[pl.BlockSpec(memory_space=ANY)] * 8,
        out_specs=[pl.BlockSpec(memory_space=ANY)] * 8,
        scratch_shapes=holds
        + [DMA((4, seq_count - 1)), DMA((4, seq_count - 1)), DMA((8,))]
        + line_sems(7, count)
        + seq_gather_sems(seq_count),
        compiler_params=pltpu.CompilerParams(collective_id=collective, has_side_effects=True),
        name="gather_start",
    )(*arrays)


def chunk_order(k, p, count):
    near = jnp.minimum(p, count - 1 - p)
    step = (k + 1) // 2
    both = jnp.where(k % 2 == 1, p - step, p + step)
    return jnp.where(k <= 2 * near, both, jnp.where(p < count - 1 - p, k, count - 1 - k))


class LineScatter:
    def __init__(self, count, places, sources, axes, bufs, sems):
        self.count, self.places = count, places
        self.sources, self.axes = sources, axes
        self.own, self.sib, self.inbox = bufs
        self.sems = sems

    def view(self, a, ref):
        return ref

    def load(self, a, q):
        i = self.places[0]
        src = slot_of(self.sources[a], self.axes[a], 2 * q + lax.rem(i, 2))
        return pltpu.make_async_copy(self.view(a, src), self.view(a, self.own[a].at[q]), self.sems[6].at[a, q])

    def to_sib(self, a, q):
        sib = self.places[2]
        src = slot_of(self.sources[a], self.axes[a], 2 * q + lax.rem(sib, 2))
        dst = self.view(a, self.sib[a].at[q])
        return remote(self.view(a, src), dst, self.sems[2].at[a, q], self.sems[5].at[a, q], fsdp=sib)

    def right(self, a, q):
        i = self.places[0]
        src, dst = self.view(a, self.own[a].at[q]), self.view(a, self.inbox[a].at[q])
        return remote(src, dst, self.sems[0].at[a, q], self.sems[3].at[a, q], fsdp=i + 2)

    def left(self, a, q):
        i, p, sib = self.places
        slot = jnp.where(q == p - 1, self.count, q)
        src, dst = self.view(a, self.own[a].at[q]), self.view(a, self.inbox[a].at[slot])
        return remote(src, dst, self.sems[1].at[a, q], self.sems[4].at[a, q], fsdp=i - 2)

    def begin_loads(self):
        for k in range(self.count):
            q = chunk_order(self.count - 1 - k, self.places[1], self.count)
            for a in range(len(self.sources)):
                self.load(a, q).start()

    def begin(self):
        for k in range(self.count):
            q = chunk_order(self.count - 1 - k, self.places[1], self.count)
            for a in range(len(self.sources)):
                self.to_sib(a, q).start()

    def add(self, a, q, others):
        own = self.own[a]
        lead = own.shape[1:-2]
        rows, width = own.shape[-2:]
        step = rows
        while step * width > 65536 and step % 16 == 0:
            step //= 2

        def strip(index):
            total = own[index].astype(F32) + self.sib[a][index].astype(F32)
            for slot in others:
                total += self.inbox[a][(slot,) + index[1:]].astype(F32)
            own[index] = total.astype(own.dtype)

        def rows_of(prefix):
            if step == rows:
                strip(prefix)
                return

            @pl.loop(0, rows // step)
            def _(k):
                strip(prefix + (pl.ds(pl.multiple_of(k * step, step), step),))

        if lead:
            for b in range(lead[0]):
                rows_of((q, b))
        else:
            rows_of((q,))

    def ready(self, a, q):
        self.load(a, q).wait()
        self.to_sib(a, q).wait_recv()

    def event(self, step):
        i, p, sib = self.places
        count = self.count
        arrays = range(len(self.sources))

        @pl.when(step >= p)
        def _():
            q = count - 1 - (step - p)
            for a in arrays:
                self.ready(a, q)

                @pl.when(p > 0)
                def _():
                    self.right(a, q).wait_recv()
                    self.add(a, q, [q])

                @pl.when(p == 0)
                def _():
                    self.add(a, q, [])

                self.right(a, q).start()

        @pl.when(step >= count - 1 - p)
        def _():
            q = step - (count - 1 - p)
            for a in arrays:
                self.ready(a, q)

                @pl.when(p < count - 1)
                def _():
                    self.left(a, q).wait_recv()
                    self.add(a, q, [q])

                @pl.when(p == count - 1)
                def _():
                    self.add(a, q, [])

                self.left(a, q).start()

    def final(self, after):
        i, p, sib = self.places
        count = self.count
        for a in range(len(self.sources)):
            self.ready(a, p)

            @pl.when(p > 0)
            def _():
                self.right(a, p).wait_recv()

            @pl.when(p < count - 1)
            def _():
                self.left(a, p).wait_recv()

            @pl.when(p == 0)
            def _():
                self.add(a, p, [count])

            @pl.when(p == count - 1)
            def _():
                self.add(a, p, [p])

            @pl.when((p > 0) & (p < count - 1))
            def _():
                self.add(a, p, [p, count])

            after(a, p)

    def run(self, after, between=None):
        @pl.loop(0, self.count - 1)
        def _(step):
            self.event(step)
            if between is not None:
                between(step)

        self.final(after)

    def finish(self):
        i, p, sib = self.places
        for a in range(len(self.sources)):
            for q in range(self.count):
                self.to_sib(a, q).wait_send()

                @pl.when(q > p)
                def _():
                    self.right(a, q).wait_send()

                @pl.when(q < p)
                def _():
                    self.left(a, q).wait_send()


class SplitScatter(LineScatter):
    def __init__(self, count, places, source, bufs, sems):
        super().__init__(count, places, [source] * 2, [0] * 2, tuple([buf] * 2 for buf in bufs), sems)
        self.half = bufs[0].shape[-1] // 2

    def cols(self, a):
        return pl.ds(a * self.half, self.half)

    def view(self, a, ref):
        return ref.at[:, self.cols(a)]

    def add(self, a, q, others):
        own = self.own[a]
        rows = own.shape[1]
        step = rows
        while step * self.half > 65536 and step % 16 == 0:
            step //= 2

        @pl.loop(0, rows // step)
        def _(k):
            index = (pl.ds(pl.multiple_of(k * step, step), step), self.cols(a))
            total = own[(q,) + index].astype(F32) + self.sib[a][(q,) + index].astype(F32)
            for slot in others:
                total += self.inbox[a][(slot,) + index].astype(F32)
            own[(q,) + index] = total.astype(own.dtype)


def end_kernel(count, seq_count, *refs):
    sources = refs[:6]
    factors = refs[6:12]
    outs = refs[12:18]
    sum_ref = refs[18]
    bufs = tuple(refs[19 + 6 * k : 25 + 6 * k] for k in range(3))
    landing = refs[37]
    sems = refs[38:45]
    send_x, recv_x, local = refs[45:48]
    held = refs[48:54]
    rows_ref, factor_sem = refs[54:56]
    seq = SeqScatter(seq_count, rows_ref, *refs[56:61])
    places = where_am_i()
    here = lax.axis_index("seq")
    width = sources[0].shape[3]
    line = LineScatter(count, places, sources, [1, 1, 1, 0, 1, 0], bufs, sems)
    line.begin_loads()
    for n in range(6):
        pltpu.make_async_copy(factors[n], held[n], factor_sem.at[n]).start()
    greet(count, places, seq_count)
    line.begin()
    own = bufs[0]

    def at_home(a, block):
        if a == 4:
            return landing.at[block]
        start = pl.multiple_of(block * width, width)
        return outs[a].at[:, pl.ds(start, width)]

    def piece(a, q, d):
        peer = lax.rem(here + d, seq_count)
        slot = 3 if a == 4 else a
        return remote(
            own[a].at[q, peer], at_home(a, here), send_x.at[slot, d - 1], recv_x.at[slot, d - 1], seq=peer
        )

    def arrived(a, d):
        origin = lax.rem(here + seq_count - d, seq_count)
        slot = 3 if a == 4 else a
        return remote(
            at_home(a, origin), at_home(a, origin), send_x.at[slot, d - 1], recv_x.at[slot, d - 1], seq=origin
        )

    def after(a, q):
        if a in (3, 5):
            pltpu.make_async_copy(own[a].at[q], outs[a], local.at[a]).start()
        else:
            for d in range(1, seq_count):
                piece(a, q, d).start()
            pltpu.make_async_copy(own[a].at[q, here], at_home(a, here), local.at[a]).start()

    def back_rows():
        for n in range(6):
            pltpu.make_async_copy(factors[n], held[n], factor_sem.at[n]).wait()
        tokens, model_width = rows_ref.shape[1:]
        tile = 512
        tiles = model_width // tile

        @pl.loop(0, seq_count * tiles)
        def _(u):
            block = u // tiles
            strip = pl.ds(pl.multiple_of(block * tokens, tokens), tokens)
            cols = pl.ds(pl.multiple_of(lax.rem(u, tiles) * tile, tile), tile)
            total = jnp.zeros((tokens, tile), F32)
            for n in range(3):
                total += lax.dot_general(
                    held[n][strip, :], held[3 + n][cols, :], (((1,), (1,)), ((), ())), preferred_element_type=F32
                )
            rows_ref[block, :, cols] = total.astype(BF)

        seq.begin_loads()
        seq.begin()

    def between(step):
        pl.when(step == 0)(back_rows)

        @pl.when(step == 1)
        def _():
            seq.relay()

    line.run(after, between)
    seq.total(sum_ref)
    for q in range(count):

        @pl.when(q == places[1])
        def _():
            for a in range(6):
                if a in (3, 5):
                    pltpu.make_async_copy(own[a].at[q], outs[a], local.at[a]).wait()
                else:
                    pltpu.make_async_copy(own[a].at[q, here], at_home(a, here), local.at[a]).wait()
                    for d in range(1, seq_count):
                        piece(a, q, d).wait_send()
                        arrived(a, d).wait_recv()

    total = landing[0]
    for block in range(1, seq_count):
        total += landing[block]
    landing[0] = total
    last = pltpu.make_async_copy(landing.at[0], outs[4], local.at[4])
    last.start()
    last.wait()
    line.finish()
    seq.finish()


def scatter_end(arrays, factors, seq_count, shards, collective):
    count = shards // 2
    gq, gk, gv, go, small, gains = arrays
    rows, width = gq.shape[2:]
    tokens, model_width = factors[0].shape[0] // seq_count, factors[3].shape[0]
    home = jax.ShapeDtypeStruct((rows, width * seq_count), BF)
    shapes = [
        home,
        home,
        home,
        jax.ShapeDtypeStruct(go.shape[1:], BF),
        jax.ShapeDtypeStruct(small.shape[2:], F32),
        jax.ShapeDtypeStruct(gains.shape[1:], F32),
        jax.ShapeDtypeStruct((tokens, model_width), F32),
    ]
    blocks, inboxes = [], []
    for a in range(6):
        shape = arrays[a].shape
        block = (shape[0],) + shape[2:] if a in (0, 1, 2, 4) else shape[1:]
        blocks.append(pltpu.VMEM((count,) + block, arrays[a].dtype))
        inboxes.append(pltpu.VMEM((count + 1,) + block, arrays[a].dtype))
    return pl.pallas_call(
        partial(end_kernel, count, seq_count),
        out_shape=shapes,
        in_specs=[pl.BlockSpec(memory_space=ANY)] * 12,
        out_specs=[pl.BlockSpec(memory_space=ANY)] * 6 + [pl.BlockSpec(memory_space=pltpu.VMEM)],
        scratch_shapes=blocks * 2
        + inboxes
        + [pltpu.VMEM((seq_count,) + small.shape[2:], F32)]
        + [DMA((6, count))] * 7
        + [DMA((4, seq_count - 1)), DMA((4, seq_count - 1)), DMA((6,))]
        + [pltpu.VMEM(x.shape, BF) for x in factors]
        + [pltpu.VMEM((seq_count, tokens, model_width), BF), DMA((6,))]
        + seq_scatter_scratch((tokens, model_width), BF, seq_count),
        compiler_params=pltpu.CompilerParams(
            collective_id=collective, has_side_effects=True, vmem_limit_bytes=62 << 20
        ),
        name="scatter_end",
    )(*arrays, *factors)


def greet_seq(seq_count):
    here = lax.axis_index("seq")
    barrier = pltpu.get_barrier_semaphore()
    for d in range(1, seq_count):
        peer = lax.rem(here + d, seq_count)
        pl.semaphore_signal(barrier, inc=1, device_id={"seq": peer}, device_id_type=MESH)
    pl.semaphore_wait(barrier, seq_count - 1)
    return here


class SeqScatter:
    def __init__(self, seq_count, x_ref, own, inbox, send, recv, local):
        here = lax.axis_index("seq")
        self.own, self.inbox, self.local, self.count = own, inbox, local, seq_count
        self.take = pltpu.make_async_copy(x_ref.at[here], own, local.at[0])
        rows = own.shape[0]
        self.half = rows // 2
        low, high = pl.ds(0, self.half), pl.ds(self.half, self.half)
        if seq_count != 4:
            self.copies = []
            for d in range(1, seq_count):
                peer = lax.rem(here + d, seq_count)
                self.copies.append(
                    remote(x_ref.at[peer], inbox.at[d - 1], send.at[d - 1], recv.at[d - 1], seq=peer)
                )
            return
        beside = here + 1 - 2 * lax.rem(here, 2)
        across = lax.rem(here + 2, 4)
        corner = 3 - here
        self.loads = [
            pltpu.make_async_copy(x_ref.at[across, low], inbox.at[3, low], local.at[1]),
            pltpu.make_async_copy(x_ref.at[beside, high], inbox.at[3, high], local.at[2]),
        ]
        plans = (
            (x_ref.at[corner, low], inbox.at[2, low], beside),
            (x_ref.at[corner, high], inbox.at[2, high], across),
            (x_ref.at[beside, low], inbox.at[0, low], beside),
            (x_ref.at[across, high], inbox.at[1, high], across),
            (inbox.at[3, low], inbox.at[1, low], across),
            (inbox.at[3, high], inbox.at[0, high], beside),
        )
        self.copies = [
            remote(src, dst, send.at[n], recv.at[n], seq=peer) for n, (src, dst, peer) in enumerate(plans)
        ]

    def begin_loads(self):
        self.take.start()
        if self.count == 4:
            for load in self.loads:
                load.start()

    def begin(self):
        for copy in self.copies[:4] if self.count == 4 else self.copies:
            copy.start()

    def strips(self, start, rows, body):
        step = min(32, rows)

        @pl.loop(0, rows // step)
        def _(k):
            body(pl.ds(pl.multiple_of(start + k * step, step), step))

    def relay(self):
        if self.count != 4:
            return
        inbox = self.inbox

        def add(strip):
            inbox[3, strip, :] = (
                inbox[3, strip, :].astype(F32) + inbox[2, strip, :].astype(F32)
            ).astype(inbox.dtype)

        for n, start in ((0, 0), (1, self.half)):
            self.loads[n].wait()
            self.copies[n].wait_recv()
            self.strips(start, self.half, add)
            self.copies[4 + n].start()

    def total(self, o_ref):
        self.take.wait()
        for copy in self.copies[2:] if self.count == 4 else self.copies:
            copy.wait_recv()
        parts = 2 if self.count == 4 else self.count - 1

        def add(strip):
            total = self.own[strip, :].astype(F32)
            for d in range(parts):
                total += self.inbox[d, strip, :].astype(F32)
            o_ref[strip, :] = total

        self.strips(0, self.own.shape[0], add)

    def finish(self):
        for copy in self.copies:
            copy.wait_send()


def seq_scatter_scratch(block, dtype, seq_count):
    boxes = 4 if seq_count == 4 else seq_count - 1
    copies = 6 if seq_count == 4 else seq_count - 1
    return [
        pltpu.VMEM(block, dtype),
        pltpu.VMEM((boxes,) + block, dtype),
        DMA((copies,)),
        DMA((copies,)),
        DMA((3,)),
    ]


class SeqGather:
    def __init__(self, seq_count, x_ref, o_ref, send, recv):
        here = lax.axis_index("seq")
        self.count = seq_count
        rows = x_ref.shape[0]
        low, high = pl.ds(0, rows // 2), pl.ds(rows // 2, rows // 2)
        if seq_count != 4:
            peers = [lax.rem(here + d, seq_count) for d in range(1, seq_count)]
            origins = [lax.rem(here + seq_count - d, seq_count) for d in range(1, seq_count)]
            out = [(x_ref, o_ref.at[here], peer) for peer in peers]
            landed = [o_ref.at[origin] for origin in origins]
        else:
            beside = here + 1 - 2 * lax.rem(here, 2)
            across = lax.rem(here + 2, 4)
            corner = 3 - here
            out = [
                (x_ref, o_ref.at[here], beside),
                (x_ref, o_ref.at[here], across),
                (o_ref.at[across, low], o_ref.at[across, low], beside),
                (o_ref.at[beside, high], o_ref.at[beside, high], across),
            ]
            landed = [o_ref.at[beside], o_ref.at[across], o_ref.at[corner, low], o_ref.at[corner, high]]
        self.sends = [
            remote(src, dst, send.at[n], recv.at[n], seq=peer) for n, (src, dst, peer) in enumerate(out)
        ]
        self.lands = [
            remote(ref, ref, send.at[n], recv.at[n], seq=out[n][2]) for n, ref in enumerate(landed)
        ]

    def begin(self):
        for copy in self.sends[:2] if self.count == 4 else self.sends:
            copy.start()

    def relay(self):
        if self.count == 4:
            for n in (0, 1):
                self.lands[n].wait_recv()
            for n in (2, 3):
                self.sends[n].start()

    def finish(self):
        for n, copy in enumerate(self.lands):
            if self.count != 4 or n > 1:
                copy.wait_recv()
        for copy in self.sends:
            copy.wait_send()


def seq_gather_sems(seq_count):
    copies = 4 if seq_count == 4 else seq_count - 1
    return [DMA((copies,)), DMA((copies,))]


def slot_targets(first, local_experts, cap, routes, targets, targets_t):
    shards, top_k, tokens = routes.shape
    earlier = lax.broadcasted_iota(jnp.int32, (tokens, tokens), 0)
    later = lax.broadcasted_iota(jnp.int32, (tokens, tokens), 1)
    upto = jnp.where(earlier <= later, 1.0, 0.0).astype(BF)
    row = lax.broadcasted_iota(jnp.int32, (8, tokens), 0)
    for j in range(shards):
        named = routes[j]
        chosen = jnp.zeros((8, tokens), F32)
        for e in range(local_experts):
            hit = jnp.max(jnp.where(named == first + e, 1.0, 0.0), axis=0, keepdims=True)
            chosen = jnp.where(row == e, hit, chosen)
        place = jnp.dot(chosen.astype(BF), upto, preferred_element_type=F32) - 1.0
        slot = jnp.where(chosen > 0.5, place + (cap * row).astype(F32), -1.0)
        targets[j] = slot[0:local_experts].astype(jnp.int32)
        targets_t[j] = slot.T[:, 0:local_experts].astype(jnp.int32)


def middle_kernel(
    count,
    seq_count,
    cap,
    x_ref,
    dy_ref,
    routes,
    o_ref,
    all_ref,
    targets,
    targets_t,
    own,
    inbox,
    xs,
    xr,
    xl,
    hold,
    s0,
    s1,
    s2,
    recv,
    local,
):
    places = where_am_i()
    i = places[0]
    seq = SeqScatter(seq_count, x_ref, own, inbox, xs, xr, xl)
    seq.begin_loads()
    take = pltpu.make_async_copy(dy_ref, hold, local.at[0])
    take.start()
    greet(count, places, seq_count)
    seq.begin()
    take.wait()
    put = pltpu.make_async_copy(hold, all_ref.at[i], local.at[1])
    put.start()
    put.wait()
    line = LineGather(count, places, [all_ref], [0], s0, s1, s2, recv)
    line.first(0)
    local_experts = targets.shape[1]
    slot_targets(i * local_experts, local_experts, cap, routes, targets, targets_t)
    for t in range(1, count):
        line.forward(t)
        if t == 1:
            seq.relay()
    seq.total(o_ref)
    line.finish()
    seq.finish()


def middle(blocks, dy, routes, local_experts, collective):
    shards, _, tokens = routes.shape
    count = shards // 2
    seq_count = blocks.shape[0]
    block = blocks.shape[1:]
    anywhere = pl.BlockSpec(memory_space=ANY)
    vmem = pl.BlockSpec(memory_space=pltpu.VMEM)
    return pl.pallas_call(
        partial(middle_kernel, count, seq_count, CAP),
        out_shape=[
            jax.ShapeDtypeStruct(block, F32),
            jax.ShapeDtypeStruct((shards,) + dy.shape, dy.dtype),
            jax.ShapeDtypeStruct((shards, local_experts, tokens), jnp.int32),
            jax.ShapeDtypeStruct((shards, tokens, local_experts), jnp.int32),
        ],
        in_specs=[anywhere, anywhere, vmem],
        out_specs=[vmem, pl.BlockSpec(memory_space=pltpu.HBM), vmem, vmem],
        scratch_shapes=seq_scatter_scratch(block, blocks.dtype, seq_count)
        + [pltpu.VMEM(dy.shape, dy.dtype)]
        + line_sems(1, count)
        + [DMA((2,))],
        compiler_params=pltpu.CompilerParams(
            collective_id=collective, has_side_effects=True, vmem_limit_bytes=32 << 20
        ),
        name="middle",
    )(blocks, dy, routes)


def turn_kernel(
    count,
    seq_count,
    x_ref,
    parts_ref,
    left_ref,
    right0,
    right1,
    o_ref,
    sum_ref,
    grad_ref,
    hold,
    send,
    recv,
    one,
    tiles_in,
    held,
    staged,
    outer_sem,
    own,
    sib,
    inbox,
    *sems,
):
    places = where_am_i()
    here = lax.axis_index("seq")
    line = SplitScatter(count, places, parts_ref, (own, sib, inbox), sems)
    grads = OuterGrads(left_ref, (right0, right1), grad_ref, (tiles_in, held, staged, outer_sem), count - 1)
    line.begin_loads()
    take = pltpu.make_async_copy(x_ref, hold, one)
    take.start()
    grads.begin()
    greet(count, places, seq_count)
    rows = SeqGather(seq_count, x_ref, o_ref, send, recv)
    rows.begin()
    line.begin()
    take.wait()
    put = pltpu.make_async_copy(hold, o_ref.at[here], one)
    put.start()

    def after(a, q):
        out = pltpu.make_async_copy(line.view(a, own.at[q]), line.view(a, sum_ref), sems[6].at[a, q])
        out.start()
        out.wait()

    def between(step):
        grads.between(step)

        @pl.when(step == 1)
        def _():
            rows.relay()

    line.run(after, between)
    grads.finish()
    put.wait()
    rows.finish()
    line.finish()


def turn_back(block, parts, expert_in, d_gate, d_up, seq_count, shards, collective):
    count = shards // 2
    part = parts.shape[1:]
    model_width = block.shape[1]
    anywhere = pl.BlockSpec(memory_space=ANY)
    return pl.pallas_call(
        partial(turn_kernel, count, seq_count),
        out_shape=[
            jax.ShapeDtypeStruct((seq_count,) + block.shape, block.dtype),
            jax.ShapeDtypeStruct(part, parts.dtype),
            jax.ShapeDtypeStruct((d_gate.shape[0], model_width, 2 * d_gate.shape[2]), BF),
        ],
        in_specs=[anywhere] * 5,
        out_specs=[anywhere] * 3,
        scratch_shapes=[pltpu.VMEM(block.shape, block.dtype)]
        + seq_gather_sems(seq_count)
        + [DMA]
        + outer_scratch(d_up, 512, 2)
        + [pltpu.VMEM((count,) + part, BF)] * 2
        + [pltpu.VMEM((count + 1,) + part, BF)]
        + [DMA((2, count))] * 7,
        compiler_params=pltpu.CompilerParams(
            collective_id=collective, has_side_effects=True, vmem_limit_bytes=60 << 20
        ),
        cost_estimate=pl.CostEstimate(flops=60_000_000_000, bytes_accessed=200_000_000, transcendentals=0),
        name="turn_back",
    )(block, parts, expert_in, d_gate, d_up)


def half_sign(shape):
    lane = lax.broadcasted_iota(jnp.int32, shape, 1)
    return jnp.where(lane < shape[1] // 2, -1.0, 1.0)


def turn(value):
    return pltpu.roll(value, value.shape[1] // 2, 1)


def block_probs(q_rows, keys, doc_col, doc_row, start, scale_by):
    end = keys.shape[0]
    scores = (
        lax.dot_general(q_rows, keys, (((1,), (1,)), ((), ())), preferred_element_type=F32) * scale_by
    )
    shape = scores.shape
    query_pos = start + lax.broadcasted_iota(jnp.int32, shape, 0)
    key_pos = lax.broadcasted_iota(jnp.int32, shape, 1)
    allowed = (doc_col == doc_row) & (key_pos <= query_pos)
    scores = jnp.where(allowed, scores, MASKED_OUT)
    weights = jnp.exp(scores - jnp.max(scores, axis=-1, keepdims=True))
    return weights * (1.0 / jnp.sum(weights, axis=-1, keepdims=True))


class SeqSum:
    def __init__(self, seq_count, sheet, inbox, send, recv):
        here = lax.axis_index("seq")
        self.sheet, self.inbox = sheet, inbox
        self.copies = []
        for d in range(1, seq_count):
            peer = lax.rem(here + d, seq_count)
            self.copies.append(remote(sheet, inbox.at[d - 1], send.at[d - 1], recv.at[d - 1], seq=peer))

    def begin(self):
        for copy in self.copies:
            copy.start()

    def total(self):
        for copy in self.copies:
            copy.wait_recv()
        total = self.sheet[...]
        for d in range(len(self.copies)):
            total += self.inbox[d]
        for copy in self.copies:
            copy.wait_send()
        return total


def attend_kernel(
    seq_count,
    row_block,
    model_width,
    q_raw,
    k_raw,
    v_ref,
    squares,
    gq,
    gk,
    cos,
    sin,
    doc_col,
    doc_row,
    o_ref,
    q_out,
    k_out,
    scales,
    inbox,
    send,
    recv,
):
    seq_len = q_raw.shape[0]

    @pl.when(pl.program_id(0) == 0)
    def _():
        greet_seq(seq_count)
        sums = SeqSum(seq_count, squares, inbox, send, recv)
        sums.begin()
        scales[...] = lax.rsqrt(sums.total() / model_width + EPSILON).T

    sign = half_sign(cos.shape)

    def rotated(raw, lane, gain):
        value = raw[...] * scales[:, lane : lane + 1] * gain[...]
        return (value * cos[...] + turn(value) * (sin[...] * sign)).astype(BF)

    q_out[...] = rotated(q_raw, 0, gq)
    k_out[...] = rotated(k_raw, 1, gk)
    scale_by = HEAD ** (-0.5)
    for start in range(0, seq_len, row_block):
        end = start + row_block
        probs = block_probs(
            q_out[start:end, :], k_out[:end, :], doc_col[start:end, :], doc_row[:, :end], start, scale_by
        )
        o_ref[start:end, :] = jnp.dot(
            probs.astype(BF), v_ref[:end, :], preferred_element_type=F32
        ).astype(BF)


def attend(q_raw, k_raw, values, squares, gq, gk, cos, sin, doc_col, doc_row, model_width, seq_count, collective):
    seq_len, width = q_raw.shape
    head = pl.BlockSpec((seq_len, HEAD), lambda h: (0, h))
    gain = pl.BlockSpec((1, HEAD), lambda h: (0, h))

    def whole(shape):
        return pl.BlockSpec(shape, lambda h: (0, 0))

    out = jax.ShapeDtypeStruct((seq_len, width), BF)
    return pl.pallas_call(
        partial(attend_kernel, seq_count, 256, model_width),
        grid=(width // HEAD,),
        out_shape=[
            out,
            out,
            out,
            jax.ShapeDtypeStruct((seq_len, 8), F32),
        ],
        in_specs=[head, head, head, whole(squares.shape), gain, gain, whole(cos.shape), whole(sin.shape)]
        + [whole(doc_col.shape), whole(doc_row.shape)],
        out_specs=[head, head, head, whole((seq_len, 8))],
        scratch_shapes=[
            pltpu.VMEM((seq_count - 1,) + squares.shape, F32),
            DMA((seq_count - 1,)),
            DMA((seq_count - 1,)),
        ],
        compiler_params=pltpu.CompilerParams(
            collective_id=collective, has_side_effects=True, vmem_limit_bytes=48 << 20
        ),
        name="attend",
    )(q_raw, k_raw, values, squares, gq, gk, cos, sin, doc_col, doc_row)


def attend_back_kernel(
    count,
    seq_count,
    heads,
    row_block,
    model_width,
    q_low,
    k_low,
    v_ref,
    do_ref,
    q_raw,
    k_raw,
    scales,
    gq,
    gk,
    cos,
    sin,
    doc_col,
    doc_row,
    parts_ref,
    dq_ref,
    dk_ref,
    dv_ref,
    gain_ref,
    sum_ref,
    dq_acc,
    dk_acc,
    dv_acc,
    uq,
    uk,
    dots,
    sheet,
    inbox,
    send,
    recv,
    own,
    sib,
    landed,
    *sems,
):
    seq_len = q_low.shape[0]
    head = pl.program_id(0)
    scale_by = HEAD ** (-0.5)
    places = where_am_i()
    line = LineScatter(count, places, [parts_ref], [0], ([own], [sib], [landed]), sems)

    @pl.when(head == 0)
    def _():
        line.begin_loads()
        greet(count, places, seq_count)
        line.begin()
        dots[...] = jnp.zeros_like(dots)

    dk_acc[...] = jnp.zeros_like(dk_acc)
    dv_acc[...] = jnp.zeros_like(dv_acc)
    for start in range(0, seq_len, row_block):
        end = start + row_block
        rows = slice(start, end)
        probs = block_probs(
            q_low[rows, :], k_low[:end, :], doc_col[rows, :], doc_row[:, :end], start, scale_by
        )
        grad_rows = do_ref[rows, :]
        grad_probs = lax.dot_general(
            grad_rows, v_ref[:end, :], (((1,), (1,)), ((), ())), preferred_element_type=F32
        )
        centre = jnp.sum(probs * grad_probs, axis=-1, keepdims=True)
        grad_scores = (probs * (grad_probs - centre)).astype(BF)
        dq_acc[rows, :] = jnp.dot(grad_scores, k_low[:end, :], preferred_element_type=F32)
        over_rows = (((0,), (0,)), ((), ()))
        dk_acc[:end, :] += lax.dot_general(
            grad_scores, q_low[rows, :], over_rows, preferred_element_type=F32
        )
        dv_acc[:end, :] += lax.dot_general(
            probs.astype(BF), grad_rows, over_rows, preferred_element_type=F32
        )
        if start == row_block:

            @pl.when(head == 0)
            def _():
                line.event(0)

    dv_ref[...] = dv_acc[...].astype(BF)
    sign = half_sign(cos.shape)
    cols = pl.ds(pl.multiple_of(head * HEAD, HEAD), HEAD)
    blocks, _, lanes = gain_ref.shape
    rows = HEAD // blocks

    def unrotated(acc, raw, gain, u_ref, lane):
        low = (acc[...] * scale_by).astype(BF).astype(F32)
        back = low * cos[...] - turn(low * sin[...]) * sign
        value = raw[:, cols]
        grad_gain = jnp.sum(back * value * scales[:, lane : lane + 1], axis=0, keepdims=True)
        u = back * gain[...]
        u_ref[:, cols] = u
        dots[:, lane : lane + 1] += jnp.sum(u * value, axis=1, keepdims=True)
        return grad_gain

    grads = (unrotated(dq_acc, q_raw, gq, uq, 0), unrotated(dk_acc, k_raw, gk, uk, 1))
    which = lax.broadcasted_iota(jnp.int32, (8, lanes), 0)
    both = jnp.where(which == 0, grads[0], jnp.where(which == 1, grads[1], 0.0))
    for block in range(blocks):
        gain_ref[block] = both if block == 0 else pltpu.roll(both, lanes - block * rows, 1)

    for step in range(1, count - 1):

        @pl.when(head == min(step, heads - 1))
        def _():
            line.event(step)

    @pl.when(head == heads - 1)
    def _():
        sheet[...] = dots[...].T
        sums = SeqSum(seq_count, sheet, inbox, send, recv)
        sums.begin()
        dots[...] = sums.total().T / model_width
        strip = 128

        @pl.loop(0, seq_len // strip)
        def _(n):
            part = pl.ds(pl.multiple_of(n * strip, strip), strip)
            for lane, u_ref, raw, out in ((0, uq, q_raw, dq_ref), (1, uk, k_raw, dk_ref)):
                scale = scales[part, lane : lane + 1]
                product = dots[part, lane : lane + 1]
                out[part, :] = (
                    scale * u_ref[part, :] - raw[part, :] * (scale * scale * scale * product)
                ).astype(BF)

        def after(a, q):
            out = pltpu.make_async_copy(own.at[q], sum_ref, sems[6].at[0, q])
            out.start()
            out.wait()

        line.final(after)
        line.finish()


def attend_back(
    q_low,
    k_low,
    values,
    d_heads,
    q_raw,
    k_raw,
    scales,
    gq,
    gk,
    cos,
    sin,
    doc_col,
    doc_row,
    parts,
    rows,
    model_width,
    seq_count,
    collective,
):
    seq_len, width = q_raw.shape
    heads = width // HEAD
    blocks = HEAD // rows
    shards = parts.shape[0]
    count = shards // 2
    part = parts.shape[1:]
    head = pl.BlockSpec((seq_len, HEAD), lambda h: (0, h))
    gain = pl.BlockSpec((1, HEAD), lambda h: (0, h))

    def whole(shape):
        return pl.BlockSpec(shape, lambda h: (0, 0))

    def once(x):
        return pl.BlockSpec(x.shape, lambda h: (0, 0), pipeline_mode=pl.Buffered(1))

    out = jax.ShapeDtypeStruct((seq_len, width), BF)
    return pl.pallas_call(
        partial(attend_back_kernel, count, seq_count, heads, 256, model_width),
        grid=(heads,),
        out_shape=[
            out,
            out,
            out,
            jax.ShapeDtypeStruct((width // rows, 8, HEAD), F32),
            jax.ShapeDtypeStruct(part, BF),
        ],
        in_specs=[head] * 4
        + [once(q_raw), once(k_raw), once(scales), gain, gain, once(cos), once(sin)]
        + [once(doc_col), once(doc_row), pl.BlockSpec(memory_space=ANY)],
        out_specs=[
            whole((seq_len, width)),
            whole((seq_len, width)),
            head,
            pl.BlockSpec((blocks, 8, HEAD), lambda h: (h, 0, 0)),
            pl.BlockSpec(memory_space=ANY),
        ],
        scratch_shapes=[pltpu.VMEM((seq_len, HEAD), F32)] * 3
        + [pltpu.VMEM((seq_len, width), F32)] * 2
        + [
            pltpu.VMEM((seq_len, 8), F32),
            pltpu.VMEM((8, seq_len), F32),
            pltpu.VMEM((seq_count - 1, 8, seq_len), F32),
            DMA((seq_count - 1,)),
            DMA((seq_count - 1,)),
        ]
        + [pltpu.VMEM((count,) + part, BF)] * 2
        + [pltpu.VMEM((count + 1,) + part, BF)]
        + [DMA((1, count))] * 7,
        compiler_params=pltpu.CompilerParams(
            collective_id=collective, has_side_effects=True, vmem_limit_bytes=60 << 20
        ),
        name="attend_back",
    )(q_low, k_low, values, d_heads, q_raw, k_raw, scales, gq, gk, cos, sin, doc_col, doc_row, parts)


def experts_in_kernel(
    count,
    cap,
    h2_ref,
    dy_ref,
    targets,
    router_t,
    wgu_ref,
    h2_out,
    x_out,
    y_out,
    act_out,
    by_up_out,
    by_gate_out,
    gate_slots,
    probs_out,
    h2,
    wgu,
    dy,
    xs,
    ys,
    acts,
    by_up,
    by_gate,
    s0,
    s1,
    s2,
    recv,
    w_sem,
    dy_sem,
    h_sem,
    out_sem,
):
    places = where_am_i()
    i, p, sib = places
    local_experts, model_width, hidden = wgu_ref.shape
    hidden = hidden // 2
    tokens = h2_ref.shape[0]
    experts = router_t.shape[0]
    own_in = pltpu.make_async_copy(h2_ref, h2.at[i], h_sem.at[0])
    own_in.start()

    def fetch(q, buf):
        src = dy_ref.at[pl.ds(2 * q, 2)]
        return pltpu.make_async_copy(src, dy.at[buf], dy_sem.at[buf])

    fetch(p, 0).start()
    for e in range(local_experts):
        pltpu.make_async_copy(wgu_ref.at[e], wgu.at[e], w_sem.at[e]).start()
    greet(count, places)
    own_in.wait()
    line = LineGather(count, places, [h2], [0], s0, s1, s2, recv)
    line.first(0)
    staged = ((xs, x_out), (ys, y_out), (acts, act_out), (by_up, by_up_out), (by_gate, by_gate_out))

    def store(n, e, q):
        rows = pl.ds(pl.multiple_of(q * 2 * cap, 2 * cap), 2 * cap)
        return pltpu.make_async_copy(staged[n][0].at[e], staged[n][1].at[e, rows], out_sem.at[n, e])

    def keep(q):
        src = h2.at[pl.ds(2 * q, 2)]
        return pltpu.make_async_copy(src, h2_out.at[pl.ds(2 * q, 2)], h_sem.at[1])

    slot_rows = lax.broadcasted_iota(jnp.int32, (local_experts * cap, tokens), 0)
    expert_rows = lax.broadcasted_iota(jnp.int32, (experts, tokens), 0)

    @pl.loop(0, count)
    def _(k):
        q = chunk_order(k, p, count)
        buf = k % 2

        @pl.when(k > 0)
        def _():
            line.forward(k)

        line.copy(0, 2 * q + lax.rem(sib, 2), 2, 0, sib).wait_recv()
        fetch(q, buf).wait()

        @pl.when(k + 1 < count)
        def _():
            fetch(chunk_order(k + 1, p, count), 1 - buf).start()

        @pl.when(k > 0)
        def _():
            for n in range(5):
                for e in range(local_experts):
                    store(n, e, q).wait()
            keep(q).wait()

        keep(q).start()
        picks = []
        for j in range(2):
            slot = 2 * q + j
            tokens_j = h2[slot]
            logits = lax.dot_general(
                router_t[...], tokens_j, (((1,), (1,)), ((), ())), preferred_element_type=F32
            )
            shifted = jnp.exp(logits - jnp.max(logits, axis=0, keepdims=True))
            probs = shifted / jnp.sum(shifted, axis=0, keepdims=True)
            probs_out[slot] = probs
            pick = None
            for e in range(local_experts):
                mask = slot_rows == targets[slot, e : e + 1, :]
                gate = jnp.sum(
                    jnp.where(expert_rows == i * local_experts + e, probs, 0.0), axis=0, keepdims=True
                )
                part = slice(e * cap, (e + 1) * cap)
                gate_slots[e, q, j * cap : (j + 1) * cap, :] = jnp.sum(
                    jnp.where(mask[part], gate, 0.0), axis=1, keepdims=True
                )
                pick = mask if pick is None else pick | mask
            picks.append(jnp.where(pick, 1.0, 0.0).astype(BF))

        block = 512

        @pl.loop(0, model_width // block)
        def _(n):
            cols = pl.ds(pl.multiple_of(n * block, block), block)
            for source, target in ((0, xs), (1, ys)):
                got = []
                for j in range(2):
                    rows = h2[2 * q + j, :, cols] if source == 0 else dy[buf, j, :, cols]
                    got.append(jnp.dot(picks[j], rows, preferred_element_type=F32))
                for e in range(local_experts):
                    part = slice(e * cap, (e + 1) * cap)
                    target[e, :, cols] = jnp.concatenate([got[0][part], got[1][part]], axis=0).astype(BF)

        for e in range(local_experts):
            store(0, e, q).start()
            store(1, e, q).start()

            @pl.when(k == 0)
            def _():
                pltpu.make_async_copy(wgu_ref.at[e], wgu.at[e], w_sem.at[e]).wait()

            wide = 256

            @pl.loop(0, hidden // wide)
            def _(n):
                cols = pl.ds(pl.multiple_of(n * wide, wide), wide)
                beyond = pl.ds(pl.multiple_of(hidden + n * wide, wide), wide)
                gate = jnp.dot(xs[e], wgu[e, :, cols], preferred_element_type=F32)
                up = jnp.dot(xs[e], wgu[e, :, beyond], preferred_element_type=F32)
                sigmoid = 1.0 / (1.0 + jnp.exp(-gate))
                silu = gate * sigmoid
                acts[e, :, cols] = (silu * up).astype(BF)
                by_up[e, :, cols] = silu.astype(BF)
                by_gate[e, :, cols] = (up * sigmoid * (1.0 + gate * (1.0 - sigmoid))).astype(BF)

            for n in (2, 3, 4):
                store(n, e, q).start()

    for n in range(5):
        for e in range(local_experts):
            store(n, e, 0).wait()
    keep(0).wait()
    sends_done(line)


def sends_done(line):
    i, p, sib = line.places
    count = line.count
    line.copy(0, i, 2, 0, sib).wait_send()

    @pl.when(p < count - 1)
    def _():
        line.copy(0, i, 0, 0, i + 2).wait_send()

    @pl.when(p > 0)
    def _():
        line.copy(0, i, 1, 0, i - 2).wait_send()

    for t in range(1, count):

        @pl.when(p - t >= 0)
        def _():
            slot = i - 2 * t

            @pl.when(p < count - 1)
            def _():
                line.copy(0, slot, 0, t, i + 2).wait_send()

            line.copy(0, slot, 2, t, sib).wait_send()

        @pl.when(p + t < count)
        def _():
            slot = i + 2 * t

            @pl.when(p > 0)
            def _():
                line.copy(0, slot, 1, t, i - 2).wait_send()

            line.copy(0, slot, 2, count + t, sib).wait_send()


def experts_in(h2, dy_all, targets, router_t, w_gate_up, collective):
    shards, tokens, model_width = dy_all.shape
    local_experts, _, hidden = w_gate_up.shape
    hidden = hidden // 2
    experts = router_t.shape[0]
    count = shards // 2
    wide = jax.ShapeDtypeStruct((local_experts, count * 2 * CAP, model_width), BF)
    thin = jax.ShapeDtypeStruct((local_experts, count * 2 * CAP, hidden), BF)
    anywhere = pl.BlockSpec(memory_space=ANY)
    vmem = pl.BlockSpec(memory_space=pltpu.VMEM)
    return pl.pallas_call(
        partial(experts_in_kernel, count, CAP),
        out_shape=[
            jax.ShapeDtypeStruct((shards, tokens, model_width), BF),
            wide,
            wide,
            thin,
            thin,
            thin,
            jax.ShapeDtypeStruct((local_experts, count, 2 * CAP, 1), F32),
            jax.ShapeDtypeStruct((shards, experts, tokens), F32),
        ],
        in_specs=[anywhere, anywhere, vmem, vmem, anywhere],
        out_specs=[anywhere] * 6 + [vmem, vmem],
        scratch_shapes=[
            pltpu.VMEM((shards, tokens, model_width), BF),
            pltpu.VMEM(w_gate_up.shape, BF),
            pltpu.VMEM((2, 2, tokens, model_width), BF),
        ]
        + [pltpu.VMEM((local_experts, 2 * CAP, model_width), BF)] * 2
        + [pltpu.VMEM((local_experts, 2 * CAP, hidden), BF)] * 3
        + line_sems(1, count)
        + [DMA((local_experts,)), DMA((2,)), DMA((2,)), DMA((5, local_experts))],
        compiler_params=pltpu.CompilerParams(
            collective_id=collective, has_side_effects=True, vmem_limit_bytes=60 << 20
        ),
        name="experts_in",
    )(h2, dy_all, targets, router_t, w_gate_up)


def experts_mid_kernel(
    cap,
    y_in,
    act_in,
    by_up_in,
    by_gate_in,
    gate_slots,
    wd_in,
    gated_out,
    d_gate_out,
    d_up_out,
    dots_ref,
    g_down_out,
    wd,
    ys,
    acts,
    by_ups,
    by_gates,
    gated,
    d_gate,
    d_up,
    staged,
    in_sem,
    out_sem,
    grad_sem,
):
    local_experts, hidden, model_width = wd_in.shape
    count = gate_slots.shape[1]
    slots = ys.shape[1]
    over_lanes = (((1,), (1,)), ((), ()))
    over_rows = (((0,), (0,)), ((), ()))
    inputs = ((y_in, ys), (wd_in, wd), (act_in, acts), (by_up_in, by_ups), (by_gate_in, by_gates))
    results = ((gated, gated_out), (d_gate, d_gate_out), (d_up, d_up_out))
    wide = 256
    tile = staged.shape[1]

    def fetch(n, e):
        return pltpu.make_async_copy(inputs[n][0].at[e], inputs[n][1].at[e], in_sem.at[n, e])

    def store(n, e):
        return pltpu.make_async_copy(results[n][0].at[e], results[n][1].at[e], out_sem.at[n, e])

    def put_grad(e, n, buf):
        rows = pl.ds(pl.multiple_of(n * tile, tile), tile)
        return pltpu.make_async_copy(staged.at[buf], g_down_out.at[e, rows], grad_sem.at[buf])

    for e in range(local_experts):
        for n in range(5):
            fetch(n, e).start()
    @pl.loop(0, local_experts)
    def _(e):
        for n in range(2):
            fetch(n, e).wait()
        gate = jnp.concatenate([gate_slots[e, q] for q in range(count)], axis=0)

        def step(n, dot):
            cols = pl.ds(pl.multiple_of(n * wide, wide), wide)
            grad_act = lax.dot_general(ys[e], wd[e, cols, :], over_lanes, preferred_element_type=F32)

            @pl.when(n == 0)
            def _():
                for kind in range(2, 5):
                    fetch(kind, e).wait()

            act = acts[e, :, cols].astype(F32)
            dot = dot + jnp.sum(act * grad_act, axis=1, keepdims=True)
            grad_act = grad_act * gate
            gated[e, :, cols] = (act * gate).astype(BF)
            d_up[e, :, cols] = (grad_act * by_ups[e, :, cols].astype(F32)).astype(BF)
            d_gate[e, :, cols] = (grad_act * by_gates[e, :, cols].astype(F32)).astype(BF)
            return dot

        dot = lax.fori_loop(0, hidden // wide, step, jnp.zeros((slots, 1), F32))
        for q in range(count):
            dots_ref[e, q] = dot[2 * cap * q : 2 * cap * (q + 1)]
        for n in range(3):
            store(n, e).start()

        @pl.loop(0, hidden // tile // 2)
        def _(m):
            for buf in range(2):
                n = 2 * m + buf

                @pl.when((m > 0) | (e > 0))
                def _():
                    put_grad(e, n, buf).wait()

                cols = pl.ds(pl.multiple_of(n * tile, tile), tile)
                staged[buf] = lax.dot_general(
                    gated[e, :, cols], ys[e], over_rows, preferred_element_type=F32
                ).astype(BF)
                put_grad(e, n, buf).start()

    for buf in range(2):
        put_grad(0, 0, buf).wait()
    for e in range(local_experts):
        for n in range(3):
            store(n, e).wait()


def experts_mid(grads, act, by_up, by_gate, gate_slots, w_down):
    local_experts, slots, model_width = grads.shape
    anywhere = pl.BlockSpec(memory_space=ANY)
    vmem = pl.BlockSpec(memory_space=pltpu.VMEM)
    thin = jax.ShapeDtypeStruct(act.shape, BF)
    return pl.pallas_call(
        partial(experts_mid_kernel, CAP),
        out_shape=[
            thin,
            thin,
            thin,
            jax.ShapeDtypeStruct(gate_slots.shape, F32),
            jax.ShapeDtypeStruct(w_down.shape, BF),
        ],
        in_specs=[anywhere] * 4 + [vmem, anywhere],
        out_specs=[anywhere] * 3 + [vmem, anywhere],
        scratch_shapes=[pltpu.VMEM(w_down.shape, BF), pltpu.VMEM(grads.shape, BF)]
        + [pltpu.VMEM(act.shape, BF)] * 6
        + [
            pltpu.VMEM((2, 256, model_width), BF),
            DMA((5, local_experts)),
            DMA((3, local_experts)),
            DMA((2,)),
        ],
        compiler_params=pltpu.CompilerParams(vmem_limit_bytes=60 << 20),
        cost_estimate=pl.CostEstimate(flops=18_000_000_000, bytes_accessed=60_000_000, transcendentals=0),
        name="experts_mid",
    )(grads, act, by_up, by_gate, gate_slots, w_down)


class StagedScatter(SplitScatter):
    def __init__(self, count, places, stage, bufs, sems):
        super().__init__(count, places, None, bufs, sems)
        self.stage = stage

    def to_sib(self, a, q):
        sib = self.places[2]
        src, dst = self.view(a, self.stage), self.view(a, self.sib[a].at[q])
        return remote(src, dst, self.sems[2].at[a, q], self.sems[5].at[a, q], fsdp=sib)

    def ready(self, a, q):
        self.to_sib(a, q).wait_recv()

    def finish(self):
        i, p, sib = self.places
        for a in range(2):
            for q in range(self.count):

                @pl.when(q > p)
                def _():
                    self.right(a, q).wait_send()

                @pl.when(q < p)
                def _():
                    self.left(a, q).wait_send()


class OuterGrads:
    def __init__(self, left, rights, out, scratch, steps):
        self.left, self.rights, self.out = left, rights, out
        self.tiles_in, self.held, self.staged, self.sems = scratch
        self.experts, self.width, _ = out.shape
        self.hidden = rights[0].shape[2]
        self.tile = self.staged.shape[1]
        self.tiles = self.width // self.tile
        self.units = self.experts * self.tiles
        self.share = -(-self.units // steps)

    def span(self, u):
        start = lax.rem(u, self.tiles) * self.tile
        return pl.ds(pl.multiple_of(start, self.tile), self.tile)

    def fetch(self, u):
        src = self.left.at[u // self.tiles, :, self.span(u)]
        return pltpu.make_async_copy(src, self.tiles_in.at[lax.rem(u, 2)], self.sems.at[0, lax.rem(u, 2)])

    def put(self, u):
        buf = lax.rem(u, 2)
        target = self.out.at[u // self.tiles, self.span(u)]
        return pltpu.make_async_copy(self.staged.at[buf], target, self.sems.at[1, buf])

    def hold(self, n):
        return pltpu.make_async_copy(self.rights[n], self.held.at[n], self.sems.at[2, n])

    def begin(self):
        for n in range(len(self.rights)):
            self.hold(n).start()
        self.fetch(0).start()

    def between(self, step):
        @pl.loop(step * self.share, jnp.minimum((step + 1) * self.share, self.units))
        def _(u):
            @pl.when(u == 0)
            def _():
                for n in range(len(self.rights)):
                    self.hold(n).wait()

            self.fetch(u).wait()

            @pl.when(u + 1 < self.units)
            def _():
                self.fetch(u + 1).start()

            @pl.when(u >= 2)
            def _():
                self.put(u - 2).wait()

            buf = lax.rem(u, 2)
            for n in range(len(self.rights)):
                self.staged[buf, :, n * self.hidden : (n + 1) * self.hidden] = lax.dot_general(
                    self.tiles_in[buf],
                    self.held[n, u // self.tiles],
                    (((0,), (0,)), ((), ())),
                    preferred_element_type=F32,
                ).astype(BF)
            self.put(u).start()

    def finish(self):
        self.put(self.units - 2).wait()
        self.put(self.units - 1).wait()


def outer_scratch(right, tile, factors):
    slots, hidden = right.shape[1:]
    return [
        pltpu.VMEM((2, slots, tile), BF),
        pltpu.VMEM((factors,) + right.shape, BF),
        pltpu.VMEM((2, tile, factors * hidden), BF),
        DMA((3, 2)),
    ]


def experts_out_kernel(
    count,
    cap,
    gated_in,
    d_gate_in,
    d_up_in,
    dots,
    targets,
    targets_t,
    probs_ref,
    router_t,
    wgu_in,
    wd_in,
    tokens_in,
    x_in,
    dy_in,
    gain_row,
    parts_a,
    parts_b,
    grad_ref,
    low_ref,
    small_ref,
    wgu,
    wd,
    gated,
    d_gate,
    d_up,
    parts,
    stage,
    own,
    sibling,
    inbox,
    w_sem,
    in_sem,
    part_sem,
    held_tokens,
    x_mid,
    dy,
    router_sum,
    row_sem,
    *sems,
):
    places = where_am_i()
    i, p, sib = places
    core = lax.rem(i, 2)
    local_experts, hidden, model_width = wd_in.shape
    tokens = targets.shape[2]
    experts = router_t.shape[0]
    first = i * local_experts
    over_lanes = (((1,), (1,)), ((), ()))
    line = StagedScatter(count, places, stage, (own, sibling, inbox), sems)
    block = 512
    take_down = pltpu.make_async_copy(wd_in, wd, w_sem.at[model_width // block])
    inputs = ((gated_in, gated), (d_gate_in, d_gate), (d_up_in, d_up))

    def weight(n):
        rows = pl.ds(pl.multiple_of(n * block, block), block)
        return pltpu.make_async_copy(wgu_in.at[:, rows], wgu.at[:, rows], w_sem.at[n])

    def fetch(n, q, buf):
        rows = pl.ds(pl.multiple_of(q * 2 * cap, 2 * cap), 2 * cap)
        return pltpu.make_async_copy(inputs[n][0].at[:, rows], inputs[n][1].at[buf], in_sem.at[n, buf])

    first_part = parts_a.shape[2]

    def put(n, q):
        src = parts.at[:, :, pl.ds(n * first_part, (parts_a, parts_b)[n].shape[2])]
        return pltpu.make_async_copy(src, (parts_a, parts_b)[n].at[pl.ds(2 * q, 2)], part_sem.at[n])

    def order(k):
        return chunk_order(count - 1 - k, p, count)

    for n in range(3):
        fetch(n, order(0), 0).start()
    for n in range(model_width // block):
        weight(n).start()
    take_down.start()
    take_x = pltpu.make_async_copy(x_in, x_mid, row_sem.at[0])
    take_dy = pltpu.make_async_copy(dy_in, dy, row_sem.at[1])
    take_x.start()
    take_dy.start()
    router_sum[...] = jnp.zeros_like(router_sum)
    greet(count, places)
    slot_rows = lax.broadcasted_iota(jnp.int32, (local_experts * cap, tokens), 0)
    slot_lanes = lax.broadcasted_iota(jnp.int32, (tokens, local_experts * cap), 1)
    expert_rows = lax.broadcasted_iota(jnp.int32, (experts, tokens), 0)

    def take_tokens(q):
        return pltpu.make_async_copy(tokens_in.at[pl.ds(2 * q, 2)], held_tokens, row_sem.at[2])

    def compute(k):
        q = order(k)
        buf = lax.rem(k, 2)
        take_tokens(q).start()
        picks, logits_low, logits_row = [], [], []
        for j in range(2):
            slot = 2 * q + j
            grad_probs = jnp.zeros((experts, tokens), F32)
            pick = None
            for e in range(local_experts):
                part = slice(e * cap, (e + 1) * cap)
                mask = (slot_rows == targets[slot, e : e + 1, :])[part]
                dot = dots[e, q, j * cap : (j + 1) * cap, :]
                row = jnp.sum(jnp.where(mask, dot, 0.0), axis=0, keepdims=True)
                grad_probs = jnp.where(expert_rows == first + e, row, grad_probs)
                hit = slot_lanes == targets_t[slot, :, e : e + 1]
                pick = hit if pick is None else pick | hit
            probs = probs_ref[slot]
            grad_logits = probs * (grad_probs - jnp.sum(probs * grad_probs, axis=0, keepdims=True))
            logits_row.append(grad_logits.astype(BF))
            picks.append(jnp.where(pick, 1.0, 0.0).astype(BF))
            logits_low.append(grad_logits.T.astype(BF))
        for n in range(3):
            fetch(n, q, buf).wait()

        @pl.when(k + 1 < count)
        def _():
            for n in range(3):
                fetch(n, order(k + 1), 1 - buf).start()

        @pl.when(k > 0)
        def _():
            line.to_sib(0, order(k - 1)).wait_send()
            line.to_sib(1, order(k - 1)).wait_send()

        @pl.loop(0, model_width // block)
        def _(n):
            cols = pl.ds(pl.multiple_of(n * block, block), block)

            @pl.when(k == 0)
            def _():
                weight(n).wait()

            grads = []
            for e in range(local_experts):
                grads.append(
                    lax.dot_general(
                        d_gate[buf, e], wgu[e, cols, 0:hidden], over_lanes, preferred_element_type=F32
                    )
                    + lax.dot_general(
                        d_up[buf, e], wgu[e, cols, hidden:], over_lanes, preferred_element_type=F32
                    )
                )
            for j in range(2):
                part = slice(j * cap, (j + 1) * cap)
                back = jnp.concatenate([value[part] for value in grads], axis=0).astype(BF)
                total = (
                    jnp.dot(picks[j], back, preferred_element_type=F32)
                    + jnp.dot(logits_low[j], router_t[:, cols], preferred_element_type=F32)
                ).astype(BF)

                @pl.when(core == j)
                def _():
                    own[q, :, cols] = total

                @pl.when(core != j)
                def _():
                    stage[:, cols] = total

            @pl.when(n == model_width // block // 2 - 1)
            def _():
                line.to_sib(0, q).start()

        line.to_sib(1, q).start()

        @pl.when(k > 0)
        def _():
            put(0, q).wait()
            put(1, q).wait()

        @pl.when(k == 0)
        def _():
            take_down.wait()

        take_tokens(q).wait()

        @pl.loop(0, model_width // block)
        def _(n):
            cols = pl.ds(pl.multiple_of(n * block, block), block)
            outs = []
            for e in range(local_experts):
                outs.append(jnp.dot(gated[buf, e], wd[e, :, cols], preferred_element_type=F32))
            for j in range(2):
                part = slice(j * cap, (j + 1) * cap)
                mine = jnp.concatenate([value[part] for value in outs], axis=0).astype(BF)
                parts[j, :, cols] = jnp.dot(picks[j], mine, preferred_element_type=F32).astype(BF)
            total = router_sum[:, cols]
            for j in range(2):
                total += jnp.dot(logits_row[j], held_tokens[j, :, cols], preferred_element_type=F32)
            router_sum[:, cols] = total

        put(0, q).start()
        put(1, q).start()

    @pl.loop(0, count)
    def _(k):
        compute(k)

        @pl.when(k < count - 1)
        def _():
            line.event(k)

    line.final(lambda a, q: None)
    put(0, 0).wait()
    put(1, 0).wait()
    line.to_sib(0, order(count - 1)).wait_send()
    line.to_sib(1, order(count - 1)).wait_send()
    take_x.wait()
    take_dy.wait()
    strip = 16

    def norm_back(n, total):
        rows = pl.ds(pl.multiple_of(n * strip, strip), strip)
        back = own[p, rows, :].astype(F32)
        x = x_mid[rows, :]
        scale = lax.rsqrt(jnp.mean(x * x, axis=1, keepdims=True) + EPSILON)
        u = gain_row[...] * back
        product = jnp.mean(u * x, axis=1, keepdims=True)
        grad = dy[rows, :].astype(F32) + scale * u - x * (scale * scale * scale * product)
        grad_ref[rows, :] = grad
        low_ref[rows, :] = grad.astype(BF)
        return total + jnp.sum(back * x * scale, axis=0, keepdims=True)

    norm_part = lax.fori_loop(0, tokens // strip, norm_back, jnp.zeros((1, model_width), F32))
    lanes = small_ref.shape[1]
    piece = 512
    for n in range(model_width // piece):
        cols = slice(n * piece, (n + 1) * piece)
        norm = jnp.broadcast_to(norm_part[:, cols], (8, piece))
        rest = jnp.zeros((lanes - experts - 8, piece), F32)
        small_ref[cols, :] = jnp.concatenate([router_sum[:, cols], norm, rest], axis=0).T

    line.finish()


def experts_out(
    gated,
    d_gate,
    d_up,
    dots,
    targets,
    targets_t,
    probs,
    router_t,
    w_gate_up,
    w_down,
    h2_all,
    x_mid,
    dy,
    gain_row,
    collective,
):
    local_experts, slots, hidden = gated.shape
    model_width = router_t.shape[1]
    shards, experts, tokens = probs.shape
    count = shards // 2
    anywhere = pl.BlockSpec(memory_space=ANY)
    vmem = pl.BlockSpec(memory_space=pltpu.VMEM)
    return pl.pallas_call(
        partial(experts_out_kernel, count, CAP),
        out_shape=[
            jax.ShapeDtypeStruct((shards, tokens, model_width // 2), BF),
            jax.ShapeDtypeStruct((shards, tokens, model_width // 2), BF),
            jax.ShapeDtypeStruct((tokens, model_width), F32),
            jax.ShapeDtypeStruct((tokens, model_width), BF),
            jax.ShapeDtypeStruct((model_width, 128), F32),
        ],
        in_specs=[anywhere] * 3 + [vmem] * 5 + [anywhere] * 5 + [vmem],
        out_specs=[anywhere, anywhere, vmem, vmem, vmem],
        scratch_shapes=[pltpu.VMEM(x.shape, BF) for x in (w_gate_up, w_down)]
        + [pltpu.VMEM((2, local_experts, 2 * CAP, hidden), BF)] * 3
        + [
            pltpu.VMEM((2, tokens, model_width), BF),
            pltpu.VMEM((tokens, model_width), BF),
            pltpu.VMEM((count, tokens, model_width), BF),
            pltpu.VMEM((count, tokens, model_width), BF),
            pltpu.VMEM((count + 1, tokens, model_width), BF),
            DMA((model_width // 512 + 1,)),
            DMA((3, 2)),
            DMA((2,)),
            pltpu.VMEM((2, tokens, model_width), BF),
            pltpu.VMEM((tokens, model_width), F32),
            pltpu.VMEM((tokens, model_width), BF),
            pltpu.VMEM((experts, model_width), F32),
            DMA((3,)),
        ]
        + [DMA((2, count))] * 7,
        compiler_params=pltpu.CompilerParams(
            collective_id=collective, has_side_effects=True, vmem_limit_bytes=67_043_328
        ),
        cost_estimate=pl.CostEstimate(flops=60_000_000_000, bytes_accessed=200_000_000, transcendentals=0),
        name="experts_out",
    )(
        gated,
        d_gate,
        d_up,
        dots,
        targets,
        targets_t,
        probs,
        router_t,
        w_gate_up,
        w_down,
        h2_all,
        x_mid,
        dy,
        gain_row,
    )


def rope_tables(seq_len, head_dim):
    half_dim = head_dim // 2
    inverse = np.float32(ROPE_BASE) ** (-(np.arange(half_dim, dtype=np.float32) * 2.0 / head_dim))
    angles = np.arange(seq_len, dtype=np.float32)[:, None] * inverse.astype(np.float32)[None, :]
    angles = np.concatenate([angles, angles], axis=-1).astype(np.float64)
    return (np.cos(angles).astype(np.float32), np.sin(angles).astype(np.float32))


def dot(left, right, sides=(1, 0), out=F32):
    return lax.dot_general(
        left, right, (((sides[0],), (sides[1],)), ((), ())), preferred_element_type=F32
    ).astype(out)


def inverse_rms(rows):
    return lax.rsqrt(jnp.mean(rows * rows, axis=-1, keepdims=True) + EPSILON)


def on_device(
    inputs,
    out_grad,
    doc_ids,
    routes,
    w_query,
    w_key,
    w_value,
    w_output,
    w_router,
    attn_gain,
    ffn_gain,
    query_gain,
    key_gain,
    w_gate,
    w_up,
    w_down,
):
    seq_count = lax.axis_size("seq")
    shards = lax.axis_size("fsdp")
    tok_rows, model_width = inputs.shape[1:]
    seq_len = tok_rows * seq_count
    rows = w_query.shape[0]
    width = model_width // seq_count
    local_experts = w_gate.shape[0]
    experts = w_router.shape[1]
    top_k = routes.shape[2]
    lanes = 128

    small = jnp.concatenate(
        [
            w_router,
            attn_gain[:, None],
            ffn_gain[:, None],
            jnp.zeros((rows, lanes - experts - 2), BF),
        ],
        axis=1,
    )
    gains = jnp.pad(jnp.stack([query_gain, key_gain]), ((0, 14), (0, lanes - rows)))
    wq, wk, wv, small_all, gains_all, routes_all, wo, x_all = gather_start(
        (w_query, w_key, w_value, small, gains, routes[0].T, w_output, inputs[0]), seq_count, shards, 0
    )
    x_all = x_all.reshape(seq_len, model_width)
    gate_up = jnp.concatenate([w_gate, w_up], axis=2)
    full_gate_up = lax.all_gather(gate_up, "seq", axis=1, tiled=True)
    full_down = lax.all_gather(w_down, "seq", axis=1, tiled=True)

    wq = wq.reshape(model_width, width)
    wk = wk.reshape(model_width, width)
    wv = wv.reshape(model_width, width)
    small_all = small_all.reshape(model_width, lanes)
    w_r = small_all[:, :experts]
    gain_a = small_all[:, experts].astype(F32)
    gain_f = small_all[:, experts + 1].astype(F32)
    gq = gains_all[:, 0, :rows].reshape(1, width).astype(F32)
    gk = gains_all[:, 1, :rows].reshape(1, width).astype(F32)

    x_float = x_all.astype(F32)
    h1 = (x_float * inverse_rms(x_float) * gain_a).astype(BF)
    h1 = lax.optimization_barrier(h1)
    q_raw, k_raw = lax.optimization_barrier((dot(h1, wq), dot(h1, wk)))
    values = dot(h1, wv, out=BF)
    squares = jnp.stack(
        [jnp.sum(q_raw * q_raw, axis=1), jnp.sum(k_raw * k_raw, axis=1)]
        + [jnp.ones((seq_len,), F32)] * 6
    )
    cos, sin = rope_tables(seq_len, HEAD)
    doc_row = doc_ids
    doc_col = doc_ids.reshape(seq_len, 1)
    attended, q_low, k_low, scales = attend(
        q_raw, k_raw, values, squares, gq, gk, cos, sin, doc_col, doc_row, model_width, seq_count, 1
    )
    wo = wo.reshape(width, model_width)
    projected = dot(attended, wo, out=BF).reshape(seq_count, tok_rows, model_width)
    rows_in = inputs[0].astype(F32)
    grad_rows = out_grad[0].astype(F32)
    summed, dy_all, targets, targets_t = middle(projected, out_grad[0], routes_all, local_experts, 2)
    x_mid = rows_in + summed
    scale_f = inverse_rms(x_mid)
    h2 = (x_mid * scale_f * gain_f).astype(BF)

    router_t = w_r.T
    h2_all, expert_in, grad_slots, act, by_up, by_gate, gate_slots, gate_probs = experts_in(
        h2, dy_all, targets, router_t, full_gate_up, 3
    )
    gated, d_gate, d_up, dots_slots, g_down = experts_mid(
        grad_slots, act, by_up, by_gate, gate_slots, full_down
    )
    parts_a, parts_b, grad_mid, grad_low, small_part = experts_out(
        gated,
        d_gate,
        d_up,
        dots_slots,
        targets,
        targets_t,
        gate_probs,
        router_t,
        full_gate_up,
        full_down,
        h2_all,
        x_mid,
        out_grad[0],
        gain_f[None],
        4,
    )

    def spread(part):
        return lax.psum_scatter(part, "seq", scatter_dimension=1, tiled=True)

    g_down = spread(g_down)
    grad_low, g_down = lax.optimization_barrier((grad_low, g_down))

    d_attn, sum_a, g_gate_up = turn_back(grad_low, parts_a, expert_in, d_gate, d_up, seq_count, shards, 5)
    g_gate_up = spread(g_gate_up)
    d_attn = d_attn.reshape(seq_len, model_width)
    d_heads = dot(d_attn, wo, (1, 1), BF)
    dq_low, dk_low, dv_low, gains_part, sum_b = attend_back(
        q_low,
        k_low,
        values,
        d_heads,
        q_raw,
        k_raw,
        scales,
        gq,
        gk,
        cos,
        sin,
        doc_col,
        doc_row,
        parts_b,
        rows,
        model_width,
        seq_count,
        6,
    )
    result = x_mid + jnp.concatenate([sum_a, sum_b], axis=1).astype(F32)

    sheet = (seq_count, shards, rows, width)
    g_query, g_key, g_value, g_output, g_small, g_gains, grad_h1 = scatter_end(
        (
            dot(h1, dq_low, (0, 0), BF).reshape(sheet),
            dot(h1, dk_low, (0, 0), BF).reshape(sheet),
            dot(h1, dv_low, (0, 0), BF).reshape(sheet),
            dot(attended, d_attn, (0, 0), BF).reshape(shards, rows, model_width),
            small_part.reshape(seq_count, shards, rows, lanes),
            gains_part,
        ),
        (dq_low, dk_low, dv_low, wq, wk, wv),
        seq_count,
        shards,
        7,
    )
    g_query, g_key, g_value = (g_query.astype(F32), g_key.astype(F32), g_value.astype(F32))

    scale_a = inverse_rms(rows_in)
    u_rows = gain_a * grad_h1
    input_grad = (
        grad_mid
        + scale_a * u_rows
        - rows_in * scale_a**3 * jnp.mean(u_rows * rows_in, axis=-1, keepdims=True)
    )
    pairs = (
        w_query.astype(F32) * g_query + w_key.astype(F32) * g_key + w_value.astype(F32) * g_value
    )
    g_attn_gain = jnp.sum(pairs, axis=1) / attn_gain.astype(F32)

    return (
        result.astype(BF)[None],
        input_grad[None],
        g_query,
        g_key,
        g_value,
        g_output.astype(F32),
        g_small[:, :experts],
        g_attn_gain,
        g_small[:, experts],
        g_gains[0, :rows],
        g_gains[1, :rows],
        g_gate_up[:, :, : g_gate_up.shape[2] // 2].astype(F32),
        g_gate_up[:, :, g_gate_up.shape[2] // 2 :].astype(F32),
        g_down.astype(F32),
    )


def solution(mesh):
    rows = P("fsdp", "seq", None)
    sheet = P(("seq", "fsdp"), None)
    line = P(("seq", "fsdp"))
    return jax.shard_map(
        on_device,
        mesh=mesh,
        in_specs=(rows, rows, P("fsdp", None), rows) + (sheet,) * 5 + (line,) * 4 + (rows,) * 3,
        out_specs=(rows, rows) + (sheet,) * 5 + (line,) * 4 + (rows,) * 3,
        check_vma=False,
    )
```
